32 devices in a mesh: grp: 8 (over y, x, core), fsdp: 4 (over z).
Axes of the slice: x: 2, y: 2, z: 4, core: 2. Of those that a mesh axis runs over, the one named last changes fastest.
Arguments:
- tokens: bfloat16 [10240, 768], P(('grp', 'fsdp')), may hold values from -6 to 6
- cotangent: bfloat16 [10240, 768], P(('grp', 'fsdp')), may hold values from -6 to 6
- prev_logits: float32 [10240, 12], P(('grp', 'fsdp')), may hold values from -6 to 6
- lengths: int32 [8, 8], P('grp'), may hold values from 64 to 256, as said below
- dealing: int32 [8, 8], P('grp'), may hold values from 0 to 7, as said below
- routes: int32 [10240, 2], P(('grp', 'fsdp')), may hold values from 0 to 11, all different within a row; in each aligned block of 320 rows (0 to 319, 320 to 639, ...) at most 80 rows name the same one
- gain_one: bfloat16 [768], P(('grp', 'fsdp')), may hold values from 0.5 to 1.5
- w_query: bfloat16 [768, 768], P('fsdp', 'grp'), may hold values from -0.21875 to 0.21875
- w_key: bfloat16 [768, 768], P('fsdp', 'grp'), may hold values from -0.21875 to 0.21875
- w_value: bfloat16 [768, 768], P('fsdp', 'grp'), may hold values from -0.21875 to 0.21875
- w_out: bfloat16 [768, 768], P('fsdp', 'grp'), may hold values from -2.5 to 2.5
- gain_two: bfloat16 [768], P(('grp', 'fsdp')), may hold values from 0.5 to 1.5
- w_router: bfloat16 [768, 12], P(('grp', 'fsdp')), may hold values from -0.109375 to 0.109375
- w_mix: bfloat16 [12, 12], replicated, may hold values from -0.875 to 0.875
- w_const: bfloat16 [768, 4], P(('grp', 'fsdp')), may hold values from -0.21875 to 0.21875
- v_const: bfloat16 [768, 2], P(('grp', 'fsdp')), may hold values from -6 to 6
- w_gate: bfloat16 [8, 768, 2048], P(None, 'fsdp', 'grp'), may hold values from -0.21875 to 0.21875
- w_up: bfloat16 [8, 768, 2048], P(None, 'fsdp', 'grp'), may hold values from -0.21875 to 0.21875
- w_down: bfloat16 [8, 2048, 768], P(None, 'grp', 'fsdp'), may hold values from -1 to 1
Outputs:
- output: bfloat16 [10240, 768], P(('grp', 'fsdp'))
- grad_tokens: float32 [10240, 768], P(('grp', 'fsdp'))
- grad_prev: float32 [10240, 12], P(('grp', 'fsdp'))
- grad_gain_one: float32 [768], P(('grp', 'fsdp'))
- grad_query: float32 [768, 768], P('fsdp', 'grp')
- grad_key: float32 [768, 768], P('fsdp', 'grp')
- grad_value: float32 [768, 768], P('fsdp', 'grp')
- grad_out_proj: float32 [768, 768], P('fsdp', 'grp')
- grad_gain_two: float32 [768], P(('grp', 'fsdp'))
- grad_router: float32 [768, 12], P(('grp', 'fsdp'))
- grad_mix: float32 [12, 12], replicated
- grad_const: float32 [768, 4], P(('grp', 'fsdp'))
- grad_vconst: float32 [768, 2], P(('grp', 'fsdp'))
- grad_gate: float32 [8, 768, 2048], P(None, 'fsdp', 'grp')
- grad_up: float32 [8, 768, 2048], P(None, 'fsdp', 'grp')
- grad_down: float32 [8, 2048, 768], P(None, 'grp', 'fsdp')
The draws below stay inside these ranges and needn't reach their ends.
Inputs may be any that keep to these rules, and one draw needn't show every extreme that they name: Row g holds the lengths of group g's 8 sequences in the given order; they sum to 1280. The two sequences that dealing sends to one device have lengths that, each rounded up to a multiple of 128, sum to 384. `dealing`: each row is a permutation of the group's sequence numbers; entries 2i and 2i + 1 name the two sequences that device i of fsdp holds, in that order. `routes`: the two experts of a row differ; no expert is named by more than 80 rows of one device.
All inputs are finite; a program needn't handle non-finite values.
Results may differ from the reference program's by a relative error of at most 0.02.
Values may be sent and summed in bfloat16 or wider, within the bound.
A program may use at most 384 MiB of HBM per device.

```python
import math
import jax
import jax.numpy as jnp
import numpy as np
from jax import lax

D = 768
HEADS = 12
HEAD_DIM = 64
FF = 2048
E = 8
CONSTS = 2
TOP = 2
BLOCK = 128
SLOT_BLOCKS = 3
EXPERTS_ALL = 12
PAD = 64
CAP = 384
TOK_DEV = 320
TOK_GRP = 1280
GROUPS = 8
SEQS = 8
TOKENS = 10240
MOST = 80


def sequence_plan(key):
    base = jax.random.fold_in(key, 7)
    per_group = SEQS // 2
    first_blocks = jax.random.randint(jax.random.fold_in(base, 1), (GROUPS, per_group), 1, SLOT_BLOCKS)
    first_pad = jax.random.randint(jax.random.fold_in(base, 2), (GROUPS, per_group), 0, PAD + 1)
    full_dev = jax.random.randint(jax.random.fold_in(base, 3), (GROUPS,), 0, per_group)
    forced = jnp.arange(per_group, dtype=jnp.int32)[None, :] == full_dev[:, None]
    first_blocks = jnp.where(forced, SLOT_BLOCKS - 1, first_blocks)
    first_pad = jnp.where(forced, 0, first_pad)
    first_len = first_blocks * BLOCK - first_pad
    second_len = (SLOT_BLOCKS - first_blocks) * BLOCK - (PAD - first_pad)
    dealt_len = jnp.stack([first_len, second_len], axis=2).reshape(GROUPS, SEQS)

    def one_order(subkey):
        return jax.random.permutation(subkey, SEQS)
    orders = jax.vmap(one_order)(jax.random.split(jax.random.fold_in(base, 4), GROUPS)).astype(jnp.int32)
    group_ids = jnp.broadcast_to(jnp.arange(GROUPS, dtype=jnp.int32)[:, None], (GROUPS, SEQS))
    lengths = jnp.zeros((GROUPS, SEQS), jnp.int32).at[group_ids, orders].set(dealt_len.astype(jnp.int32))
    return (lengths, orders)


def draw_lengths(key, part):
    return sequence_plan(key)[0]


def draw_dealing(key, part):
    return sequence_plan(key)[1]


def level_of(key, dims, cuts, smallest, top_value):
    def one(dim, blocks):
        draws = jax.random.uniform(jax.random.fold_in(jax.random.fold_in(key, 6), dim), (blocks,), jnp.float32, smallest / len(cuts), top_value / len(cuts))
        return jnp.repeat(jnp.exp(draws), dims[dim] // blocks).reshape((-1,) + (1,) * (len(dims) - dim - 1))

    loudness = one(*cuts[0])
    for cut in cuts[1:]:
        loudness = loudness * one(*cut)
    return loudness


def shared_out(stream_key, own, number, rows, count, top, bound, slope):
    order = jax.random.permutation(stream_key, count)
    packed, ordinary = shares(count, rows * top, bound, slope, True), shares(count, rows * top, bound, slope, False)
    places = jnp.arange(count)

    def named(tallies, rotation):
        used = int((tallies > 0).sum())
        fixed = max(1, used // 4)
        shifted = fixed + (places - fixed + rotation * (used - fixed)) % max(1, count - fixed)
        return jnp.zeros((count,), jnp.int32).at[order[jnp.where(places < fixed, places, shifted)]].set(jnp.asarray(tallies, jnp.int32))

    tallies = jnp.where(number % 4 == 0, named(packed, number // 4), named(ordinary, number - number // 4 - 1))
    mixed = jax.random.permutation(jax.random.fold_in(own, 3), count)
    giver, taker = mixed[0:count // 2 * 2:2], mixed[1:count // 2 * 2:2]
    slack = jnp.minimum(tallies[giver] - 1, bound - tallies[taker]) // 2
    slack = jnp.where((giver == order[0]) | (taker == order[0]) | (tallies[taker] == 0), 0, jnp.maximum(slack, 0))
    shifted = jax.random.randint(jax.random.fold_in(own, 4), (count // 2,), 0, 1 << 20) % (slack + 1)
    tallies = tallies.at[giver].add(-shifted).at[taker].add(shifted)
    labels = jnp.searchsorted(jnp.cumsum(tallies), jnp.arange(rows * top), side="right").astype(jnp.int32)
    listing = labels.reshape(top, rows).T
    listing = listing[jax.random.permutation(jax.random.fold_in(own, 1), rows)]
    rotation = jax.random.randint(jax.random.fold_in(own, 2), (rows, 1), 0, top)
    return jnp.take_along_axis(listing, (jnp.arange(top)[None, :] + rotation) % top, axis=1)


def shares(count, total, reach, lean, full):
    loads = [(1 << 20) // math.isqrt(standing ** lean) + 1 for standing in range(1, count + 1)]
    largest = reach if full else min(reach, max(-(-total // count), total * loads[0] // sum(loads)))
    least = 1 if total - largest >= count - 1 else 0
    holding, spare = [largest] + [least] * (count - 1), total - largest - least * (count - 1)
    while spare > 0:
        candidates = [i for i in range(1, count) if holding[i] < largest] or [i for i in range(1, count) if holding[i] < reach]
        whole, remaining = sum([loads[i] for i in candidates]), spare
        for i in candidates:
            extra = min(reach - holding[i], max(1, remaining * loads[i] // whole), spare)
            holding[i] = holding[i] + extra
            spare = spare - extra
    return np.array(holding)


def centred(stream_key, shape, spread, limit, cuts=(), held_as=jnp.bfloat16):
    array = spread * jax.random.normal(stream_key, shape, jnp.float32)
    if cuts:
        array = array * level_of(stream_key, shape, cuts, -0.22, 0.18)
    return jnp.clip(array, -limit, limit).astype(held_as)


def setup_inputs(seed: int = 0) -> dict:
    splits = jax.random.split(jax.random.key(seed), 20)
    tokens = centred(splits[0], (TOKENS, D), 1.0, 6.0, ((0, 32),))
    cotangent = centred(splits[1], (TOKENS, D), 1.0, 6.0, ((0, 32),))
    prev_logits = centred(splits[2], (TOKENS, EXPERTS_ALL), 1.0, 6.0, ((0, 32),), jnp.float32)
    lengths = draw_lengths(jax.random.fold_in(splits[19], 71), 0)
    dealing = draw_dealing(jax.random.fold_in(splits[19], 71), 0)
    routes_keys = jax.random.split(jax.random.fold_in(splits[5], 1), TOKENS // TOK_DEV)
    routes_turns = jax.random.permutation(jax.random.fold_in(splits[5], 3), TOKENS // TOK_DEV)
    routes = jax.vmap(lambda own, number: shared_out(jax.random.fold_in(splits[5], 2), own, number, TOK_DEV, EXPERTS_ALL, TOP, MOST, 0))(routes_keys, routes_turns).reshape((TOKENS, TOP))
    gain_one = jnp.clip(1.0 + 0.1 * jax.random.normal(splits[6], (D,), jnp.float32), 0.5, 1.5).astype(jnp.bfloat16)
    w_query = centred(splits[7], (D, D), D ** -0.5, 0.21875, ((0, 4), (1, 8)))
    w_key = centred(splits[8], (D, D), D ** -0.5, 0.21875, ((0, 4), (1, 8)))
    w_value = centred(splits[9], (D, D), D ** -0.5, 0.21875, ((0, 4), (1, 8)))
    w_out = centred(splits[10], (D, D), (D // 128) ** -0.5, 2.5, ((0, 4), (1, 8)))
    gain_two = jnp.clip(1.0 + 0.1 * jax.random.normal(splits[11], (D,), jnp.float32), 0.5, 1.5).astype(jnp.bfloat16)
    w_router = centred(splits[12], (D, EXPERTS_ALL), (4 * D) ** -0.5, 0.109375, ((0, 32),))
    w_mix = centred(splits[13], (EXPERTS_ALL, EXPERTS_ALL), (4 * EXPERTS_ALL) ** -0.5, 0.875)
    w_const = centred(splits[14], (D, 2 * CONSTS), D ** -0.5, 0.21875, ((0, 32),))
    v_const = centred(splits[15], (D, CONSTS), 1.0, 6.0, ((0, 32),))
    w_gate = centred(splits[16], (E, D, FF), D ** -0.5, 0.21875, ((1, 4), (2, 8)))
    w_up = centred(splits[17], (E, D, FF), D ** -0.5, 0.21875, ((1, 4), (2, 8)))
    w_down = centred(splits[18], (E, FF, D), (FF // 64) ** -0.5, 1.0, ((1, 8), (2, 4)))
    return dict(tokens=tokens, cotangent=cotangent, prev_logits=prev_logits, lengths=lengths, dealing=dealing, routes=routes, gain_one=gain_one, w_query=w_query, w_key=w_key, w_value=w_value, w_out=w_out, gain_two=gain_two, w_router=w_router, w_mix=w_mix, w_const=w_const, v_const=v_const, w_gate=w_gate, w_up=w_up, w_down=w_down)


@jax.custom_vjp
def low(v):
    return lax.optimization_barrier(v.astype(jnp.bfloat16)).astype(jnp.float32)

@jax.custom_vjp
def low_back(v):
    return v

def low_keep(v):
    return (low(v), None)

def low_pass(kept, grad):
    return (grad,)

def back_keep(v):
    return (v, None)

def back_low(kept, grad):
    return (low(grad),)
low.defvjp(low_keep, low_pass)
low_back.defvjp(back_keep, back_low)
NORM_EPS = 1e-05
EXACT = lax.Precision.HIGHEST

def matmul(left_side, right_side):
    return jnp.dot(left_side, right_side, precision=EXACT, preferred_element_type=jnp.float32)

def rms_scale(values, gain_vec):
    return values * lax.rsqrt(lax.optimization_barrier(jnp.mean(values * values, axis=-1, keepdims=True)) + NORM_EPS) * gain_vec

def rotation_tables(positions, head_dim):
    half_dim = head_dim // 2
    inv_freq = jnp.exp(jnp.arange(half_dim, dtype=jnp.float32) * (-2.0 * math.log(10000.0) / head_dim))
    angles = positions.astype(jnp.float32)[:, None] * inv_freq[None, :]
    return (jnp.cos(angles), jnp.sin(angles))

def rotate(values, cos_table, sin_table):
    row_count = values.shape[0]
    half_dim = cos_table.shape[1]
    heads_view = values.reshape(row_count, -1, 2 * half_dim)
    front_half = heads_view[:, :, :half_dim]
    back_half = heads_view[:, :, half_dim:]
    cos_view = cos_table[:, None, :]
    sin_view = sin_table[:, None, :]
    turned = jnp.concatenate([front_half * cos_view - back_half * sin_view, back_half * cos_view + front_half * sin_view], axis=2)
    return turned.reshape(row_count, -1)

def take_rows(table_rows, row_index):
    return jnp.take(table_rows, row_index, axis=0)

def layout(lengths, dealing):
    per_group = SEQS // 2
    seq_starts = jnp.cumsum(lengths, axis=1) - lengths
    padded = (lengths + BLOCK - 1) // BLOCK * BLOCK
    dealt_len = jnp.take_along_axis(lengths, dealing, axis=1)
    dealt_pad = jnp.take_along_axis(padded, dealing, axis=1)
    dealt_start = jnp.take_along_axis(seq_starts, dealing, axis=1)
    row_ids = jnp.arange(CAP, dtype=jnp.int32)[None, None, :]
    lead_pad = dealt_pad[:, 0::2][:, :, None]
    second = row_ids >= lead_pad
    position = row_ids - jnp.where(second, lead_pad, 0)
    seq_limit = jnp.where(second, dealt_len[:, 1::2][:, :, None], dealt_len[:, 0::2][:, :, None])
    live_rows = position < seq_limit
    source = jnp.where(second, dealt_start[:, 1::2][:, :, None], dealt_start[:, 0::2][:, :, None]) + position
    source = jnp.where(live_rows, source, TOK_GRP).reshape(GROUPS, per_group * CAP).astype(jnp.int32)

    def fill_target(source_row):
        return jnp.zeros((TOK_GRP,), jnp.int32).at[source_row].set(jnp.arange(per_group * CAP, dtype=jnp.int32), mode='drop')
    target = jax.vmap(fill_target)(source)
    shape_blocks = (GROUPS * per_group, CAP)
    return (source, position.reshape(shape_blocks).astype(jnp.int32), second.reshape(shape_blocks), live_rows.reshape(shape_blocks), target)

def reference(tokens, cotangent, prev_logits, lengths, dealing, routes, gain_one, w_query, w_key, w_value, w_out, gain_two, w_router, w_mix, w_const, v_const, w_gate, w_up, w_down):
    per_group = SEQS // 2
    block_count = GROUPS * per_group
    source, position, second, live_rows, target = layout(lengths, dealing)
    scale = HEAD_DIM ** (-0.5)

    def forward(tokens_f, prev_f, gain_one_f, query_w, key_w, value_w, out_w, gain_two_f, router_w, mix_w, const_w, vconst_f, gate_w_all, up_w_all, down_w_all):

        def attend_block(block_x, block_pos, block_seg, block_live):
            normed_one = low(rms_scale(block_x, gain_one_f))
            cos_table, sin_table = rotation_tables(block_pos, HEAD_DIM)
            query = low(rotate(low_back(matmul(normed_one, query_w)), cos_table, sin_table))
            keyed = low(rotate(low_back(matmul(normed_one, key_w)), cos_table, sin_table))
            values_proj = low(low_back(matmul(normed_one, value_w)))
            allowed = (block_seg[:, None] == block_seg[None, :]) & (block_pos[None, :] <= block_pos[:, None]) & block_live[None, :]
            query_heads = query.reshape(CAP, HEADS, HEAD_DIM)
            key_heads = keyed.reshape(CAP, HEADS, HEAD_DIM)
            value_heads = values_proj.reshape(CAP, HEADS, HEAD_DIM)
            scores = low_back(jnp.einsum('qhd,khd->hqk', query_heads, key_heads, precision=EXACT) * scale)
            scores = jnp.where(allowed[None], scores, -1e+30)
            row_top = lax.optimization_barrier(jnp.max(scores, axis=-1, keepdims=True))
            weights_exp = jnp.exp(scores - row_top)
            attn_probs = weights_exp / lax.optimization_barrier(jnp.sum(weights_exp, axis=-1, keepdims=True))
            mixed = jnp.einsum('hqk,khd->qhd', low(attn_probs), value_heads, precision=EXACT).reshape(CAP, D)
            mixed = low(low_back(mixed))
            return low(low_back(matmul(mixed, out_w)))

        def expert_block(resid_rows, prev_rows, route_rows):
            normed = rms_scale(resid_rows, gain_two_f)
            narrow = low(normed)
            logits = matmul(narrow, router_w) + matmul(prev_rows, mix_w)
            route_probs = jax.nn.softmax(logits, axis=-1)
            expert_ids = jnp.arange(EXPERTS_ALL, dtype=jnp.int32)
            chosen = lax.optimization_barrier(jnp.sum((route_rows[:, :, None] == expert_ids[None, None, :]).astype(jnp.float32), axis=1))
            gate_weights = route_probs * chosen
            result = resid_rows + gate_weights[:, E + 1:E + 2] * normed
            const_logits = matmul(narrow, const_w)
            for const_idx in range(CONSTS):
                const_mix = jax.nn.softmax(const_logits[:, 2 * const_idx:2 * const_idx + 2], axis=-1)
                branch = const_mix[:, 0:1] * normed + const_mix[:, 1:2] * vconst_f[:, const_idx][None, :]
                result = result + gate_weights[:, E + 2 + const_idx:E + 3 + const_idx] * branch
            for expert in range(E):
                gate_part = low_back(matmul(narrow, gate_w_all[expert]))
                up_part = low_back(matmul(narrow, up_w_all[expert]))
                hidden = low(jax.nn.silu(gate_part) * up_part)
                result = result + gate_weights[:, expert:expert + 1] * low_back(matmul(hidden, down_w_all[expert]))
            return result
        grouped = tokens_f.reshape(GROUPS, TOK_GRP, D)
        padded_in = jnp.concatenate([grouped, jnp.zeros((GROUPS, 1, D), jnp.float32)], axis=1)
        dealt = low_back(jax.vmap(take_rows)(padded_in, source)).reshape(block_count, CAP, D)
        attn_out = lax.map(jax.checkpoint(lambda items: attend_block(items[0], items[1], items[2], items[3])), (dealt, position, second, live_rows))
        attn_out = attn_out.reshape(GROUPS, per_group * CAP, D)
        returned = jax.vmap(take_rows)(attn_out, target).reshape(TOKENS, D)
        resid = tokens_f + returned
        result = lax.map(jax.checkpoint(lambda items: expert_block(items[0], items[1], items[2])), (resid.reshape(block_count, TOK_DEV, D), prev_f.reshape(block_count, TOK_DEV, EXPERTS_ALL), routes.reshape(block_count, TOK_DEV, TOP)))
        return result.reshape(TOKENS, D)
    output, pullback = jax.vjp(forward, tokens.astype(jnp.float32), prev_logits, gain_one.astype(jnp.float32), w_query.astype(jnp.float32), w_key.astype(jnp.float32), w_value.astype(jnp.float32), w_out.astype(jnp.float32), gain_two.astype(jnp.float32), w_router.astype(jnp.float32), w_mix.astype(jnp.float32), w_const.astype(jnp.float32), v_const.astype(jnp.float32), w_gate.astype(jnp.float32), w_up.astype(jnp.float32), w_down.astype(jnp.float32))
    gradients = pullback(cotangent.astype(jnp.float32))
    return (output.astype(jnp.bfloat16), gradients[0], gradients[1], gradients[2], gradients[3], gradients[4], gradients[5], gradients[6], gradients[7], gradients[8], gradients[9], gradients[10], gradients[11], gradients[12], gradients[13], gradients[14])
```

```python
import math

import jax
import jax.numpy as jnp
from jax import lax
from jax.experimental import pallas as pl
from jax.experimental.pallas import tpu as pltpu
from jax.sharding import PartitionSpec as P

HEADS = 12
HEAD_DIM = 64
E = 8
CONSTS = 2
BLOCK = 128
EXPERTS_ALL = 12
CAP = 384
TOK_DEV = 320
MOST = 80


NORM_EPS = 1e-05
EXACT = lax.Precision.HIGHEST


def rotation_tables(positions, head_dim):
    half_dim = head_dim // 2
    inv_freq = jnp.exp(
        jnp.arange(half_dim, dtype=jnp.float32) * (-2.0 * math.log(10000.0) / head_dim)
    )
    angles = positions.astype(jnp.float32)[:, None] * inv_freq[None, :]
    return (jnp.cos(angles), jnp.sin(angles))


def rotate(values, cos_table, sin_table):
    row_count = values.shape[0]
    half_dim = cos_table.shape[1]
    heads_view = values.reshape(row_count, -1, 2 * half_dim)
    front_half = heads_view[:, :, :half_dim]
    back_half = heads_view[:, :, half_dim:]
    cos_view = cos_table[:, None, :]
    sin_view = sin_table[:, None, :]
    turned = jnp.concatenate(
        [
            front_half * cos_view - back_half * sin_view,
            back_half * cos_view + front_half * sin_view,
        ],
        axis=2,
    )
    return turned.reshape(row_count, -1)


def exact_dot(left_side, right_side):
    return jnp.dot(left_side, right_side, precision=EXACT, preferred_element_type=jnp.float32)


def per_device(
    tokens,
    cotangent,
    prev_logits,
    lengths,
    dealing,
    routes,
    gain_one,
    w_query,
    w_key,
    w_value,
    w_out,
    gain_two,
    w_router,
    w_mix,
    w_const,
    v_const,
    w_gate,
    w_up,
    w_down,
):
    groups = lax.axis_size("grp")
    dealers = lax.axis_size("fsdp")
    device = lax.axis_index("fsdp")
    model_width = tokens.shape[1]
    per_shard = model_width // (groups * dealers)
    pairs = HEADS // 2
    pair_width = 2 * HEAD_DIM
    scale = HEAD_DIM ** (-0.5)
    seq_len = lengths[0]
    deal_order = dealing[0]
    seq_count = seq_len.shape[0]
    seq_ids = jnp.arange(seq_count, dtype=jnp.int32)
    seq_ends = jnp.cumsum(seq_len)
    starts = seq_ends - seq_len
    padded = (seq_len + BLOCK - 1) // BLOCK * BLOCK
    order_hot = (deal_order[:, None] == seq_ids[None, :]).astype(jnp.int32)
    dealt_len = jnp.sum(order_hot * seq_len[None, :], axis=1)
    dealt_pad = jnp.sum(order_hot * padded[None, :], axis=1)
    dealt_start = jnp.sum(order_hot * starts[None, :], axis=1)
    slot_of = jnp.sum(order_hot * seq_ids[:, None], axis=0)
    pair_index = 2 * device
    row_ids = jnp.arange(CAP, dtype=jnp.int32)
    in_second = row_ids >= dealt_pad[pair_index]
    position = row_ids - jnp.where(in_second, dealt_pad[pair_index], 0)
    seq_limit = jnp.where(in_second, dealt_len[pair_index + 1], dealt_len[pair_index])
    live_rows = position < seq_limit
    source = jnp.where(in_second, dealt_start[pair_index + 1], dealt_start[pair_index]) + position
    source = jnp.where(live_rows, source, -1)
    given_rows = device * TOK_DEV + jnp.arange(TOK_DEV, dtype=jnp.int32)
    seq_hot = (
        (given_rows[:, None] >= starts[None, :]) & (given_rows[:, None] < seq_ends[None, :])
    ).astype(jnp.int32)
    offset_in = given_rows - jnp.sum(seq_hot * starts[None, :], axis=1)
    slot_rank = jnp.sum(seq_hot * slot_of[None, :], axis=1)
    is_second = slot_rank % 2
    lead_pad = jnp.take(dealt_pad, slot_rank - is_second)
    target = slot_rank // 2 * CAP + jnp.where(is_second == 1, lead_pad, 0) + offset_in

    def deal(values):
        shard_rows = lax.all_gather(values, "fsdp", axis=0, tiled=True)
        row_span = shard_rows.shape[0]
        inside = (source >= 0) & (source < row_span)
        taken_rows = jnp.take(shard_rows, jnp.clip(source, 0, row_span - 1), axis=0)
        return jnp.where(inside[:, None], taken_rows, jnp.zeros((CAP, model_width), jnp.bfloat16))

    def give_back(values):
        shard_rows = lax.all_gather(values, "fsdp", axis=0, tiled=True)
        row_span = shard_rows.shape[0]
        inside = (target >= 0) & (target < row_span)
        taken_rows = jnp.take(shard_rows, jnp.clip(target, 0, row_span - 1), axis=0)
        return jnp.where(
            inside[:, None], taken_rows, jnp.zeros((TOK_DEV, model_width), jnp.bfloat16)
        )

    def collect():
        gate_in, up_in, down_in = (w_gate, w_up, w_down)
        sectioned = (
            lax.all_gather(gain_one, "fsdp", axis=0, tiled=True),
            lax.all_gather(w_query, "fsdp", axis=0, tiled=True),
            lax.all_gather(w_key, "fsdp", axis=0, tiled=True),
            lax.all_gather(w_value, "fsdp", axis=0, tiled=True),
            lax.all_gather(w_out, "fsdp", axis=0, tiled=True),
            lax.all_gather(gain_two, "fsdp", axis=0, tiled=True),
            lax.all_gather(w_router, "fsdp", axis=0, tiled=True),
            lax.all_gather(w_const, "fsdp", axis=0, tiled=True),
            lax.all_gather(v_const, "fsdp", axis=0, tiled=True),
            lax.all_gather(gate_in, "fsdp", axis=1, tiled=True),
            lax.all_gather(up_in, "fsdp", axis=1, tiled=True),
            lax.all_gather(down_in, "fsdp", axis=2, tiled=True),
        )
        (
            part_g1,
            part_q,
            part_k,
            part_v,
            part_o,
            part_g2,
            part_r,
            part_c,
            part_vc,
            part_gate,
            part_up,
            part_down,
        ) = sectioned
        small = (
            lax.all_gather(part_g1, "grp", axis=0, tiled=True),
            lax.all_gather(part_q, "grp", axis=1, tiled=True),
            lax.all_gather(part_k, "grp", axis=1, tiled=True),
            lax.all_gather(part_v, "grp", axis=1, tiled=True),
            lax.all_gather(part_o, "grp", axis=1, tiled=True),
            lax.all_gather(part_g2, "grp", axis=0, tiled=True),
            lax.all_gather(part_r, "grp", axis=0, tiled=True),
            lax.all_gather(part_c, "grp", axis=0, tiled=True),
            lax.all_gather(part_vc, "grp", axis=0, tiled=True),
        )
        experts = (
            lax.all_gather(part_gate, "grp", axis=2, tiled=True),
            lax.all_gather(part_up, "grp", axis=2, tiled=True),
            lax.all_gather(part_down, "grp", axis=1, tiled=True),
        )
        return tuple(small) + tuple(experts)

    (
        gain1,
        weight_q,
        weight_k,
        weight_v,
        weight_o,
        gain2,
        router,
        wconst,
        vconst,
        wgate,
        wup,
        wdown,
    ) = collect()
    dealt = deal(tokens)
    dealt_f = dealt.astype(jnp.float32)
    inv_one = lax.rsqrt(jnp.mean(dealt_f * dealt_f, axis=1, keepdims=True) + NORM_EPS)
    unit_one = dealt_f * inv_one
    gain1_f = gain1.astype(jnp.float32)
    normed_one = (unit_one * gain1_f).astype(jnp.bfloat16)
    cos_table, sin_table = rotation_tables(position, HEAD_DIM)
    query = rotate(
        jnp.dot(normed_one, weight_q, preferred_element_type=jnp.float32), cos_table, sin_table
    ).astype(jnp.bfloat16)
    keyed = rotate(
        jnp.dot(normed_one, weight_k, preferred_element_type=jnp.float32), cos_table, sin_table
    ).astype(jnp.bfloat16)
    values_proj = jnp.dot(normed_one, weight_v, preferred_element_type=jnp.float32).astype(
        jnp.bfloat16
    )
    allowed = (
        (in_second[:, None] == in_second[None, :])
        & (position[None, :] <= position[:, None])
        & live_rows[None, :]
    )

    def by_pairs(values):
        return values.reshape(CAP, pairs, pair_width).transpose(1, 0, 2)

    def from_pairs(values):
        return values.transpose(1, 0, 2).reshape(CAP, model_width)

    def pair_scores(q_pair, k_pair):
        query_heads = q_pair.reshape(CAP, 2, HEAD_DIM)
        key_heads = k_pair.reshape(CAP, 2, HEAD_DIM)
        scores = (
            jnp.einsum("qhd,khd->hqk", query_heads, key_heads, preferred_element_type=jnp.float32)
            * scale
        )
        return (jnp.where(allowed[None], scores, -1e30), query_heads, key_heads)

    def attend(pair_items):
        q_pair, k_pair, v_pair = pair_items
        scores, query_heads, key_heads = pair_scores(q_pair, k_pair)
        row_top = jnp.max(scores, axis=-1, keepdims=True)
        weights_exp = jnp.exp(scores - row_top)
        row_total = jnp.sum(weights_exp, axis=-1, keepdims=True)
        attn_probs = weights_exp / row_total
        value_heads = v_pair.reshape(CAP, 2, HEAD_DIM)
        mixed_pair = jnp.einsum(
            "hqk,khd->qhd",
            attn_probs.astype(jnp.bfloat16),
            value_heads,
            preferred_element_type=jnp.float32,
        )
        return (mixed_pair.reshape(CAP, pair_width), (row_top + jnp.log(row_total))[:, :, 0])

    mixed_pairs, log_sums = lax.map(
        attend, (by_pairs(query), by_pairs(keyed), by_pairs(values_proj))
    )
    mixed = from_pairs(mixed_pairs).astype(jnp.bfloat16)
    attn_out = jnp.dot(mixed, weight_o, preferred_element_type=jnp.float32).astype(jnp.bfloat16)
    returned = give_back(attn_out)
    resid = tokens.astype(jnp.float32) + returned.astype(jnp.float32)
    inv_two = lax.rsqrt(jnp.mean(resid * resid, axis=1, keepdims=True) + NORM_EPS)
    unit_two = resid * inv_two
    gain2_f = gain2.astype(jnp.float32)
    normed = unit_two * gain2_f
    narrow = normed.astype(jnp.bfloat16)
    mix_f = w_mix.astype(jnp.float32)
    router_f = router.astype(jnp.float32)
    wconst_f = wconst.astype(jnp.float32)
    logits = jnp.dot(narrow, router, preferred_element_type=jnp.float32) + exact_dot(
        prev_logits, mix_f
    )
    logit_top = jnp.max(logits, axis=1, keepdims=True)
    logit_exp = jnp.exp(logits - logit_top)
    route_probs = logit_exp / jnp.sum(logit_exp, axis=1, keepdims=True)
    expert_ids = jnp.arange(EXPERTS_ALL, dtype=jnp.int32)
    chosen = (
        (routes[:, 0:1] == expert_ids[None, :]) | (routes[:, 1:2] == expert_ids[None, :])
    ).astype(jnp.float32)
    gate_weights = route_probs * chosen
    result = resid + gate_weights[:, E + 1 : E + 2] * normed
    const_logits = jnp.dot(narrow, wconst, preferred_element_type=jnp.float32)
    vconst_f = vconst.astype(jnp.float32)
    const_mixes = []
    const_branches = []
    for const_idx in range(CONSTS):
        part_logits = const_logits[:, 2 * const_idx : 2 * const_idx + 2]
        part_exp = jnp.exp(part_logits - jnp.max(part_logits, axis=1, keepdims=True))
        const_mix = part_exp / jnp.sum(part_exp, axis=1, keepdims=True)
        branch = const_mix[:, 0:1] * normed + const_mix[:, 1:2] * vconst_f[:, const_idx][None, :]
        const_mixes.append(const_mix)
        const_branches.append(branch)
        result = result + gate_weights[:, E + 2 + const_idx : E + 3 + const_idx] * branch
    slot_list = []
    filled_list = []
    slot_gate_list = []
    for expert in range(E):
        member = (routes[:, 0] == expert) | (routes[:, 1] == expert)
        place_at = jnp.cumsum(member.astype(jnp.int32)) - 1
        slot_table = (
            jnp.zeros((MOST,), jnp.int32)
            .at[jnp.where(member, place_at, MOST)]
            .set(jnp.arange(TOK_DEV, dtype=jnp.int32), mode="drop")
        )
        filled = jnp.arange(MOST, dtype=jnp.int32) < jnp.sum(member.astype(jnp.int32))
        slot_list.append(slot_table)
        filled_list.append(filled)
        slot_gate_list.append(jnp.where(filled, jnp.take(gate_weights[:, expert], slot_table), 0.0))
    slot_tables = jnp.stack(slot_list, axis=0)
    filled_all = jnp.stack(filled_list, axis=0)
    slot_gates = jnp.stack(slot_gate_list, axis=0)
    expert_kept = []
    out_list = []
    for expert in range(E):
        picked = jnp.take(narrow, slot_tables[expert], axis=0)
        gate_part = jnp.dot(picked, wgate[expert], preferred_element_type=jnp.float32)
        up_part = jnp.dot(picked, wup[expert], preferred_element_type=jnp.float32)
        hidden = (jax.nn.silu(gate_part) * up_part).astype(jnp.bfloat16)
        out_list.append(jnp.dot(hidden, wdown[expert], preferred_element_type=jnp.float32))
        expert_kept.append((picked, gate_part, up_part, hidden))
    expert_outs = jnp.stack(out_list, axis=0)
    for expert in range(E):
        result = result.at[slot_tables[expert]].add(
            slot_gates[expert][:, None] * expert_outs[expert]
        )
    output = result.astype(jnp.bfloat16)
    (
        gain1,
        weight_q,
        weight_k,
        weight_v,
        weight_o,
        gain2,
        router,
        wconst,
        vconst,
        wgate,
        wup,
        wdown,
    ) = collect()
    gain1_f = gain1.astype(jnp.float32)
    gain2_f = gain2.astype(jnp.float32)
    router_f = router.astype(jnp.float32)
    wconst_f = wconst.astype(jnp.float32)
    vconst_f = vconst.astype(jnp.float32)
    grad_out = cotangent.astype(jnp.float32)
    d_gate_cols = [jnp.zeros((TOK_DEV,), jnp.float32) for expert in range(EXPERTS_ALL)]
    d_gate_cols[E + 1] = jnp.sum(grad_out * normed, axis=1)
    d_normed = gate_weights[:, E + 1 : E + 2] * grad_out
    d_const_parts = []
    d_vconst_cols = []
    for const_idx in range(CONSTS):
        const_mix = const_mixes[const_idx]
        gate_col = gate_weights[:, E + 2 + const_idx]
        d_gate_cols[E + 2 + const_idx] = jnp.sum(grad_out * const_branches[const_idx], axis=1)
        d_piece = gate_col[:, None] * grad_out
        d_normed = d_normed + const_mix[:, 0:1] * d_piece
        d_cmix = jnp.stack(
            [
                jnp.sum(d_piece * normed, axis=1),
                jnp.sum(d_piece * vconst_f[:, const_idx][None, :], axis=1),
            ],
            axis=1,
        )
        d_const_parts.append(
            const_mix * (d_cmix - jnp.sum(const_mix * d_cmix, axis=1, keepdims=True))
        )
        d_vconst_cols.append(exact_dot(const_mix[:, 1] * gate_col, grad_out))
    d_const_logits = jnp.concatenate(d_const_parts, axis=1)
    grad_rows_all = jnp.take(grad_out, slot_tables.reshape(-1), axis=0).reshape(
        E, MOST, model_width
    )
    d_slot_gates = jnp.where(filled_all, jnp.sum(grad_rows_all * expert_outs, axis=2), 0.0)
    for expert in range(E):
        d_gate_cols[expert] = (
            jnp.zeros((TOK_DEV,), jnp.float32).at[slot_tables[expert]].add(d_slot_gates[expert])
        )
    d_expert_all = (slot_gates[:, :, None] * grad_rows_all).astype(jnp.bfloat16)
    d_wgate_list = []
    d_wup_list = []
    d_wdown_list = []
    d_picked_list = []
    for expert in range(E):
        picked, gate_part, up_part, hidden = expert_kept[expert]
        d_expert = d_expert_all[expert]
        d_wdown_list.append(jnp.dot(hidden.T, d_expert, preferred_element_type=jnp.float32))
        d_hidden = jnp.dot(d_expert, wdown[expert].T, preferred_element_type=jnp.float32)
        sigmoid_g = jax.nn.sigmoid(gate_part)
        d_up_part = (d_hidden * gate_part * sigmoid_g).astype(jnp.bfloat16)
        d_gate_part = (
            d_hidden * up_part * sigmoid_g * (1.0 + gate_part * (1.0 - sigmoid_g))
        ).astype(jnp.bfloat16)
        d_wgate_list.append(jnp.dot(picked.T, d_gate_part, preferred_element_type=jnp.float32))
        d_wup_list.append(jnp.dot(picked.T, d_up_part, preferred_element_type=jnp.float32))
        d_picked_list.append(
            jnp.dot(d_gate_part, wgate[expert].T, preferred_element_type=jnp.float32)
            + jnp.dot(d_up_part, wup[expert].T, preferred_element_type=jnp.float32)
        )
    d_picked_all = jnp.stack(d_picked_list, axis=0)
    d_wgate_full = jnp.stack(d_wgate_list, axis=0)
    d_wup_full = jnp.stack(d_wup_list, axis=0)
    d_wdown_full = jnp.stack(d_wdown_list, axis=0)
    d_narrow = jnp.zeros((TOK_DEV, model_width), jnp.float32)
    for expert in range(E):
        d_narrow = d_narrow.at[slot_tables[expert]].add(
            jnp.where(filled_all[expert][:, None], d_picked_all[expert], 0.0)
        )
    d_gate_w = jnp.stack(d_gate_cols, axis=1)
    d_probs = d_gate_w * chosen
    d_logits = route_probs * (d_probs - jnp.sum(route_probs * d_probs, axis=1, keepdims=True))
    narrow_f = narrow.astype(jnp.float32)
    d_narrow = d_narrow + exact_dot(d_logits, router_f.T) + exact_dot(d_const_logits, wconst_f.T)
    d_router_full = exact_dot(narrow_f.T, d_logits)
    d_wconst_full = exact_dot(narrow_f.T, d_const_logits)
    d_vconst_full = jnp.stack(d_vconst_cols, axis=1)
    d_mix_full = exact_dot(prev_logits.T, d_logits)
    grad_prev = exact_dot(d_logits, mix_f.T)
    d_normed_total = d_normed + d_narrow
    d_gain2_full = jnp.sum(d_normed_total * unit_two, axis=0)
    d_unit_two = d_normed_total * gain2_f
    d_resid = grad_out + inv_two * (
        d_unit_two - unit_two * jnp.mean(d_unit_two * unit_two, axis=1, keepdims=True)
    )
    d_attn = deal(d_resid.astype(jnp.bfloat16))
    d_wo_full = jnp.dot(mixed.T, d_attn, preferred_element_type=jnp.float32)
    d_mixed = jnp.dot(d_attn, weight_o.T, preferred_element_type=jnp.float32).astype(jnp.bfloat16)

    def attend_back(pair_items):
        q_pair, k_pair, v_pair, dm_pair, lse_pair = pair_items
        scores, query_heads, key_heads = pair_scores(q_pair, k_pair)
        attn_probs = jnp.where(allowed[None], jnp.exp(scores - lse_pair[:, :, None]), 0.0)
        value_heads = v_pair.reshape(CAP, 2, HEAD_DIM)
        dm_heads = dm_pair.reshape(CAP, 2, HEAD_DIM)
        d_p = jnp.einsum("qhd,khd->hqk", dm_heads, value_heads, preferred_element_type=jnp.float32)
        row_delta = jnp.sum(attn_probs * d_p, axis=-1, keepdims=True)
        d_scores = (attn_probs * (d_p - row_delta)).astype(jnp.bfloat16)
        d_q = (
            jnp.einsum("hqk,khd->qhd", d_scores, key_heads, preferred_element_type=jnp.float32)
            * scale
        )
        d_k = (
            jnp.einsum("hqk,qhd->khd", d_scores, query_heads, preferred_element_type=jnp.float32)
            * scale
        )
        d_v = jnp.einsum(
            "hqk,qhd->khd",
            attn_probs.astype(jnp.bfloat16),
            dm_heads,
            preferred_element_type=jnp.float32,
        )
        return (
            d_q.reshape(CAP, pair_width),
            d_k.reshape(CAP, pair_width),
            d_v.reshape(CAP, pair_width),
        )

    dq_pairs, dk_pairs, dv_pairs = lax.map(
        attend_back,
        (by_pairs(query), by_pairs(keyed), by_pairs(values_proj), by_pairs(d_mixed), log_sums),
    )
    d_query = rotate(from_pairs(dq_pairs), cos_table, -sin_table).astype(jnp.bfloat16)
    d_key = rotate(from_pairs(dk_pairs), cos_table, -sin_table).astype(jnp.bfloat16)
    d_value = from_pairs(dv_pairs).astype(jnp.bfloat16)
    d_wq_full = jnp.dot(normed_one.T, d_query, preferred_element_type=jnp.float32)
    d_wk_full = jnp.dot(normed_one.T, d_key, preferred_element_type=jnp.float32)
    d_wv_full = jnp.dot(normed_one.T, d_value, preferred_element_type=jnp.float32)
    d_normed_one = (
        jnp.dot(d_query, weight_q.T, preferred_element_type=jnp.float32)
        + jnp.dot(d_key, weight_k.T, preferred_element_type=jnp.float32)
        + jnp.dot(d_value, weight_v.T, preferred_element_type=jnp.float32)
    )
    d_gain1_full = jnp.sum(d_normed_one * unit_one, axis=0)
    d_unit_one = d_normed_one * gain1_f
    d_dealt = (
        inv_one * (d_unit_one - unit_one * jnp.mean(d_unit_one * unit_one, axis=1, keepdims=True))
    ).astype(jnp.bfloat16)
    grad_tokens = d_resid + give_back(d_dealt).astype(jnp.float32)

    def regroup(grads_in):
        tail_shape = grads_in.shape[1:]
        split_view = grads_in.reshape((groups, dealers, per_shard) + tail_shape)
        return jnp.swapaxes(split_view, 0, 1).reshape((model_width,) + tail_shape)

    mix_tile = jnp.broadcast_to(d_mix_full[None], (dealers, EXPERTS_ALL, EXPERTS_ALL))
    sectioned = (
        lax.psum_scatter(
            regroup(d_gain1_full).astype(jnp.bfloat16), "fsdp", scatter_dimension=0, tiled=True
        ).astype(jnp.float32),
        lax.psum_scatter(
            d_wq_full.astype(jnp.bfloat16), "fsdp", scatter_dimension=0, tiled=True
        ).astype(jnp.float32),
        lax.psum_scatter(
            d_wk_full.astype(jnp.bfloat16), "fsdp", scatter_dimension=0, tiled=True
        ).astype(jnp.float32),
        lax.psum_scatter(
            d_wv_full.astype(jnp.bfloat16), "fsdp", scatter_dimension=0, tiled=True
        ).astype(jnp.float32),
        lax.psum_scatter(
            d_wo_full.astype(jnp.bfloat16), "fsdp", scatter_dimension=0, tiled=True
        ).astype(jnp.float32),
        lax.psum_scatter(
            regroup(d_gain2_full).astype(jnp.bfloat16), "fsdp", scatter_dimension=0, tiled=True
        ).astype(jnp.float32),
        lax.psum_scatter(
            regroup(d_router_full).astype(jnp.bfloat16), "fsdp", scatter_dimension=0, tiled=True
        ).astype(jnp.float32),
        lax.psum_scatter(
            regroup(d_wconst_full).astype(jnp.bfloat16), "fsdp", scatter_dimension=0, tiled=True
        ).astype(jnp.float32),
        lax.psum_scatter(
            regroup(d_vconst_full).astype(jnp.bfloat16), "fsdp", scatter_dimension=0, tiled=True
        ).astype(jnp.float32),
        lax.psum_scatter(
            mix_tile.astype(jnp.bfloat16), "fsdp", scatter_dimension=0, tiled=True
        ).astype(jnp.float32),
        lax.psum_scatter(
            d_wgate_full.astype(jnp.bfloat16), "fsdp", scatter_dimension=1, tiled=True
        ).astype(jnp.float32),
        lax.psum_scatter(
            d_wup_full.astype(jnp.bfloat16), "fsdp", scatter_dimension=1, tiled=True
        ).astype(jnp.float32),
        lax.psum_scatter(
            d_wdown_full.astype(jnp.bfloat16), "fsdp", scatter_dimension=2, tiled=True
        ).astype(jnp.float32),
    )
    s_g1, s_q, s_k, s_v, s_o, s_g2, s_r, s_c, s_vc, s_mix, s_gate, s_up, s_down = sectioned
    summed = (
        lax.psum_scatter(s_g1.astype(jnp.bfloat16), "grp", scatter_dimension=0, tiled=True).astype(
            jnp.float32
        ),
        lax.psum_scatter(s_q.astype(jnp.bfloat16), "grp", scatter_dimension=1, tiled=True).astype(
            jnp.float32
        ),
        lax.psum_scatter(s_k.astype(jnp.bfloat16), "grp", scatter_dimension=1, tiled=True).astype(
            jnp.float32
        ),
        lax.psum_scatter(s_v.astype(jnp.bfloat16), "grp", scatter_dimension=1, tiled=True).astype(
            jnp.float32
        ),
        lax.psum_scatter(s_o.astype(jnp.bfloat16), "grp", scatter_dimension=1, tiled=True).astype(
            jnp.float32
        ),
        lax.psum_scatter(s_g2.astype(jnp.bfloat16), "grp", scatter_dimension=0, tiled=True).astype(
            jnp.float32
        ),
        lax.psum_scatter(s_r.astype(jnp.bfloat16), "grp", scatter_dimension=0, tiled=True).astype(
            jnp.float32
        ),
        lax.psum_scatter(s_c.astype(jnp.bfloat16), "grp", scatter_dimension=0, tiled=True).astype(
            jnp.float32
        ),
        lax.psum_scatter(s_vc.astype(jnp.bfloat16), "grp", scatter_dimension=0, tiled=True).astype(
            jnp.float32
        ),
        lax.psum_scatter(
            jnp.broadcast_to(s_mix, (groups, EXPERTS_ALL, EXPERTS_ALL)).astype(jnp.bfloat16),
            "grp",
            scatter_dimension=0,
            tiled=True,
        ).astype(jnp.float32),
    )
    (
        grad_gain_one,
        grad_query,
        grad_key,
        grad_value,
        grad_out_proj,
        grad_gain_two,
        grad_router,
        grad_const,
        grad_vconst,
        mix_part,
    ) = summed
    grad_mix = mix_part[0]
    grad_gate, grad_up, grad_down = (
        lax.psum_scatter(
            s_gate.astype(jnp.bfloat16), "grp", scatter_dimension=2, tiled=True
        ).astype(jnp.float32),
        lax.psum_scatter(s_up.astype(jnp.bfloat16), "grp", scatter_dimension=2, tiled=True).astype(
            jnp.float32
        ),
        lax.psum_scatter(
            s_down.astype(jnp.bfloat16), "grp", scatter_dimension=1, tiled=True
        ).astype(jnp.float32),
    )
    return (
        output,
        grad_tokens,
        grad_prev,
        grad_gain_one,
        grad_query,
        grad_key,
        grad_value,
        grad_out_proj,
        grad_gain_two,
        grad_router,
        grad_mix,
        grad_const,
        grad_vconst,
        grad_gate,
        grad_up,
        grad_down,
    )


HALO = 256
KEYS = HALO + TOK_DEV
ROWS = E * MOST
WIDE = 896
NEG = -1e30
F32 = jnp.float32
BF16 = jnp.bfloat16
NT = (((1,), (1,)), ((), ()))
TN = (((0,), (0,)), ((), ()))
NN = (((1,), (0,)), ((), ()))


def mm(a, b, dims=NN):
    return lax.dot_general(a, b, dims, preferred_element_type=F32)


def lane_iota(rows, width=128):
    return lax.broadcasted_iota(jnp.int32, (rows, width), 1)


def pick(values, lane_mask):
    return jnp.sum(jnp.where(lane_mask, values, 0.0), axis=1, keepdims=True)


def split_mm(mat, wide, dims):
    high = wide.astype(BF16)
    low = (wide - high.astype(F32)).astype(BF16)
    return mm(mat, high, dims) + mm(mat, low, dims)


def params(mb, **kw):
    return pltpu.CompilerParams(vmem_limit_bytes=mb << 20, **kw)


def whole(count):
    return [pl.BlockSpec(memory_space=pltpu.VMEM) for _ in range(count)]


def sds(shape, dtype):
    return jax.ShapeDtypeStruct(shape, dtype)


def prepare_kernel(own_ref, routes_ref, cot_ref, wg_ref, wu_ref, wd_ref, slots_ref, *outs):
    own = own_ref[0]
    g_refs, w_refs = outs[:E], outs[E:]
    lanes = lane_iota(TOK_DEV)
    r0 = routes_ref[:, 0:1]
    r1 = routes_ref[:, 1:2]
    hot0 = lanes == r0
    hot1 = lanes == r1
    member = jnp.where(hot0 | hot1, 1.0, 0.0).astype(BF16)
    earlier = (
        lax.broadcasted_iota(jnp.int32, (TOK_DEV, TOK_DEV), 1)
        < lax.broadcasted_iota(jnp.int32, (TOK_DEV, TOK_DEV), 0)
    )
    rank = mm(jnp.where(earlier, 1.0, 0.0).astype(BF16), member)
    c0 = jnp.where(
        r0 < E, lax.rem(r0 - own + E, E) * MOST + pick(rank, hot0).astype(jnp.int32), -1
    )
    c1 = jnp.where(
        r1 < E, lax.rem(r1 - own + E, E) * MOST + pick(rank, hot1).astype(jnp.int32), -1
    )
    slots_ref[...] = jnp.where(lanes == 0, c0, jnp.where(lanes == 1, c1, -1))
    cols = lane_iota(TOK_DEV, ROWS)
    spread = jnp.where((cols == c0) | (cols == c1), 1.0, 0.0).astype(BF16)
    rows = mm(spread, cot_ref[...], TN).astype(BF16)
    for k in range(E):
        g_refs[k][...] = rows[k * MOST : (k + 1) * MOST]
        expert = lax.rem(own + k, E)
        w_refs[k][0] = wg_ref[expert]
        w_refs[k][1] = wu_ref[expert]
        w_refs[k][2] = wd_ref[expert].T


def prepare(own, routes, cotangent, w_gate, w_up, w_down):
    tile = w_gate.shape[1:]
    width = cotangent.shape[1]
    return pl.pallas_call(
        prepare_kernel,
        out_shape=[sds((TOK_DEV, 128), jnp.int32)]
        + [sds((MOST, width), BF16)] * E
        + [sds((3,) + tile, BF16)] * E,
        in_specs=[pl.BlockSpec(memory_space=pltpu.SMEM)] + whole(5),
        out_specs=whole(1 + 2 * E),
        compiler_params=params(56),
        name="prepare",
    )(own, routes, cotangent, w_gate, w_up, w_down)


def turn(values, cos, sin):
    half = HEAD_DIM // 2
    width = values.shape[1]
    reps = width // 128
    front = lax.rem(lane_iota(values.shape[0], width), HEAD_DIM) < half
    swapped = jnp.where(
        front, pltpu.roll(values, width - half, 1), pltpu.roll(values, half, 1)
    )
    cos_w = jnp.concatenate([cos] * reps, axis=1)
    sin_w = jnp.concatenate([sin] * reps, axis=1)
    return values * cos_w + swapped * sin_w


QBLOCKS = [(0, 128), (128, 128), (256, 64)]


def allowed_mask(pos_ref, first, count):
    ii = lax.broadcasted_iota(jnp.int32, (count, 384), 0) + HALO
    jj = lax.broadcasted_iota(jnp.int32, (count, 384), 1)
    return (jj <= ii) & (jj >= ii - pos_ref[pl.ds(first, count), 0:1])


def key_span(first):
    return min(384, KEYS - first)


def forward_kernel(
    tok_ref,
    halo_ref,
    g1_ref,
    g2_ref,
    cos_ref,
    sin_ref,
    pos_ref,
    wq_ref,
    wk_ref,
    wv_ref,
    wo_ref,
    wr_ref,
    vc_ref,
    mixed_prev_ref,
    routes_ref,
    slots_ref,
    q_ref,
    k_ref,
    v_ref,
    n1_ref,
    inv1_ref,
    mix_ref,
    lse_ref,
    resid_ref,
    part_ref,
    probs_ref,
    cols_ref,
    *x_refs,
):
    scale = HEAD_DIM ** (-0.5)
    rows = jnp.concatenate([halo_ref[...], tok_ref[...]], axis=0).astype(F32)
    inv1 = lax.rsqrt(jnp.mean(rows * rows, axis=1, keepdims=True) + NORM_EPS)
    inv1_ref[...] = jnp.broadcast_to(inv1, (KEYS, 128))
    n1_ref[...] = (rows * inv1 * g1_ref[...]).astype(BF16)

    def project(i, _):
        span = pl.ds(pl.multiple_of(i * 256, 256), 256)
        cos = cos_ref[...]
        sin = sin_ref[...]
        q = mm(n1_ref[HALO:, :], wq_ref[:, span])
        q_ref[:, span] = turn(q, cos[HALO:], sin[HALO:]).astype(BF16)
        k = mm(n1_ref[...], wk_ref[:, span])
        k_ref[:, span] = turn(k, cos, sin).astype(BF16)
        v_ref[:, span] = mm(n1_ref[...], wv_ref[:, span]).astype(BF16)
        return 0

    lax.fori_loop(0, q_ref.shape[1] // 256, project, 0)
    lse_ref[...] = jnp.zeros((TOK_DEV, 128), F32)

    def pair(p, _):
        span = pl.ds(pl.multiple_of(p * 128, 128), 128)
        for first, count in QBLOCKS:
            keys = key_span(first)
            ok = allowed_mask(pos_ref, first, count)[:, :keys]
            q = q_ref[pl.ds(first, count), span]
            k = k_ref[pl.ds(first, keys), span]
            v = v_ref[pl.ds(first, keys), span]
            lane = lane_iota(count)
            out = None
            lse = lse_ref[pl.ds(first, count), :]
            for h in range(2):
                mine = (lane < HEAD_DIM) if h == 0 else (lane >= HEAD_DIM)
                qh = jnp.where(mine, q, jnp.zeros_like(q))
                s = jnp.where(ok, mm(qh, k, NT) * scale, NEG)
                top = jnp.max(s, axis=1, keepdims=True)
                e = jnp.exp(s - top)
                total = jnp.sum(e, axis=1, keepdims=True)
                o = mm((e / total).astype(BF16), v)
                out = o if h == 0 else jnp.where(mine, o, out)
                lse = jnp.where(lane == 2 * p + h, top + jnp.log(total), lse)
            mix_ref[pl.ds(first, count), span] = out.astype(BF16)
            lse_ref[pl.ds(first, count), :] = lse
        return 0

    lax.fori_loop(0, HEADS // 2, pair, 0)
    attn_out = mm(mix_ref[...], wo_ref[...]).astype(BF16)
    resid = tok_ref[...].astype(F32) + attn_out.astype(F32)
    resid_ref[...] = resid
    inv2 = lax.rsqrt(jnp.mean(resid * resid, axis=1, keepdims=True) + NORM_EPS)
    normed = resid * inv2 * g2_ref[...]
    narrow = normed.astype(BF16)
    lanes = lane_iota(TOK_DEV)
    raw = mm(narrow, wr_ref[...])
    logits = jnp.where(lanes < EXPERTS_ALL, raw + mixed_prev_ref[...], NEG)
    top = jnp.max(logits, axis=1, keepdims=True)
    e = jnp.exp(logits - top)
    probs = e / jnp.sum(e, axis=1, keepdims=True)
    probs_ref[...] = probs
    r0 = routes_ref[:, 0:1]
    r1 = routes_ref[:, 1:2]
    gate0 = pick(probs, lanes == r0)
    gate1 = pick(probs, lanes == r1)

    def gate_of(expert):
        return jnp.where(r0 == expert, gate0, 0.0) + jnp.where(r1 == expert, gate1, 0.0)

    gate_id = gate_of(E + 1)
    part = resid + gate_id * normed
    cols = jnp.where(lanes == 0, gate0, 0.0)
    cols = jnp.where(lanes == 1, gate1, cols)
    cols = jnp.where(lanes == 2, gate_id, cols)
    cols = jnp.where(lanes == 3, inv2, cols)
    for c in range(CONSTS):
        la = pick(raw, lanes == 16 + 2 * c)
        lb = pick(raw, lanes == 17 + 2 * c)
        big = jnp.maximum(la, lb)
        ea = jnp.exp(la - big)
        eb = jnp.exp(lb - big)
        ma = ea / (ea + eb)
        mb = eb / (ea + eb)
        gate_c = gate_of(E + 2 + c)
        part = part + gate_c * (ma * normed + mb * vc_ref[c : c + 1, :])
        cols = jnp.where(lanes == 4 + 3 * c, gate_c, cols)
        cols = jnp.where(lanes == 5 + 3 * c, ma, cols)
        cols = jnp.where(lanes == 6 + 3 * c, mb, cols)
    part_ref[...] = part
    cols_ref[...] = cols
    c0 = slots_ref[:, 0:1]
    c1 = slots_ref[:, 1:2]
    slot = lane_iota(TOK_DEV, ROWS)
    hot0 = jnp.where(slot == c0, 1.0, 0.0).astype(BF16)
    hot1 = jnp.where(slot == c1, 1.0, 0.0).astype(BF16)

    def two_parts(gate):
        high = gate.astype(BF16).astype(F32)
        return jnp.where(lanes == 0, high, jnp.where(lanes == 1, gate - high, 0.0)).astype(BF16)

    x = mm(hot0 + hot1, narrow, TN).astype(BF16)
    gates = (mm(hot0, two_parts(gate0), TN) + mm(hot1, two_parts(gate1), TN)).astype(BF16)
    for k in range(E):
        x_refs[k][:, : x.shape[1]] = x[k * MOST : (k + 1) * MOST]
        x_refs[k][:, x.shape[1] :] = gates[k * MOST : (k + 1) * MOST]


def forward(tok, halo, g1, g2, cos, sin, pos, wq, wk, wv, wo, wr, vc, mixed_prev, routes, slots):
    width = tok.shape[1]
    return pl.pallas_call(
        forward_kernel,
        out_shape=[
            sds((TOK_DEV, width), BF16),
            sds((KEYS, width), BF16),
            sds((KEYS, width), BF16),
            sds((KEYS, width), BF16),
            sds((KEYS, 128), F32),
            sds((TOK_DEV, width), BF16),
            sds((TOK_DEV, 128), F32),
            sds((TOK_DEV, width), F32),
            sds((TOK_DEV, width), F32),
            sds((TOK_DEV, 128), F32),
            sds((TOK_DEV, 128), F32),
        ]
        + [sds((MOST, WIDE), BF16)] * E,
        in_specs=whole(16),
        out_specs=whole(11 + E),
        compiler_params=params(56),
        name="forward",
    )(tok, halo, g1, g2, cos, sin, pos, wq, wk, wv, wo, wr, vc, mixed_prev, routes, slots)


def expert_kernel(own_ref, *refs):
    lo = 4
    x_refs = refs[:lo]
    g_refs = refs[lo : 2 * lo]
    t_refs = refs[2 * lo : 2 * lo + E]
    od_refs = refs[2 * lo + E : 3 * lo + E]
    gt_refs = refs[3 * lo + E : 3 * lo + 2 * E]
    w_refs = refs[3 * lo + 2 * E : 3 * lo + 2 * E + 3]
    acc_refs = refs[3 * lo + 2 * E + 3 :]
    own = own_ref[0]
    tile = t_refs[0].shape[1:]
    width = w_refs[0].shape[0]
    his = w_refs[0].shape[1] // tile[1]

    def place(k):
        source = lax.rem(own - k + E, E)
        row = pl.multiple_of(source // his * tile[0], tile[0])
        col = pl.multiple_of(lax.rem(source, his) * tile[1], tile[1])
        return pl.ds(row, tile[0]), pl.ds(col, tile[1])

    for k in range(E):
        at = place(k)
        for w in range(3):
            w_refs[w][at] = t_refs[k][w]
    for w in range(3):
        acc_refs[w][...] = jnp.zeros_like(acc_refs[w])
    rows = x_refs[0].shape[0]
    step = rows // 2
    for j in range(lo):

        def block(i, _, j=j):
            at = pl.ds(pl.multiple_of(i * step, step), step)
            x = x_refs[j][at, :width]
            gate = (
                x_refs[j][at, width : width + 1].astype(F32)
                + x_refs[j][at, width + 1 : width + 2].astype(F32)
            )
            d_exp = (g_refs[j][at, :].astype(F32) * gate).astype(BF16)
            wg = w_refs[0][...]
            wu = w_refs[1][...]
            wd = w_refs[2][...]
            a = mm(x, wg)
            b = mm(x, wu)
            sig = 1.0 / (1.0 + jnp.exp(-a))
            hidden = (a * sig * b).astype(BF16)
            od_refs[j][at, :width] = mm(hidden, wd, NT).astype(BF16)
            dh = mm(d_exp, wd)
            d_up = (dh * a * sig).astype(BF16)
            d_gate = (dh * b * sig * (1.0 + a * (1.0 - sig))).astype(BF16)
            od_refs[j][at, width:] = (mm(d_gate, wg, NT) + mm(d_up, wu, NT)).astype(BF16)
            acc_refs[0][...] += mm(x, d_gate, TN)
            acc_refs[1][...] += mm(x, d_up, TN)
            acc_refs[2][...] += mm(d_exp, hidden, TN)
            return 0

        lax.fori_loop(0, rows // step, block, 0)
    for k in range(E):
        at = place(k)
        for w in range(3):
            gt_refs[k][w] = acc_refs[w][at].astype(BF16)


def experts(own, x, g, tiles, his):
    tile = tiles[0].shape[1:]
    width = g[0].shape[1]
    lo = len(x)
    rows = x[0].shape[0]
    full = (width, tile[1] * his)
    return pl.pallas_call(
        expert_kernel,
        out_shape=[sds((rows, 2 * width), BF16)] * lo + [sds((3,) + tile, BF16)] * E,
        in_specs=[pl.BlockSpec(memory_space=pltpu.SMEM)] + whole(2 * lo + E),
        out_specs=whole(lo + E),
        scratch_shapes=[pltpu.VMEM(full, BF16)] * 3 + [pltpu.VMEM(full, F32)] * 3,
        compiler_params=params(60),
        name="experts",
    )(own, *x, *g, *tiles)


def combine_kernel(
    cot_ref,
    resid_ref,
    part_ref,
    probs_ref,
    cols_ref,
    slots_ref,
    routes_ref,
    g2_ref,
    wr_ref,
    vc_ref,
    *refs,
):
    od_refs = refs[:E]
    out_ref, dres_ref, dl_ref, dw_ref, dv_ref, dg2_ref = refs[E:]
    width = cot_ref.shape[1]
    g = cot_ref[...].astype(F32)
    lanes = lane_iota(TOK_DEV)
    cols = cols_ref[...]

    def col(i):
        return pick(cols, lanes == i)

    gate0, gate1, gate_id, inv2 = col(0), col(1), col(2), col(3)
    resid = resid_ref[...]
    unit2 = resid * inv2
    normed = unit2 * g2_ref[...]
    narrow = normed.astype(BF16)
    od = jnp.concatenate([r[...] for r in od_refs], axis=0)
    slot = lane_iota(TOK_DEV, ROWS)
    hot0 = jnp.where(slot == slots_ref[:, 0:1], 1.0, 0.0).astype(BF16)
    hot1 = jnp.where(slot == slots_ref[:, 1:2], 1.0, 0.0).astype(BF16)
    y0 = mm(hot0, od[:, :width])
    y1 = mm(hot1, od[:, :width])
    out_ref[...] = (part_ref[...] + gate0 * y0 + gate1 * y1).astype(BF16)
    a_n = jnp.sum(g * normed, axis=1, keepdims=True)
    dg0 = jnp.sum(g * y0, axis=1, keepdims=True)
    dg1 = jnp.sum(g * y1, axis=1, keepdims=True)
    r0 = routes_ref[:, 0:1]
    r1 = routes_ref[:, 1:2]
    dg0 = jnp.where(r0 == E + 1, a_n, dg0)
    dg1 = jnp.where(r1 == E + 1, a_n, dg1)
    g_scale = gate_id
    dl = jnp.zeros((TOK_DEV, 128), F32)
    vmix = jnp.zeros((TOK_DEV, 128), F32)
    for c in range(CONSTS):
        gate_c, ma, mb = col(4 + 3 * c), col(5 + 3 * c), col(6 + 3 * c)
        a_v = jnp.sum(g * vc_ref[c : c + 1, :], axis=1, keepdims=True)
        branch = ma * a_n + mb * a_v
        dg0 = jnp.where(r0 == E + 2 + c, branch, dg0)
        dg1 = jnp.where(r1 == E + 2 + c, branch, dg1)
        g_scale = g_scale + gate_c * ma
        da = gate_c * a_n
        db = gate_c * a_v
        mean = ma * da + mb * db
        dl = jnp.where(lanes == 16 + 2 * c, ma * (da - mean), dl)
        dl = jnp.where(lanes == 17 + 2 * c, mb * (db - mean), dl)
        vmix = jnp.where(lanes == c, gate_c * mb, vmix)
    probs = probs_ref[...]
    d_probs = jnp.where(lanes == r0, dg0, 0.0) + jnp.where(lanes == r1, dg1, 0.0)
    d_logits = probs * (d_probs - jnp.sum(probs * d_probs, axis=1, keepdims=True))
    dl = jnp.where(lanes < EXPERTS_ALL, d_logits, dl)
    dl_ref[...] = dl
    high = dl.astype(BF16)
    low = (dl - high.astype(F32)).astype(BF16)
    wr = wr_ref[...]
    d_normed = g_scale * g + mm(hot0 + hot1, od[:, width:])
    d_normed = d_normed + mm(high, wr, NT) + mm(low, wr, NT)
    dw_ref[...] = mm(high, narrow, TN) + mm(low, narrow, TN)
    vhigh = vmix.astype(BF16)
    vlow = (vmix - vhigh.astype(F32)).astype(BF16)
    dv_ref[...] = mm(vhigh, cot_ref[...], TN) + mm(vlow, cot_ref[...], TN)
    dg2_ref[...] = jnp.broadcast_to(
        jnp.sum(d_normed * unit2, axis=0, keepdims=True), dg2_ref.shape
    )
    n = d_normed * g2_ref[...]
    dres_ref[...] = g + inv2 * (n - unit2 * jnp.mean(n * unit2, axis=1, keepdims=True))


def combine(cot, resid, part, probs, cols, slots, routes, g2, wr, vc, od):
    width = cot.shape[1]
    return pl.pallas_call(
        combine_kernel,
        out_shape=[
            sds((TOK_DEV, width), BF16),
            sds((TOK_DEV, width), F32),
            sds((TOK_DEV, 128), F32),
            sds((128, width), F32),
            sds((128, width), F32),
            sds((8, width), F32),
        ],
        in_specs=whole(10 + E),
        out_specs=whole(6),
        compiler_params=params(56),
        name="combine",
    )(cot, resid, part, probs, cols, slots, routes, g2, wr, vc, *od)


def backward_kernel(
    dres_ref,
    wq_ref,
    wk_ref,
    wv_ref,
    wo_ref,
    q_ref,
    k_ref,
    v_ref,
    n1_ref,
    inv1_ref,
    mix_ref,
    lse_ref,
    cos_ref,
    sin_ref,
    pos_ref,
    tok_ref,
    halo_ref,
    gw_ref,
    down_ref,
    dhalo_ref,
    dg1_ref,
    dm_ref,
    dq_ref,
    dk_ref,
    dv_ref,
    dqr_ref,
    dkr_ref,
    dvr_ref,
):
    scale = HEAD_DIM ** (-0.5)
    width = dres_ref.shape[1]
    d_attn = dres_ref[...].astype(BF16)
    gw_ref[3] = mm(mix_ref[...], d_attn, TN).astype(BF16)
    dm_ref[...] = mm(d_attn, wo_ref[...], NT).astype(BF16)
    dk_ref[...] = jnp.zeros_like(dk_ref)
    dv_ref[...] = jnp.zeros_like(dv_ref)

    def pair(p, _):
        span = pl.ds(pl.multiple_of(p * 128, 128), 128)
        for first, count in QBLOCKS:
            keys = key_span(first)
            ok = allowed_mask(pos_ref, first, count)[:, :keys]
            q = q_ref[pl.ds(first, count), span]
            dm = dm_ref[pl.ds(first, count), span]
            k = k_ref[pl.ds(first, keys), span]
            v = v_ref[pl.ds(first, keys), span]
            lane = lane_iota(count)
            key_lane = lane_iota(keys)
            lse = lse_ref[pl.ds(first, count), :]
            dq = dk = dv = None
            for h in range(2):
                mine = (lane < HEAD_DIM) if h == 0 else (lane >= HEAD_DIM)
                key_mine = (key_lane < HEAD_DIM) if h == 0 else (key_lane >= HEAD_DIM)
                qh = jnp.where(mine, q, jnp.zeros_like(q))
                dmh = jnp.where(mine, dm, jnp.zeros_like(dm))
                s = jnp.where(ok, mm(qh, k, NT) * scale, NEG)
                probs = jnp.where(ok, jnp.exp(s - pick(lse, lane == 2 * p + h)), 0.0)
                dp = mm(dmh, v, NT)
                delta = jnp.sum(probs * dp, axis=1, keepdims=True)
                ds = (probs * (dp - delta)).astype(BF16)
                pb = probs.astype(BF16)
                dqh = mm(ds, k)
                dkh = mm(ds, q, TN)
                dvh = mm(pb, dm, TN)
                dq = dqh if h == 0 else jnp.where(mine, dqh, dq)
                dk = dkh if h == 0 else jnp.where(key_mine, dkh, dk)
                dv = dvh if h == 0 else jnp.where(key_mine, dvh, dv)
            dq_ref[pl.ds(first, count), span] = dq * scale
            dk_ref[pl.ds(first, keys), span] += dk * scale
            dv_ref[pl.ds(first, keys), span] += dv
        return 0

    lax.fori_loop(0, HEADS // 2, pair, 0)

    def finish(i, _):
        span = pl.ds(pl.multiple_of(i * 256, 256), 256)
        cos = cos_ref[...]
        sin = sin_ref[...]
        dqr_ref[:, span] = turn(dq_ref[:, span], cos[HALO:], -sin[HALO:]).astype(BF16)
        dkr_ref[:, span] = turn(dk_ref[:, span], cos, -sin).astype(BF16)
        dvr_ref[:, span] = dv_ref[:, span].astype(BF16)
        return 0

    lax.fori_loop(0, width // 256, finish, 0)
    gw_ref[0] = mm(n1_ref[HALO:, :], dqr_ref[...], TN).astype(BF16)
    gw_ref[1] = mm(n1_ref[...], dkr_ref[...], TN).astype(BF16)
    gw_ref[2] = mm(n1_ref[...], dvr_ref[...], TN).astype(BF16)
    d_all = mm(dkr_ref[...], wk_ref[...], NT) + mm(dvr_ref[...], wv_ref[...], NT)
    d_own = d_all[HALO:] + mm(dqr_ref[...], wq_ref[...], NT)
    inv1 = inv1_ref[:, 0:1]
    unit_own = tok_ref[...].astype(F32) * inv1[HALO:]
    unit_halo = halo_ref[...].astype(F32) * inv1[:HALO]
    d_halo = d_all[:HALO]
    dg1 = jnp.sum(d_own * unit_own, axis=0, keepdims=True) + jnp.sum(
        d_halo * unit_halo, axis=0, keepdims=True
    )
    dg1_ref[...] = jnp.broadcast_to(dg1, dg1_ref.shape)
    down_ref[...] = d_own
    dhalo_ref[...] = d_halo.astype(BF16)


def backward(dres, wq, wk, wv, wo, q, k, v, n1, inv1, mix, lse, cos, sin, pos, tok, halo):
    width = tok.shape[1]
    return pl.pallas_call(
        backward_kernel,
        out_shape=[
            sds((4, width, width), BF16),
            sds((TOK_DEV, width), F32),
            sds((HALO, width), BF16),
            sds((8, width), F32),
        ],
        in_specs=whole(17),
        out_specs=whole(4),
        scratch_shapes=[
            pltpu.VMEM((TOK_DEV, width), BF16),
            pltpu.VMEM((TOK_DEV, width), F32),
            pltpu.VMEM((KEYS, width), F32),
            pltpu.VMEM((KEYS, width), F32),
            pltpu.VMEM((TOK_DEV, width), BF16),
            pltpu.VMEM((KEYS, width), BF16),
            pltpu.VMEM((KEYS, width), BF16),
        ],
        compiler_params=params(60),
        name="backward",
    )(dres, wq, wk, wv, wo, q, k, v, n1, inv1, mix, lse, cos, sin, pos, tok, halo)


def finish_kernel(dres_ref, down_ref, back_ref, tok_ref, inv1_ref, g1_ref, out_ref):
    width = tok_ref.shape[1]
    inv1 = inv1_ref[HALO:, 0:1]
    unit = tok_ref[...].astype(F32) * inv1
    back = jnp.concatenate(
        [jnp.zeros((TOK_DEV - HALO, width), F32), back_ref[...].astype(F32)], axis=0
    )
    m = (down_ref[...] + back) * g1_ref[...]
    d_dealt = inv1 * (m - unit * jnp.mean(m * unit, axis=1, keepdims=True))
    out_ref[...] = dres_ref[...] + d_dealt.astype(BF16).astype(F32)


def finish(dres, down, back, tok, inv1, g1):
    return pl.pallas_call(
        finish_kernel,
        out_shape=sds(dres.shape, F32),
        in_specs=whole(6),
        out_specs=pl.BlockSpec(memory_space=pltpu.VMEM),
        compiler_params=params(40),
        name="finish",
    )(dres, down, back, tok, inv1, g1)


def store_kernel(own_ref, *refs):
    t_refs = refs[:E]
    gate_ref, up_ref, down_ref = refs[E:]
    own = own_ref[0]
    for k in range(E):
        expert = lax.rem(own + k, E)
        gate_ref[expert] = t_refs[k][0].astype(F32)
        up_ref[expert] = t_refs[k][1].astype(F32)
        down_ref[expert] = t_refs[k][2].astype(F32).T


def store(own, tiles):
    rows, cols = tiles[0].shape[1:]
    return pl.pallas_call(
        store_kernel,
        out_shape=[sds((E, rows, cols), F32)] * 2 + [sds((E, cols, rows), F32)],
        in_specs=[pl.BlockSpec(memory_space=pltpu.SMEM)] + whole(E),
        out_specs=whole(3),
        compiler_params=params(40),
        name="store",
    )(own, *tiles)


def fast_device(
    tokens,
    cotangent,
    prev_logits,
    lengths,
    dealing,
    routes,
    gain_one,
    w_query,
    w_key,
    w_value,
    w_out,
    gain_two,
    w_router,
    w_mix,
    w_const,
    v_const,
    w_gate,
    w_up,
    w_down,
):
    groups = lax.axis_size("grp")
    ranks = lax.axis_size("fsdp")
    his = E // ranks
    lo = groups // his
    g_id = lax.axis_index("grp")
    f_id = lax.axis_index("fsdp")
    width = tokens.shape[1]
    axes = ("grp", "fsdp")
    own = (f_id * his + g_id // lo).astype(jnp.int32).reshape(1)

    def member_perm(k):
        pairs = []
        for g in range(groups):
            for f in range(ranks):
                m = (f * his + g // lo + k) % E
                pairs.append((g * ranks + f, (m % his * lo + g % lo) * ranks + m // his))
        return pairs

    def to_member(x, k):
        return x if k == 0 else lax.ppermute(x, axes, member_perm(k))

    def near_perm(j):
        return [(g, g ^ j) for g in range(groups)]

    def near(x, j):
        return x if j == 0 else lax.ppermute(x, "grp", near_perm(j))

    prep = prepare(own, routes, cotangent, w_gate, w_up, w_down)
    slots, g_rows, w_tiles = prep[0], prep[1 : 1 + E], prep[1 + E :]
    halo = lax.ppermute(
        tokens[TOK_DEV - HALO :], "fsdp", [(f, f + 1) for f in range(ranks - 1)]
    )
    packed = jnp.stack([w_query, w_key, w_value, w_out])
    packed = lax.all_gather(packed, axes, axis=0, tiled=False)
    packed = packed.reshape((groups, ranks) + packed.shape[1:])
    full = packed.transpose(2, 1, 3, 0, 4).reshape(4, width, width)
    wq, wk, wv, wo = full[0], full[1], full[2], full[3]
    per = gain_one.shape[0]
    small = jnp.concatenate(
        [gain_one[:, None], gain_two[:, None], v_const, w_router, w_const], axis=1
    )
    small = lax.all_gather(small, axes, axis=0, tiled=True)
    g1 = small[:, 0][None, :].astype(F32)
    g2 = small[:, 1][None, :].astype(F32)
    vc = small[:, 2 : 2 + CONSTS].T.astype(F32)
    wr = jnp.zeros((width, 128), BF16)
    wr = wr.at[:, :EXPERTS_ALL].set(small[:, 2 + CONSTS : 2 + CONSTS + EXPERTS_ALL])
    wr = wr.at[:, 16 : 16 + 2 * CONSTS].set(small[:, 2 + CONSTS + EXPERTS_ALL :])
    tiles = [to_member(w_tiles[k], k) for k in range(E)]
    g_in = [to_member(g_rows[k], k) for k in range(E)]
    g_mine = jnp.concatenate(g_in, axis=0)
    g_all = [near(g_mine, j) for j in range(lo)]

    seq_len = lengths[0]
    count = seq_len.shape[0]
    ids = jnp.arange(count, dtype=jnp.int32)
    ends = jnp.sum(jnp.where(ids[:, None] >= ids[None, :], seq_len[None, :], 0), axis=1)
    row = f_id * TOK_DEV + jnp.arange(-HALO, TOK_DEV, dtype=jnp.int32)
    begin = jnp.max(jnp.where(ends[None, :] <= row[:, None], ends[None, :], 0), axis=1)
    pos = jnp.maximum(row - begin, 0)
    cos, sin = rotation_tables(pos, HEAD_DIM)
    cos = jnp.concatenate([cos] * 4, axis=1)
    sin = jnp.concatenate([-sin, sin, -sin, sin], axis=1)
    pos_own = jnp.broadcast_to(pos[HALO:, None], (TOK_DEV, 128))
    mixed_prev = exact_dot(prev_logits, w_mix.astype(F32))
    mixed_prev = jnp.pad(mixed_prev, ((0, 0), (0, 128 - EXPERTS_ALL)))

    fwd = forward(
        tokens, halo, g1, g2, cos, sin, pos_own, wq, wk, wv, wo, wr, vc, mixed_prev, routes, slots
    )
    q, k, v, n1, inv1, mix, lse, resid, part, probs, cols = fwd[:11]
    x_in = [to_member(fwd[11 + i], i) for i in range(E)]
    x_mine = jnp.concatenate(x_in, axis=0)
    x_all = [near(x_mine, j) for j in range(lo)]
    done = experts(own, x_all, g_all, tiles, his)
    od, g_tiles = done[:lo], done[lo:]

    def add(a, b):
        return (a.astype(F32) + b.astype(F32)).astype(BF16)

    half = near(jnp.concatenate([od[1], od[3]], axis=0), 1)
    here = add(od[0], half[:ROWS])
    there = add(od[2], half[ROWS:])
    od_sum = add(here, near(there, 2))

    def back_perm(i):
        return [(b, a) for a, b in member_perm(i)]

    od_back = []
    for i in range(E):
        rows = od_sum[i * MOST : (i + 1) * MOST]
        od_back.append(rows if i == 0 else lax.ppermute(rows, axes, back_perm(i)))
    output, d_resid, dl, dw, dv, dg2 = combine(
        cotangent, resid, part, probs, cols, slots, routes, g2, wr, vc, od_back
    )
    d_logits = dl[:, :EXPERTS_ALL]
    grad_prev = exact_dot(d_logits, w_mix.astype(F32).T)
    d_mix = exact_dot(prev_logits.T, d_logits)
    gw, down, d_halo, dg1 = backward(
        d_resid, wq, wk, wv, wo, q, k, v, n1, inv1, mix, lse, cos, sin, pos_own, tokens, halo
    )
    back = lax.ppermute(d_halo, "fsdp", [(f + 1, f) for f in range(ranks - 1)])
    grad_tokens = finish(d_resid, down, back, tokens, inv1, g1)
    tiles_back = [
        g_tiles[i] if i == 0 else lax.ppermute(g_tiles[i], axes, back_perm(i)) for i in range(E)
    ]
    grad_gate, grad_up, grad_down = store(own, tiles_back)

    cols_per = width // groups
    rows_per = width // ranks
    gw = gw.reshape(4, width, groups, cols_per).transpose(2, 0, 1, 3)
    gw = lax.psum_scatter(gw, "grp", scatter_dimension=0, tiled=False)
    gw = gw.reshape(4, ranks, rows_per, cols_per).transpose(1, 0, 2, 3)
    gw = lax.psum_scatter(gw, "fsdp", scatter_dimension=0, tiled=False).astype(F32)
    tiny = jnp.concatenate(
        [
            dg1[:1],
            dg2[:1],
            dv[:CONSTS],
            dw[:EXPERTS_ALL],
            dw[16 : 16 + 2 * CONSTS],
            jnp.pad(d_mix.reshape(1, -1), ((0, 0), (0, width - EXPERTS_ALL * EXPERTS_ALL))),
        ],
        axis=0,
    )
    tiny = lax.psum(tiny, axes)
    grad_mix = tiny[-1, : EXPERTS_ALL * EXPERTS_ALL].reshape(EXPERTS_ALL, EXPERTS_ALL)
    at = (g_id * ranks + f_id) * per
    mine = lax.dynamic_slice(tiny, (0, at), (tiny.shape[0], per))
    n_small = 2 + CONSTS
    return (
        output,
        grad_tokens,
        grad_prev,
        mine[0],
        gw[0],
        gw[1],
        gw[2],
        gw[3],
        mine[1],
        mine[n_small : n_small + EXPERTS_ALL].T,
        grad_mix,
        mine[n_small + EXPERTS_ALL : n_small + EXPERTS_ALL + 2 * CONSTS].T,
        mine[2:n_small].T,
        grad_gate,
        grad_up,
        grad_down,
    )


def suits(mesh):
    ranks, groups = mesh.shape["fsdp"], mesh.shape["grp"]
    return E % ranks == 0 and groups % (E // ranks) == 0 and groups // (E // ranks) == 4


def solution(mesh):
    return jax.shard_map(
        fast_device if suits(mesh) else per_device,
        mesh=mesh,
        in_specs=(
            P(("grp", "fsdp"), None),
            P(("grp", "fsdp"), None),
            P(("grp", "fsdp"), None),
            P("grp", None),
            P("grp", None),
            P(("grp", "fsdp"), None),
            P(("grp", "fsdp")),
            P("fsdp", "grp"),
            P("fsdp", "grp"),
            P("fsdp", "grp"),
            P("fsdp", "grp"),
            P(("grp", "fsdp")),
            P(("grp", "fsdp"), None),
            P(),
            P(("grp", "fsdp"), None),
            P(("grp", "fsdp"), None),
            P(None, "fsdp", "grp"),
            P(None, "fsdp", "grp"),
            P(None, "grp", "fsdp"),
        ),
        out_specs=(
            P(("grp", "fsdp"), None),
            P(("grp", "fsdp"), None),
            P(("grp", "fsdp"), None),
            P(("grp", "fsdp")),
            P("fsdp", "grp"),
            P("fsdp", "grp"),
            P("fsdp", "grp"),
            P("fsdp", "grp"),
            P(("grp", "fsdp")),
            P(("grp", "fsdp"), None),
            P(),
            P(("grp", "fsdp"), None),
            P(("grp", "fsdp"), None),
            P(None, "fsdp", "grp"),
            P(None, "fsdp", "grp"),
            P(None, "grp", "fsdp"),
        ),
        check_vma=False,
    )
```

```python
import math

import jax
import jax.numpy as jnp
from jax import lax
from jax.experimental import pallas as pl
from jax.experimental.pallas import tpu as pltpu
from jax.sharding import PartitionSpec as P

HEADS = 12
HEAD_DIM = 64
E = 8
CONSTS = 2
BLOCK = 128
EXPERTS_ALL = 12
CAP = 384
TOK_DEV = 320
MOST = 80


NORM_EPS = 1e-05
EXACT = lax.Precision.HIGHEST


def rotation_tables(positions, head_dim):
    half_dim = head_dim // 2
    inv_freq = jnp.exp(
        jnp.arange(half_dim, dtype=jnp.float32) * (-2.0 * math.log(10000.0) / head_dim)
    )
    angles = positions.astype(jnp.float32)[:, None] * inv_freq[None, :]
    return (jnp.cos(angles), jnp.sin(angles))


def rotate(values, cos_table, sin_table):
    row_count = values.shape[0]
    half_dim = cos_table.shape[1]
    heads_view = values.reshape(row_count, -1, 2 * half_dim)
    front_half = heads_view[:, :, :half_dim]
    back_half = heads_view[:, :, half_dim:]
    cos_view = cos_table[:, None, :]
    sin_view = sin_table[:, None, :]
    turned = jnp.concatenate(
        [
            front_half * cos_view - back_half * sin_view,
            back_half * cos_view + front_half * sin_view,
        ],
        axis=2,
    )
    return turned.reshape(row_count, -1)


def exact_dot(left_side, right_side):
    return jnp.dot(left_side, right_side, precision=EXACT, preferred_element_type=jnp.float32)


def per_device(
    tokens,
    cotangent,
    prev_logits,
    lengths,
    dealing,
    routes,
    gain_one,
    w_query,
    w_key,
    w_value,
    w_out,
    gain_two,
    w_router,
    w_mix,
    w_const,
    v_const,
    w_gate,
    w_up,
    w_down,
):
    groups = lax.axis_size("grp")
    dealers = lax.axis_size("fsdp")
    device = lax.axis_index("fsdp")
    model_width = tokens.shape[1]
    per_shard = model_width // (groups * dealers)
    pairs = HEADS // 2
    pair_width = 2 * HEAD_DIM
    scale = HEAD_DIM ** (-0.5)
    seq_len = lengths[0]
    deal_order = dealing[0]
    seq_count = seq_len.shape[0]
    seq_ids = jnp.arange(seq_count, dtype=jnp.int32)
    seq_ends = jnp.cumsum(seq_len)
    starts = seq_ends - seq_len
    padded = (seq_len + BLOCK - 1) // BLOCK * BLOCK
    order_hot = (deal_order[:, None] == seq_ids[None, :]).astype(jnp.int32)
    dealt_len = jnp.sum(order_hot * seq_len[None, :], axis=1)
    dealt_pad = jnp.sum(order_hot * padded[None, :], axis=1)
    dealt_start = jnp.sum(order_hot * starts[None, :], axis=1)
    slot_of = jnp.sum(order_hot * seq_ids[:, None], axis=0)
    pair_index = 2 * device
    row_ids = jnp.arange(CAP, dtype=jnp.int32)
    in_second = row_ids >= dealt_pad[pair_index]
    position = row_ids - jnp.where(in_second, dealt_pad[pair_index], 0)
    seq_limit = jnp.where(in_second, dealt_len[pair_index + 1], dealt_len[pair_index])
    live_rows = position < seq_limit
    source = jnp.where(in_second, dealt_start[pair_index + 1], dealt_start[pair_index]) + position
    source = jnp.where(live_rows, source, -1)
    given_rows = device * TOK_DEV + jnp.arange(TOK_DEV, dtype=jnp.int32)
    seq_hot = (
        (given_rows[:, None] >= starts[None, :]) & (given_rows[:, None] < seq_ends[None, :])
    ).astype(jnp.int32)
    offset_in = given_rows - jnp.sum(seq_hot * starts[None, :], axis=1)
    slot_rank = jnp.sum(seq_hot * slot_of[None, :], axis=1)
    is_second = slot_rank % 2
    lead_pad = jnp.take(dealt_pad, slot_rank - is_second)
    target = slot_rank // 2 * CAP + jnp.where(is_second == 1, lead_pad, 0) + offset_in

    def deal(values):
        shard_rows = lax.all_gather(values, "fsdp", axis=0, tiled=True)
        row_span = shard_rows.shape[0]
        inside = (source >= 0) & (source < row_span)
        taken_rows = jnp.take(shard_rows, jnp.clip(source, 0, row_span - 1), axis=0)
        return jnp.where(inside[:, None], taken_rows, jnp.zeros((CAP, model_width), jnp.bfloat16))

    def give_back(values):
        shard_rows = lax.all_gather(values, "fsdp", axis=0, tiled=True)
        row_span = shard_rows.shape[0]
        inside = (target >= 0) & (target < row_span)
        taken_rows = jnp.take(shard_rows, jnp.clip(target, 0, row_span - 1), axis=0)
        return jnp.where(
            inside[:, None], taken_rows, jnp.zeros((TOK_DEV, model_width), jnp.bfloat16)
        )

    def collect():
        gate_in, up_in, down_in = (w_gate, w_up, w_down)
        sectioned = (
            lax.all_gather(gain_one, "fsdp", axis=0, tiled=True),
            lax.all_gather(w_query, "fsdp", axis=0, tiled=True),
            lax.all_gather(w_key, "fsdp", axis=0, tiled=True),
            lax.all_gather(w_value, "fsdp", axis=0, tiled=True),
            lax.all_gather(w_out, "fsdp", axis=0, tiled=True),
            lax.all_gather(gain_two, "fsdp", axis=0, tiled=True),
            lax.all_gather(w_router, "fsdp", axis=0, tiled=True),
            lax.all_gather(w_const, "fsdp", axis=0, tiled=True),
            lax.all_gather(v_const, "fsdp", axis=0, tiled=True),
            lax.all_gather(gate_in, "fsdp", axis=1, tiled=True),
            lax.all_gather(up_in, "fsdp", axis=1, tiled=True),
            lax.all_gather(down_in, "fsdp", axis=2, tiled=True),
        )
        (
            part_g1,
            part_q,
            part_k,
            part_v,
            part_o,
            part_g2,
            part_r,
            part_c,
            part_vc,
            part_gate,
            part_up,
            part_down,
        ) = sectioned
        small = (
            lax.all_gather(part_g1, "grp", axis=0, tiled=True),
            lax.all_gather(part_q, "grp", axis=1, tiled=True),
            lax.all_gather(part_k, "grp", axis=1, tiled=True),
            lax.all_gather(part_v, "grp", axis=1, tiled=True),
            lax.all_gather(part_o, "grp", axis=1, tiled=True),
            lax.all_gather(part_g2, "grp", axis=0, tiled=True),
            lax.all_gather(part_r, "grp", axis=0, tiled=True),
            lax.all_gather(part_c, "grp", axis=0, tiled=True),
            lax.all_gather(part_vc, "grp", axis=0, tiled=True),
        )
        experts = (
            lax.all_gather(part_gate, "grp", axis=2, tiled=True),
            lax.all_gather(part_up, "grp", axis=2, tiled=True),
            lax.all_gather(part_down, "grp", axis=1, tiled=True),
        )
        return tuple(small) + tuple(experts)

    (
        gain1,
        weight_q,
        weight_k,
        weight_v,
        weight_o,
        gain2,
        router,
        wconst,
        vconst,
        wgate,
        wup,
        wdown,
    ) = collect()
    dealt = deal(tokens)
    dealt_f = dealt.astype(jnp.float32)
    inv_one = lax.rsqrt(jnp.mean(dealt_f * dealt_f, axis=1, keepdims=True) + NORM_EPS)
    unit_one = dealt_f * inv_one
    gain1_f = gain1.astype(jnp.float32)
    normed_one = (unit_one * gain1_f).astype(jnp.bfloat16)
    cos_table, sin_table = rotation_tables(position, HEAD_DIM)
    query = rotate(
        jnp.dot(normed_one, weight_q, preferred_element_type=jnp.float32), cos_table, sin_table
    ).astype(jnp.bfloat16)
    keyed = rotate(
        jnp.dot(normed_one, weight_k, preferred_element_type=jnp.float32), cos_table, sin_table
    ).astype(jnp.bfloat16)
    values_proj = jnp.dot(normed_one, weight_v, preferred_element_type=jnp.float32).astype(
        jnp.bfloat16
    )
    allowed = (
        (in_second[:, None] == in_second[None, :])
        & (position[None, :] <= position[:, None])
        & live_rows[None, :]
    )

    def by_pairs(values):
        return values.reshape(CAP, pairs, pair_width).transpose(1, 0, 2)

    def from_pairs(values):
        return values.transpose(1, 0, 2).reshape(CAP, model_width)

    def pair_scores(q_pair, k_pair):
        query_heads = q_pair.reshape(CAP, 2, HEAD_DIM)
        key_heads = k_pair.reshape(CAP, 2, HEAD_DIM)
        scores = (
            jnp.einsum("qhd,khd->hqk", query_heads, key_heads, preferred_element_type=jnp.float32)
            * scale
        )
        return (jnp.where(allowed[None], scores, -1e30), query_heads, key_heads)

    def attend(pair_items):
        q_pair, k_pair, v_pair = pair_items
        scores, query_heads, key_heads = pair_scores(q_pair, k_pair)
        row_top = jnp.max(scores, axis=-1, keepdims=True)
        weights_exp = jnp.exp(scores - row_top)
        row_total = jnp.sum(weights_exp, axis=-1, keepdims=True)
        attn_probs = weights_exp / row_total
        value_heads = v_pair.reshape(CAP, 2, HEAD_DIM)
        mixed_pair = jnp.einsum(
            "hqk,khd->qhd",
            attn_probs.astype(jnp.bfloat16),
            value_heads,
            preferred_element_type=jnp.float32,
        )
        return (mixed_pair.reshape(CAP, pair_width), (row_top + jnp.log(row_total))[:, :, 0])

    mixed_pairs, log_sums = lax.map(
        attend, (by_pairs(query), by_pairs(keyed), by_pairs(values_proj))
    )
    mixed = from_pairs(mixed_pairs).astype(jnp.bfloat16)
    attn_out = jnp.dot(mixed, weight_o, preferred_element_type=jnp.float32).astype(jnp.bfloat16)
    returned = give_back(attn_out)
    resid = tokens.astype(jnp.float32) + returned.astype(jnp.float32)
    inv_two = lax.rsqrt(jnp.mean(resid * resid, axis=1, keepdims=True) + NORM_EPS)
    unit_two = resid * inv_two
    gain2_f = gain2.astype(jnp.float32)
    normed = unit_two * gain2_f
    narrow = normed.astype(jnp.bfloat16)
    mix_f = w_mix.astype(jnp.float32)
    router_f = router.astype(jnp.float32)
    wconst_f = wconst.astype(jnp.float32)
    logits = jnp.dot(narrow, router, preferred_element_type=jnp.float32) + exact_dot(
        prev_logits, mix_f
    )
    logit_top = jnp.max(logits, axis=1, keepdims=True)
    logit_exp = jnp.exp(logits - logit_top)
    route_probs = logit_exp / jnp.sum(logit_exp, axis=1, keepdims=True)
    expert_ids = jnp.arange(EXPERTS_ALL, dtype=jnp.int32)
    chosen = (
        (routes[:, 0:1] == expert_ids[None, :]) | (routes[:, 1:2] == expert_ids[None, :])
    ).astype(jnp.float32)
    gate_weights = route_probs * chosen
    result = resid + gate_weights[:, E + 1 : E + 2] * normed
    const_logits = jnp.dot(narrow, wconst, preferred_element_type=jnp.float32)
    vconst_f = vconst.astype(jnp.float32)
    const_mixes = []
    const_branches = []
    for const_idx in range(CONSTS):
        part_logits = const_logits[:, 2 * const_idx : 2 * const_idx + 2]
        part_exp = jnp.exp(part_logits - jnp.max(part_logits, axis=1, keepdims=True))
        const_mix = part_exp / jnp.sum(part_exp, axis=1, keepdims=True)
        branch = const_mix[:, 0:1] * normed + const_mix[:, 1:2] * vconst_f[:, const_idx][None, :]
        const_mixes.append(const_mix)
        const_branches.append(branch)
        result = result + gate_weights[:, E + 2 + const_idx : E + 3 + const_idx] * branch
    slot_list = []
    filled_list = []
    slot_gate_list = []
    for expert in range(E):
        member = (routes[:, 0] == expert) | (routes[:, 1] == expert)
        place_at = jnp.cumsum(member.astype(jnp.int32)) - 1
        slot_table = (
            jnp.zeros((MOST,), jnp.int32)
            .at[jnp.where(member, place_at, MOST)]
            .set(jnp.arange(TOK_DEV, dtype=jnp.int32), mode="drop")
        )
        filled = jnp.arange(MOST, dtype=jnp.int32) < jnp.sum(member.astype(jnp.int32))
        slot_list.append(slot_table)
        filled_list.append(filled)
        slot_gate_list.append(jnp.where(filled, jnp.take(gate_weights[:, expert], slot_table), 0.0))
    slot_tables = jnp.stack(slot_list, axis=0)
    filled_all = jnp.stack(filled_list, axis=0)
    slot_gates = jnp.stack(slot_gate_list, axis=0)
    expert_kept = []
    out_list = []
    for expert in range(E):
        picked = jnp.take(narrow, slot_tables[expert], axis=0)
        gate_part = jnp.dot(picked, wgate[expert], preferred_element_type=jnp.float32)
        up_part = jnp.dot(picked, wup[expert], preferred_element_type=jnp.float32)
        hidden = (jax.nn.silu(gate_part) * up_part).astype(jnp.bfloat16)
        out_list.append(jnp.dot(hidden, wdown[expert], preferred_element_type=jnp.float32))
        expert_kept.append((picked, gate_part, up_part, hidden))
    expert_outs = jnp.stack(out_list, axis=0)
    for expert in range(E):
        result = result.at[slot_tables[expert]].add(
            slot_gates[expert][:, None] * expert_outs[expert]
        )
    output = result.astype(jnp.bfloat16)
    (
        gain1,
        weight_q,
        weight_k,
        weight_v,
        weight_o,
        gain2,
        router,
        wconst,
        vconst,
        wgate,
        wup,
        wdown,
    ) = collect()
    gain1_f = gain1.astype(jnp.float32)
    gain2_f = gain2.astype(jnp.float32)
    router_f = router.astype(jnp.float32)
    wconst_f = wconst.astype(jnp.float32)
    vconst_f = vconst.astype(jnp.float32)
    grad_out = cotangent.astype(jnp.float32)
    d_gate_cols = [jnp.zeros((TOK_DEV,), jnp.float32) for expert in range(EXPERTS_ALL)]
    d_gate_cols[E + 1] = jnp.sum(grad_out * normed, axis=1)
    d_normed = gate_weights[:, E + 1 : E + 2] * grad_out
    d_const_parts = []
    d_vconst_cols = []
    for const_idx in range(CONSTS):
        const_mix = const_mixes[const_idx]
        gate_col = gate_weights[:, E + 2 + const_idx]
        d_gate_cols[E + 2 + const_idx] = jnp.sum(grad_out * const_branches[const_idx], axis=1)
        d_piece = gate_col[:, None] * grad_out
        d_normed = d_normed + const_mix[:, 0:1] * d_piece
        d_cmix = jnp.stack(
            [
                jnp.sum(d_piece * normed, axis=1),
                jnp.sum(d_piece * vconst_f[:, const_idx][None, :], axis=1),
            ],
            axis=1,
        )
        d_const_parts.append(
            const_mix * (d_cmix - jnp.sum(const_mix * d_cmix, axis=1, keepdims=True))
        )
        d_vconst_cols.append(exact_dot(const_mix[:, 1] * gate_col, grad_out))
    d_const_logits = jnp.concatenate(d_const_parts, axis=1)
    grad_rows_all = jnp.take(grad_out, slot_tables.reshape(-1), axis=0).reshape(
        E, MOST, model_width
    )
    d_slot_gates = jnp.where(filled_all, jnp.sum(grad_rows_all * expert_outs, axis=2), 0.0)
    for expert in range(E):
        d_gate_cols[expert] = (
            jnp.zeros((TOK_DEV,), jnp.float32).at[slot_tables[expert]].add(d_slot_gates[expert])
        )
    d_expert_all = (slot_gates[:, :, None] * grad_rows_all).astype(jnp.bfloat16)
    d_wgate_list = []
    d_wup_list = []
    d_wdown_list = []
    d_picked_list = []
    for expert in range(E):
        picked, gate_part, up_part, hidden = expert_kept[expert]
        d_expert = d_expert_all[expert]
        d_wdown_list.append(jnp.dot(hidden.T, d_expert, preferred_element_type=jnp.float32))
        d_hidden = jnp.dot(d_expert, wdown[expert].T, preferred_element_type=jnp.float32)
        sigmoid_g = jax.nn.sigmoid(gate_part)
        d_up_part = (d_hidden * gate_part * sigmoid_g).astype(jnp.bfloat16)
        d_gate_part = (
            d_hidden * up_part * sigmoid_g * (1.0 + gate_part * (1.0 - sigmoid_g))
        ).astype(jnp.bfloat16)
        d_wgate_list.append(jnp.dot(picked.T, d_gate_part, preferred_element_type=jnp.float32))
        d_wup_list.append(jnp.dot(picked.T, d_up_part, preferred_element_type=jnp.float32))
        d_picked_list.append(
            jnp.dot(d_gate_part, wgate[expert].T, preferred_element_type=jnp.float32)
            + jnp.dot(d_up_part, wup[expert].T, preferred_element_type=jnp.float32)
        )
    d_picked_all = jnp.stack(d_picked_list, axis=0)
    d_wgate_full = jnp.stack(d_wgate_list, axis=0)
    d_wup_full = jnp.stack(d_wup_list, axis=0)
    d_wdown_full = jnp.stack(d_wdown_list, axis=0)
    d_narrow = jnp.zeros((TOK_DEV, model_width), jnp.float32)
    for expert in range(E):
        d_narrow = d_narrow.at[slot_tables[expert]].add(
            jnp.where(filled_all[expert][:, None], d_picked_all[expert], 0.0)
        )
    d_gate_w = jnp.stack(d_gate_cols, axis=1)
    d_probs = d_gate_w * chosen
    d_logits = route_probs * (d_probs - jnp.sum(route_probs * d_probs, axis=1, keepdims=True))
    narrow_f = narrow.astype(jnp.float32)
    d_narrow = d_narrow + exact_dot(d_logits, router_f.T) + exact_dot(d_const_logits, wconst_f.T)
    d_router_full = exact_dot(narrow_f.T, d_logits)
    d_wconst_full = exact_dot(narrow_f.T, d_const_logits)
    d_vconst_full = jnp.stack(d_vconst_cols, axis=1)
    d_mix_full = exact_dot(prev_logits.T, d_logits)
    grad_prev = exact_dot(d_logits, mix_f.T)
    d_normed_total = d_normed + d_narrow
    d_gain2_full = jnp.sum(d_normed_total * unit_two, axis=0)
    d_unit_two = d_normed_total * gain2_f
    d_resid = grad_out + inv_two * (
        d_unit_two - unit_two * jnp.mean(d_unit_two * unit_two, axis=1, keepdims=True)
    )
    d_attn = deal(d_resid.astype(jnp.bfloat16))
    d_wo_full = jnp.dot(mixed.T, d_attn, preferred_element_type=jnp.float32)
    d_mixed = jnp.dot(d_attn, weight_o.T, preferred_element_type=jnp.float32).astype(jnp.bfloat16)

    def attend_back(pair_items):
        q_pair, k_pair, v_pair, dm_pair, lse_pair = pair_items
        scores, query_heads, key_heads = pair_scores(q_pair, k_pair)
        attn_probs = jnp.where(allowed[None], jnp.exp(scores - lse_pair[:, :, None]), 0.0)
        value_heads = v_pair.reshape(CAP, 2, HEAD_DIM)
        dm_heads = dm_pair.reshape(CAP, 2, HEAD_DIM)
        d_p = jnp.einsum("qhd,khd->hqk", dm_heads, value_heads, preferred_element_type=jnp.float32)
        row_delta = jnp.sum(attn_probs * d_p, axis=-1, keepdims=True)
        d_scores = (attn_probs * (d_p - row_delta)).astype(jnp.bfloat16)
        d_q = (
            jnp.einsum("hqk,khd->qhd", d_scores, key_heads, preferred_element_type=jnp.float32)
            * scale
        )
        d_k = (
            jnp.einsum("hqk,qhd->khd", d_scores, query_heads, preferred_element_type=jnp.float32)
            * scale
        )
        d_v = jnp.einsum(
            "hqk,qhd->khd",
            attn_probs.astype(jnp.bfloat16),
            dm_heads,
            preferred_element_type=jnp.float32,
        )
        return (
            d_q.reshape(CAP, pair_width),
            d_k.reshape(CAP, pair_width),
            d_v.reshape(CAP, pair_width),
        )

    dq_pairs, dk_pairs, dv_pairs = lax.map(
        attend_back,
        (by_pairs(query), by_pairs(keyed), by_pairs(values_proj), by_pairs(d_mixed), log_sums),
    )
    d_query = rotate(from_pairs(dq_pairs), cos_table, -sin_table).astype(jnp.bfloat16)
    d_key = rotate(from_pairs(dk_pairs), cos_table, -sin_table).astype(jnp.bfloat16)
    d_value = from_pairs(dv_pairs).astype(jnp.bfloat16)
    d_wq_full = jnp.dot(normed_one.T, d_query, preferred_element_type=jnp.float32)
    d_wk_full = jnp.dot(normed_one.T, d_key, preferred_element_type=jnp.float32)
    d_wv_full = jnp.dot(normed_one.T, d_value, preferred_element_type=jnp.float32)
    d_normed_one = (
        jnp.dot(d_query, weight_q.T, preferred_element_type=jnp.float32)
        + jnp.dot(d_key, weight_k.T, preferred_element_type=jnp.float32)
        + jnp.dot(d_value, weight_v.T, preferred_element_type=jnp.float32)
    )
    d_gain1_full = jnp.sum(d_normed_one * unit_one, axis=0)
    d_unit_one = d_normed_one * gain1_f
    d_dealt = (
        inv_one * (d_unit_one - unit_one * jnp.mean(d_unit_one * unit_one, axis=1, keepdims=True))
    ).astype(jnp.bfloat16)
    grad_tokens = d_resid + give_back(d_dealt).astype(jnp.float32)

    def regroup(grads_in):
        tail_shape = grads_in.shape[1:]
        split_view = grads_in.reshape((groups, dealers, per_shard) + tail_shape)
        return jnp.swapaxes(split_view, 0, 1).reshape((model_width,) + tail_shape)

    mix_tile = jnp.broadcast_to(d_mix_full[None], (dealers, EXPERTS_ALL, EXPERTS_ALL))
    sectioned = (
        lax.psum_scatter(
            regroup(d_gain1_full).astype(jnp.bfloat16), "fsdp", scatter_dimension=0, tiled=True
        ).astype(jnp.float32),
        lax.psum_scatter(
            d_wq_full.astype(jnp.bfloat16), "fsdp", scatter_dimension=0, tiled=True
        ).astype(jnp.float32),
        lax.psum_scatter(
            d_wk_full.astype(jnp.bfloat16), "fsdp", scatter_dimension=0, tiled=True
        ).astype(jnp.float32),
        lax.psum_scatter(
            d_wv_full.astype(jnp.bfloat16), "fsdp", scatter_dimension=0, tiled=True
        ).astype(jnp.float32),
        lax.psum_scatter(
            d_wo_full.astype(jnp.bfloat16), "fsdp", scatter_dimension=0, tiled=True
        ).astype(jnp.float32),
        lax.psum_scatter(
            regroup(d_gain2_full).astype(jnp.bfloat16), "fsdp", scatter_dimension=0, tiled=True
        ).astype(jnp.float32),
        lax.psum_scatter(
            regroup(d_router_full).astype(jnp.bfloat16), "fsdp", scatter_dimension=0, tiled=True
        ).astype(jnp.float32),
        lax.psum_scatter(
            regroup(d_wconst_full).astype(jnp.bfloat16), "fsdp", scatter_dimension=0, tiled=True
        ).astype(jnp.float32),
        lax.psum_scatter(
            regroup(d_vconst_full).astype(jnp.bfloat16), "fsdp", scatter_dimension=0, tiled=True
        ).astype(jnp.float32),
        lax.psum_scatter(
            mix_tile.astype(jnp.bfloat16), "fsdp", scatter_dimension=0, tiled=True
        ).astype(jnp.float32),
        lax.psum_scatter(
            d_wgate_full.astype(jnp.bfloat16), "fsdp", scatter_dimension=1, tiled=True
        ).astype(jnp.float32),
        lax.psum_scatter(
            d_wup_full.astype(jnp.bfloat16), "fsdp", scatter_dimension=1, tiled=True
        ).astype(jnp.float32),
        lax.psum_scatter(
            d_wdown_full.astype(jnp.bfloat16), "fsdp", scatter_dimension=2, tiled=True
        ).astype(jnp.float32),
    )
    s_g1, s_q, s_k, s_v, s_o, s_g2, s_r, s_c, s_vc, s_mix, s_gate, s_up, s_down = sectioned
    summed = (
        lax.psum_scatter(s_g1.astype(jnp.bfloat16), "grp", scatter_dimension=0, tiled=True).astype(
            jnp.float32
        ),
        lax.psum_scatter(s_q.astype(jnp.bfloat16), "grp", scatter_dimension=1, tiled=True).astype(
            jnp.float32
        ),
        lax.psum_scatter(s_k.astype(jnp.bfloat16), "grp", scatter_dimension=1, tiled=True).astype(
            jnp.float32
        ),
        lax.psum_scatter(s_v.astype(jnp.bfloat16), "grp", scatter_dimension=1, tiled=True).astype(
            jnp.float32
        ),
        lax.psum_scatter(s_o.astype(jnp.bfloat16), "grp", scatter_dimension=1, tiled=True).astype(
            jnp.float32
        ),
        lax.psum_scatter(s_g2.astype(jnp.bfloat16), "grp", scatter_dimension=0, tiled=True).astype(
            jnp.float32
        ),
        lax.psum_scatter(s_r.astype(jnp.bfloat16), "grp", scatter_dimension=0, tiled=True).astype(
            jnp.float32
        ),
        lax.psum_scatter(s_c.astype(jnp.bfloat16), "grp", scatter_dimension=0, tiled=True).astype(
            jnp.float32
        ),
        lax.psum_scatter(s_vc.astype(jnp.bfloat16), "grp", scatter_dimension=0, tiled=True).astype(
            jnp.float32
        ),
        lax.psum_scatter(
            jnp.broadcast_to(s_mix, (groups, EXPERTS_ALL, EXPERTS_ALL)).astype(jnp.bfloat16),
            "grp",
            scatter_dimension=0,
            tiled=True,
        ).astype(jnp.float32),
    )
    (
        grad_gain_one,
        grad_query,
        grad_key,
        grad_value,
        grad_out_proj,
        grad_gain_two,
        grad_router,
        grad_const,
        grad_vconst,
        mix_part,
    ) = summed
    grad_mix = mix_part[0]
    grad_gate, grad_up, grad_down = (
        lax.psum_scatter(
            s_gate.astype(jnp.bfloat16), "grp", scatter_dimension=2, tiled=True
        ).astype(jnp.float32),
        lax.psum_scatter(s_up.astype(jnp.bfloat16), "grp", scatter_dimension=2, tiled=True).astype(
            jnp.float32
        ),
        lax.psum_scatter(
            s_down.astype(jnp.bfloat16), "grp", scatter_dimension=1, tiled=True
        ).astype(jnp.float32),
    )
    return (
        output,
        grad_tokens,
        grad_prev,
        grad_gain_one,
        grad_query,
        grad_key,
        grad_value,
        grad_out_proj,
        grad_gain_two,
        grad_router,
        grad_mix,
        grad_const,
        grad_vconst,
        grad_gate,
        grad_up,
        grad_down,
    )


HALO = 256
KEYS = HALO + TOK_DEV
ROWS = E * MOST
WIDE = 896
NEG = -1e30
F32 = jnp.float32
BF16 = jnp.bfloat16
NT = (((1,), (1,)), ((), ()))
TN = (((0,), (0,)), ((), ()))
NN = (((1,), (0,)), ((), ()))


def mm(a, b, dims=NN):
    return lax.dot_general(a, b, dims, preferred_element_type=F32)


def lane_iota(rows, width=128):
    return lax.broadcasted_iota(jnp.int32, (rows, width), 1)


def pick(values, lane_mask):
    return jnp.sum(jnp.where(lane_mask, values, 0.0), axis=1, keepdims=True)


def split_mm(mat, wide, dims):
    high = wide.astype(BF16)
    low = (wide - high.astype(F32)).astype(BF16)
    return mm(mat, high, dims) + mm(mat, low, dims)


def params(mb, **kw):
    return pltpu.CompilerParams(vmem_limit_bytes=mb << 20, **kw)


def whole(count):
    return [pl.BlockSpec(memory_space=pltpu.VMEM) for _ in range(count)]


def sds(shape, dtype):
    return jax.ShapeDtypeStruct(shape, dtype)


MESH_ID = pl.DeviceIdType.MESH


def send(src, dst, send_sem, recv_sem, device):
    pltpu.make_async_remote_copy(
        src_ref=src,
        dst_ref=dst,
        send_sem=send_sem,
        recv_sem=recv_sem,
        device_id=device,
        device_id_type=MESH_ID,
    ).start()


def settle(ref, sem):
    pltpu.make_async_copy(ref, ref, sem).wait()


def flip(a, b):
    return a + b - 2 * a * b


def xor4(a, b):
    return flip(a // 2, b // 2) * 2 + flip(lax.rem(a, 2), lax.rem(b, 2))


def aligned(value, to):
    return pl.multiple_of(value, to)


class Place:
    def __init__(self, his, lo):
        self.g = lax.axis_index("grp")
        self.f = lax.axis_index("fsdp")
        self.his, self.lo = his, lo
        self.hi = self.g // lo
        self.l = lax.rem(self.g, lo)
        self.m = self.f * his + self.hi
        core = lax.rem(self.g, 2)
        side = lax.rem(self.g // 2, 2)
        self.core_peer = self.g + 1 - 2 * core
        self.side_peer = self.g + 2 - 4 * side
        self.l1 = lax.rem(self.core_peer, lo)
        self.l2 = lax.rem(self.side_peer, lo)
        self.l3 = lo - 1 - self.l

    def member(self, j, hh):
        f = xor4(self.f, j)
        hi = flip(self.hi, hh)
        return f * self.his + hi, (hi * self.lo + self.l, f)

    def others(self):
        peers = []
        for j in range(4):
            for hh in range(self.his):
                if j or hh:
                    peers.append(self.member(j, hh)[1])
        return peers


def greet(peers):
    barrier = pltpu.get_barrier_semaphore()
    for peer in peers:
        pl.semaphore_signal(barrier, inc=1, device_id=peer, device_id_type=MESH_ID)
    pl.semaphore_wait(barrier, len(peers))


def turn(values, cos, sin):
    half = HEAD_DIM // 2
    width = values.shape[1]
    reps = width // 128
    front = lax.rem(lane_iota(values.shape[0], width), HEAD_DIM) < half
    swapped = jnp.where(
        front, pltpu.roll(values, width - half, 1), pltpu.roll(values, half, 1)
    )
    cos_w = jnp.concatenate([cos] * reps, axis=1)
    sin_w = jnp.concatenate([sin] * reps, axis=1)
    return values * cos_w + swapped * sin_w


QBLOCKS = [(0, 128), (128, 128), (256, 64)]


def allowed_mask(pos_ref, first, count):
    ii = lax.broadcasted_iota(jnp.int32, (count, 384), 0) + HALO
    jj = lax.broadcasted_iota(jnp.int32, (count, 384), 1)
    return (jj <= ii) & (jj >= ii - pos_ref[pl.ds(first, count), 0:1])


def key_span(first):
    return min(384, KEYS - first)


def begin_kernel(
    tile_ref,
    tok_ref,
    cot_ref,
    routes_ref,
    cos_ref,
    sin_ref,
    pos_ref,
    mixed_prev_ref,
    wd_ref,
    wg_hbm,
    wu_hbm,
    wf_ref,
    s_ref,
    halo_ref,
    slots_ref,
    q_ref,
    k_ref,
    v_ref,
    n1_ref,
    inv1_ref,
    mix_ref,
    lse_ref,
    resid_ref,
    part_ref,
    probs_ref,
    cols_ref,
    x_ref,
    gates_ref,
    w_hbm,
    g_hbm,
    p_ref,
    wdt_ref,
    grow_ref,
    zs,
    ps,
    cs,
    hs,
    gs,
    ws,
    gas,
    agr,
    hr,
    gr,
    wr,
    gqr,
):
    lo, ranks = g_hbm.shape[:2]
    his = E // ranks
    at = Place(his, lo)
    width = tok_ref.shape[1]
    head_rows = wd_ref.shape[2]
    ff = wd_ref.shape[1]
    part_cols = width // p_ref.shape[0]
    diag = lo * (1 - at.hi) + at.l2
    upper = lo * (1 - at.hi) + at.l
    near = [(at.core_peer, at.f), (at.side_peer, at.f), (upper, at.f), (diag, at.f)]
    greet(at.others() + [near[0], near[1], near[3]])

    p_ref[at.g, at.f] = tile_ref[...]
    for j in range(1, ranks):
        f2 = xor4(at.f, j)
        send(tile_ref, p_ref.at[at.g, at.f], zs.at[j], agr.at[at.g, at.f], (at.g, f2))

    def spread(j, f2, src):
        for t, peer in enumerate(near):
            send(src, p_ref.at[at.g, f2], ps.at[j, t], agr.at[at.g, f2], peer)

    spread(0, at.f, tile_ref)
    halo_rows = halo_ref.shape[0]
    tail = tok_ref.at[pl.ds(tok_ref.shape[0] - halo_rows, halo_rows)]

    @pl.when(at.f < ranks - 1)
    def _():
        send(tail, halo_ref, hs, hr, (at.g, at.f + 1))

    @pl.when(at.f == 0)
    def _():
        halo_ref[...] = jnp.zeros_like(halo_ref)

    lanes = lane_iota(TOK_DEV)
    r0 = routes_ref[:, 0:1]
    r1 = routes_ref[:, 1:2]
    hot0 = lanes == r0
    hot1 = lanes == r1
    named = jnp.where(hot0 | hot1, 1.0, 0.0).astype(BF16)
    earlier = (
        lax.broadcasted_iota(jnp.int32, (TOK_DEV, TOK_DEV), 1)
        < lax.broadcasted_iota(jnp.int32, (TOK_DEV, TOK_DEV), 0)
    )
    rank = mm(jnp.where(earlier, 1.0, 0.0).astype(BF16), named)
    rank0 = pick(rank, hot0).astype(jnp.int32)
    rank1 = pick(rank, hot1).astype(jnp.int32)
    c0 = jnp.where(r0 < E, r0 * MOST + rank0, -1)
    c1 = jnp.where(r1 < E, r1 * MOST + rank1, -1)
    slots_ref[...] = jnp.where(lanes == 0, c0, jnp.where(lanes == 1, c1, -1))
    slot = lane_iota(TOK_DEV, ROWS)
    spots0 = jnp.where(slot == c0, 1.0, 0.0).astype(BF16)
    spots1 = jnp.where(slot == c1, 1.0, 0.0).astype(BF16)
    grow_ref[...] = mm(spots0 + spots1, cot_ref[...], TN).astype(BF16)
    for e in range(E):
        wdt_ref[e] = wd_ref[e].T

    for j in range(1, ranks):
        f2 = xor4(at.f, j)
        settle(p_ref.at[at.g, f2], agr.at[at.g, f2])
        spread(j, f2, p_ref.at[at.g, f2])

    own_rows = pl.ds(aligned(at.f * head_rows, 16), head_rows)
    own_cols = pl.ds(aligned(at.hi * ff, 128), ff)
    own_spot = pl.ds(aligned(at.hi * MOST, 16), MOST)
    for j in range(ranks):
        for hh in range(his):
            e, peer = at.member(j, hh)
            rows = grow_ref.at[pl.ds(aligned(e * MOST, 16), MOST)]
            spot = g_hbm.at[at.l, at.f, own_spot]
            sources = (wg_hbm.at[e], wu_hbm.at[e], wdt_ref.at[e])
            if j == 0 and hh == 0:
                pltpu.make_async_copy(rows, spot, gr.at[at.m]).start()
                for w in range(3):
                    pltpu.make_async_copy(
                        sources[w], w_hbm.at[w, own_rows, own_cols], wr.at[at.m, w]
                    ).start()
            else:
                k = j * his + hh
                send(rows, spot, gs.at[k], gr.at[at.m], peer)
                for w in range(3):
                    send(
                        sources[w],
                        w_hbm.at[w, own_rows, own_cols],
                        ws.at[k, w],
                        wr.at[at.m, w],
                        peer,
                    )

    for j in range(ranks):
        f2 = xor4(at.f, j)
        for t in range(1, 4):
            g2 = near[t][0]
            settle(p_ref.at[g2, f2], agr.at[g2, f2])
            send(p_ref.at[g2, f2], p_ref.at[g2, f2], cs.at[t - 1, j], agr.at[g2, f2], near[0])
    sibling_upper = lo * (1 - at.hi) + at.l1
    for j in range(ranks):
        f2 = xor4(at.f, j)
        for g2 in (
            at.core_peer,
            at.hi * lo + at.l3,
            sibling_upper,
            lo * (1 - at.hi) + at.l3,
        ):
            settle(p_ref.at[g2, f2], agr.at[g2, f2])

    per = (p_ref.shape[2] - head_rows) // 8 * 24
    groups = p_ref.shape[0]
    for g2 in range(groups):
        for f2 in range(ranks):
            piece = p_ref[g2, f2, head_rows : head_rows + 8, :].astype(F32)
            for i in range(per // 8):
                base = (g2 * ranks + f2) * per + 8 * i
                s_ref[base : base + 8, :] = piece[:, 128 * i : 128 * i + 128]

    def lay(f2, _):
        rows = pl.ds(aligned(f2 * head_rows, 16), head_rows)
        for w in range(4):
            for half in range(2):
                pieces = [
                    p_ref[
                        half * (groups // 2) + i,
                        f2,
                        0:head_rows,
                        w * part_cols : (w + 1) * part_cols,
                    ]
                    for i in range(groups // 2)
                ]
                wf_ref[w, rows, half * (width // 2) : (half + 1) * (width // 2)] = (
                    jnp.concatenate(pieces, axis=1)
                )
        return 0

    lax.fori_loop(0, ranks, lay, 0)

    @pl.when(at.f > 0)
    def _():
        settle(halo_ref, hr)

    scale = HEAD_DIM ** (-0.5)
    flat = s_ref[...].T
    g1 = flat[SMALL_G1 : SMALL_G1 + 1, :]
    g2 = flat[SMALL_G1 + 1 : SMALL_G1 + 2, :]
    vc = flat[SMALL_VC : SMALL_VC + CONSTS, :]
    rows = jnp.concatenate([halo_ref[...], tok_ref[...]], axis=0).astype(F32)
    inv1 = lax.rsqrt(jnp.mean(rows * rows, axis=1, keepdims=True) + NORM_EPS)
    inv1_ref[...] = jnp.broadcast_to(inv1, (KEYS, 128))
    n1_ref[...] = (rows * inv1 * g1).astype(BF16)

    def project(i, _):
        span = pl.ds(pl.multiple_of(i * 256, 256), 256)
        cos = cos_ref[...]
        sin = sin_ref[...]
        q = mm(n1_ref[HALO:, :], wf_ref[0, :, span])
        q_ref[:, span] = turn(q, cos[HALO:], sin[HALO:]).astype(BF16)
        k = mm(n1_ref[...], wf_ref[1, :, span])
        k_ref[:, span] = turn(k, cos, sin).astype(BF16)
        v_ref[:, span] = mm(n1_ref[...], wf_ref[2, :, span]).astype(BF16)
        return 0

    lax.fori_loop(0, width // 256, project, 0)
    lse_ref[...] = jnp.zeros((TOK_DEV, 128), F32)

    for f2 in range(ranks):
        for h2 in range(his):
            settle(
                g_hbm.at[at.l, f2, h2 * MOST : (h2 + 1) * MOST], gr.at[f2 * his + h2]
            )
    send(g_hbm.at[at.l], g_hbm.at[at.l], gas.at[0], gqr.at[0], near[0])
    send(g_hbm.at[at.l], g_hbm.at[at.l], gas.at[1], gqr.at[1], near[1])

    def pair(p, _):
        span = pl.ds(pl.multiple_of(p * 128, 128), 128)
        for first, count in QBLOCKS:
            keys = key_span(first)
            ok = allowed_mask(pos_ref, first, count)[:, :keys]
            q = q_ref[pl.ds(first, count), span]
            k = k_ref[pl.ds(first, keys), span]
            v = v_ref[pl.ds(first, keys), span]
            lane = lane_iota(count)
            out = None
            lse = lse_ref[pl.ds(first, count), :]
            for h in range(2):
                mine = (lane < HEAD_DIM) if h == 0 else (lane >= HEAD_DIM)
                qh = jnp.where(mine, q, jnp.zeros_like(q))
                sc = jnp.where(ok, mm(qh, k, NT) * scale, NEG)
                top = jnp.max(sc, axis=1, keepdims=True)
                ex = jnp.exp(sc - top)
                total = jnp.sum(ex, axis=1, keepdims=True)
                o = mm((ex / total).astype(BF16), v)
                out = o if h == 0 else jnp.where(mine, o, out)
                lse = jnp.where(lane == 2 * p + h, top + jnp.log(total), lse)
            mix_ref[pl.ds(first, count), span] = out.astype(BF16)
            lse_ref[pl.ds(first, count), :] = lse
        return 0

    lax.fori_loop(0, HEADS // 2, pair, 0)
    settle(g_hbm.at[at.l2], gqr.at[1])
    send(g_hbm.at[at.l2], g_hbm.at[at.l2], gas.at[2], gqr.at[2], near[0])

    attn_out = mm(mix_ref[...], wf_ref[3]).astype(BF16)
    resid = tok_ref[...].astype(F32) + attn_out.astype(F32)
    resid_ref[...] = resid
    inv2 = lax.rsqrt(jnp.mean(resid * resid, axis=1, keepdims=True) + NORM_EPS)
    normed = resid * inv2 * g2
    narrow = normed.astype(BF16)
    raw = mm(narrow, s_ref[...].astype(BF16))
    logits = jnp.where(lanes < EXPERTS_ALL, raw + mixed_prev_ref[...], NEG)
    top = jnp.max(logits, axis=1, keepdims=True)
    ex = jnp.exp(logits - top)
    probs = ex / jnp.sum(ex, axis=1, keepdims=True)
    probs_ref[...] = probs
    gate0 = pick(probs, hot0)
    gate1 = pick(probs, hot1)

    def gate_of(expert):
        return jnp.where(r0 == expert, gate0, 0.0) + jnp.where(r1 == expert, gate1, 0.0)

    gate_id = gate_of(E + 1)
    part = resid + gate_id * normed
    cols = jnp.where(lanes == 0, gate0, 0.0)
    cols = jnp.where(lanes == 1, gate1, cols)
    cols = jnp.where(lanes == 2, gate_id, cols)
    cols = jnp.where(lanes == 3, inv2, cols)
    for c in range(CONSTS):
        la = pick(raw, lanes == SMALL_C + 2 * c)
        lb = pick(raw, lanes == SMALL_C + 1 + 2 * c)
        big = jnp.maximum(la, lb)
        ea = jnp.exp(la - big)
        eb = jnp.exp(lb - big)
        ma = ea / (ea + eb)
        mb = eb / (ea + eb)
        gate_c = gate_of(E + 2 + c)
        part = part + gate_c * (ma * normed + mb * vc[c : c + 1, :])
        cols = jnp.where(lanes == 4 + 3 * c, gate_c, cols)
        cols = jnp.where(lanes == 5 + 3 * c, ma, cols)
        cols = jnp.where(lanes == 6 + 3 * c, mb, cols)
    part_ref[...] = part
    cols_ref[...] = cols
    x_ref[...] = mm(spots0 + spots1, narrow, TN).astype(BF16)
    wide0 = jnp.where(r0 < E, r0 * 128 + rank0, -1)
    wide1 = jnp.where(r1 < E, r1 * 128 + rank1, -1)
    for e in range(E):
        lane = lanes + e * 128
        row = jnp.sum(
            jnp.where(lane == wide0, gate0, 0.0) + jnp.where(lane == wide1, gate1, 0.0),
            axis=0,
            keepdims=True,
        )
        gates_ref[e] = jnp.broadcast_to(row, (8, 128))

    settle(g_hbm.at[at.l1], gqr.at[0])
    settle(g_hbm.at[at.l3], gqr.at[2])
    for f2 in range(ranks):
        for h2 in range(his):
            for w in range(3):
                block = w_hbm.at[
                    w, f2 * head_rows : (f2 + 1) * head_rows, h2 * ff : (h2 + 1) * ff
                ]
                settle(block, wr.at[f2 * his + h2, w])
    for j in range(1, ranks):
        settle(tile_ref, zs.at[j])
    for j in range(ranks):
        for t in range(4):
            settle(tile_ref, ps.at[j, t])
        for t in range(3):
            settle(tile_ref, cs.at[t, j])

    @pl.when(at.f < ranks - 1)
    def _():
        settle(tail, hs)

    for k in range(1, E):
        settle(grow_ref.at[0:MOST], gs.at[k])
        for w in range(3):
            settle(wdt_ref.at[0], ws.at[k, w])
    for i in range(3):
        settle(g_hbm.at[at.l], gas.at[i])


SMALL_G1 = EXPERTS_ALL
SMALL_VC = SMALL_G1 + 2
SMALL_C = SMALL_VC + CONSTS


def begin(tile, tok, cot, routes, cos, sin, pos, mixed_prev, w_down, w_gate, w_up, groups, ranks):
    width = tok.shape[1]
    lo = groups * ranks // E
    his = E // ranks
    ff = w_down.shape[1]
    head_rows = w_down.shape[2]
    dma = pltpu.SemaphoreType.DMA
    any_spec = pl.BlockSpec(memory_space=pl.ANY)
    return pl.pallas_call(
        begin_kernel,
        out_shape=[
            sds((4, width, width), BF16),
            sds((width, 128), F32),
            sds((HALO, width), BF16),
            sds((TOK_DEV, 128), jnp.int32),
            sds((TOK_DEV, width), BF16),
            sds((KEYS, width), BF16),
            sds((KEYS, width), BF16),
            sds((KEYS, width), BF16),
            sds((KEYS, 128), F32),
            sds((TOK_DEV, width), BF16),
            sds((TOK_DEV, 128), F32),
            sds((TOK_DEV, width), F32),
            sds((TOK_DEV, width), F32),
            sds((TOK_DEV, 128), F32),
            sds((TOK_DEV, 128), F32),
            sds((ROWS, width), BF16),
            sds((E, 8, 128), F32),
            sds((3, width, ff * his), BF16),
            sds((lo, ranks, his * MOST, width), BF16),
        ],
        in_specs=whole(9) + [any_spec, any_spec],
        out_specs=whole(17) + [any_spec, any_spec],
        scratch_shapes=[
            pltpu.VMEM((groups, ranks) + tile.shape, BF16),
            pltpu.VMEM((E, head_rows, ff), BF16),
            pltpu.VMEM((ROWS, width), BF16),
            dma((4,)),
            dma((4, 4)),
            dma((3, 4)),
            dma,
            dma((E,)),
            dma((E, 3)),
            dma((3,)),
            dma((groups, ranks)),
            dma,
            dma((E,)),
            dma((E, 3)),
            dma((3,)),
        ],
        compiler_params=params(60, collective_id=1, has_side_effects=True),
        name="begin",
    )(tile, tok, cot, routes, cos, sin, pos, mixed_prev, w_down, w_gate, w_up)


def moe_kernel(
    x_ref,
    gates_ref,
    w_ref,
    g_ref,
    back_ref,
    *rest,
):
    gt_refs = rest[:E]
    (
        xb_ref,
        gb_ref,
        od_ref,
        r1_ref,
        r2_ref,
        acc_ref,
        xs,
        gs,
        qs,
        gqs,
        d1s,
        d2s,
        bs,
        xr,
        gr,
        qr,
        gqr,
        d1r,
        d2r,
        br,
    ) = rest[E:]
    lo, ranks = g_ref.shape[:2]
    his = E // ranks
    width = x_ref.shape[1]
    at = Place(his, lo)
    core = (at.core_peer, at.f)
    side = (at.side_peer, at.f)
    greet(at.others() + [core, side])
    own_spot = pl.ds(aligned(at.hi * MOST, 16), MOST)

    for j in range(ranks):
        for hh in range(his):
            e, peer = at.member(j, hh)
            k = j * his + hh
            rows = x_ref.at[pl.ds(aligned(e * MOST, 16), MOST)]
            spot = xb_ref.at[at.f, at.l, own_spot]
            if k == 0:
                pltpu.make_async_copy(rows, spot, xr.at[at.m]).start()
                pltpu.make_async_copy(
                    gates_ref.at[e], gb_ref.at[at.f, at.l, at.hi], gr.at[at.m]
                ).start()
            else:
                send(rows, spot, xs.at[k], xr.at[at.m], peer)
                send(
                    gates_ref.at[e], gb_ref.at[at.f, at.l, at.hi], gs.at[k], gr.at[at.m], peer
                )
    acc_ref[...] = jnp.zeros_like(acc_ref)

    def take(j):
        fj = xor4(at.f, j)
        for hh in range(his):
            hi = flip(at.hi, hh)
            m = fj * his + hi
            settle(xb_ref.at[fj, at.l, pl.ds(aligned(hi * MOST, 16), MOST)], xr.at[m])
            settle(gb_ref.at[fj, at.l, hi], gr.at[m])
        for i, peer in enumerate((core, side)):
            send(xb_ref.at[fj, at.l], xb_ref.at[fj, at.l], qs.at[fj, i], qr.at[fj, i], peer)
            send(gb_ref.at[fj, at.l], gb_ref.at[fj, at.l], gqs.at[fj, i], gqr.at[fj, i], peer)

    def pass_on(j):
        fj = xor4(at.f, j)
        settle(xb_ref.at[fj, at.l2], qr.at[fj, 1])
        settle(gb_ref.at[fj, at.l2], gqr.at[fj, 1])
        send(xb_ref.at[fj, at.l2], xb_ref.at[fj, at.l2], qs.at[fj, 2], qr.at[fj, 2], core)
        send(gb_ref.at[fj, at.l2], gb_ref.at[fj, at.l2], gqs.at[fj, 2], gqr.at[fj, 2], core)

    def compute(j):
        fj = xor4(at.f, j)
        settle(xb_ref.at[fj, at.l1], qr.at[fj, 0])
        settle(gb_ref.at[fj, at.l1], gqr.at[fj, 0])
        settle(xb_ref.at[fj, at.l3], qr.at[fj, 2])
        settle(gb_ref.at[fj, at.l3], gqr.at[fj, 2])
        rows = lo * his * MOST
        x = jnp.concatenate([xb_ref[fj, i] for i in range(lo)], axis=0)
        g = jnp.concatenate([g_ref[i, fj] for i in range(lo)], axis=0)
        diagonal = lax.broadcasted_iota(jnp.int32, (MOST, 128), 0) == lane_iota(MOST)
        gate = jnp.concatenate(
            [
                pick(jnp.broadcast_to(gb_ref[fj, i, h][0:1, :], (MOST, 128)), diagonal)
                for i in range(lo)
                for h in range(his)
            ],
            axis=0,
        )
        d_exp = (g.astype(F32) * gate).astype(BF16)
        wg = w_ref[0]
        wu = w_ref[1]
        wd = w_ref[2]
        a = mm(x, wg)
        b = mm(x, wu)
        sig = 1.0 / (1.0 + jnp.exp(-a))
        hidden = (a * sig * b).astype(BF16)
        shape = (lo, his * MOST, width)
        od_ref[fj, :, :, :width] = mm(hidden, wd, NT).astype(BF16).reshape(shape)
        dh = mm(d_exp, wd)
        d_up = (dh * a * sig).astype(BF16)
        d_gate = (dh * b * sig * (1.0 + a * (1.0 - sig))).astype(BF16)
        od_ref[fj, :, :, width:] = (
            (mm(d_gate, wg, NT) + mm(d_up, wu, NT)).astype(BF16).reshape(shape)
        )
        acc_ref[0] += mm(x, d_gate, TN)
        acc_ref[1] += mm(x, d_up, TN)
        acc_ref[2] += mm(d_exp, hidden, TN)

    def to_core(j):
        fj = xor4(at.f, j)
        send(od_ref.at[fj, at.l1], r1_ref.at[fj, 0], d1s.at[fj, 0], d1r.at[fj, 0], core)
        send(od_ref.at[fj, at.l3], r1_ref.at[fj, 1], d1s.at[fj, 1], d1r.at[fj, 1], core)

    def add(ref, other):
        ref[...] = (ref[...].astype(F32) + other[...].astype(F32)).astype(BF16)

    def to_side(j):
        fj = xor4(at.f, j)
        settle(r1_ref.at[fj, 1], d1r.at[fj, 1])
        add(od_ref.at[fj, at.l2], r1_ref.at[fj, 1])
        send(od_ref.at[fj, at.l2], r2_ref.at[fj], d2s.at[fj], d2r.at[fj], side)
        settle(r1_ref.at[fj, 0], d1r.at[fj, 0])
        add(od_ref.at[fj, at.l], r1_ref.at[fj, 0])

    def to_home(j):
        fj = xor4(at.f, j)
        settle(r2_ref.at[fj], d2r.at[fj])
        add(od_ref.at[fj, at.l], r2_ref.at[fj])
        for hh in range(his):
            hi = flip(at.hi, hh)
            m = fj * his + hi
            rows = od_ref.at[fj, at.l, pl.ds(aligned(hi * MOST, 16), MOST)]
            peer = (hi * lo + at.l, fj)

            def away(rows=rows, peer=peer, m=m):
                send(rows, back_ref.at[at.m], bs.at[m], br.at[at.m], peer)

            if hh:
                away()
            else:

                @pl.when(j == 0)
                def _(rows=rows):
                    pltpu.make_async_copy(rows, back_ref.at[at.m], br.at[at.m]).start()

                pl.when(j > 0)(away)

    take(0)
    take(1)

    def step(t, _):
        @pl.when(t < ranks)
        def _():
            pass_on(t)
            compute(t)
            to_core(t)

        @pl.when(t + 2 < ranks)
        def _():
            take(t + 2)

        @pl.when((t >= 1) & (t <= ranks))
        def _():
            to_side(t - 1)

        @pl.when(t >= 2)
        def _():
            to_home(t - 2)

        return 0

    lax.fori_loop(0, ranks + 2, step, 0)

    tile = gt_refs[0].shape[1:]
    for k in range(E):
        source = lax.rem(at.m - k + E, E)
        rows = pl.ds(aligned(source // his * tile[0], 16), tile[0])
        cols = pl.ds(aligned(lax.rem(source, his) * tile[1], 128), tile[1])
        for w in range(3):
            gt_refs[k][w] = acc_ref[w, rows, cols].astype(BF16)

    for m in range(E):
        settle(back_ref.at[m], br.at[m])
    for k in range(1, E):
        settle(x_ref.at[0:MOST], xs.at[k])
        settle(gates_ref.at[0], gs.at[k])
    for f2 in range(ranks):
        for i in range(3):
            settle(xb_ref.at[0, 0], qs.at[f2, i])
            settle(gb_ref.at[0, 0], gqs.at[f2, i])
        for i in range(2):
            settle(r1_ref.at[0, 0], d1s.at[f2, i])
        settle(r2_ref.at[0], d2s.at[f2])
    for j in range(ranks):
        for hh in range(his):
            if j or hh:
                m = at.member(j, hh)[0]
                settle(back_ref.at[0], bs.at[m])


def moe(x, gates, w, g, tile):
    lo, ranks, block, width = g.shape
    dma = pltpu.SemaphoreType.DMA
    his = E // ranks
    return pl.pallas_call(
        moe_kernel,
        out_shape=[sds((E, MOST, 2 * width), BF16)] + [sds((3,) + tile, BF16)] * E,
        in_specs=whole(4),
        out_specs=whole(1 + E),
        scratch_shapes=[
            pltpu.VMEM((ranks, lo, block, width), BF16),
            pltpu.VMEM((ranks, lo, his, 8, 128), F32),
            pltpu.VMEM((ranks, lo, block, 2 * width), BF16),
            pltpu.VMEM((ranks, 2, block, 2 * width), BF16),
            pltpu.VMEM((ranks, block, 2 * width), BF16),
            pltpu.VMEM(w.shape, F32),
            dma((E,)),
            dma((E,)),
            dma((4, 3)),
            dma((4, 3)),
            dma((4, 2)),
            dma((4,)),
            dma((E,)),
            dma((E,)),
            dma((E,)),
            dma((4, 3)),
            dma((4, 3)),
            dma((4, 2)),
            dma((4,)),
            dma((E,)),
        ],
        compiler_params=params(62, collective_id=2, has_side_effects=True),
        name="moe",
    )(x, gates, w, g)


def combine_kernel(
    cot_ref,
    resid_ref,
    part_ref,
    probs_ref,
    cols_ref,
    slots_ref,
    routes_ref,
    s_ref,
    od_ref,
    out_ref,
    dres_ref,
    dl_ref,
    dw_ref,
    dv_ref,
    dg2_ref,
):
    width = cot_ref.shape[1]
    flat = s_ref[...].T
    g2 = flat[SMALL_G1 + 1 : SMALL_G1 + 2, :]
    vc = flat[SMALL_VC : SMALL_VC + CONSTS, :]
    g = cot_ref[...].astype(F32)
    lanes = lane_iota(TOK_DEV)
    cols = cols_ref[...]

    def col(i):
        return pick(cols, lanes == i)

    gate0, gate1, gate_id, inv2 = col(0), col(1), col(2), col(3)
    resid = resid_ref[...]
    unit2 = resid * inv2
    normed = unit2 * g2
    narrow = normed.astype(BF16)
    od = od_ref[...].reshape(ROWS, 2 * width)
    slot = lane_iota(TOK_DEV, ROWS)
    hot0 = jnp.where(slot == slots_ref[:, 0:1], 1.0, 0.0).astype(BF16)
    hot1 = jnp.where(slot == slots_ref[:, 1:2], 1.0, 0.0).astype(BF16)
    y0 = mm(hot0, od[:, :width])
    y1 = mm(hot1, od[:, :width])
    out_ref[...] = (part_ref[...] + gate0 * y0 + gate1 * y1).astype(BF16)
    a_n = jnp.sum(g * normed, axis=1, keepdims=True)
    dg0 = jnp.sum(g * y0, axis=1, keepdims=True)
    dg1 = jnp.sum(g * y1, axis=1, keepdims=True)
    r0 = routes_ref[:, 0:1]
    r1 = routes_ref[:, 1:2]
    dg0 = jnp.where(r0 == E + 1, a_n, dg0)
    dg1 = jnp.where(r1 == E + 1, a_n, dg1)
    g_scale = gate_id
    dl = jnp.zeros((TOK_DEV, 128), F32)
    vmix = jnp.zeros((TOK_DEV, 128), F32)
    for c in range(CONSTS):
        gate_c, ma, mb = col(4 + 3 * c), col(5 + 3 * c), col(6 + 3 * c)
        a_v = jnp.sum(g * vc[c : c + 1, :], axis=1, keepdims=True)
        branch = ma * a_n + mb * a_v
        dg0 = jnp.where(r0 == E + 2 + c, branch, dg0)
        dg1 = jnp.where(r1 == E + 2 + c, branch, dg1)
        g_scale = g_scale + gate_c * ma
        da = gate_c * a_n
        db = gate_c * a_v
        mean = ma * da + mb * db
        dl = jnp.where(lanes == SMALL_C + 2 * c, ma * (da - mean), dl)
        dl = jnp.where(lanes == SMALL_C + 1 + 2 * c, mb * (db - mean), dl)
        vmix = jnp.where(lanes == c, gate_c * mb, vmix)
    probs = probs_ref[...]
    d_probs = jnp.where(lanes == r0, dg0, 0.0) + jnp.where(lanes == r1, dg1, 0.0)
    d_logits = probs * (d_probs - jnp.sum(probs * d_probs, axis=1, keepdims=True))
    dl = jnp.where(lanes < EXPERTS_ALL, d_logits, dl)
    dl_ref[...] = dl
    high = dl.astype(BF16)
    low = (dl - high.astype(F32)).astype(BF16)
    wr = s_ref[...].astype(BF16)
    d_normed = g_scale * g + mm(hot0 + hot1, od[:, width:])
    d_normed = d_normed + mm(high, wr, NT) + mm(low, wr, NT)
    dw_ref[...] = mm(high, narrow, TN) + mm(low, narrow, TN)
    vhigh = vmix.astype(BF16)
    vlow = (vmix - vhigh.astype(F32)).astype(BF16)
    dv_ref[...] = mm(vhigh, cot_ref[...], TN) + mm(vlow, cot_ref[...], TN)
    dg2_ref[...] = jnp.broadcast_to(
        jnp.sum(d_normed * unit2, axis=0, keepdims=True), dg2_ref.shape
    )
    n = d_normed * g2
    dres_ref[...] = g + inv2 * (n - unit2 * jnp.mean(n * unit2, axis=1, keepdims=True))


def combine(cot, resid, part, probs, cols, slots, routes, small, od):
    width = cot.shape[1]
    return pl.pallas_call(
        combine_kernel,
        out_shape=[
            sds((TOK_DEV, width), BF16),
            sds((TOK_DEV, width), F32),
            sds((TOK_DEV, 128), F32),
            sds((128, width), F32),
            sds((128, width), F32),
            sds((8, width), F32),
        ],
        in_specs=whole(9),
        out_specs=whole(6),
        compiler_params=params(56),
        name="combine",
    )(cot, resid, part, probs, cols, slots, routes, small, od)


def backward_kernel(
    dres_ref,
    wf_ref,
    q_ref,
    k_ref,
    v_ref,
    n1_ref,
    inv1_ref,
    mix_ref,
    lse_ref,
    cos_ref,
    sin_ref,
    pos_ref,
    tok_ref,
    halo_ref,
    gw_ref,
    down_ref,
    dhalo_ref,
    dg1_ref,
    dm_ref,
    dq_ref,
    dk_ref,
    dv_ref,
    dqr_ref,
    dkr_ref,
    dvr_ref,
):
    scale = HEAD_DIM ** (-0.5)
    width = dres_ref.shape[1]
    d_attn = dres_ref[...].astype(BF16)
    gw_ref[3] = mm(mix_ref[...], d_attn, TN).astype(BF16)
    dm_ref[...] = mm(d_attn, wf_ref[3], NT).astype(BF16)
    dk_ref[...] = jnp.zeros_like(dk_ref)
    dv_ref[...] = jnp.zeros_like(dv_ref)

    def pair(p, _):
        span = pl.ds(pl.multiple_of(p * 128, 128), 128)
        for first, count in QBLOCKS:
            keys = key_span(first)
            ok = allowed_mask(pos_ref, first, count)[:, :keys]
            q = q_ref[pl.ds(first, count), span]
            dm = dm_ref[pl.ds(first, count), span]
            k = k_ref[pl.ds(first, keys), span]
            v = v_ref[pl.ds(first, keys), span]
            lane = lane_iota(count)
            key_lane = lane_iota(keys)
            lse = lse_ref[pl.ds(first, count), :]
            dq = dk = dv = None
            for h in range(2):
                mine = (lane < HEAD_DIM) if h == 0 else (lane >= HEAD_DIM)
                key_mine = (key_lane < HEAD_DIM) if h == 0 else (key_lane >= HEAD_DIM)
                qh = jnp.where(mine, q, jnp.zeros_like(q))
                dmh = jnp.where(mine, dm, jnp.zeros_like(dm))
                s = jnp.where(ok, mm(qh, k, NT) * scale, NEG)
                probs = jnp.where(ok, jnp.exp(s - pick(lse, lane == 2 * p + h)), 0.0)
                dp = mm(dmh, v, NT)
                delta = jnp.sum(probs * dp, axis=1, keepdims=True)
                ds = (probs * (dp - delta)).astype(BF16)
                pb = probs.astype(BF16)
                dqh = mm(ds, k)
                dkh = mm(ds, q, TN)
                dvh = mm(pb, dm, TN)
                dq = dqh if h == 0 else jnp.where(mine, dqh, dq)
                dk = dkh if h == 0 else jnp.where(key_mine, dkh, dk)
                dv = dvh if h == 0 else jnp.where(key_mine, dvh, dv)
            dq_ref[pl.ds(first, count), span] = dq * scale
            dk_ref[pl.ds(first, keys), span] += dk * scale
            dv_ref[pl.ds(first, keys), span] += dv
        return 0

    lax.fori_loop(0, HEADS // 2, pair, 0)

    def finish(i, _):
        span = pl.ds(pl.multiple_of(i * 256, 256), 256)
        cos = cos_ref[...]
        sin = sin_ref[...]
        dqr_ref[:, span] = turn(dq_ref[:, span], cos[HALO:], -sin[HALO:]).astype(BF16)
        dkr_ref[:, span] = turn(dk_ref[:, span], cos, -sin).astype(BF16)
        dvr_ref[:, span] = dv_ref[:, span].astype(BF16)
        return 0

    lax.fori_loop(0, width // 256, finish, 0)
    gw_ref[0] = mm(n1_ref[HALO:, :], dqr_ref[...], TN).astype(BF16)
    gw_ref[1] = mm(n1_ref[...], dkr_ref[...], TN).astype(BF16)
    gw_ref[2] = mm(n1_ref[...], dvr_ref[...], TN).astype(BF16)
    d_all = mm(dkr_ref[...], wf_ref[1], NT) + mm(dvr_ref[...], wf_ref[2], NT)
    d_own = d_all[HALO:] + mm(dqr_ref[...], wf_ref[0], NT)
    inv1 = inv1_ref[:, 0:1]
    unit_own = tok_ref[...].astype(F32) * inv1[HALO:]
    unit_halo = halo_ref[...].astype(F32) * inv1[:HALO]
    d_halo = d_all[:HALO]
    dg1 = jnp.sum(d_own * unit_own, axis=0, keepdims=True) + jnp.sum(
        d_halo * unit_halo, axis=0, keepdims=True
    )
    dg1_ref[...] = jnp.broadcast_to(dg1, dg1_ref.shape)
    down_ref[...] = d_own
    dhalo_ref[...] = d_halo.astype(BF16)


def backward(dres, wf, q, k, v, n1, inv1, mix, lse, cos, sin, pos, tok, halo):
    width = tok.shape[1]
    return pl.pallas_call(
        backward_kernel,
        out_shape=[
            sds((4, width, width), BF16),
            sds((TOK_DEV, width), F32),
            sds((HALO, width), BF16),
            sds((8, width), F32),
        ],
        in_specs=whole(14),
        out_specs=whole(4),
        scratch_shapes=[
            pltpu.VMEM((TOK_DEV, width), BF16),
            pltpu.VMEM((TOK_DEV, width), F32),
            pltpu.VMEM((KEYS, width), F32),
            pltpu.VMEM((KEYS, width), F32),
            pltpu.VMEM((TOK_DEV, width), BF16),
            pltpu.VMEM((KEYS, width), BF16),
            pltpu.VMEM((KEYS, width), BF16),
        ],
        compiler_params=params(60),
        name="backward",
    )(dres, wf, q, k, v, n1, inv1, mix, lse, cos, sin, pos, tok, halo)


def finish_kernel(dres_ref, down_ref, back_ref, tok_ref, inv1_ref, s_ref, out_ref):
    width = tok_ref.shape[1]
    inv1 = inv1_ref[HALO:, 0:1]
    unit = tok_ref[...].astype(F32) * inv1
    back = jnp.concatenate(
        [jnp.zeros((TOK_DEV - HALO, width), F32), back_ref[...].astype(F32)], axis=0
    )
    g1 = s_ref[...].T[SMALL_G1 : SMALL_G1 + 1, :]
    m = (down_ref[...] + back) * g1
    d_dealt = inv1 * (m - unit * jnp.mean(m * unit, axis=1, keepdims=True))
    out_ref[...] = dres_ref[...] + d_dealt.astype(BF16).astype(F32)


def finish(dres, down, back, tok, inv1, small):
    return pl.pallas_call(
        finish_kernel,
        out_shape=sds(dres.shape, F32),
        in_specs=whole(6),
        out_specs=pl.BlockSpec(memory_space=pltpu.VMEM),
        compiler_params=params(40),
        name="finish",
    )(dres, down, back, tok, inv1, small)


def store_kernel(own_ref, *refs):
    t_refs = refs[:E]
    gate_ref, up_ref, down_ref = refs[E:]
    own = own_ref[0]
    for k in range(E):
        expert = lax.rem(own + k, E)
        gate_ref[expert] = t_refs[k][0].astype(F32)
        up_ref[expert] = t_refs[k][1].astype(F32)
        down_ref[expert] = t_refs[k][2].astype(F32).T


def store(own, tiles):
    rows, cols = tiles[0].shape[1:]
    return pl.pallas_call(
        store_kernel,
        out_shape=[sds((E, rows, cols), F32)] * 2 + [sds((E, cols, rows), F32)],
        in_specs=[pl.BlockSpec(memory_space=pltpu.SMEM)] + whole(E),
        out_specs=whole(3),
        compiler_params=params(40),
        name="store",
    )(own, *tiles)


def fast_device(
    tokens,
    cotangent,
    prev_logits,
    lengths,
    dealing,
    routes,
    gain_one,
    w_query,
    w_key,
    w_value,
    w_out,
    gain_two,
    w_router,
    w_mix,
    w_const,
    v_const,
    w_gate,
    w_up,
    w_down,
):
    groups = lax.axis_size("grp")
    ranks = lax.axis_size("fsdp")
    his = E // ranks
    lo = groups // his
    g_id = lax.axis_index("grp")
    f_id = lax.axis_index("fsdp")
    width = tokens.shape[1]
    axes = ("grp", "fsdp")
    own = (f_id * his + g_id // lo).astype(jnp.int32).reshape(1)
    per = gain_one.shape[0]

    small = jnp.concatenate(
        [w_router, gain_one[:, None], gain_two[:, None], v_const, w_const], axis=1
    )
    small = jnp.pad(small, ((0, 0), (0, 128 - small.shape[1])))
    small = small.reshape(per // 8, 8, 128).transpose(1, 0, 2).reshape(8, per // 8 * 128)
    tile = jnp.concatenate([w_query, w_key, w_value, w_out], axis=1)
    tile = jnp.concatenate([tile, small], axis=0)

    seq_len = lengths[0]
    count = seq_len.shape[0]
    ids = jnp.arange(count, dtype=jnp.int32)
    ends = jnp.sum(jnp.where(ids[:, None] >= ids[None, :], seq_len[None, :], 0), axis=1)
    row = f_id * TOK_DEV + jnp.arange(-HALO, TOK_DEV, dtype=jnp.int32)
    start = jnp.max(jnp.where(ends[None, :] <= row[:, None], ends[None, :], 0), axis=1)
    pos = jnp.maximum(row - start, 0)
    cos, sin = rotation_tables(pos, HEAD_DIM)
    cos = jnp.concatenate([cos] * 4, axis=1)
    sin = jnp.concatenate([-sin, sin, -sin, sin], axis=1)
    pos_own = jnp.broadcast_to(pos[HALO:, None], (TOK_DEV, 128))
    mixed_prev = exact_dot(prev_logits, w_mix.astype(F32))
    mixed_prev = jnp.pad(mixed_prev, ((0, 0), (0, 128 - EXPERTS_ALL)))

    outs = begin(
        tile,
        tokens,
        cotangent,
        routes,
        cos,
        sin,
        pos_own,
        mixed_prev,
        w_down,
        w_gate,
        w_up,
        groups,
        ranks,
    )
    wf, small, halo, slots, q, k, v, n1, inv1, mix, lse, resid, part, probs, cols = outs[:15]
    x, gates, w_all, g_all = outs[15:]
    done = moe(x, gates, w_all, g_all, w_gate.shape[1:])
    od_back, g_tiles = done[0], done[1:]
    output, d_resid, dl, dw, dv, dg2 = combine(
        cotangent, resid, part, probs, cols, slots, routes, small, od_back
    )
    d_logits = dl[:, :EXPERTS_ALL]
    grad_prev = exact_dot(d_logits, w_mix.astype(F32).T)
    d_mix = exact_dot(prev_logits.T, d_logits)
    gw, down, d_halo, dg1 = backward(
        d_resid, wf, q, k, v, n1, inv1, mix, lse, cos, sin, pos_own, tokens, halo
    )
    back = lax.ppermute(d_halo, "fsdp", [(f + 1, f) for f in range(ranks - 1)])
    grad_tokens = finish(d_resid, down, back, tokens, inv1, small)

    def back_perm(k):
        pairs = []
        for g in range(groups):
            for f in range(ranks):
                m = (f * his + g // lo + k) % E
                pairs.append(((m % his * lo + g % lo) * ranks + m // his, g * ranks + f))
        return pairs

    tiles_back = [
        g_tiles[i] if i == 0 else lax.ppermute(g_tiles[i], axes, back_perm(i)) for i in range(E)
    ]
    grad_gate, grad_up, grad_down = store(own, tiles_back)

    cols_per = width // groups
    rows_per = width // ranks
    gw = gw.reshape(4, width, groups, cols_per).transpose(2, 0, 1, 3)
    gw = lax.psum_scatter(gw, "grp", scatter_dimension=0, tiled=False)
    gw = gw.reshape(4, ranks, rows_per, cols_per).transpose(1, 0, 2, 3)
    gw = lax.psum_scatter(gw, "fsdp", scatter_dimension=0, tiled=False).astype(F32)
    tiny = jnp.concatenate(
        [
            dg1[:1],
            dg2[:1],
            dv[:CONSTS],
            dw[:EXPERTS_ALL],
            dw[SMALL_C : SMALL_C + 2 * CONSTS],
            jnp.pad(d_mix.reshape(1, -1), ((0, 0), (0, width - EXPERTS_ALL * EXPERTS_ALL))),
        ],
        axis=0,
    )
    tiny = lax.psum(tiny, axes)
    grad_mix = tiny[-1, : EXPERTS_ALL * EXPERTS_ALL].reshape(EXPERTS_ALL, EXPERTS_ALL)
    first = (g_id * ranks + f_id) * per
    mine = lax.dynamic_slice(tiny, (0, first), (tiny.shape[0], per))
    n_small = 2 + CONSTS
    return (
        output,
        grad_tokens,
        grad_prev,
        mine[0],
        gw[0],
        gw[1],
        gw[2],
        gw[3],
        mine[1],
        mine[n_small : n_small + EXPERTS_ALL].T,
        grad_mix,
        mine[n_small + EXPERTS_ALL : n_small + EXPERTS_ALL + 2 * CONSTS].T,
        mine[2:n_small].T,
        grad_gate,
        grad_up,
        grad_down,
    )


def suits(mesh):
    return mesh.shape["fsdp"] == 4 and mesh.shape["grp"] == 8


def solution(mesh):
    return jax.shard_map(
        fast_device if suits(mesh) else per_device,
        mesh=mesh,
        in_specs=(
            P(("grp", "fsdp"), None),
            P(("grp", "fsdp"), None),
            P(("grp", "fsdp"), None),
            P("grp", None),
            P("grp", None),
            P(("grp", "fsdp"), None),
            P(("grp", "fsdp")),
            P("fsdp", "grp"),
            P("fsdp", "grp"),
            P("fsdp", "grp"),
            P("fsdp", "grp"),
            P(("grp", "fsdp")),
            P(("grp", "fsdp"), None),
            P(),
            P(("grp", "fsdp"), None),
            P(("grp", "fsdp"), None),
            P(None, "fsdp", "grp"),
            P(None, "fsdp", "grp"),
            P(None, "grp", "fsdp"),
        ),
        out_specs=(
            P(("grp", "fsdp"), None),
            P(("grp", "fsdp"), None),
            P(("grp", "fsdp"), None),
            P(("grp", "fsdp")),
            P("fsdp", "grp"),
            P("fsdp", "grp"),
            P("fsdp", "grp"),
            P("fsdp", "grp"),
            P(("grp", "fsdp")),
            P(("grp", "fsdp"), None),
            P(),
            P(("grp", "fsdp"), None),
            P(("grp", "fsdp"), None),
            P(None, "fsdp", "grp"),
            P(None, "fsdp", "grp"),
            P(None, "grp", "fsdp"),
        ),
        check_vma=False,
    )
```

```python
import math

import jax
import jax.numpy as jnp
from jax import lax
from jax.experimental import pallas as pl
from jax.experimental.pallas import tpu as pltpu
from jax.sharding import PartitionSpec as P

HEADS = 12
HEAD_DIM = 64
E = 8
CONSTS = 2
BLOCK = 128
EXPERTS_ALL = 12
CAP = 384
TOK_DEV = 320
MOST = 80


NORM_EPS = 1e-05
EXACT = lax.Precision.HIGHEST


def rotation_tables(positions, head_dim):
    half_dim = head_dim // 2
    inv_freq = jnp.exp(
        jnp.arange(half_dim, dtype=jnp.float32) * (-2.0 * math.log(10000.0) / head_dim)
    )
    angles = positions.astype(jnp.float32)[:, None] * inv_freq[None, :]
    return (jnp.cos(angles), jnp.sin(angles))


def rotate(values, cos_table, sin_table):
    row_count = values.shape[0]
    half_dim = cos_table.shape[1]
    heads_view = values.reshape(row_count, -1, 2 * half_dim)
    front_half = heads_view[:, :, :half_dim]
    back_half = heads_view[:, :, half_dim:]
    cos_view = cos_table[:, None, :]
    sin_view = sin_table[:, None, :]
    turned = jnp.concatenate(
        [
            front_half * cos_view - back_half * sin_view,
            back_half * cos_view + front_half * sin_view,
        ],
        axis=2,
    )
    return turned.reshape(row_count, -1)


def exact_dot(left_side, right_side):
    return jnp.dot(left_side, right_side, precision=EXACT, preferred_element_type=jnp.float32)


def per_device(
    tokens,
    cotangent,
    prev_logits,
    lengths,
    dealing,
    routes,
    gain_one,
    w_query,
    w_key,
    w_value,
    w_out,
    gain_two,
    w_router,
    w_mix,
    w_const,
    v_const,
    w_gate,
    w_up,
    w_down,
):
    groups = lax.axis_size("grp")
    dealers = lax.axis_size("fsdp")
    device = lax.axis_index("fsdp")
    model_width = tokens.shape[1]
    per_shard = model_width // (groups * dealers)
    pairs = HEADS // 2
    pair_width = 2 * HEAD_DIM
    scale = HEAD_DIM ** (-0.5)
    seq_len = lengths[0]
    deal_order = dealing[0]
    seq_count = seq_len.shape[0]
    seq_ids = jnp.arange(seq_count, dtype=jnp.int32)
    seq_ends = jnp.cumsum(seq_len)
    starts = seq_ends - seq_len
    padded = (seq_len + BLOCK - 1) // BLOCK * BLOCK
    order_hot = (deal_order[:, None] == seq_ids[None, :]).astype(jnp.int32)
    dealt_len = jnp.sum(order_hot * seq_len[None, :], axis=1)
    dealt_pad = jnp.sum(order_hot * padded[None, :], axis=1)
    dealt_start = jnp.sum(order_hot * starts[None, :], axis=1)
    slot_of = jnp.sum(order_hot * seq_ids[:, None], axis=0)
    pair_index = 2 * device
    row_ids = jnp.arange(CAP, dtype=jnp.int32)
    in_second = row_ids >= dealt_pad[pair_index]
    position = row_ids - jnp.where(in_second, dealt_pad[pair_index], 0)
    seq_limit = jnp.where(in_second, dealt_len[pair_index + 1], dealt_len[pair_index])
    live_rows = position < seq_limit
    source = jnp.where(in_second, dealt_start[pair_index + 1], dealt_start[pair_index]) + position
    source = jnp.where(live_rows, source, -1)
    given_rows = device * TOK_DEV + jnp.arange(TOK_DEV, dtype=jnp.int32)
    seq_hot = (
        (given_rows[:, None] >= starts[None, :]) & (given_rows[:, None] < seq_ends[None, :])
    ).astype(jnp.int32)
    offset_in = given_rows - jnp.sum(seq_hot * starts[None, :], axis=1)
    slot_rank = jnp.sum(seq_hot * slot_of[None, :], axis=1)
    is_second = slot_rank % 2
    lead_pad = jnp.take(dealt_pad, slot_rank - is_second)
    target = slot_rank // 2 * CAP + jnp.where(is_second == 1, lead_pad, 0) + offset_in

    def deal(values):
        shard_rows = lax.all_gather(values, "fsdp", axis=0, tiled=True)
        row_span = shard_rows.shape[0]
        inside = (source >= 0) & (source < row_span)
        taken_rows = jnp.take(shard_rows, jnp.clip(source, 0, row_span - 1), axis=0)
        return jnp.where(inside[:, None], taken_rows, jnp.zeros((CAP, model_width), jnp.bfloat16))

    def give_back(values):
        shard_rows = lax.all_gather(values, "fsdp", axis=0, tiled=True)
        row_span = shard_rows.shape[0]
        inside = (target >= 0) & (target < row_span)
        taken_rows = jnp.take(shard_rows, jnp.clip(target, 0, row_span - 1), axis=0)
        return jnp.where(
            inside[:, None], taken_rows, jnp.zeros((TOK_DEV, model_width), jnp.bfloat16)
        )

    def collect():
        gate_in, up_in, down_in = (w_gate, w_up, w_down)
        sectioned = (
            lax.all_gather(gain_one, "fsdp", axis=0, tiled=True),
            lax.all_gather(w_query, "fsdp", axis=0, tiled=True),
            lax.all_gather(w_key, "fsdp", axis=0, tiled=True),
            lax.all_gather(w_value, "fsdp", axis=0, tiled=True),
            lax.all_gather(w_out, "fsdp", axis=0, tiled=True),
            lax.all_gather(gain_two, "fsdp", axis=0, tiled=True),
            lax.all_gather(w_router, "fsdp", axis=0, tiled=True),
            lax.all_gather(w_const, "fsdp", axis=0, tiled=True),
            lax.all_gather(v_const, "fsdp", axis=0, tiled=True),
            lax.all_gather(gate_in, "fsdp", axis=1, tiled=True),
            lax.all_gather(up_in, "fsdp", axis=1, tiled=True),
            lax.all_gather(down_in, "fsdp", axis=2, tiled=True),
        )
        (
            part_g1,
            part_q,
            part_k,
            part_v,
            part_o,
            part_g2,
            part_r,
            part_c,
            part_vc,
            part_gate,
            part_up,
            part_down,
        ) = sectioned
        small = (
            lax.all_gather(part_g1, "grp", axis=0, tiled=True),
            lax.all_gather(part_q, "grp", axis=1, tiled=True),
            lax.all_gather(part_k, "grp", axis=1, tiled=True),
            lax.all_gather(part_v, "grp", axis=1, tiled=True),
            lax.all_gather(part_o, "grp", axis=1, tiled=True),
            lax.all_gather(part_g2, "grp", axis=0, tiled=True),
            lax.all_gather(part_r, "grp", axis=0, tiled=True),
            lax.all_gather(part_c, "grp", axis=0, tiled=True),
            lax.all_gather(part_vc, "grp", axis=0, tiled=True),
        )
        experts = (
            lax.all_gather(part_gate, "grp", axis=2, tiled=True),
            lax.all_gather(part_up, "grp", axis=2, tiled=True),
            lax.all_gather(part_down, "grp", axis=1, tiled=True),
        )
        return tuple(small) + tuple(experts)

    (
        gain1,
        weight_q,
        weight_k,
        weight_v,
        weight_o,
        gain2,
        router,
        wconst,
        vconst,
        wgate,
        wup,
        wdown,
    ) = collect()
    dealt = deal(tokens)
    dealt_f = dealt.astype(jnp.float32)
    inv_one = lax.rsqrt(jnp.mean(dealt_f * dealt_f, axis=1, keepdims=True) + NORM_EPS)
    unit_one = dealt_f * inv_one
    gain1_f = gain1.astype(jnp.float32)
    normed_one = (unit_one * gain1_f).astype(jnp.bfloat16)
    cos_table, sin_table = rotation_tables(position, HEAD_DIM)
    query = rotate(
        jnp.dot(normed_one, weight_q, preferred_element_type=jnp.float32), cos_table, sin_table
    ).astype(jnp.bfloat16)
    keyed = rotate(
        jnp.dot(normed_one, weight_k, preferred_element_type=jnp.float32), cos_table, sin_table
    ).astype(jnp.bfloat16)
    values_proj = jnp.dot(normed_one, weight_v, preferred_element_type=jnp.float32).astype(
        jnp.bfloat16
    )
    allowed = (
        (in_second[:, None] == in_second[None, :])
        & (position[None, :] <= position[:, None])
        & live_rows[None, :]
    )

    def by_pairs(values):
        return values.reshape(CAP, pairs, pair_width).transpose(1, 0, 2)

    def from_pairs(values):
        return values.transpose(1, 0, 2).reshape(CAP, model_width)

    def pair_scores(q_pair, k_pair):
        query_heads = q_pair.reshape(CAP, 2, HEAD_DIM)
        key_heads = k_pair.reshape(CAP, 2, HEAD_DIM)
        scores = (
            jnp.einsum("qhd,khd->hqk", query_heads, key_heads, preferred_element_type=jnp.float32)
            * scale
        )
        return (jnp.where(allowed[None], scores, -1e30), query_heads, key_heads)

    def attend(pair_items):
        q_pair, k_pair, v_pair = pair_items
        scores, query_heads, key_heads = pair_scores(q_pair, k_pair)
        row_top = jnp.max(scores, axis=-1, keepdims=True)
        weights_exp = jnp.exp(scores - row_top)
        row_total = jnp.sum(weights_exp, axis=-1, keepdims=True)
        attn_probs = weights_exp / row_total
        value_heads = v_pair.reshape(CAP, 2, HEAD_DIM)
        mixed_pair = jnp.einsum(
            "hqk,khd->qhd",
            attn_probs.astype(jnp.bfloat16),
            value_heads,
            preferred_element_type=jnp.float32,
        )
        return (mixed_pair.reshape(CAP, pair_width), (row_top + jnp.log(row_total))[:, :, 0])

    mixed_pairs, log_sums = lax.map(
        attend, (by_pairs(query), by_pairs(keyed), by_pairs(values_proj))
    )
    mixed = from_pairs(mixed_pairs).astype(jnp.bfloat16)
    attn_out = jnp.dot(mixed, weight_o, preferred_element_type=jnp.float32).astype(jnp.bfloat16)
    returned = give_back(attn_out)
    resid = tokens.astype(jnp.float32) + returned.astype(jnp.float32)
    inv_two = lax.rsqrt(jnp.mean(resid * resid, axis=1, keepdims=True) + NORM_EPS)
    unit_two = resid * inv_two
    gain2_f = gain2.astype(jnp.float32)
    normed = unit_two * gain2_f
    narrow = normed.astype(jnp.bfloat16)
    mix_f = w_mix.astype(jnp.float32)
    router_f = router.astype(jnp.float32)
    wconst_f = wconst.astype(jnp.float32)
    logits = jnp.dot(narrow, router, preferred_element_type=jnp.float32) + exact_dot(
        prev_logits, mix_f
    )
    logit_top = jnp.max(logits, axis=1, keepdims=True)
    logit_exp = jnp.exp(logits - logit_top)
    route_probs = logit_exp / jnp.sum(logit_exp, axis=1, keepdims=True)
    expert_ids = jnp.arange(EXPERTS_ALL, dtype=jnp.int32)
    chosen = (
        (routes[:, 0:1] == expert_ids[None, :]) | (routes[:, 1:2] == expert_ids[None, :])
    ).astype(jnp.float32)
    gate_weights = route_probs * chosen
    result = resid + gate_weights[:, E + 1 : E + 2] * normed
    const_logits = jnp.dot(narrow, wconst, preferred_element_type=jnp.float32)
    vconst_f = vconst.astype(jnp.float32)
    const_mixes = []
    const_branches = []
    for const_idx in range(CONSTS):
        part_logits = const_logits[:, 2 * const_idx : 2 * const_idx + 2]
        part_exp = jnp.exp(part_logits - jnp.max(part_logits, axis=1, keepdims=True))
        const_mix = part_exp / jnp.sum(part_exp, axis=1, keepdims=True)
        branch = const_mix[:, 0:1] * normed + const_mix[:, 1:2] * vconst_f[:, const_idx][None, :]
        const_mixes.append(const_mix)
        const_branches.append(branch)
        result = result + gate_weights[:, E + 2 + const_idx : E + 3 + const_idx] * branch
    slot_list = []
    filled_list = []
    slot_gate_list = []
    for expert in range(E):
        member = (routes[:, 0] == expert) | (routes[:, 1] == expert)
        place_at = jnp.cumsum(member.astype(jnp.int32)) - 1
        slot_table = (
            jnp.zeros((MOST,), jnp.int32)
            .at[jnp.where(member, place_at, MOST)]
            .set(jnp.arange(TOK_DEV, dtype=jnp.int32), mode="drop")
        )
        filled = jnp.arange(MOST, dtype=jnp.int32) < jnp.sum(member.astype(jnp.int32))
        slot_list.append(slot_table)
        filled_list.append(filled)
        slot_gate_list.append(jnp.where(filled, jnp.take(gate_weights[:, expert], slot_table), 0.0))
    slot_tables = jnp.stack(slot_list, axis=0)
    filled_all = jnp.stack(filled_list, axis=0)
    slot_gates = jnp.stack(slot_gate_list, axis=0)
    expert_kept = []
    out_list = []
    for expert in range(E):
        picked = jnp.take(narrow, slot_tables[expert], axis=0)
        gate_part = jnp.dot(picked, wgate[expert], preferred_element_type=jnp.float32)
        up_part = jnp.dot(picked, wup[expert], preferred_element_type=jnp.float32)
        hidden = (jax.nn.silu(gate_part) * up_part).astype(jnp.bfloat16)
        out_list.append(jnp.dot(hidden, wdown[expert], preferred_element_type=jnp.float32))
        expert_kept.append((picked, gate_part, up_part, hidden))
    expert_outs = jnp.stack(out_list, axis=0)
    for expert in range(E):
        result = result.at[slot_tables[expert]].add(
            slot_gates[expert][:, None] * expert_outs[expert]
        )
    output = result.astype(jnp.bfloat16)
    (
        gain1,
        weight_q,
        weight_k,
        weight_v,
        weight_o,
        gain2,
        router,
        wconst,
        vconst,
        wgate,
        wup,
        wdown,
    ) = collect()
    gain1_f = gain1.astype(jnp.float32)
    gain2_f = gain2.astype(jnp.float32)
    router_f = router.astype(jnp.float32)
    wconst_f = wconst.astype(jnp.float32)
    vconst_f = vconst.astype(jnp.float32)
    grad_out = cotangent.astype(jnp.float32)
    d_gate_cols = [jnp.zeros((TOK_DEV,), jnp.float32) for expert in range(EXPERTS_ALL)]
    d_gate_cols[E + 1] = jnp.sum(grad_out * normed, axis=1)
    d_normed = gate_weights[:, E + 1 : E + 2] * grad_out
    d_const_parts = []
    d_vconst_cols = []
    for const_idx in range(CONSTS):
        const_mix = const_mixes[const_idx]
        gate_col = gate_weights[:, E + 2 + const_idx]
        d_gate_cols[E + 2 + const_idx] = jnp.sum(grad_out * const_branches[const_idx], axis=1)
        d_piece = gate_col[:, None] * grad_out
        d_normed = d_normed + const_mix[:, 0:1] * d_piece
        d_cmix = jnp.stack(
            [
                jnp.sum(d_piece * normed, axis=1),
                jnp.sum(d_piece * vconst_f[:, const_idx][None, :], axis=1),
            ],
            axis=1,
        )
        d_const_parts.append(
            const_mix * (d_cmix - jnp.sum(const_mix * d_cmix, axis=1, keepdims=True))
        )
        d_vconst_cols.append(exact_dot(const_mix[:, 1] * gate_col, grad_out))
    d_const_logits = jnp.concatenate(d_const_parts, axis=1)
    grad_rows_all = jnp.take(grad_out, slot_tables.reshape(-1), axis=0).reshape(
        E, MOST, model_width
    )
    d_slot_gates = jnp.where(filled_all, jnp.sum(grad_rows_all * expert_outs, axis=2), 0.0)
    for expert in range(E):
        d_gate_cols[expert] = (
            jnp.zeros((TOK_DEV,), jnp.float32).at[slot_tables[expert]].add(d_slot_gates[expert])
        )
    d_expert_all = (slot_gates[:, :, None] * grad_rows_all).astype(jnp.bfloat16)
    d_wgate_list = []
    d_wup_list = []
    d_wdown_list = []
    d_picked_list = []
    for expert in range(E):
        picked, gate_part, up_part, hidden = expert_kept[expert]
        d_expert = d_expert_all[expert]
        d_wdown_list.append(jnp.dot(hidden.T, d_expert, preferred_element_type=jnp.float32))
        d_hidden = jnp.dot(d_expert, wdown[expert].T, preferred_element_type=jnp.float32)
        sigmoid_g = jax.nn.sigmoid(gate_part)
        d_up_part = (d_hidden * gate_part * sigmoid_g).astype(jnp.bfloat16)
        d_gate_part = (
            d_hidden * up_part * sigmoid_g * (1.0 + gate_part * (1.0 - sigmoid_g))
        ).astype(jnp.bfloat16)
        d_wgate_list.append(jnp.dot(picked.T, d_gate_part, preferred_element_type=jnp.float32))
        d_wup_list.append(jnp.dot(picked.T, d_up_part, preferred_element_type=jnp.float32))
        d_picked_list.append(
            jnp.dot(d_gate_part, wgate[expert].T, preferred_element_type=jnp.float32)
            + jnp.dot(d_up_part, wup[expert].T, preferred_element_type=jnp.float32)
        )
    d_picked_all = jnp.stack(d_picked_list, axis=0)
    d_wgate_full = jnp.stack(d_wgate_list, axis=0)
    d_wup_full = jnp.stack(d_wup_list, axis=0)
    d_wdown_full = jnp.stack(d_wdown_list, axis=0)
    d_narrow = jnp.zeros((TOK_DEV, model_width), jnp.float32)
    for expert in range(E):
        d_narrow = d_narrow.at[slot_tables[expert]].add(
            jnp.where(filled_all[expert][:, None], d_picked_all[expert], 0.0)
        )
    d_gate_w = jnp.stack(d_gate_cols, axis=1)
    d_probs = d_gate_w * chosen
    d_logits = route_probs * (d_probs - jnp.sum(route_probs * d_probs, axis=1, keepdims=True))
    narrow_f = narrow.astype(jnp.float32)
    d_narrow = d_narrow + exact_dot(d_logits, router_f.T) + exact_dot(d_const_logits, wconst_f.T)
    d_router_full = exact_dot(narrow_f.T, d_logits)
    d_wconst_full = exact_dot(narrow_f.T, d_const_logits)
    d_vconst_full = jnp.stack(d_vconst_cols, axis=1)
    d_mix_full = exact_dot(prev_logits.T, d_logits)
    grad_prev = exact_dot(d_logits, mix_f.T)
    d_normed_total = d_normed + d_narrow
    d_gain2_full = jnp.sum(d_normed_total * unit_two, axis=0)
    d_unit_two = d_normed_total * gain2_f
    d_resid = grad_out + inv_two * (
        d_unit_two - unit_two * jnp.mean(d_unit_two * unit_two, axis=1, keepdims=True)
    )
    d_attn = deal(d_resid.astype(jnp.bfloat16))
    d_wo_full = jnp.dot(mixed.T, d_attn, preferred_element_type=jnp.float32)
    d_mixed = jnp.dot(d_attn, weight_o.T, preferred_element_type=jnp.float32).astype(jnp.bfloat16)

    def attend_back(pair_items):
        q_pair, k_pair, v_pair, dm_pair, lse_pair = pair_items
        scores, query_heads, key_heads = pair_scores(q_pair, k_pair)
        attn_probs = jnp.where(allowed[None], jnp.exp(scores - lse_pair[:, :, None]), 0.0)
        value_heads = v_pair.reshape(CAP, 2, HEAD_DIM)
        dm_heads = dm_pair.reshape(CAP, 2, HEAD_DIM)
        d_p = jnp.einsum("qhd,khd->hqk", dm_heads, value_heads, preferred_element_type=jnp.float32)
        row_delta = jnp.sum(attn_probs * d_p, axis=-1, keepdims=True)
        d_scores = (attn_probs * (d_p - row_delta)).astype(jnp.bfloat16)
        d_q = (
            jnp.einsum("hqk,khd->qhd", d_scores, key_heads, preferred_element_type=jnp.float32)
            * scale
        )
        d_k = (
            jnp.einsum("hqk,qhd->khd", d_scores, query_heads, preferred_element_type=jnp.float32)
            * scale
        )
        d_v = jnp.einsum(
            "hqk,qhd->khd",
            attn_probs.astype(jnp.bfloat16),
            dm_heads,
            preferred_element_type=jnp.float32,
        )
        return (
            d_q.reshape(CAP, pair_width),
            d_k.reshape(CAP, pair_width),
            d_v.reshape(CAP, pair_width),
        )

    dq_pairs, dk_pairs, dv_pairs = lax.map(
        attend_back,
        (by_pairs(query), by_pairs(keyed), by_pairs(values_proj), by_pairs(d_mixed), log_sums),
    )
    d_query = rotate(from_pairs(dq_pairs), cos_table, -sin_table).astype(jnp.bfloat16)
    d_key = rotate(from_pairs(dk_pairs), cos_table, -sin_table).astype(jnp.bfloat16)
    d_value = from_pairs(dv_pairs).astype(jnp.bfloat16)
    d_wq_full = jnp.dot(normed_one.T, d_query, preferred_element_type=jnp.float32)
    d_wk_full = jnp.dot(normed_one.T, d_key, preferred_element_type=jnp.float32)
    d_wv_full = jnp.dot(normed_one.T, d_value, preferred_element_type=jnp.float32)
    d_normed_one = (
        jnp.dot(d_query, weight_q.T, preferred_element_type=jnp.float32)
        + jnp.dot(d_key, weight_k.T, preferred_element_type=jnp.float32)
        + jnp.dot(d_value, weight_v.T, preferred_element_type=jnp.float32)
    )
    d_gain1_full = jnp.sum(d_normed_one * unit_one, axis=0)
    d_unit_one = d_normed_one * gain1_f
    d_dealt = (
        inv_one * (d_unit_one - unit_one * jnp.mean(d_unit_one * unit_one, axis=1, keepdims=True))
    ).astype(jnp.bfloat16)
    grad_tokens = d_resid + give_back(d_dealt).astype(jnp.float32)

    def regroup(grads_in):
        tail_shape = grads_in.shape[1:]
        split_view = grads_in.reshape((groups, dealers, per_shard) + tail_shape)
        return jnp.swapaxes(split_view, 0, 1).reshape((model_width,) + tail_shape)

    mix_tile = jnp.broadcast_to(d_mix_full[None], (dealers, EXPERTS_ALL, EXPERTS_ALL))
    sectioned = (
        lax.psum_scatter(
            regroup(d_gain1_full).astype(jnp.bfloat16), "fsdp", scatter_dimension=0, tiled=True
        ).astype(jnp.float32),
        lax.psum_scatter(
            d_wq_full.astype(jnp.bfloat16), "fsdp", scatter_dimension=0, tiled=True
        ).astype(jnp.float32),
        lax.psum_scatter(
            d_wk_full.astype(jnp.bfloat16), "fsdp", scatter_dimension=0, tiled=True
        ).astype(jnp.float32),
        lax.psum_scatter(
            d_wv_full.astype(jnp.bfloat16), "fsdp", scatter_dimension=0, tiled=True
        ).astype(jnp.float32),
        lax.psum_scatter(
            d_wo_full.astype(jnp.bfloat16), "fsdp", scatter_dimension=0, tiled=True
        ).astype(jnp.float32),
        lax.psum_scatter(
            regroup(d_gain2_full).astype(jnp.bfloat16), "fsdp", scatter_dimension=0, tiled=True
        ).astype(jnp.float32),
        lax.psum_scatter(
            regroup(d_router_full).astype(jnp.bfloat16), "fsdp", scatter_dimension=0, tiled=True
        ).astype(jnp.float32),
        lax.psum_scatter(
            regroup(d_wconst_full).astype(jnp.bfloat16), "fsdp", scatter_dimension=0, tiled=True
        ).astype(jnp.float32),
        lax.psum_scatter(
            regroup(d_vconst_full).astype(jnp.bfloat16), "fsdp", scatter_dimension=0, tiled=True
        ).astype(jnp.float32),
        lax.psum_scatter(
            mix_tile.astype(jnp.bfloat16), "fsdp", scatter_dimension=0, tiled=True
        ).astype(jnp.float32),
        lax.psum_scatter(
            d_wgate_full.astype(jnp.bfloat16), "fsdp", scatter_dimension=1, tiled=True
        ).astype(jnp.float32),
        lax.psum_scatter(
            d_wup_full.astype(jnp.bfloat16), "fsdp", scatter_dimension=1, tiled=True
        ).astype(jnp.float32),
        lax.psum_scatter(
            d_wdown_full.astype(jnp.bfloat16), "fsdp", scatter_dimension=2, tiled=True
        ).astype(jnp.float32),
    )
    s_g1, s_q, s_k, s_v, s_o, s_g2, s_r, s_c, s_vc, s_mix, s_gate, s_up, s_down = sectioned
    summed = (
        lax.psum_scatter(s_g1.astype(jnp.bfloat16), "grp", scatter_dimension=0, tiled=True).astype(
            jnp.float32
        ),
        lax.psum_scatter(s_q.astype(jnp.bfloat16), "grp", scatter_dimension=1, tiled=True).astype(
            jnp.float32
        ),
        lax.psum_scatter(s_k.astype(jnp.bfloat16), "grp", scatter_dimension=1, tiled=True).astype(
            jnp.float32
        ),
        lax.psum_scatter(s_v.astype(jnp.bfloat16), "grp", scatter_dimension=1, tiled=True).astype(
            jnp.float32
        ),
        lax.psum_scatter(s_o.astype(jnp.bfloat16), "grp", scatter_dimension=1, tiled=True).astype(
            jnp.float32
        ),
        lax.psum_scatter(s_g2.astype(jnp.bfloat16), "grp", scatter_dimension=0, tiled=True).astype(
            jnp.float32
        ),
        lax.psum_scatter(s_r.astype(jnp.bfloat16), "grp", scatter_dimension=0, tiled=True).astype(
            jnp.float32
        ),
        lax.psum_scatter(s_c.astype(jnp.bfloat16), "grp", scatter_dimension=0, tiled=True).astype(
            jnp.float32
        ),
        lax.psum_scatter(s_vc.astype(jnp.bfloat16), "grp", scatter_dimension=0, tiled=True).astype(
            jnp.float32
        ),
        lax.psum_scatter(
            jnp.broadcast_to(s_mix, (groups, EXPERTS_ALL, EXPERTS_ALL)).astype(jnp.bfloat16),
            "grp",
            scatter_dimension=0,
            tiled=True,
        ).astype(jnp.float32),
    )
    (
        grad_gain_one,
        grad_query,
        grad_key,
        grad_value,
        grad_out_proj,
        grad_gain_two,
        grad_router,
        grad_const,
        grad_vconst,
        mix_part,
    ) = summed
    grad_mix = mix_part[0]
    grad_gate, grad_up, grad_down = (
        lax.psum_scatter(
            s_gate.astype(jnp.bfloat16), "grp", scatter_dimension=2, tiled=True
        ).astype(jnp.float32),
        lax.psum_scatter(s_up.astype(jnp.bfloat16), "grp", scatter_dimension=2, tiled=True).astype(
            jnp.float32
        ),
        lax.psum_scatter(
            s_down.astype(jnp.bfloat16), "grp", scatter_dimension=1, tiled=True
        ).astype(jnp.float32),
    )
    return (
        output,
        grad_tokens,
        grad_prev,
        grad_gain_one,
        grad_query,
        grad_key,
        grad_value,
        grad_out_proj,
        grad_gain_two,
        grad_router,
        grad_mix,
        grad_const,
        grad_vconst,
        grad_gate,
        grad_up,
        grad_down,
    )


HALO = 256
KEYS = HALO + TOK_DEV
ROWS = E * MOST
WIDE = 896
NEG = -1e30
F32 = jnp.float32
BF16 = jnp.bfloat16
NT = (((1,), (1,)), ((), ()))
TN = (((0,), (0,)), ((), ()))
NN = (((1,), (0,)), ((), ()))


def mm(a, b, dims=NN):
    return lax.dot_general(a, b, dims, preferred_element_type=F32)


def lane_iota(rows, width=128):
    return lax.broadcasted_iota(jnp.int32, (rows, width), 1)


def pick(values, lane_mask):
    return jnp.sum(jnp.where(lane_mask, values, 0.0), axis=1, keepdims=True)


def params(mb, **kw):
    return pltpu.CompilerParams(vmem_limit_bytes=mb << 20, **kw)


def whole(count):
    return [pl.BlockSpec(memory_space=pltpu.VMEM) for _ in range(count)]


def sds(shape, dtype):
    return jax.ShapeDtypeStruct(shape, dtype)


MESH_ID = pl.DeviceIdType.MESH


def send(src, dst, send_sem, recv_sem, device):
    pltpu.make_async_remote_copy(
        src_ref=src,
        dst_ref=dst,
        send_sem=send_sem,
        recv_sem=recv_sem,
        device_id=device,
        device_id_type=MESH_ID,
    ).start()


def settle(ref, sem):
    pltpu.make_async_copy(ref, ref, sem).wait()


def flip(a, b):
    return a + b - 2 * a * b


def xor4(a, b):
    return flip(a // 2, b // 2) * 2 + flip(lax.rem(a, 2), lax.rem(b, 2))


def aligned(value, to):
    return pl.multiple_of(value, to)


class Place:
    def __init__(self, his, lo):
        self.g = lax.axis_index("grp")
        self.f = lax.axis_index("fsdp")
        self.his, self.lo = his, lo
        self.hi = self.g // lo
        self.l = lax.rem(self.g, lo)
        self.m = self.f * his + self.hi
        core = lax.rem(self.g, 2)
        side = lax.rem(self.g // 2, 2)
        self.core_peer = self.g + 1 - 2 * core
        self.side_peer = self.g + 2 - 4 * side
        self.l1 = lax.rem(self.core_peer, lo)
        self.l2 = lax.rem(self.side_peer, lo)
        self.l3 = lo - 1 - self.l

    def member(self, j, hh):
        f = xor4(self.f, j)
        hi = flip(self.hi, hh)
        return f * self.his + hi, (hi * self.lo + self.l, f)

    def others(self):
        peers = []
        for j in range(4):
            for hh in range(self.his):
                if j or hh:
                    peers.append(self.member(j, hh)[1])
        return peers


def greet(peers):
    barrier = pltpu.get_barrier_semaphore()
    for peer in peers:
        pl.semaphore_signal(barrier, inc=1, device_id=peer, device_id_type=MESH_ID)
    pl.semaphore_wait(barrier, len(peers))


def turn(values, cos, sin):
    half = HEAD_DIM // 2
    width = values.shape[1]
    reps = width // 128
    front = lax.rem(lane_iota(values.shape[0], width), HEAD_DIM) < half
    swapped = jnp.where(
        front, pltpu.roll(values, width - half, 1), pltpu.roll(values, half, 1)
    )
    cos_w = jnp.concatenate([cos] * reps, axis=1)
    sin_w = jnp.concatenate([sin] * reps, axis=1)
    return values * cos_w + swapped * sin_w


QBLOCKS = [(0, 128), (128, 128), (256, 64)]


def allowed_mask(pos_ref, first, count):
    ii = lax.broadcasted_iota(jnp.int32, (count, 384), 0) + HALO
    jj = lax.broadcasted_iota(jnp.int32, (count, 384), 1)
    return (jj <= ii) & (jj >= ii - pos_ref[pl.ds(first, count), 0:1])


def key_span(first):
    return min(384, KEYS - first)


def begin_kernel(
    tile_ref,
    tok_ref,
    cot_ref,
    routes_ref,
    cos_ref,
    sin_ref,
    pos_ref,
    prev_ref,
    wmix_ref,
    wd_ref,
    wg_hbm,
    wu_hbm,
    wf_ref,
    s_ref,
    halo_ref,
    slots_ref,
    q_ref,
    k_ref,
    v_ref,
    n1_ref,
    inv1_ref,
    mix_ref,
    lse_ref,
    resid_ref,
    part_ref,
    probs_ref,
    cols_ref,
    x_ref,
    gates_ref,
    w_hbm,
    g_hbm,
    p_ref,
    wdt_ref,
    grow_ref,
    zs,
    ps,
    cs,
    hs,
    gs,
    ws,
    gas,
    agr,
    hr,
    gr,
    wr,
    gqr,
):
    lo, ranks = g_hbm.shape[:2]
    his = E // ranks
    at = Place(his, lo)
    width = tok_ref.shape[1]
    head_rows = wd_ref.shape[2]
    ff = wd_ref.shape[1]
    part_cols = width // p_ref.shape[0]
    diag = lo * (1 - at.hi) + at.l2
    upper = lo * (1 - at.hi) + at.l
    near = [(at.core_peer, at.f), (at.side_peer, at.f), (upper, at.f), (diag, at.f)]
    greet(at.others() + [near[0], near[1], near[3]])

    p_ref[at.g, at.f] = tile_ref[...]
    for j in range(1, ranks):
        f2 = xor4(at.f, j)
        send(tile_ref, p_ref.at[at.g, at.f], zs.at[j], agr.at[at.g, at.f], (at.g, f2))

    def spread(j, f2, src):
        for t, peer in enumerate(near):
            send(src, p_ref.at[at.g, f2], ps.at[j, t], agr.at[at.g, f2], peer)

    spread(0, at.f, tile_ref)
    halo_rows = halo_ref.shape[0]
    tail = tok_ref.at[pl.ds(tok_ref.shape[0] - halo_rows, halo_rows)]

    @pl.when(at.f < ranks - 1)
    def _():
        send(tail, halo_ref, hs, hr, (at.g, at.f + 1))

    @pl.when(at.f == 0)
    def _():
        halo_ref[...] = jnp.zeros_like(halo_ref)

    lanes = lane_iota(TOK_DEV)
    r0 = routes_ref[:, 0:1]
    r1 = routes_ref[:, 1:2]
    hot0 = lanes == r0
    hot1 = lanes == r1
    named = jnp.where(hot0 | hot1, 1.0, 0.0).astype(BF16)
    earlier = (
        lax.broadcasted_iota(jnp.int32, (TOK_DEV, TOK_DEV), 1)
        < lax.broadcasted_iota(jnp.int32, (TOK_DEV, TOK_DEV), 0)
    )
    rank = mm(jnp.where(earlier, 1.0, 0.0).astype(BF16), named)
    rank0 = pick(rank, hot0).astype(jnp.int32)
    rank1 = pick(rank, hot1).astype(jnp.int32)
    c0 = jnp.where(r0 < E, r0 * MOST + rank0, -1)
    c1 = jnp.where(r1 < E, r1 * MOST + rank1, -1)
    slots_ref[...] = jnp.where(lanes == 0, c0, jnp.where(lanes == 1, c1, -1))
    slot = lane_iota(TOK_DEV, ROWS)
    spots0 = jnp.where(slot == c0, 1.0, 0.0).astype(BF16)
    spots1 = jnp.where(slot == c1, 1.0, 0.0).astype(BF16)
    grow_ref[...] = mm(spots0 + spots1, cot_ref[...], TN).astype(BF16)
    for e in range(E):
        wdt_ref[e] = wd_ref[e].T

    for j in range(1, ranks):
        f2 = xor4(at.f, j)
        settle(p_ref.at[at.g, f2], agr.at[at.g, f2])
        spread(j, f2, p_ref.at[at.g, f2])

    own_rows = pl.ds(aligned(at.f * head_rows, 16), head_rows)
    own_cols = pl.ds(aligned(at.hi * ff, 128), ff)
    own_spot = pl.ds(aligned(at.hi * MOST, 16), MOST)
    for j in range(ranks):
        for hh in range(his):
            e, peer = at.member(j, hh)
            rows = grow_ref.at[pl.ds(aligned(e * MOST, 16), MOST)]
            spot = g_hbm.at[at.l, at.f, own_spot]
            sources = (wg_hbm.at[e], wu_hbm.at[e], wdt_ref.at[e])
            if j == 0 and hh == 0:
                pltpu.make_async_copy(rows, spot, gr.at[at.m]).start()
                for w in range(3):
                    pltpu.make_async_copy(
                        sources[w], w_hbm.at[w, own_rows, own_cols], wr.at[at.m, w]
                    ).start()
            else:
                k = j * his + hh
                send(rows, spot, gs.at[k], gr.at[at.m], peer)
                for w in range(3):
                    send(
                        sources[w],
                        w_hbm.at[w, own_rows, own_cols],
                        ws.at[k, w],
                        wr.at[at.m, w],
                        peer,
                    )

    for j in range(ranks):
        f2 = xor4(at.f, j)
        for t in range(1, 4):
            g2 = near[t][0]
            settle(p_ref.at[g2, f2], agr.at[g2, f2])
            send(p_ref.at[g2, f2], p_ref.at[g2, f2], cs.at[t - 1, j], agr.at[g2, f2], near[0])
    sibling_upper = lo * (1 - at.hi) + at.l1
    for j in range(ranks):
        f2 = xor4(at.f, j)
        for g2 in (
            at.core_peer,
            at.hi * lo + at.l3,
            sibling_upper,
            lo * (1 - at.hi) + at.l3,
        ):
            settle(p_ref.at[g2, f2], agr.at[g2, f2])

    per = (p_ref.shape[2] - head_rows) // 8 * 24
    groups = p_ref.shape[0]
    for g2 in range(groups):
        for f2 in range(ranks):
            piece = p_ref[g2, f2, head_rows : head_rows + 8, :].astype(F32)
            for i in range(per // 8):
                base = (g2 * ranks + f2) * per + 8 * i
                s_ref[base : base + 8, :] = piece[:, 128 * i : 128 * i + 128]

    def lay(f2, _):
        rows = pl.ds(aligned(f2 * head_rows, 16), head_rows)
        for w in range(4):
            for half in range(2):
                pieces = [
                    p_ref[
                        half * (groups // 2) + i,
                        f2,
                        0:head_rows,
                        w * part_cols : (w + 1) * part_cols,
                    ]
                    for i in range(groups // 2)
                ]
                wf_ref[w, rows, half * (width // 2) : (half + 1) * (width // 2)] = (
                    jnp.concatenate(pieces, axis=1)
                )
        return 0

    lax.fori_loop(0, ranks, lay, 0)

    @pl.when(at.f > 0)
    def _():
        settle(halo_ref, hr)

    scale = HEAD_DIM ** (-0.5)
    flat = s_ref[...].T
    g1 = flat[SMALL_G1 : SMALL_G1 + 1, :]
    g2 = flat[SMALL_G1 + 1 : SMALL_G1 + 2, :]
    vc = flat[SMALL_VC : SMALL_VC + CONSTS, :]
    rows = jnp.concatenate([halo_ref[...], tok_ref[...]], axis=0).astype(F32)
    inv1 = lax.rsqrt(jnp.mean(rows * rows, axis=1, keepdims=True) + NORM_EPS)
    inv1_ref[...] = jnp.broadcast_to(inv1, (KEYS, 128))
    n1_ref[...] = (rows * inv1 * g1).astype(BF16)

    def project(i, _):
        span = pl.ds(pl.multiple_of(i * 256, 256), 256)
        cos = cos_ref[...]
        sin = sin_ref[...]
        q = mm(n1_ref[HALO:, :], wf_ref[0, :, span])
        q_ref[:, span] = turn(q, cos[HALO:], sin[HALO:]).astype(BF16)
        k = mm(n1_ref[...], wf_ref[1, :, span])
        k_ref[:, span] = turn(k, cos, sin).astype(BF16)
        v_ref[:, span] = mm(n1_ref[...], wf_ref[2, :, span]).astype(BF16)
        return 0

    lax.fori_loop(0, width // 256, project, 0)
    lse_ref[...] = jnp.zeros((TOK_DEV, 128), F32)

    for f2 in range(ranks):
        for h2 in range(his):
            settle(
                g_hbm.at[at.l, f2, h2 * MOST : (h2 + 1) * MOST], gr.at[f2 * his + h2]
            )
    send(g_hbm.at[at.l], g_hbm.at[at.l], gas.at[0], gqr.at[0], near[0])
    send(g_hbm.at[at.l], g_hbm.at[at.l], gas.at[1], gqr.at[1], near[1])

    def pair(p, _):
        span = pl.ds(pl.multiple_of(p * 128, 128), 128)
        for first, count in QBLOCKS:
            keys = key_span(first)
            ok = allowed_mask(pos_ref, first, count)[:, :keys]
            q = q_ref[pl.ds(first, count), span]
            k = k_ref[pl.ds(first, keys), span]
            v = v_ref[pl.ds(first, keys), span]
            lane = lane_iota(count)
            out = None
            lse = lse_ref[pl.ds(first, count), :]
            for h in range(2):
                mine = (lane < HEAD_DIM) if h == 0 else (lane >= HEAD_DIM)
                qh = jnp.where(mine, q, jnp.zeros_like(q))
                sc = jnp.where(ok, mm(qh, k, NT) * scale, NEG)
                top = jnp.max(sc, axis=1, keepdims=True)
                ex = jnp.exp(sc - top)
                total = jnp.sum(ex, axis=1, keepdims=True)
                o = mm((ex / total).astype(BF16), v)
                out = o if h == 0 else jnp.where(mine, o, out)
                lse = jnp.where(lane == 2 * p + h, top + jnp.log(total), lse)
            mix_ref[pl.ds(first, count), span] = out.astype(BF16)
            lse_ref[pl.ds(first, count), :] = lse
        return 0

    lax.fori_loop(0, HEADS // 2, pair, 0)
    settle(g_hbm.at[at.l2], gqr.at[1])
    send(g_hbm.at[at.l2], g_hbm.at[at.l2], gas.at[2], gqr.at[2], near[0])

    attn_out = mm(mix_ref[...], wf_ref[3]).astype(BF16)
    resid = tok_ref[...].astype(F32) + attn_out.astype(F32)
    resid_ref[...] = resid
    inv2 = lax.rsqrt(jnp.mean(resid * resid, axis=1, keepdims=True) + NORM_EPS)
    normed = resid * inv2 * g2
    narrow = normed.astype(BF16)
    raw = mm(narrow, s_ref[...].astype(BF16))
    prev = prev_ref[...]
    wmix = wmix_ref[...]
    phigh = prev.astype(BF16)
    prest = prev - phigh.astype(F32)
    pmid = prest.astype(BF16)
    plow = (prest - pmid.astype(F32)).astype(BF16)
    mixed_prev = mm(phigh, wmix) + (mm(pmid, wmix) + mm(plow, wmix))
    logits = jnp.where(lanes < EXPERTS_ALL, raw + mixed_prev, NEG)
    top = jnp.max(logits, axis=1, keepdims=True)
    ex = jnp.exp(logits - top)
    probs = ex / jnp.sum(ex, axis=1, keepdims=True)
    probs_ref[...] = probs
    gate0 = pick(probs, hot0)
    gate1 = pick(probs, hot1)

    def gate_of(expert):
        return jnp.where(r0 == expert, gate0, 0.0) + jnp.where(r1 == expert, gate1, 0.0)

    gate_id = gate_of(E + 1)
    part = resid + gate_id * normed
    cols = jnp.where(lanes == 0, gate0, 0.0)
    cols = jnp.where(lanes == 1, gate1, cols)
    cols = jnp.where(lanes == 2, gate_id, cols)
    cols = jnp.where(lanes == 3, inv2, cols)
    for c in range(CONSTS):
        la = pick(raw, lanes == SMALL_C + 2 * c)
        lb = pick(raw, lanes == SMALL_C + 1 + 2 * c)
        big = jnp.maximum(la, lb)
        ea = jnp.exp(la - big)
        eb = jnp.exp(lb - big)
        ma = ea / (ea + eb)
        mb = eb / (ea + eb)
        gate_c = gate_of(E + 2 + c)
        part = part + gate_c * (ma * normed + mb * vc[c : c + 1, :])
        cols = jnp.where(lanes == 4 + 3 * c, gate_c, cols)
        cols = jnp.where(lanes == 5 + 3 * c, ma, cols)
        cols = jnp.where(lanes == 6 + 3 * c, mb, cols)
    part_ref[...] = part
    cols_ref[...] = cols
    x_ref[...] = mm(spots0 + spots1, narrow, TN).astype(BF16)
    wide0 = jnp.where(r0 < E, r0 * 128 + rank0, -1)
    wide1 = jnp.where(r1 < E, r1 * 128 + rank1, -1)
    for e in range(E):
        lane = lanes + e * 128
        row = jnp.sum(
            jnp.where(lane == wide0, gate0, 0.0) + jnp.where(lane == wide1, gate1, 0.0),
            axis=0,
            keepdims=True,
        )
        gates_ref[e] = jnp.broadcast_to(row, (8, 128))

    settle(g_hbm.at[at.l1], gqr.at[0])
    settle(g_hbm.at[at.l3], gqr.at[2])
    for f2 in range(ranks):
        for h2 in range(his):
            for w in range(3):
                block = w_hbm.at[
                    w, f2 * head_rows : (f2 + 1) * head_rows, h2 * ff : (h2 + 1) * ff
                ]
                settle(block, wr.at[f2 * his + h2, w])
    for j in range(1, ranks):
        settle(tile_ref, zs.at[j])
    for j in range(ranks):
        for t in range(4):
            settle(tile_ref, ps.at[j, t])
        for t in range(3):
            settle(tile_ref, cs.at[t, j])

    @pl.when(at.f < ranks - 1)
    def _():
        settle(tail, hs)

    for k in range(1, E):
        settle(grow_ref.at[0:MOST], gs.at[k])
        for w in range(3):
            settle(wdt_ref.at[0], ws.at[k, w])
    for i in range(3):
        settle(g_hbm.at[at.l], gas.at[i])


SMALL_G1 = EXPERTS_ALL
SMALL_VC = SMALL_G1 + 2
SMALL_C = SMALL_VC + CONSTS


def begin(
    tile, tok, cot, routes, cos, sin, pos, prev, wmix, w_down, w_gate, w_up, groups, ranks
):
    width = tok.shape[1]
    lo = groups * ranks // E
    his = E // ranks
    ff = w_down.shape[1]
    head_rows = w_down.shape[2]
    dma = pltpu.SemaphoreType.DMA
    any_spec = pl.BlockSpec(memory_space=pl.ANY)
    return pl.pallas_call(
        begin_kernel,
        out_shape=[
            sds((4, width, width), BF16),
            sds((width, 128), F32),
            sds((HALO, width), BF16),
            sds((TOK_DEV, 128), jnp.int32),
            sds((TOK_DEV, width), BF16),
            sds((KEYS, width), BF16),
            sds((KEYS, width), BF16),
            sds((KEYS, width), BF16),
            sds((KEYS, 128), F32),
            sds((TOK_DEV, width), BF16),
            sds((TOK_DEV, 128), F32),
            sds((TOK_DEV, width), F32),
            sds((TOK_DEV, width), F32),
            sds((TOK_DEV, 128), F32),
            sds((TOK_DEV, 128), F32),
            sds((ROWS, width), BF16),
            sds((E, 8, 128), F32),
            sds((3, width, ff * his), BF16),
            sds((lo, ranks, his * MOST, width), BF16),
        ],
        in_specs=whole(10) + [any_spec, any_spec],
        out_specs=whole(17) + [any_spec, any_spec],
        scratch_shapes=[
            pltpu.VMEM((groups, ranks) + tile.shape, BF16),
            pltpu.VMEM((E, head_rows, ff), BF16),
            pltpu.VMEM((ROWS, width), BF16),
            dma((4,)),
            dma((4, 4)),
            dma((3, 4)),
            dma,
            dma((E,)),
            dma((E, 3)),
            dma((3,)),
            dma((groups, ranks)),
            dma,
            dma((E,)),
            dma((E, 3)),
            dma((3,)),
        ],
        compiler_params=params(60, collective_id=1, has_side_effects=True),
        name="begin",
    )(tile, tok, cot, routes, cos, sin, pos, prev, wmix, w_down, w_gate, w_up)


def moe_kernel(
    x_ref,
    gates_ref,
    w_ref,
    g_ref,
    back_ref,
    gw_ref,
    xb_ref,
    gb_ref,
    od_ref,
    r1_ref,
    r2_ref,
    acc_ref,
    xs,
    gs,
    qs,
    gqs,
    d1s,
    d2s,
    bs,
    xr,
    gr,
    qr,
    gqr,
    d1r,
    d2r,
    br,
):
    lo, ranks = g_ref.shape[:2]
    his = E // ranks
    width = x_ref.shape[1]
    at = Place(his, lo)
    core = (at.core_peer, at.f)
    side = (at.side_peer, at.f)
    greet(at.others() + [core, side])
    own_spot = pl.ds(aligned(at.hi * MOST, 16), MOST)

    for j in range(ranks):
        for hh in range(his):
            e, peer = at.member(j, hh)
            k = j * his + hh
            rows = x_ref.at[pl.ds(aligned(e * MOST, 16), MOST)]
            spot = xb_ref.at[at.f, at.l, own_spot]
            if k == 0:
                pltpu.make_async_copy(rows, spot, xr.at[at.m]).start()
                pltpu.make_async_copy(
                    gates_ref.at[e], gb_ref.at[at.f, at.l, at.hi], gr.at[at.m]
                ).start()
            else:
                send(rows, spot, xs.at[k], xr.at[at.m], peer)
                send(
                    gates_ref.at[e], gb_ref.at[at.f, at.l, at.hi], gs.at[k], gr.at[at.m], peer
                )
    acc_ref[...] = jnp.zeros_like(acc_ref)

    def take(j):
        fj = xor4(at.f, j)
        for hh in range(his):
            hi = flip(at.hi, hh)
            m = fj * his + hi
            settle(xb_ref.at[fj, at.l, pl.ds(aligned(hi * MOST, 16), MOST)], xr.at[m])
            settle(gb_ref.at[fj, at.l, hi], gr.at[m])
        for i, peer in enumerate((core, side)):
            send(xb_ref.at[fj, at.l], xb_ref.at[fj, at.l], qs.at[fj, i], qr.at[fj, i], peer)
            send(gb_ref.at[fj, at.l], gb_ref.at[fj, at.l], gqs.at[fj, i], gqr.at[fj, i], peer)

    def pass_on(j):
        fj = xor4(at.f, j)
        settle(xb_ref.at[fj, at.l2], qr.at[fj, 1])
        settle(gb_ref.at[fj, at.l2], gqr.at[fj, 1])
        send(xb_ref.at[fj, at.l2], xb_ref.at[fj, at.l2], qs.at[fj, 2], qr.at[fj, 2], core)
        send(gb_ref.at[fj, at.l2], gb_ref.at[fj, at.l2], gqs.at[fj, 2], gqr.at[fj, 2], core)

    def compute(j):
        fj = xor4(at.f, j)
        settle(xb_ref.at[fj, at.l1], qr.at[fj, 0])
        settle(gb_ref.at[fj, at.l1], gqr.at[fj, 0])
        settle(xb_ref.at[fj, at.l3], qr.at[fj, 2])
        settle(gb_ref.at[fj, at.l3], gqr.at[fj, 2])
        rows = lo * his * MOST
        x = jnp.concatenate([xb_ref[fj, i] for i in range(lo)], axis=0)
        g = jnp.concatenate([g_ref[i, fj] for i in range(lo)], axis=0)
        diagonal = lax.broadcasted_iota(jnp.int32, (MOST, 128), 0) == lane_iota(MOST)
        gate = jnp.concatenate(
            [
                pick(jnp.broadcast_to(gb_ref[fj, i, h][0:1, :], (MOST, 128)), diagonal)
                for i in range(lo)
                for h in range(his)
            ],
            axis=0,
        )
        d_exp = (g.astype(F32) * gate).astype(BF16)
        wg = w_ref[0]
        wu = w_ref[1]
        wd = w_ref[2]
        a = mm(x, wg)
        b = mm(x, wu)
        sig = 1.0 / (1.0 + jnp.exp(-a))
        hidden = (a * sig * b).astype(BF16)
        shape = (lo, his * MOST, width)
        od_ref[fj, :, :, :width] = mm(hidden, wd, NT).astype(BF16).reshape(shape)
        dh = mm(d_exp, wd)
        d_up = (dh * a * sig).astype(BF16)
        d_gate = (dh * b * sig * (1.0 + a * (1.0 - sig))).astype(BF16)
        od_ref[fj, :, :, width:] = (
            (mm(d_gate, wg, NT) + mm(d_up, wu, NT)).astype(BF16).reshape(shape)
        )
        acc_ref[0] += mm(x, d_gate, TN)
        acc_ref[1] += mm(x, d_up, TN)
        acc_ref[2] += mm(d_exp, hidden, TN)

    def to_core(j):
        fj = xor4(at.f, j)
        send(od_ref.at[fj, at.l1], r1_ref.at[fj, 0], d1s.at[fj, 0], d1r.at[fj, 0], core)
        send(od_ref.at[fj, at.l3], r1_ref.at[fj, 1], d1s.at[fj, 1], d1r.at[fj, 1], core)

    def add(ref, other):
        ref[...] = (ref[...].astype(F32) + other[...].astype(F32)).astype(BF16)

    def to_side(j):
        fj = xor4(at.f, j)
        settle(r1_ref.at[fj, 1], d1r.at[fj, 1])
        add(od_ref.at[fj, at.l2], r1_ref.at[fj, 1])
        send(od_ref.at[fj, at.l2], r2_ref.at[fj], d2s.at[fj], d2r.at[fj], side)
        settle(r1_ref.at[fj, 0], d1r.at[fj, 0])
        add(od_ref.at[fj, at.l], r1_ref.at[fj, 0])

    def to_home(j):
        fj = xor4(at.f, j)
        settle(r2_ref.at[fj], d2r.at[fj])
        add(od_ref.at[fj, at.l], r2_ref.at[fj])
        for hh in range(his):
            hi = flip(at.hi, hh)
            m = fj * his + hi
            rows = od_ref.at[fj, at.l, pl.ds(aligned(hi * MOST, 16), MOST)]
            peer = (hi * lo + at.l, fj)

            def away(rows=rows, peer=peer, m=m):
                send(rows, back_ref.at[at.m], bs.at[m], br.at[at.m], peer)

            if hh:
                away()
            else:

                @pl.when(j == 0)
                def _(rows=rows):
                    pltpu.make_async_copy(rows, back_ref.at[at.m], br.at[at.m]).start()

                pl.when(j > 0)(away)

    take(0)
    take(1)

    def step(t, _):
        @pl.when(t < ranks)
        def _():
            pass_on(t)
            compute(t)
            to_core(t)

        @pl.when(t + 2 < ranks)
        def _():
            take(t + 2)

        @pl.when((t >= 1) & (t <= ranks))
        def _():
            to_side(t - 1)

        @pl.when(t >= 2)
        def _():
            to_home(t - 2)

        return 0

    lax.fori_loop(0, ranks + 2, step, 0)

    gw_ref[...] = acc_ref[...].astype(BF16)
    for m in range(E):
        settle(back_ref.at[m], br.at[m])
    for k in range(1, E):
        settle(x_ref.at[0:MOST], xs.at[k])
        settle(gates_ref.at[0], gs.at[k])
    for f2 in range(ranks):
        for i in range(3):
            settle(xb_ref.at[0, 0], qs.at[f2, i])
            settle(gb_ref.at[0, 0], gqs.at[f2, i])
        for i in range(2):
            settle(r1_ref.at[0, 0], d1s.at[f2, i])
        settle(r2_ref.at[0], d2s.at[f2])
    for j in range(ranks):
        for hh in range(his):
            if j or hh:
                m = at.member(j, hh)[0]
                settle(back_ref.at[0], bs.at[m])


def moe(x, gates, w, g):
    lo, ranks, block, width = g.shape
    dma = pltpu.SemaphoreType.DMA
    his = E // ranks
    return pl.pallas_call(
        moe_kernel,
        out_shape=[sds((E, MOST, 2 * width), BF16), sds(w.shape, BF16)],
        in_specs=whole(4),
        out_specs=whole(2),
        scratch_shapes=[
            pltpu.VMEM((ranks, lo, block, width), BF16),
            pltpu.VMEM((ranks, lo, his, 8, 128), F32),
            pltpu.VMEM((ranks, lo, block, 2 * width), BF16),
            pltpu.VMEM((ranks, 2, block, 2 * width), BF16),
            pltpu.VMEM((ranks, block, 2 * width), BF16),
            pltpu.VMEM(w.shape, F32),
            dma((E,)),
            dma((E,)),
            dma((4, 3)),
            dma((4, 3)),
            dma((4, 2)),
            dma((4,)),
            dma((E,)),
            dma((E,)),
            dma((E,)),
            dma((4, 3)),
            dma((4, 3)),
            dma((4, 2)),
            dma((4,)),
            dma((E,)),
        ],
        compiler_params=params(62, collective_id=2, has_side_effects=True),
        name="moe",
    )(x, gates, w, g)


def end_kernel(
    cot_ref,
    resid_ref,
    part_ref,
    probs_ref,
    cols_ref,
    slots_ref,
    routes_ref,
    prev_ref,
    wmix_ref,
    s_ref,
    od_ref,
    gw_ref,
    wf_ref,
    q_ref,
    k_ref,
    v_ref,
    n1_ref,
    inv1_ref,
    mix_ref,
    lse_ref,
    cos_ref,
    sin_ref,
    pos_ref,
    tok_ref,
    halo_ref,
    out_ref,
    dres_ref,
    gprev_ref,
    down_ref,
    back_ref,
    t_ref,
    fin_ref,
    gmix_ref,
    flat_ref,
    dhalo_ref,
    dm_ref,
    dq_ref,
    dk_ref,
    dv_ref,
    dqr_ref,
    dkr_ref,
    dvr_ref,
    full_ref,
    p_ref,
    r1_ref,
    r2_ref,
    r3_ref,
    r4_ref,
    mx_ref,
    mr_ref,
    mz_ref,
    ts,
    tr,
    hs,
    hr,
    s1,
    e1,
    s2,
    e2,
    s3,
    e3,
    s4,
    e4,
    ms,
    me,
    zs,
    ze,
):
    ranks = p_ref.shape[1]
    his = E // ranks
    groups = p_ref.shape[0]
    lo = groups // his
    at = Place(his, lo)
    width = cot_ref.shape[1]
    tile = t_ref.shape[2:]
    core = (at.core_peer, at.f)
    side = (at.side_peer, at.f)
    upper = (lo * (1 - at.hi) + at.l, at.f)
    greet(at.others() + [core, side])

    for j in range(ranks):
        for hh in range(his):
            e, peer = at.member(j, hh)
            rows = pl.ds(aligned(e // his * tile[0], 16), tile[0])
            lanes_at = pl.ds(aligned(lax.rem(e, his) * tile[1], 128), tile[1])
            n = j * his + hh
            for w in range(3):
                block = gw_ref.at[w, rows, lanes_at]
                if n == 0:
                    pltpu.make_async_copy(block, t_ref.at[at.m, w], tr.at[at.m, w]).start()
                else:
                    send(block, t_ref.at[at.m, w], ts.at[n, w], tr.at[at.m, w], peer)

    flat = s_ref[...].T
    gain1 = flat[SMALL_G1 : SMALL_G1 + 1, :]
    gain2 = flat[SMALL_G1 + 1 : SMALL_G1 + 2, :]
    vc = flat[SMALL_VC : SMALL_VC + CONSTS, :]
    g = cot_ref[...].astype(F32)
    lanes = lane_iota(TOK_DEV)
    cols = cols_ref[...]

    def col(i):
        return pick(cols, lanes == i)

    gate0, gate1, gate_id, inv2 = col(0), col(1), col(2), col(3)
    resid = resid_ref[...]
    unit2 = resid * inv2
    normed = unit2 * gain2
    narrow = normed.astype(BF16)
    od = od_ref[...].reshape(ROWS, 2 * width)
    slot = lane_iota(TOK_DEV, ROWS)
    hot0 = jnp.where(slot == slots_ref[:, 0:1], 1.0, 0.0).astype(BF16)
    hot1 = jnp.where(slot == slots_ref[:, 1:2], 1.0, 0.0).astype(BF16)
    y0 = mm(hot0, od[:, :width])
    y1 = mm(hot1, od[:, :width])
    out_ref[...] = (part_ref[...] + gate0 * y0 + gate1 * y1).astype(BF16)
    a_n = jnp.sum(g * normed, axis=1, keepdims=True)
    dg0 = jnp.sum(g * y0, axis=1, keepdims=True)
    dg1 = jnp.sum(g * y1, axis=1, keepdims=True)
    r0 = routes_ref[:, 0:1]
    r1 = routes_ref[:, 1:2]
    dg0 = jnp.where(r0 == E + 1, a_n, dg0)
    dg1 = jnp.where(r1 == E + 1, a_n, dg1)
    g_scale = gate_id
    dl = jnp.zeros((TOK_DEV, 128), F32)
    vmix = jnp.zeros((TOK_DEV, 128), F32)
    for c in range(CONSTS):
        gate_c, ma, mb = col(4 + 3 * c), col(5 + 3 * c), col(6 + 3 * c)
        a_v = jnp.sum(g * vc[c : c + 1, :], axis=1, keepdims=True)
        branch = ma * a_n + mb * a_v
        dg0 = jnp.where(r0 == E + 2 + c, branch, dg0)
        dg1 = jnp.where(r1 == E + 2 + c, branch, dg1)
        g_scale = g_scale + gate_c * ma
        da = gate_c * a_n
        db = gate_c * a_v
        mean = ma * da + mb * db
        dl = jnp.where(lanes == SMALL_C + 2 * c, ma * (da - mean), dl)
        dl = jnp.where(lanes == SMALL_C + 1 + 2 * c, mb * (db - mean), dl)
        vmix = jnp.where(lanes == SMALL_VC + c, gate_c * mb, vmix)
    probs = probs_ref[...]
    d_probs = jnp.where(lanes == r0, dg0, 0.0) + jnp.where(lanes == r1, dg1, 0.0)
    d_logits = probs * (d_probs - jnp.sum(probs * d_probs, axis=1, keepdims=True))
    dl = jnp.where(lanes < EXPERTS_ALL, d_logits, dl)
    high = dl.astype(BF16)
    low = (dl - high.astype(F32)).astype(BF16)
    wr = s_ref[...].astype(BF16)
    d_normed = g_scale * g + mm(hot0 + hot1, od[:, width:])
    d_normed = d_normed + mm(high, wr, NT) + mm(low, wr, NT)
    vhigh = vmix.astype(BF16)
    vlow = (vmix - vhigh.astype(F32)).astype(BF16)
    tiny = mm(high, narrow, TN) + mm(low, narrow, TN)
    tiny = tiny + mm(vhigh, cot_ref[...], TN) + mm(vlow, cot_ref[...], TN)
    row_id = lax.broadcasted_iota(jnp.int32, (128, width), 0)
    dg2 = jnp.sum(d_normed * unit2, axis=0, keepdims=True)
    flat_ref[...] = jnp.where(row_id == SMALL_G1 + 1, dg2, tiny)
    n = d_normed * gain2
    dres_ref[...] = g + inv2 * (n - unit2 * jnp.mean(n * unit2, axis=1, keepdims=True))
    wmix = wmix_ref[...]
    gprev_ref[...] = mm(high, wmix, NT) + mm(low, wmix, NT)
    prev = prev_ref[...]
    phigh = prev.astype(BF16)
    plow = (prev - phigh.astype(F32)).astype(BF16)
    d_mix = mm(phigh, high, TN) + mm(phigh, low, TN) + mm(plow, high, TN)
    mx_ref[0] = d_mix[0:16]
    send(mx_ref.at[0], mr_ref.at[0], ms.at[0], me.at[0], core)

    scale = HEAD_DIM ** (-0.5)
    d_attn = dres_ref[...].astype(BF16)
    full_ref[3] = mm(mix_ref[...], d_attn, TN).astype(BF16)
    dm_ref[...] = mm(d_attn, wf_ref[3], NT).astype(BF16)
    dk_ref[...] = jnp.zeros_like(dk_ref)
    dv_ref[...] = jnp.zeros_like(dv_ref)

    def pair(p, _):
        span = pl.ds(pl.multiple_of(p * 128, 128), 128)
        for first, count in QBLOCKS:
            keys = key_span(first)
            ok = allowed_mask(pos_ref, first, count)[:, :keys]
            q = q_ref[pl.ds(first, count), span]
            dm = dm_ref[pl.ds(first, count), span]
            k = k_ref[pl.ds(first, keys), span]
            v = v_ref[pl.ds(first, keys), span]
            lane = lane_iota(count)
            key_lane = lane_iota(keys)
            lse = lse_ref[pl.ds(first, count), :]
            dq = dk = dv = None
            for h in range(2):
                mine = (lane < HEAD_DIM) if h == 0 else (lane >= HEAD_DIM)
                key_mine = (key_lane < HEAD_DIM) if h == 0 else (key_lane >= HEAD_DIM)
                qh = jnp.where(mine, q, jnp.zeros_like(q))
                dmh = jnp.where(mine, dm, jnp.zeros_like(dm))
                s = jnp.where(ok, mm(qh, k, NT) * scale, NEG)
                pr = jnp.where(ok, jnp.exp(s - pick(lse, lane == 2 * p + h)), 0.0)
                dp = mm(dmh, v, NT)
                delta = jnp.sum(pr * dp, axis=1, keepdims=True)
                ds = (pr * (dp - delta)).astype(BF16)
                pb = pr.astype(BF16)
                dqh = mm(ds, k)
                dkh = mm(ds, q, TN)
                dvh = mm(pb, dm, TN)
                dq = dqh if h == 0 else jnp.where(mine, dqh, dq)
                dk = dkh if h == 0 else jnp.where(key_mine, dkh, dk)
                dv = dvh if h == 0 else jnp.where(key_mine, dvh, dv)
            dq_ref[pl.ds(first, count), span] = dq * scale
            dk_ref[pl.ds(first, keys), span] += dk * scale
            dv_ref[pl.ds(first, keys), span] += dv
        return 0

    lax.fori_loop(0, HEADS // 2, pair, 0)

    def unturn(i, _):
        span = pl.ds(pl.multiple_of(i * 256, 256), 256)
        cos = cos_ref[...]
        sin = sin_ref[...]
        dqr_ref[:, span] = turn(dq_ref[:, span], cos[HALO:], -sin[HALO:]).astype(BF16)
        dkr_ref[:, span] = turn(dk_ref[:, span], cos, -sin).astype(BF16)
        dvr_ref[:, span] = dv_ref[:, span].astype(BF16)
        return 0

    lax.fori_loop(0, width // 256, unturn, 0)
    d_all = mm(dkr_ref[...], wf_ref[1], NT) + mm(dvr_ref[...], wf_ref[2], NT)
    dhalo_ref[...] = (d_all[:HALO] * gain1).astype(BF16)

    @pl.when(at.f > 0)
    def _():
        send(dhalo_ref, back_ref, hs, hr, (at.g, at.f - 1))

    @pl.when(at.f == ranks - 1)
    def _():
        back_ref[...] = jnp.zeros_like(back_ref)

    full_ref[0] = mm(n1_ref[HALO:, :], dqr_ref[...], TN).astype(BF16)
    full_ref[1] = mm(n1_ref[...], dkr_ref[...], TN).astype(BF16)
    full_ref[2] = mm(n1_ref[...], dvr_ref[...], TN).astype(BF16)
    d_own = d_all[HALO:] + mm(dqr_ref[...], wf_ref[0], NT)
    inv1 = inv1_ref[:, 0:1]
    unit_own = tok_ref[...].astype(F32) * inv1[HALO:]
    unit_halo = halo_ref[...].astype(F32) * inv1[:HALO]
    dg1 = jnp.sum(d_own * unit_own, axis=0, keepdims=True) + jnp.sum(
        d_all[:HALO] * unit_halo, axis=0, keepdims=True
    )
    down_ref[...] = d_own * gain1
    flat_ref[...] = jnp.where(row_id == SMALL_G1, dg1, flat_ref[...])

    part_cols = width // groups
    head_rows = width // ranks

    def pack(f2, _):
        rows = pl.ds(aligned(f2 * head_rows, 16), head_rows)
        for g2 in range(groups):
            pieces = [
                full_ref[w, rows, g2 * part_cols : (g2 + 1) * part_cols] for w in range(4)
            ]
            p_ref[g2, f2, 0:head_rows, :] = jnp.concatenate(pieces, axis=1)
        return 0

    lax.fori_loop(0, ranks, pack, 0)
    column = flat_ref[...].T
    per = width // (groups * ranks)
    for g2 in range(groups):
        for f2 in range(ranks):
            base = (g2 * ranks + f2) * per
            pieces = [column[base + 8 * i : base + 8 * i + 8, :] for i in range(per // 8)]
            p_ref[g2, f2, head_rows : head_rows + 8, :] = jnp.concatenate(
                pieces, axis=1
            ).astype(BF16)

    def add(ref, other):
        ref[...] = (ref[...].astype(F32) + other[...].astype(F32)).astype(BF16)

    c = lax.rem(at.g, 2)
    x = lax.rem(at.g // 2, 2)
    y = at.hi

    def block(y2, x2, c2):
        return (y2 * 2 + x2) * 2 + c2

    half = ranks // 2
    quads = [(1 - y, 1 - x), (y, 1 - x), (1 - y, x), (y, x)]
    for i, (y2, x2) in enumerate(quads):
        spot = y2 * 2 + x2
        send(p_ref.at[block(y2, x2, 1 - c)], r1_ref.at[spot], s1.at[i], e1.at[spot], core)
    settle(mr_ref.at[0], me.at[0])
    mx_ref[1] = mx_ref[0] + mr_ref[0]
    send(mx_ref.at[1], mr_ref.at[1], ms.at[1], me.at[1], side)
    for i, (y2, x2) in enumerate(quads):
        spot = y2 * 2 + x2
        settle(r1_ref.at[spot], e1.at[spot])
        add(p_ref.at[block(y2, x2, c)], r1_ref.at[spot])
        if i == 0:
            here = p_ref.at[block(1 - y, 1 - x, c)]
            send(here.at[0:half], r2_ref.at[0, 1 - y], s2.at[0, 0], e2.at[0, 1 - y], side)
            send(here.at[half:], r2_ref.at[1, 1 - x], s2.at[1, 0], e2.at[1, 1 - x], upper)
        if i == 1:
            here = p_ref.at[block(y, 1 - x, c)]
            send(here.at[0:half], r2_ref.at[0, y], s2.at[0, 1], e2.at[0, y], side)
        if i == 2:
            here = p_ref.at[block(1 - y, x, c)]
            send(here.at[half:], r2_ref.at[1, x], s2.at[1, 1], e2.at[1, x], upper)
    settle(mr_ref.at[1], me.at[1])
    mx_ref[2] = mx_ref[1] + mr_ref[1]
    send(mx_ref.at[2], mr_ref.at[2], ms.at[2], me.at[2], upper)
    settle(r2_ref.at[0, 1 - y], e2.at[0, 1 - y])
    add(p_ref.at[block(1 - y, x, c), 0:half], r2_ref.at[0, 1 - y])
    send(
        p_ref.at[block(1 - y, x, c), 0:half], r3_ref.at[0], s3.at[0], e3.at[0], upper
    )
    settle(r2_ref.at[1, 1 - x], e2.at[1, 1 - x])
    add(p_ref.at[block(y, 1 - x, c), half:], r2_ref.at[1, 1 - x])
    send(p_ref.at[block(y, 1 - x, c), half:], r3_ref.at[1], s3.at[1], e3.at[1], side)
    settle(r2_ref.at[0, y], e2.at[0, y])
    add(p_ref.at[at.g, 0:half], r2_ref.at[0, y])
    settle(r2_ref.at[1, x], e2.at[1, x])
    add(p_ref.at[at.g, half:], r2_ref.at[1, x])
    settle(mr_ref.at[2], me.at[2])
    mx_ref[3] = mx_ref[2] + mr_ref[2]
    mz_ref[at.f] = mx_ref[3]
    for i in range(2):
        settle(r3_ref.at[i], e3.at[i])
        add(p_ref.at[at.g, i * half : (i + 1) * half], r3_ref.at[i])
    for j in range(1, ranks):
        f2 = xor4(at.f, j)
        send(p_ref.at[at.g, f2], r4_ref.at[at.f], s4.at[j], e4.at[at.f], (at.g, f2))
        send(mx_ref.at[3], mz_ref.at[at.f], zs.at[j], ze.at[at.f], (at.g, f2))
    total = p_ref[at.g, at.f].astype(F32)
    for j in range(1, ranks):
        f2 = xor4(at.f, j)
        settle(r4_ref.at[f2], e4.at[f2])
        total = total + r4_ref[f2].astype(F32)
        settle(mz_ref.at[f2], ze.at[f2])
    fin_ref[...] = total
    gmix_ref[...] = (mz_ref[0] + mz_ref[1]) + (mz_ref[2] + mz_ref[3])

    for m in range(E):
        for w in range(3):
            settle(t_ref.at[m, w], tr.at[m, w])
    for i in range(1, E):
        for w in range(3):
            settle(t_ref.at[0, w], ts.at[i, w])

    @pl.when(at.f > 0)
    def _():
        settle(dhalo_ref, hs)

    @pl.when(at.f < ranks - 1)
    def _():
        settle(back_ref, hr)

    for i in range(4):
        settle(r1_ref.at[0], s1.at[i])
    for i in range(2):
        for n2 in range(2):
            settle(r2_ref.at[0, 0], s2.at[i, n2])
        settle(r3_ref.at[0], s3.at[i])
    for i in range(3):
        settle(mr_ref.at[0], ms.at[i])
    for j in range(1, ranks):
        settle(r4_ref.at[0], s4.at[j])
        settle(mz_ref.at[0], zs.at[j])


def end(groups, ranks, tile, *args):
    cot = args[0]
    width = cot.shape[1]
    dma = pltpu.SemaphoreType.DMA
    vm = pltpu.VMEM
    block = (width // ranks + 8, 4 * (width // groups))
    half = ranks // 2
    return pl.pallas_call(
        end_kernel,
        out_shape=[
            sds((TOK_DEV, width), BF16),
            sds((TOK_DEV, width), F32),
            sds((TOK_DEV, 128), F32),
            sds((TOK_DEV, width), F32),
            sds((HALO, width), BF16),
            sds((E, 3) + tile, BF16),
            sds(block, F32),
            sds((16, 128), F32),
        ],
        in_specs=whole(25),
        out_specs=whole(8),
        scratch_shapes=[
            vm((128, width), F32),
            vm((HALO, width), BF16),
            vm((TOK_DEV, width), BF16),
            vm((TOK_DEV, width), F32),
            vm((KEYS, width), F32),
            vm((KEYS, width), F32),
            vm((TOK_DEV, width), BF16),
            vm((KEYS, width), BF16),
            vm((KEYS, width), BF16),
            vm((4, width, width), BF16),
            vm((groups, ranks) + block, BF16),
            vm((4, ranks) + block, BF16),
            vm((2, 2, half) + block, BF16),
            vm((2, half) + block, BF16),
            vm((ranks,) + block, BF16),
            vm((4, 16, 128), F32),
            vm((3, 16, 128), F32),
            vm((ranks, 16, 128), F32),
            dma((E, 3)),
            dma((E, 3)),
            dma,
            dma,
            dma((4,)),
            dma((4,)),
            dma((2, 2)),
            dma((2, 2)),
            dma((2,)),
            dma((2,)),
            dma((4,)),
            dma((4,)),
            dma((3,)),
            dma((3,)),
            dma((4,)),
            dma((4,)),
        ],
        compiler_params=params(63, collective_id=3, has_side_effects=True),
        name="end",
    )(*args)


def store_kernel(
    t_ref,
    fin_ref,
    dres_ref,
    down_ref,
    back_ref,
    tok_ref,
    inv1_ref,
    gate_ref,
    up_ref,
    downw_ref,
    gq_ref,
    gk_ref,
    gv_ref,
    go_ref,
    small_ref,
    gtok_ref,
):
    for e in range(E):
        gate_ref[e] = t_ref[e, 0].astype(F32)
        up_ref[e] = t_ref[e, 1].astype(F32)
        downw_ref[e] = t_ref[e, 2].astype(F32).T
    head_rows, part_cols = gq_ref.shape
    for w, ref in enumerate((gq_ref, gk_ref, gv_ref, go_ref)):
        ref[...] = fin_ref[0:head_rows, w * part_cols : (w + 1) * part_cols]
    for i in range(small_ref.shape[0] // 8):
        small_ref[8 * i : 8 * i + 8, :] = fin_ref[
            head_rows : head_rows + 8, 128 * i : 128 * i + 128
        ]
    width = tok_ref.shape[1]
    inv1 = inv1_ref[HALO:, 0:1]
    unit = tok_ref[...].astype(F32) * inv1
    m = jnp.concatenate(
        [down_ref[: TOK_DEV - HALO, :], down_ref[TOK_DEV - HALO :, :] + back_ref[...]], axis=0
    )
    d_dealt = inv1 * (m - unit * jnp.mean(m * unit, axis=1, keepdims=True))
    gtok_ref[...] = dres_ref[...] + d_dealt.astype(BF16).astype(F32)


def store(t, fin, dres, down, back, tok, inv1, groups, ranks):
    width = tok.shape[1]
    rows, cols = t.shape[2:]
    per = width // (groups * ranks)
    return pl.pallas_call(
        store_kernel,
        out_shape=[sds((E, rows, cols), F32)] * 2
        + [sds((E, cols, rows), F32)]
        + [sds((width // ranks, width // groups), F32)] * 4
        + [sds((per, 128), F32), sds(tok.shape, F32)],
        in_specs=whole(7),
        out_specs=whole(9),
        compiler_params=params(48),
        name="store",
    )(t, fin, dres, down, back, tok, inv1)


def fast_device(
    tokens,
    cotangent,
    prev_logits,
    lengths,
    dealing,
    routes,
    gain_one,
    w_query,
    w_key,
    w_value,
    w_out,
    gain_two,
    w_router,
    w_mix,
    w_const,
    v_const,
    w_gate,
    w_up,
    w_down,
):
    groups = lax.axis_size("grp")
    ranks = lax.axis_size("fsdp")
    f_id = lax.axis_index("fsdp")
    width = tokens.shape[1]
    per = gain_one.shape[0]

    small = jnp.concatenate(
        [w_router, gain_one[:, None], gain_two[:, None], v_const, w_const], axis=1
    )
    small = jnp.pad(small, ((0, 0), (0, 128 - small.shape[1])))
    small = small.reshape(per // 8, 8, 128).transpose(1, 0, 2).reshape(8, per // 8 * 128)
    tile = jnp.concatenate([w_query, w_key, w_value, w_out], axis=1)
    tile = jnp.concatenate([tile, small], axis=0)

    seq_len = lengths[0]
    count = seq_len.shape[0]
    ids = jnp.arange(count, dtype=jnp.int32)
    ends = jnp.sum(jnp.where(ids[:, None] >= ids[None, :], seq_len[None, :], 0), axis=1)
    row = f_id * TOK_DEV + jnp.arange(-HALO, TOK_DEV, dtype=jnp.int32)
    start = jnp.max(jnp.where(ends[None, :] <= row[:, None], ends[None, :], 0), axis=1)
    pos = jnp.maximum(row - start, 0)
    cos, sin = rotation_tables(pos, HEAD_DIM)
    cos = jnp.concatenate([cos] * 4, axis=1)
    sin = jnp.concatenate([-sin, sin, -sin, sin], axis=1)
    pos_own = jnp.broadcast_to(pos[HALO:, None], (TOK_DEV, 128))
    prev = jnp.pad(prev_logits, ((0, 0), (0, 128 - EXPERTS_ALL)))
    wmix = jnp.pad(w_mix, ((0, 128 - EXPERTS_ALL), (0, 128 - EXPERTS_ALL)))

    outs = begin(
        tile,
        tokens,
        cotangent,
        routes,
        cos,
        sin,
        pos_own,
        prev,
        wmix,
        w_down,
        w_gate,
        w_up,
        groups,
        ranks,
    )
    wf, small, halo, slots, q, k, v, n1, inv1, mix, lse, resid, part, probs, cols = outs[:15]
    x, gates, w_all, g_all = outs[15:]
    od_back, gw = moe(x, gates, w_all, g_all)
    output, dres, gprev, down, back, tiles, fin, gmix = end(
        groups,
        ranks,
        w_gate.shape[1:],
        cotangent,
        resid,
        part,
        probs,
        cols,
        slots,
        routes,
        prev,
        wmix,
        small,
        od_back,
        gw,
        wf,
        q,
        k,
        v,
        n1,
        inv1,
        mix,
        lse,
        cos,
        sin,
        pos_own,
        tokens,
        halo,
    )
    grad_gate, grad_up, grad_down, gq, gk, gv, go, tiny, grad_tokens = store(
        tiles, fin, dres, down, back, tokens, inv1, groups, ranks
    )
    return (
        output,
        grad_tokens,
        gprev[:, :EXPERTS_ALL],
        tiny[:, SMALL_G1],
        gq,
        gk,
        gv,
        go,
        tiny[:, SMALL_G1 + 1],
        tiny[:, :EXPERTS_ALL],
        gmix[:EXPERTS_ALL, :EXPERTS_ALL],
        tiny[:, SMALL_C : SMALL_C + 2 * CONSTS],
        tiny[:, SMALL_VC : SMALL_VC + CONSTS],
        grad_gate,
        grad_up,
        grad_down,
    )


def suits(mesh):
    return mesh.shape["fsdp"] == 4 and mesh.shape["grp"] == 8


def solution(mesh):
    return jax.shard_map(
        fast_device if suits(mesh) else per_device,
        mesh=mesh,
        in_specs=(
            P(("grp", "fsdp"), None),
            P(("grp", "fsdp"), None),
            P(("grp", "fsdp"), None),
            P("grp", None),
            P("grp", None),
            P(("grp", "fsdp"), None),
            P(("grp", "fsdp")),
            P("fsdp", "grp"),
            P("fsdp", "grp"),
            P("fsdp", "grp"),
            P("fsdp", "grp"),
            P(("grp", "fsdp")),
            P(("grp", "fsdp"), None),
            P(),
            P(("grp", "fsdp"), None),
            P(("grp", "fsdp"), None),
            P(None, "fsdp", "grp"),
            P(None, "fsdp", "grp"),
            P(None, "grp", "fsdp"),
        ),
        out_specs=(
            P(("grp", "fsdp"), None),
            P(("grp", "fsdp"), None),
            P(("grp", "fsdp"), None),
            P(("grp", "fsdp")),
            P("fsdp", "grp"),
            P("fsdp", "grp"),
            P("fsdp", "grp"),
            P("fsdp", "grp"),
            P(("grp", "fsdp")),
            P(("grp", "fsdp"), None),
            P(),
            P(("grp", "fsdp"), None),
            P(("grp", "fsdp"), None),
            P(None, "fsdp", "grp"),
            P(None, "fsdp", "grp"),
            P(None, "grp", "fsdp"),
        ),
        check_vma=False,
    )
```

```python
import math

import jax
import jax.numpy as jnp
from jax import lax
from jax.experimental import pallas as pl
from jax.experimental.pallas import tpu as pltpu
from jax.sharding import PartitionSpec as P

HEADS = 12
HEAD_DIM = 64
E = 8
CONSTS = 2
BLOCK = 128
EXPERTS_ALL = 12
CAP = 384
TOK_DEV = 320
MOST = 80


NORM_EPS = 1e-05
EXACT = lax.Precision.HIGHEST


def rotation_tables(positions, head_dim):
    half_dim = head_dim // 2
    inv_freq = jnp.exp(
        jnp.arange(half_dim, dtype=jnp.float32) * (-2.0 * math.log(10000.0) / head_dim)
    )
    angles = positions.astype(jnp.float32)[:, None] * inv_freq[None, :]
    return (jnp.cos(angles), jnp.sin(angles))


def rotate(values, cos_table, sin_table):
    row_count = values.shape[0]
    half_dim = cos_table.shape[1]
    heads_view = values.reshape(row_count, -1, 2 * half_dim)
    front_half = heads_view[:, :, :half_dim]
    back_half = heads_view[:, :, half_dim:]
    cos_view = cos_table[:, None, :]
    sin_view = sin_table[:, None, :]
    turned = jnp.concatenate(
        [
            front_half * cos_view - back_half * sin_view,
            back_half * cos_view + front_half * sin_view,
        ],
        axis=2,
    )
    return turned.reshape(row_count, -1)


def exact_dot(left_side, right_side):
    return jnp.dot(left_side, right_side, precision=EXACT, preferred_element_type=jnp.float32)


def per_device(
    tokens,
    cotangent,
    prev_logits,
    lengths,
    dealing,
    routes,
    gain_one,
    w_query,
    w_key,
    w_value,
    w_out,
    gain_two,
    w_router,
    w_mix,
    w_const,
    v_const,
    w_gate,
    w_up,
    w_down,
):
    groups = lax.axis_size("grp")
    dealers = lax.axis_size("fsdp")
    device = lax.axis_index("fsdp")
    model_width = tokens.shape[1]
    per_shard = model_width // (groups * dealers)
    pairs = HEADS // 2
    pair_width = 2 * HEAD_DIM
    scale = HEAD_DIM ** (-0.5)
    seq_len = lengths[0]
    deal_order = dealing[0]
    seq_count = seq_len.shape[0]
    seq_ids = jnp.arange(seq_count, dtype=jnp.int32)
    seq_ends = jnp.cumsum(seq_len)
    starts = seq_ends - seq_len
    padded = (seq_len + BLOCK - 1) // BLOCK * BLOCK
    order_hot = (deal_order[:, None] == seq_ids[None, :]).astype(jnp.int32)
    dealt_len = jnp.sum(order_hot * seq_len[None, :], axis=1)
    dealt_pad = jnp.sum(order_hot * padded[None, :], axis=1)
    dealt_start = jnp.sum(order_hot * starts[None, :], axis=1)
    slot_of = jnp.sum(order_hot * seq_ids[:, None], axis=0)
    pair_index = 2 * device
    row_ids = jnp.arange(CAP, dtype=jnp.int32)
    in_second = row_ids >= dealt_pad[pair_index]
    position = row_ids - jnp.where(in_second, dealt_pad[pair_index], 0)
    seq_limit = jnp.where(in_second, dealt_len[pair_index + 1], dealt_len[pair_index])
    live_rows = position < seq_limit
    source = jnp.where(in_second, dealt_start[pair_index + 1], dealt_start[pair_index]) + position
    source = jnp.where(live_rows, source, -1)
    given_rows = device * TOK_DEV + jnp.arange(TOK_DEV, dtype=jnp.int32)
    seq_hot = (
        (given_rows[:, None] >= starts[None, :]) & (given_rows[:, None] < seq_ends[None, :])
    ).astype(jnp.int32)
    offset_in = given_rows - jnp.sum(seq_hot * starts[None, :], axis=1)
    slot_rank = jnp.sum(seq_hot * slot_of[None, :], axis=1)
    is_second = slot_rank % 2
    lead_pad = jnp.take(dealt_pad, slot_rank - is_second)
    target = slot_rank // 2 * CAP + jnp.where(is_second == 1, lead_pad, 0) + offset_in

    def deal(values):
        shard_rows = lax.all_gather(values, "fsdp", axis=0, tiled=True)
        row_span = shard_rows.shape[0]
        inside = (source >= 0) & (source < row_span)
        taken_rows = jnp.take(shard_rows, jnp.clip(source, 0, row_span - 1), axis=0)
        return jnp.where(inside[:, None], taken_rows, jnp.zeros((CAP, model_width), jnp.bfloat16))

    def give_back(values):
        shard_rows = lax.all_gather(values, "fsdp", axis=0, tiled=True)
        row_span = shard_rows.shape[0]
        inside = (target >= 0) & (target < row_span)
        taken_rows = jnp.take(shard_rows, jnp.clip(target, 0, row_span - 1), axis=0)
        return jnp.where(
            inside[:, None], taken_rows, jnp.zeros((TOK_DEV, model_width), jnp.bfloat16)
        )

    def collect():
        gate_in, up_in, down_in = (w_gate, w_up, w_down)
        sectioned = (
            lax.all_gather(gain_one, "fsdp", axis=0, tiled=True),
            lax.all_gather(w_query, "fsdp", axis=0, tiled=True),
            lax.all_gather(w_key, "fsdp", axis=0, tiled=True),
            lax.all_gather(w_value, "fsdp", axis=0, tiled=True),
            lax.all_gather(w_out, "fsdp", axis=0, tiled=True),
            lax.all_gather(gain_two, "fsdp", axis=0, tiled=True),
            lax.all_gather(w_router, "fsdp", axis=0, tiled=True),
            lax.all_gather(w_const, "fsdp", axis=0, tiled=True),
            lax.all_gather(v_const, "fsdp", axis=0, tiled=True),
            lax.all_gather(gate_in, "fsdp", axis=1, tiled=True),
            lax.all_gather(up_in, "fsdp", axis=1, tiled=True),
            lax.all_gather(down_in, "fsdp", axis=2, tiled=True),
        )
        (
            part_g1,
            part_q,
            part_k,
            part_v,
            part_o,
            part_g2,
            part_r,
            part_c,
            part_vc,
            part_gate,
            part_up,
            part_down,
        ) = sectioned
        small = (
            lax.all_gather(part_g1, "grp", axis=0, tiled=True),
            lax.all_gather(part_q, "grp", axis=1, tiled=True),
            lax.all_gather(part_k, "grp", axis=1, tiled=True),
            lax.all_gather(part_v, "grp", axis=1, tiled=True),
            lax.all_gather(part_o, "grp", axis=1, tiled=True),
            lax.all_gather(part_g2, "grp", axis=0, tiled=True),
            lax.all_gather(part_r, "grp", axis=0, tiled=True),
            lax.all_gather(part_c, "grp", axis=0, tiled=True),
            lax.all_gather(part_vc, "grp", axis=0, tiled=True),
        )
        experts = (
            lax.all_gather(part_gate, "grp", axis=2, tiled=True),
            lax.all_gather(part_up, "grp", axis=2, tiled=True),
            lax.all_gather(part_down, "grp", axis=1, tiled=True),
        )
        return tuple(small) + tuple(experts)

    (
        gain1,
        weight_q,
        weight_k,
        weight_v,
        weight_o,
        gain2,
        router,
        wconst,
        vconst,
        wgate,
        wup,
        wdown,
    ) = collect()
    dealt = deal(tokens)
    dealt_f = dealt.astype(jnp.float32)
    inv_one = lax.rsqrt(jnp.mean(dealt_f * dealt_f, axis=1, keepdims=True) + NORM_EPS)
    unit_one = dealt_f * inv_one
    gain1_f = gain1.astype(jnp.float32)
    normed_one = (unit_one * gain1_f).astype(jnp.bfloat16)
    cos_table, sin_table = rotation_tables(position, HEAD_DIM)
    query = rotate(
        jnp.dot(normed_one, weight_q, preferred_element_type=jnp.float32), cos_table, sin_table
    ).astype(jnp.bfloat16)
    keyed = rotate(
        jnp.dot(normed_one, weight_k, preferred_element_type=jnp.float32), cos_table, sin_table
    ).astype(jnp.bfloat16)
    values_proj = jnp.dot(normed_one, weight_v, preferred_element_type=jnp.float32).astype(
        jnp.bfloat16
    )
    allowed = (
        (in_second[:, None] == in_second[None, :])
        & (position[None, :] <= position[:, None])
        & live_rows[None, :]
    )

    def by_pairs(values):
        return values.reshape(CAP, pairs, pair_width).transpose(1, 0, 2)

    def from_pairs(values):
        return values.transpose(1, 0, 2).reshape(CAP, model_width)

    def pair_scores(q_pair, k_pair):
        query_heads = q_pair.reshape(CAP, 2, HEAD_DIM)
        key_heads = k_pair.reshape(CAP, 2, HEAD_DIM)
        scores = (
            jnp.einsum("qhd,khd->hqk", query_heads, key_heads, preferred_element_type=jnp.float32)
            * scale
        )
        return (jnp.where(allowed[None], scores, -1e30), query_heads, key_heads)

    def attend(pair_items):
        q_pair, k_pair, v_pair = pair_items
        scores, query_heads, key_heads = pair_scores(q_pair, k_pair)
        row_top = jnp.max(scores, axis=-1, keepdims=True)
        weights_exp = jnp.exp(scores - row_top)
        row_total = jnp.sum(weights_exp, axis=-1, keepdims=True)
        attn_probs = weights_exp / row_total
        value_heads = v_pair.reshape(CAP, 2, HEAD_DIM)
        mixed_pair = jnp.einsum(
            "hqk,khd->qhd",
            attn_probs.astype(jnp.bfloat16),
            value_heads,
            preferred_element_type=jnp.float32,
        )
        return (mixed_pair.reshape(CAP, pair_width), (row_top + jnp.log(row_total))[:, :, 0])

    mixed_pairs, log_sums = lax.map(
        attend, (by_pairs(query), by_pairs(keyed), by_pairs(values_proj))
    )
    mixed = from_pairs(mixed_pairs).astype(jnp.bfloat16)
    attn_out = jnp.dot(mixed, weight_o, preferred_element_type=jnp.float32).astype(jnp.bfloat16)
    returned = give_back(attn_out)
    resid = tokens.astype(jnp.float32) + returned.astype(jnp.float32)
    inv_two = lax.rsqrt(jnp.mean(resid * resid, axis=1, keepdims=True) + NORM_EPS)
    unit_two = resid * inv_two
    gain2_f = gain2.astype(jnp.float32)
    normed = unit_two * gain2_f
    narrow = normed.astype(jnp.bfloat16)
    mix_f = w_mix.astype(jnp.float32)
    router_f = router.astype(jnp.float32)
    wconst_f = wconst.astype(jnp.float32)
    logits = jnp.dot(narrow, router, preferred_element_type=jnp.float32) + exact_dot(
        prev_logits, mix_f
    )
    logit_top = jnp.max(logits, axis=1, keepdims=True)
    logit_exp = jnp.exp(logits - logit_top)
    route_probs = logit_exp / jnp.sum(logit_exp, axis=1, keepdims=True)
    expert_ids = jnp.arange(EXPERTS_ALL, dtype=jnp.int32)
    chosen = (
        (routes[:, 0:1] == expert_ids[None, :]) | (routes[:, 1:2] == expert_ids[None, :])
    ).astype(jnp.float32)
    gate_weights = route_probs * chosen
    result = resid + gate_weights[:, E + 1 : E + 2] * normed
    const_logits = jnp.dot(narrow, wconst, preferred_element_type=jnp.float32)
    vconst_f = vconst.astype(jnp.float32)
    const_mixes = []
    const_branches = []
    for const_idx in range(CONSTS):
        part_logits = const_logits[:, 2 * const_idx : 2 * const_idx + 2]
        part_exp = jnp.exp(part_logits - jnp.max(part_logits, axis=1, keepdims=True))
        const_mix = part_exp / jnp.sum(part_exp, axis=1, keepdims=True)
        branch = const_mix[:, 0:1] * normed + const_mix[:, 1:2] * vconst_f[:, const_idx][None, :]
        const_mixes.append(const_mix)
        const_branches.append(branch)
        result = result + gate_weights[:, E + 2 + const_idx : E + 3 + const_idx] * branch
    slot_list = []
    filled_list = []
    slot_gate_list = []
    for expert in range(E):
        member = (routes[:, 0] == expert) | (routes[:, 1] == expert)
        place_at = jnp.cumsum(member.astype(jnp.int32)) - 1
        slot_table = (
            jnp.zeros((MOST,), jnp.int32)
            .at[jnp.where(member, place_at, MOST)]
            .set(jnp.arange(TOK_DEV, dtype=jnp.int32), mode="drop")
        )
        filled = jnp.arange(MOST, dtype=jnp.int32) < jnp.sum(member.astype(jnp.int32))
        slot_list.append(slot_table)
        filled_list.append(filled)
        slot_gate_list.append(jnp.where(filled, jnp.take(gate_weights[:, expert], slot_table), 0.0))
    slot_tables = jnp.stack(slot_list, axis=0)
    filled_all = jnp.stack(filled_list, axis=0)
    slot_gates = jnp.stack(slot_gate_list, axis=0)
    expert_kept = []
    out_list = []
    for expert in range(E):
        picked = jnp.take(narrow, slot_tables[expert], axis=0)
        gate_part = jnp.dot(picked, wgate[expert], preferred_element_type=jnp.float32)
        up_part = jnp.dot(picked, wup[expert], preferred_element_type=jnp.float32)
        hidden = (jax.nn.silu(gate_part) * up_part).astype(jnp.bfloat16)
        out_list.append(jnp.dot(hidden, wdown[expert], preferred_element_type=jnp.float32))
        expert_kept.append((picked, gate_part, up_part, hidden))
    expert_outs = jnp.stack(out_list, axis=0)
    for expert in range(E):
        result = result.at[slot_tables[expert]].add(
            slot_gates[expert][:, None] * expert_outs[expert]
        )
    output = result.astype(jnp.bfloat16)
    (
        gain1,
        weight_q,
        weight_k,
        weight_v,
        weight_o,
        gain2,
        router,
        wconst,
        vconst,
        wgate,
        wup,
        wdown,
    ) = collect()
    gain1_f = gain1.astype(jnp.float32)
    gain2_f = gain2.astype(jnp.float32)
    router_f = router.astype(jnp.float32)
    wconst_f = wconst.astype(jnp.float32)
    vconst_f = vconst.astype(jnp.float32)
    grad_out = cotangent.astype(jnp.float32)
    d_gate_cols = [jnp.zeros((TOK_DEV,), jnp.float32) for expert in range(EXPERTS_ALL)]
    d_gate_cols[E + 1] = jnp.sum(grad_out * normed, axis=1)
    d_normed = gate_weights[:, E + 1 : E + 2] * grad_out
    d_const_parts = []
    d_vconst_cols = []
    for const_idx in range(CONSTS):
        const_mix = const_mixes[const_idx]
        gate_col = gate_weights[:, E + 2 + const_idx]
        d_gate_cols[E + 2 + const_idx] = jnp.sum(grad_out * const_branches[const_idx], axis=1)
        d_piece = gate_col[:, None] * grad_out
        d_normed = d_normed + const_mix[:, 0:1] * d_piece
        d_cmix = jnp.stack(
            [
                jnp.sum(d_piece * normed, axis=1),
                jnp.sum(d_piece * vconst_f[:, const_idx][None, :], axis=1),
            ],
            axis=1,
        )
        d_const_parts.append(
            const_mix * (d_cmix - jnp.sum(const_mix * d_cmix, axis=1, keepdims=True))
        )
        d_vconst_cols.append(exact_dot(const_mix[:, 1] * gate_col, grad_out))
    d_const_logits = jnp.concatenate(d_const_parts, axis=1)
    grad_rows_all = jnp.take(grad_out, slot_tables.reshape(-1), axis=0).reshape(
        E, MOST, model_width
    )
    d_slot_gates = jnp.where(filled_all, jnp.sum(grad_rows_all * expert_outs, axis=2), 0.0)
    for expert in range(E):
        d_gate_cols[expert] = (
            jnp.zeros((TOK_DEV,), jnp.float32).at[slot_tables[expert]].add(d_slot_gates[expert])
        )
    d_expert_all = (slot_gates[:, :, None] * grad_rows_all).astype(jnp.bfloat16)
    d_wgate_list = []
    d_wup_list = []
    d_wdown_list = []
    d_picked_list = []
    for expert in range(E):
        picked, gate_part, up_part, hidden = expert_kept[expert]
        d_expert = d_expert_all[expert]
        d_wdown_list.append(jnp.dot(hidden.T, d_expert, preferred_element_type=jnp.float32))
        d_hidden = jnp.dot(d_expert, wdown[expert].T, preferred_element_type=jnp.float32)
        sigmoid_g = jax.nn.sigmoid(gate_part)
        d_up_part = (d_hidden * gate_part * sigmoid_g).astype(jnp.bfloat16)
        d_gate_part = (
            d_hidden * up_part * sigmoid_g * (1.0 + gate_part * (1.0 - sigmoid_g))
        ).astype(jnp.bfloat16)
        d_wgate_list.append(jnp.dot(picked.T, d_gate_part, preferred_element_type=jnp.float32))
        d_wup_list.append(jnp.dot(picked.T, d_up_part, preferred_element_type=jnp.float32))
        d_picked_list.append(
            jnp.dot(d_gate_part, wgate[expert].T, preferred_element_type=jnp.float32)
            + jnp.dot(d_up_part, wup[expert].T, preferred_element_type=jnp.float32)
        )
    d_picked_all = jnp.stack(d_picked_list, axis=0)
    d_wgate_full = jnp.stack(d_wgate_list, axis=0)
    d_wup_full = jnp.stack(d_wup_list, axis=0)
    d_wdown_full = jnp.stack(d_wdown_list, axis=0)
    d_narrow = jnp.zeros((TOK_DEV, model_width), jnp.float32)
    for expert in range(E):
        d_narrow = d_narrow.at[slot_tables[expert]].add(
            jnp.where(filled_all[expert][:, None], d_picked_all[expert], 0.0)
        )
    d_gate_w = jnp.stack(d_gate_cols, axis=1)
    d_probs = d_gate_w * chosen
    d_logits = route_probs * (d_probs - jnp.sum(route_probs * d_probs, axis=1, keepdims=True))
    narrow_f = narrow.astype(jnp.float32)
    d_narrow = d_narrow + exact_dot(d_logits, router_f.T) + exact_dot(d_const_logits, wconst_f.T)
    d_router_full = exact_dot(narrow_f.T, d_logits)
    d_wconst_full = exact_dot(narrow_f.T, d_const_logits)
    d_vconst_full = jnp.stack(d_vconst_cols, axis=1)
    d_mix_full = exact_dot(prev_logits.T, d_logits)
    grad_prev = exact_dot(d_logits, mix_f.T)
    d_normed_total = d_normed + d_narrow
    d_gain2_full = jnp.sum(d_normed_total * unit_two, axis=0)
    d_unit_two = d_normed_total * gain2_f
    d_resid = grad_out + inv_two * (
        d_unit_two - unit_two * jnp.mean(d_unit_two * unit_two, axis=1, keepdims=True)
    )
    d_attn = deal(d_resid.astype(jnp.bfloat16))
    d_wo_full = jnp.dot(mixed.T, d_attn, preferred_element_type=jnp.float32)
    d_mixed = jnp.dot(d_attn, weight_o.T, preferred_element_type=jnp.float32).astype(jnp.bfloat16)

    def attend_back(pair_items):
        q_pair, k_pair, v_pair, dm_pair, lse_pair = pair_items
        scores, query_heads, key_heads = pair_scores(q_pair, k_pair)
        attn_probs = jnp.where(allowed[None], jnp.exp(scores - lse_pair[:, :, None]), 0.0)
        value_heads = v_pair.reshape(CAP, 2, HEAD_DIM)
        dm_heads = dm_pair.reshape(CAP, 2, HEAD_DIM)
        d_p = jnp.einsum("qhd,khd->hqk", dm_heads, value_heads, preferred_element_type=jnp.float32)
        row_delta = jnp.sum(attn_probs * d_p, axis=-1, keepdims=True)
        d_scores = (attn_probs * (d_p - row_delta)).astype(jnp.bfloat16)
        d_q = (
            jnp.einsum("hqk,khd->qhd", d_scores, key_heads, preferred_element_type=jnp.float32)
            * scale
        )
        d_k = (
            jnp.einsum("hqk,qhd->khd", d_scores, query_heads, preferred_element_type=jnp.float32)
            * scale
        )
        d_v = jnp.einsum(
            "hqk,qhd->khd",
            attn_probs.astype(jnp.bfloat16),
            dm_heads,
            preferred_element_type=jnp.float32,
        )
        return (
            d_q.reshape(CAP, pair_width),
            d_k.reshape(CAP, pair_width),
            d_v.reshape(CAP, pair_width),
        )

    dq_pairs, dk_pairs, dv_pairs = lax.map(
        attend_back,
        (by_pairs(query), by_pairs(keyed), by_pairs(values_proj), by_pairs(d_mixed), log_sums),
    )
    d_query = rotate(from_pairs(dq_pairs), cos_table, -sin_table).astype(jnp.bfloat16)
    d_key = rotate(from_pairs(dk_pairs), cos_table, -sin_table).astype(jnp.bfloat16)
    d_value = from_pairs(dv_pairs).astype(jnp.bfloat16)
    d_wq_full = jnp.dot(normed_one.T, d_query, preferred_element_type=jnp.float32)
    d_wk_full = jnp.dot(normed_one.T, d_key, preferred_element_type=jnp.float32)
    d_wv_full = jnp.dot(normed_one.T, d_value, preferred_element_type=jnp.float32)
    d_normed_one = (
        jnp.dot(d_query, weight_q.T, preferred_element_type=jnp.float32)
        + jnp.dot(d_key, weight_k.T, preferred_element_type=jnp.float32)
        + jnp.dot(d_value, weight_v.T, preferred_element_type=jnp.float32)
    )
    d_gain1_full = jnp.sum(d_normed_one * unit_one, axis=0)
    d_unit_one = d_normed_one * gain1_f
    d_dealt = (
        inv_one * (d_unit_one - unit_one * jnp.mean(d_unit_one * unit_one, axis=1, keepdims=True))
    ).astype(jnp.bfloat16)
    grad_tokens = d_resid + give_back(d_dealt).astype(jnp.float32)

    def regroup(grads_in):
        tail_shape = grads_in.shape[1:]
        split_view = grads_in.reshape((groups, dealers, per_shard) + tail_shape)
        return jnp.swapaxes(split_view, 0, 1).reshape((model_width,) + tail_shape)

    mix_tile = jnp.broadcast_to(d_mix_full[None], (dealers, EXPERTS_ALL, EXPERTS_ALL))
    sectioned = (
        lax.psum_scatter(
            regroup(d_gain1_full).astype(jnp.bfloat16), "fsdp", scatter_dimension=0, tiled=True
        ).astype(jnp.float32),
        lax.psum_scatter(
            d_wq_full.astype(jnp.bfloat16), "fsdp", scatter_dimension=0, tiled=True
        ).astype(jnp.float32),
        lax.psum_scatter(
            d_wk_full.astype(jnp.bfloat16), "fsdp", scatter_dimension=0, tiled=True
        ).astype(jnp.float32),
        lax.psum_scatter(
            d_wv_full.astype(jnp.bfloat16), "fsdp", scatter_dimension=0, tiled=True
        ).astype(jnp.float32),
        lax.psum_scatter(
            d_wo_full.astype(jnp.bfloat16), "fsdp", scatter_dimension=0, tiled=True
        ).astype(jnp.float32),
        lax.psum_scatter(
            regroup(d_gain2_full).astype(jnp.bfloat16), "fsdp", scatter_dimension=0, tiled=True
        ).astype(jnp.float32),
        lax.psum_scatter(
            regroup(d_router_full).astype(jnp.bfloat16), "fsdp", scatter_dimension=0, tiled=True
        ).astype(jnp.float32),
        lax.psum_scatter(
            regroup(d_wconst_full).astype(jnp.bfloat16), "fsdp", scatter_dimension=0, tiled=True
        ).astype(jnp.float32),
        lax.psum_scatter(
            regroup(d_vconst_full).astype(jnp.bfloat16), "fsdp", scatter_dimension=0, tiled=True
        ).astype(jnp.float32),
        lax.psum_scatter(
            mix_tile.astype(jnp.bfloat16), "fsdp", scatter_dimension=0, tiled=True
        ).astype(jnp.float32),
        lax.psum_scatter(
            d_wgate_full.astype(jnp.bfloat16), "fsdp", scatter_dimension=1, tiled=True
        ).astype(jnp.float32),
        lax.psum_scatter(
            d_wup_full.astype(jnp.bfloat16), "fsdp", scatter_dimension=1, tiled=True
        ).astype(jnp.float32),
        lax.psum_scatter(
            d_wdown_full.astype(jnp.bfloat16), "fsdp", scatter_dimension=2, tiled=True
        ).astype(jnp.float32),
    )
    s_g1, s_q, s_k, s_v, s_o, s_g2, s_r, s_c, s_vc, s_mix, s_gate, s_up, s_down = sectioned
    summed = (
        lax.psum_scatter(s_g1.astype(jnp.bfloat16), "grp", scatter_dimension=0, tiled=True).astype(
            jnp.float32
        ),
        lax.psum_scatter(s_q.astype(jnp.bfloat16), "grp", scatter_dimension=1, tiled=True).astype(
            jnp.float32
        ),
        lax.psum_scatter(s_k.astype(jnp.bfloat16), "grp", scatter_dimension=1, tiled=True).astype(
            jnp.float32
        ),
        lax.psum_scatter(s_v.astype(jnp.bfloat16), "grp", scatter_dimension=1, tiled=True).astype(
            jnp.float32
        ),
        lax.psum_scatter(s_o.astype(jnp.bfloat16), "grp", scatter_dimension=1, tiled=True).astype(
            jnp.float32
        ),
        lax.psum_scatter(s_g2.astype(jnp.bfloat16), "grp", scatter_dimension=0, tiled=True).astype(
            jnp.float32
        ),
        lax.psum_scatter(s_r.astype(jnp.bfloat16), "grp", scatter_dimension=0, tiled=True).astype(
            jnp.float32
        ),
        lax.psum_scatter(s_c.astype(jnp.bfloat16), "grp", scatter_dimension=0, tiled=True).astype(
            jnp.float32
        ),
        lax.psum_scatter(s_vc.astype(jnp.bfloat16), "grp", scatter_dimension=0, tiled=True).astype(
            jnp.float32
        ),
        lax.psum_scatter(
            jnp.broadcast_to(s_mix, (groups, EXPERTS_ALL, EXPERTS_ALL)).astype(jnp.bfloat16),
            "grp",
            scatter_dimension=0,
            tiled=True,
        ).astype(jnp.float32),
    )
    (
        grad_gain_one,
        grad_query,
        grad_key,
        grad_value,
        grad_out_proj,
        grad_gain_two,
        grad_router,
        grad_const,
        grad_vconst,
        mix_part,
    ) = summed
    grad_mix = mix_part[0]
    grad_gate, grad_up, grad_down = (
        lax.psum_scatter(
            s_gate.astype(jnp.bfloat16), "grp", scatter_dimension=2, tiled=True
        ).astype(jnp.float32),
        lax.psum_scatter(s_up.astype(jnp.bfloat16), "grp", scatter_dimension=2, tiled=True).astype(
            jnp.float32
        ),
        lax.psum_scatter(
            s_down.astype(jnp.bfloat16), "grp", scatter_dimension=1, tiled=True
        ).astype(jnp.float32),
    )
    return (
        output,
        grad_tokens,
        grad_prev,
        grad_gain_one,
        grad_query,
        grad_key,
        grad_value,
        grad_out_proj,
        grad_gain_two,
        grad_router,
        grad_mix,
        grad_const,
        grad_vconst,
        grad_gate,
        grad_up,
        grad_down,
    )


HALO = 256
KEYS = HALO + TOK_DEV
ROWS = E * MOST
NEG = -1e30
F32 = jnp.float32
BF16 = jnp.bfloat16
NT = (((1,), (1,)), ((), ()))
TN = (((0,), (0,)), ((), ()))
NN = (((1,), (0,)), ((), ()))


def mm(a, b, dims=NN):
    return lax.dot_general(a, b, dims, preferred_element_type=F32)


def lane_iota(rows, width=128):
    return lax.broadcasted_iota(jnp.int32, (rows, width), 1)


def pick(values, lane_mask):
    return jnp.sum(jnp.where(lane_mask, values, 0.0), axis=1, keepdims=True)


def params(mb, **kw):
    return pltpu.CompilerParams(vmem_limit_bytes=mb << 20, **kw)


def whole(count):
    return [pl.BlockSpec(memory_space=pltpu.VMEM) for _ in range(count)]


def sds(shape, dtype):
    return jax.ShapeDtypeStruct(shape, dtype)


MESH_ID = pl.DeviceIdType.MESH


def send(src, dst, send_sem, recv_sem, device):
    pltpu.make_async_remote_copy(
        src_ref=src,
        dst_ref=dst,
        send_sem=send_sem,
        recv_sem=recv_sem,
        device_id=device,
        device_id_type=MESH_ID,
    ).start()


def settle(ref, sem):
    pltpu.make_async_copy(ref, ref, sem).wait()


def flip(a, b):
    return a + b - 2 * a * b


def xor4(a, b):
    return flip(a // 2, b // 2) * 2 + flip(lax.rem(a, 2), lax.rem(b, 2))


def aligned(value, to):
    return pl.multiple_of(value, to)


class Place:
    def __init__(self, his, lo):
        self.g = lax.axis_index("grp")
        self.f = lax.axis_index("fsdp")
        self.his, self.lo = his, lo
        self.hi = self.g // lo
        self.l = lax.rem(self.g, lo)
        self.m = self.f * his + self.hi
        core = lax.rem(self.g, 2)
        side = lax.rem(self.g // 2, 2)
        self.core_peer = self.g + 1 - 2 * core
        self.side_peer = self.g + 2 - 4 * side
        self.l1 = lax.rem(self.core_peer, lo)
        self.l2 = lax.rem(self.side_peer, lo)
        self.l3 = lo - 1 - self.l

    def member(self, j, hh):
        f = xor4(self.f, j)
        hi = flip(self.hi, hh)
        return f * self.his + hi, (hi * self.lo + self.l, f)

    def others(self):
        peers = []
        for j in range(4):
            for hh in range(self.his):
                if j or hh:
                    peers.append(self.member(j, hh)[1])
        return peers


def call(peers):
    barrier = pltpu.get_barrier_semaphore()
    for peer in peers:
        pl.semaphore_signal(barrier, inc=1, device_id=peer, device_id_type=MESH_ID)


def answer(peers):
    pl.semaphore_wait(pltpu.get_barrier_semaphore(), len(peers))


def turn(values, cos, sin):
    half = HEAD_DIM // 2
    width = values.shape[1]
    reps = width // 128
    front = lax.rem(lane_iota(values.shape[0], width), HEAD_DIM) < half
    swapped = jnp.where(
        front, pltpu.roll(values, width - half, 1), pltpu.roll(values, half, 1)
    )
    cos_w = jnp.concatenate([cos] * reps, axis=1)
    sin_w = jnp.concatenate([sin] * reps, axis=1)
    return values * cos_w + swapped * sin_w


QBLOCKS = [(0, 128), (128, 128), (256, 64)]


def allowed_mask(pos_ref, first, count, lane):
    ii = lax.broadcasted_iota(jnp.int32, (count, 384), 0) + HALO
    jj = lax.broadcasted_iota(jnp.int32, (count, 384), 1)
    pos = pos_ref[pl.ds(first, count), lane : lane + 1].astype(jnp.int32)
    return (jj <= ii) & (jj >= ii - pos)


def key_span(first):
    return min(384, KEYS - first)


KEPT = (
    ("wf", (4, None, None), BF16),
    ("s", (None, 128), F32),
    ("halo", (HALO, None), BF16),
    ("q", (TOK_DEV, None), BF16),
    ("k", (KEYS, None), BF16),
    ("v", (KEYS, None), BF16),
    ("n1", (KEYS, None), BF16),
    ("inv1", (KEYS, 128), F32),
    ("mix", (TOK_DEV, None), BF16),
    ("lse", (TOK_DEV, 128), F32),
    ("resid", (TOK_DEV, None), F32),
    ("part", (TOK_DEV, None), F32),
    ("probs", (TOK_DEV, 128), F32),
    ("cols", (TOK_DEV, 128), F32),
    ("cos", (KEYS, 128), F32),
    ("sin", (KEYS, 128), F32),
)


def kept_shape(dims, width):
    return tuple(width if d is None else d for d in dims)


def by_name(refs):
    return {name: ref for (name, _, _), ref in zip(KEPT, refs)}


def token_places(len_ref, at):
    row = lax.broadcasted_iota(jnp.int32, (KEYS, 128), 0) + (at.f * TOK_DEV - HALO)
    first = jnp.zeros((KEYS, 128), jnp.int32)
    reached = jnp.int32(0)
    for i in range(len_ref.shape[1]):
        reached = reached + len_ref[0, i]
        first = jnp.where(row >= reached, reached, first)
    return jnp.maximum(row - first, 0)


def ahead_kernel(
    len_ref,
    routes_ref,
    prev_ref,
    wmix_ref,
    router_ref,
    gain1_ref,
    gain2_ref,
    const_ref,
    vconst_ref,
    wq_ref,
    wk_ref,
    wv_ref,
    wo_ref,
    tok_ref,
    cot_ref,
    wg_hbm,
    wu_hbm,
    wd_hbm,
    *rest,
):
    n = len(KEPT)
    kept_hbm = by_name(rest[:n])
    op_hbm, gw_hbm, back_hbm, dgb_hbm = rest[n : n + 4]
    kept = by_name(rest[n + 4 : 2 * n + 4])
    (
        tile_ref,
        small_ref,
        p_ref,
        grow_ref,
        x_ref,
        gates_ref,
        w_ref,
        g_ref,
        xb_ref,
        gb_ref,
        od_ref,
        op_ref,
        r1_ref,
        r2_ref,
        dgp_ref,
        dr1_ref,
        dr2_ref,
        acc_ref,
        gw_ref,
        back_ref,
        dgb_ref,
        keep_sem,
        last_sem,
        zs,
        ps,
        cs,
        hs,
        gs,
        ws,
        gas,
        agr,
        hr,
        gr,
        wr,
        gqr,
        xs,
        ts,
        qs,
        tqs,
        d1s,
        t1s,
        d2s,
        t2s,
        bs,
        tbs,
        xr,
        tr,
        qr,
        tqr,
        d1r,
        t1r,
        d2r,
        t2r,
        br,
        tbr,
    ) = rest[2 * n + 4 :]
    wf_ref, s_ref, halo_ref = kept["wf"], kept["s"], kept["halo"]
    q_ref, k_ref, v_ref, n1_ref = kept["q"], kept["k"], kept["v"], kept["n1"]
    mix_ref, lse_ref = kept["mix"], kept["lse"]
    lo, ranks = g_ref.shape[:2]
    his = E // ranks
    at = Place(his, lo)
    width = tok_ref.shape[1]
    head_rows, part_cols = wq_ref.shape
    ff = wg_hbm.shape[2]
    diag = lo * (1 - at.hi) + at.l2
    upper = lo * (1 - at.hi) + at.l
    near = [(at.core_peer, at.f), (at.side_peer, at.f), (upper, at.f), (diag, at.f)]
    core, side = near[0], near[1]
    peers = at.others() + [near[0], near[1], near[3]]
    call(peers)

    def keep(*names):
        for name in names:
            i = [k[0] for k in KEPT].index(name)
            pltpu.make_async_copy(kept[name], kept_hbm[name], keep_sem.at[i]).start()

    tile_ref[0:head_rows, :] = jnp.concatenate(
        [wq_ref[...], wk_ref[...], wv_ref[...], wo_ref[...]], axis=1
    )
    small_ref[...] = jnp.zeros_like(small_ref)
    per = router_ref.shape[1]
    small_ref[0:EXPERTS_ALL, 0:per] = router_ref[...].astype(F32)
    small_ref[SMALL_G1 : SMALL_G1 + 1, 0:per] = gain1_ref[...].astype(F32)
    small_ref[SMALL_G1 + 1 : SMALL_G1 + 2, 0:per] = gain2_ref[...].astype(F32)
    small_ref[SMALL_VC : SMALL_VC + CONSTS, 0:per] = vconst_ref[...].astype(F32)
    small_ref[SMALL_C : SMALL_C + 2 * CONSTS, 0:per] = const_ref[...].astype(F32)
    turned = small_ref[...].T
    tile_ref[head_rows : head_rows + 8, :] = jnp.concatenate(
        [turned[8 * i : 8 * i + 8, :] for i in range(per // 8)], axis=1
    ).astype(BF16)
    answer(peers)

    p_ref[at.g, at.f] = tile_ref[...]
    for j in range(1, ranks):
        f2 = xor4(at.f, j)
        send(tile_ref, p_ref.at[at.g, at.f], zs.at[j], agr.at[at.g, at.f], (at.g, f2))

    def spread(j, f2, src):
        for t, peer in enumerate(near):
            send(src, p_ref.at[at.g, f2], ps.at[j, t], agr.at[at.g, f2], peer)

    spread(0, at.f, tile_ref)
    halo_rows = halo_ref.shape[0]
    tail = tok_ref.at[pl.ds(tok_ref.shape[0] - halo_rows, halo_rows)]

    @pl.when(at.f < ranks - 1)
    def _():
        send(tail, halo_ref, hs, hr, (at.g, at.f + 1))

    @pl.when(at.f == 0)
    def _():
        halo_ref[...] = jnp.zeros_like(halo_ref)

    lanes = lane_iota(TOK_DEV)
    routes = jnp.concatenate(
        [
            jnp.broadcast_to(routes_ref[0:1, :], (8, TOK_DEV)),
            jnp.broadcast_to(routes_ref[1:2, :], (8, TOK_DEV)),
        ],
        axis=0,
    ).T
    r0 = routes[:, 0:1]
    r1 = routes[:, 8:9]
    hot0 = lanes == r0
    hot1 = lanes == r1
    named = jnp.where(hot0 | hot1, 1.0, 0.0).astype(BF16)
    earlier = (
        lax.broadcasted_iota(jnp.int32, (TOK_DEV, TOK_DEV), 1)
        < lax.broadcasted_iota(jnp.int32, (TOK_DEV, TOK_DEV), 0)
    )
    rank = mm(jnp.where(earlier, 1.0, 0.0).astype(BF16), named)
    rank0 = pick(rank, hot0).astype(jnp.int32)
    rank1 = pick(rank, hot1).astype(jnp.int32)
    c0 = jnp.where(r0 < E, r0 * MOST + rank0, -1)
    c1 = jnp.where(r1 < E, r1 * MOST + rank1, -1)
    slot = lane_iota(TOK_DEV, ROWS)
    spots0 = jnp.where(slot == c0, 1.0, 0.0).astype(BF16)
    spots1 = jnp.where(slot == c1, 1.0, 0.0).astype(BF16)
    grow_ref[...] = mm(spots0 + spots1, cot_ref[...], TN).astype(BF16)

    for j in range(1, ranks):
        f2 = xor4(at.f, j)
        settle(p_ref.at[at.g, f2], agr.at[at.g, f2])
        spread(j, f2, p_ref.at[at.g, f2])

    own_rows = pl.ds(aligned(at.f * head_rows, 16), head_rows)
    own_cols = pl.ds(aligned(at.hi * ff, 128), ff)
    own_spot = pl.ds(aligned(at.hi * MOST, 16), MOST)
    for j in range(ranks):
        for hh in range(his):
            e, peer = at.member(j, hh)
            rows = grow_ref.at[pl.ds(aligned(e * MOST, 16), MOST)]
            spot = g_ref.at[at.l, at.f, own_spot]
            sources = (wg_hbm.at[e], wu_hbm.at[e], wd_hbm.at[e])
            if j == 0 and hh == 0:
                pltpu.make_async_copy(rows, spot, gr.at[at.m]).start()
                for w in range(3):
                    pltpu.make_async_copy(
                        sources[w], w_ref.at[w, own_rows, own_cols], wr.at[at.m, w]
                    ).start()
            else:
                k = j * his + hh
                send(rows, spot, gs.at[k], gr.at[at.m], peer)
                for w in range(3):
                    send(
                        sources[w],
                        w_ref.at[w, own_rows, own_cols],
                        ws.at[k, w],
                        wr.at[at.m, w],
                        peer,
                    )

    pos = token_places(len_ref, at).astype(F32)
    half_dim = HEAD_DIM // 2
    lane_k = lane_iota(KEYS)
    freq = jnp.exp(
        lax.rem(lane_k, half_dim).astype(F32) * (-2.0 * math.log(10000.0) / HEAD_DIM)
    )
    kept["cos"][...] = jnp.cos(pos * freq)
    sine = jnp.sin(pos * freq)
    kept["sin"][...] = jnp.where(lax.rem(lane_k, HEAD_DIM) < half_dim, -sine, sine)
    pos_own = pos[HALO:]
    pos_ref = kept["cols"]
    pos_ref[...] = pos_own

    for j in range(ranks):
        f2 = xor4(at.f, j)
        for t in range(1, 4):
            g2 = near[t][0]
            settle(p_ref.at[g2, f2], agr.at[g2, f2])
            send(p_ref.at[g2, f2], p_ref.at[g2, f2], cs.at[t - 1, j], agr.at[g2, f2], near[0])
    sibling_upper = lo * (1 - at.hi) + at.l1
    for j in range(ranks):
        f2 = xor4(at.f, j)
        for g2 in (
            at.core_peer,
            at.hi * lo + at.l3,
            sibling_upper,
            lo * (1 - at.hi) + at.l3,
        ):
            settle(p_ref.at[g2, f2], agr.at[g2, f2])

    groups = p_ref.shape[0]
    for g2 in range(groups):
        for f2 in range(ranks):
            piece = p_ref[g2, f2, head_rows : head_rows + 8, :].astype(F32)
            for i in range(per // 8):
                base = (g2 * ranks + f2) * per + 8 * i
                s_ref[base : base + 8, :] = piece[:, 128 * i : 128 * i + 128]

    def lay(f2, _):
        rows = pl.ds(aligned(f2 * head_rows, 16), head_rows)
        for w in range(4):
            for half in range(2):
                pieces = [
                    p_ref[
                        half * (groups // 2) + i,
                        f2,
                        0:head_rows,
                        w * part_cols : (w + 1) * part_cols,
                    ]
                    for i in range(groups // 2)
                ]
                wf_ref[w, rows, half * (width // 2) : (half + 1) * (width // 2)] = (
                    jnp.concatenate(pieces, axis=1)
                )
        return 0

    lax.fori_loop(0, ranks, lay, 0)

    @pl.when(at.f > 0)
    def _():
        settle(halo_ref, hr)

    scale = HEAD_DIM ** (-0.5)
    flat = s_ref[...].T
    g1 = flat[SMALL_G1 : SMALL_G1 + 1, :]
    g2 = flat[SMALL_G1 + 1 : SMALL_G1 + 2, :]
    vc = flat[SMALL_VC : SMALL_VC + CONSTS, :]
    keep("wf", "s", "halo")
    rows = jnp.concatenate([halo_ref[...], tok_ref[...]], axis=0).astype(F32)
    inv1 = lax.rsqrt(jnp.mean(rows * rows, axis=1, keepdims=True) + NORM_EPS)
    kept["inv1"][...] = jnp.broadcast_to(inv1, (KEYS, 128))
    n1_ref[...] = (rows * inv1 * g1).astype(BF16)

    def project(i, _):
        span = pl.ds(pl.multiple_of(i * 256, 256), 256)
        cos = kept["cos"][...]
        sin = kept["sin"][...]
        q = mm(n1_ref[HALO:, :], wf_ref[0, :, span])
        q_ref[:, span] = turn(q, cos[HALO:], sin[HALO:]).astype(BF16)
        k = mm(n1_ref[...], wf_ref[1, :, span])
        k_ref[:, span] = turn(k, cos, sin).astype(BF16)
        v_ref[:, span] = mm(n1_ref[...], wf_ref[2, :, span]).astype(BF16)
        return 0

    lax.fori_loop(0, width // 256, project, 0)
    keep("q", "k", "v", "n1", "inv1", "cos", "sin")
    lse_ref[...] = jnp.zeros((TOK_DEV, 128), F32)

    for f2 in range(ranks):
        for h2 in range(his):
            settle(
                g_ref.at[at.l, f2, h2 * MOST : (h2 + 1) * MOST], gr.at[f2 * his + h2]
            )
    send(g_ref.at[at.l], g_ref.at[at.l], gas.at[0], gqr.at[0], near[0])
    send(g_ref.at[at.l], g_ref.at[at.l], gas.at[1], gqr.at[1], near[1])

    def pair(p, _):
        span = pl.ds(pl.multiple_of(p * 128, 128), 128)
        for first, count in QBLOCKS:
            keys = key_span(first)
            ok = allowed_mask(pos_ref, first, count, 0)[:, :keys]
            q = q_ref[pl.ds(first, count), span]
            k = k_ref[pl.ds(first, keys), span]
            v = v_ref[pl.ds(first, keys), span]
            lane = lane_iota(count)
            out = None
            lse = lse_ref[pl.ds(first, count), :]
            for h in range(2):
                mine = (lane < HEAD_DIM) if h == 0 else (lane >= HEAD_DIM)
                qh = jnp.where(mine, q, jnp.zeros_like(q))
                sc = jnp.where(ok, mm(qh, k, NT) * scale, NEG)
                top = jnp.max(sc, axis=1, keepdims=True)
                ex = jnp.exp(sc - top)
                total = jnp.sum(ex, axis=1, keepdims=True)
                o = mm((ex / total).astype(BF16), v)
                out = o if h == 0 else jnp.where(mine, o, out)
                lse = jnp.where(lane == 2 * p + h, top + jnp.log(total), lse)
            mix_ref[pl.ds(first, count), span] = out.astype(BF16)
            lse_ref[pl.ds(first, count), :] = lse
        return 0

    lax.fori_loop(0, HEADS // 2, pair, 0)
    settle(g_ref.at[at.l2], gqr.at[1])
    send(g_ref.at[at.l2], g_ref.at[at.l2], gas.at[2], gqr.at[2], near[0])

    attn_out = mm(mix_ref[...], wf_ref[3]).astype(BF16)
    resid = tok_ref[...].astype(F32) + attn_out.astype(F32)
    kept["resid"][...] = resid
    inv2 = lax.rsqrt(jnp.mean(resid * resid, axis=1, keepdims=True) + NORM_EPS)
    normed = resid * inv2 * g2
    narrow = normed.astype(BF16)
    raw = mm(narrow, s_ref[...].astype(BF16))
    prev = prev_ref[...]
    wmix = jnp.concatenate(
        [wmix_ref[...].astype(F32), jnp.zeros((EXPERTS_ALL, 128 - EXPERTS_ALL), F32)], axis=1
    ).astype(BF16)
    phigh = prev.astype(BF16)
    prest = prev - phigh.astype(F32)
    pmid = prest.astype(BF16)
    plow = (prest - pmid.astype(F32)).astype(BF16)
    mixed_prev = mm(phigh, wmix, TN) + (mm(pmid, wmix, TN) + mm(plow, wmix, TN))
    logits = jnp.where(lanes < EXPERTS_ALL, raw + mixed_prev, NEG)
    top = jnp.max(logits, axis=1, keepdims=True)
    ex = jnp.exp(logits - top)
    probs = ex / jnp.sum(ex, axis=1, keepdims=True)
    kept["probs"][...] = probs
    gate0 = pick(probs, hot0)
    gate1 = pick(probs, hot1)

    def gate_of(expert):
        return jnp.where(r0 == expert, gate0, 0.0) + jnp.where(r1 == expert, gate1, 0.0)

    gate_id = gate_of(E + 1)
    part = resid + gate_id * normed
    cols = jnp.where(lanes == 0, gate0, 0.0)
    cols = jnp.where(lanes == 1, gate1, cols)
    cols = jnp.where(lanes == 2, gate_id, cols)
    cols = jnp.where(lanes == 3, inv2, cols)
    for c in range(CONSTS):
        la = pick(raw, lanes == SMALL_C + 2 * c)
        lb = pick(raw, lanes == SMALL_C + 1 + 2 * c)
        big = jnp.maximum(la, lb)
        ea = jnp.exp(la - big)
        eb = jnp.exp(lb - big)
        ma = ea / (ea + eb)
        mb = eb / (ea + eb)
        gate_c = gate_of(E + 2 + c)
        part = part + gate_c * (ma * normed + mb * vc[c : c + 1, :])
        cols = jnp.where(lanes == 4 + 3 * c, gate_c, cols)
        cols = jnp.where(lanes == 5 + 3 * c, ma, cols)
        cols = jnp.where(lanes == 6 + 3 * c, mb, cols)
    kept["part"][...] = part
    wide0 = jnp.where(r0 < E, r0 * 128 + rank0, -1)
    wide1 = jnp.where(r1 < E, r1 * 128 + rank1, -1)
    more = (pos_own[:, 0:1], c0, c1, r0, r1, wide0, wide1)
    for i, value in enumerate(more):
        cols = jnp.where(lanes == COL_POS + i, value.astype(F32), cols)
    kept["cols"][...] = cols
    keep("mix", "lse", "resid", "part", "probs", "cols")
    x_ref[...] = mm(spots0 + spots1, narrow, TN).astype(BF16)
    for e in range(E):
        lane = lanes + e * 128
        row = jnp.sum(
            jnp.where(lane == wide0, gate0, 0.0) + jnp.where(lane == wide1, gate1, 0.0),
            axis=0,
            keepdims=True,
        )
        gates_ref[e] = jnp.broadcast_to(row, (8, 128))


    for j in range(ranks):
        for hh in range(his):
            e, peer = at.member(j, hh)
            k = j * his + hh
            rows = x_ref.at[pl.ds(aligned(e * MOST, 16), MOST)]
            spot = xb_ref.at[at.f, at.l, own_spot]
            if k == 0:
                pltpu.make_async_copy(rows, spot, xr.at[at.m]).start()
                pltpu.make_async_copy(
                    gates_ref.at[e], gb_ref.at[at.f, at.l, at.hi], tr.at[at.m]
                ).start()
            else:
                send(rows, spot, xs.at[k], xr.at[at.m], peer)
                send(
                    gates_ref.at[e], gb_ref.at[at.f, at.l, at.hi], ts.at[k], tr.at[at.m], peer
                )
    acc_ref[...] = jnp.zeros_like(acc_ref)

    def take(j):
        fj = xor4(at.f, j)
        for hh in range(his):
            hi = flip(at.hi, hh)
            m = fj * his + hi
            settle(xb_ref.at[fj, at.l, pl.ds(aligned(hi * MOST, 16), MOST)], xr.at[m])
            settle(gb_ref.at[fj, at.l, hi], tr.at[m])
        for i, peer in enumerate((core, side)):
            send(xb_ref.at[fj, at.l], xb_ref.at[fj, at.l], qs.at[fj, i], qr.at[fj, i], peer)
            send(gb_ref.at[fj, at.l], gb_ref.at[fj, at.l], tqs.at[fj, i], tqr.at[fj, i], peer)

    def pass_on(j):
        fj = xor4(at.f, j)
        settle(xb_ref.at[fj, at.l2], qr.at[fj, 1])
        settle(gb_ref.at[fj, at.l2], tqr.at[fj, 1])
        send(xb_ref.at[fj, at.l2], xb_ref.at[fj, at.l2], qs.at[fj, 2], qr.at[fj, 2], core)
        send(gb_ref.at[fj, at.l2], gb_ref.at[fj, at.l2], tqs.at[fj, 2], tqr.at[fj, 2], core)

    def compute(j):
        fj = xor4(at.f, j)
        settle(xb_ref.at[fj, at.l1], qr.at[fj, 0])
        settle(gb_ref.at[fj, at.l1], tqr.at[fj, 0])
        settle(xb_ref.at[fj, at.l3], qr.at[fj, 2])
        settle(gb_ref.at[fj, at.l3], tqr.at[fj, 2])
        diagonal = lax.broadcasted_iota(jnp.int32, (MOST, 128), 0) == lane_iota(MOST)
        pair_rows = 2 * his * MOST

        def rows_of(i, _):
            l2 = pl.ds(2 * i, 2)
            x = xb_ref[fj, l2].reshape(pair_rows, width)
            g = g_ref[l2, fj].reshape(pair_rows, width)
            gate = jnp.concatenate(
                [
                    pick(
                        jnp.broadcast_to(gb_ref[fj, 2 * i + i2, h][0:1, :], (MOST, 128)), diagonal
                    )
                    for i2 in range(2)
                    for h in range(his)
                ],
                axis=0,
            )
            d_exp = (g.astype(F32) * gate).astype(BF16)
            wg = w_ref[0]
            wu = w_ref[1]
            wd = w_ref[2]
            a = mm(x, wg)
            b = mm(x, wu)
            sig = 1.0 / (1.0 + jnp.exp(-a))
            hidden = (a * sig * b).astype(BF16)
            shape = (2, his * MOST, width)
            op_ref[fj, l2] = mm(hidden, wd, NT).astype(BF16).reshape(shape)
            dh_raw = mm(g, wd)
            d_route = jnp.sum(hidden.astype(F32) * dh_raw, axis=1, keepdims=True)
            for i2 in range(2):
                for h in range(his):
                    first = (i2 * his + h) * MOST
                    line = jnp.sum(
                        jnp.where(diagonal, d_route[first : first + MOST], 0.0),
                        axis=0,
                        keepdims=True,
                    )
                    dgp_ref[fj, 2 * i + i2, h] = jnp.broadcast_to(line, (8, 128))
            dh = dh_raw * gate
            d_up = (dh * a * sig).astype(BF16)
            d_gate = (dh * b * sig * (1.0 + a * (1.0 - sig))).astype(BF16)
            od_ref[fj, l2] = (mm(d_gate, wg, NT) + mm(d_up, wu, NT)).astype(BF16).reshape(shape)
            acc_ref[0] += mm(x, d_gate, TN)
            acc_ref[1] += mm(x, d_up, TN)
            acc_ref[2] += mm(d_exp, hidden, TN)
            return 0

        lax.fori_loop(0, lo // 2, rows_of, 0)
        pltpu.make_async_copy(op_ref.at[fj], op_hbm.at[fj], last_sem.at[fj]).start()

    def to_core(j):
        fj = xor4(at.f, j)
        send(od_ref.at[fj, at.l1], r1_ref.at[fj, 0], d1s.at[fj, 0], d1r.at[fj, 0], core)
        send(od_ref.at[fj, at.l3], r1_ref.at[fj, 1], d1s.at[fj, 1], d1r.at[fj, 1], core)
        send(dgp_ref.at[fj, at.l1], dr1_ref.at[fj, 0], t1s.at[fj, 0], t1r.at[fj, 0], core)
        send(dgp_ref.at[fj, at.l3], dr1_ref.at[fj, 1], t1s.at[fj, 1], t1r.at[fj, 1], core)

    def add(ref, other):
        ref[...] = (ref[...].astype(F32) + other[...].astype(F32)).astype(BF16)

    def to_side(j):
        fj = xor4(at.f, j)
        settle(r1_ref.at[fj, 1], d1r.at[fj, 1])
        add(od_ref.at[fj, at.l2], r1_ref.at[fj, 1])
        send(od_ref.at[fj, at.l2], r2_ref.at[fj], d2s.at[fj], d2r.at[fj], side)
        settle(dr1_ref.at[fj, 1], t1r.at[fj, 1])
        dgp_ref[fj, at.l2] += dr1_ref[fj, 1]
        send(dgp_ref.at[fj, at.l2], dr2_ref.at[fj], t2s.at[fj], t2r.at[fj], side)
        settle(r1_ref.at[fj, 0], d1r.at[fj, 0])
        add(od_ref.at[fj, at.l], r1_ref.at[fj, 0])
        settle(dr1_ref.at[fj, 0], t1r.at[fj, 0])
        dgp_ref[fj, at.l] += dr1_ref[fj, 0]

    def to_home(j):
        fj = xor4(at.f, j)
        settle(r2_ref.at[fj], d2r.at[fj])
        add(od_ref.at[fj, at.l], r2_ref.at[fj])
        settle(dr2_ref.at[fj], t2r.at[fj])
        dgp_ref[fj, at.l] += dr2_ref[fj]
        for hh in range(his):
            hi = flip(at.hi, hh)
            m = fj * his + hi
            rows = od_ref.at[fj, at.l, pl.ds(aligned(hi * MOST, 16), MOST)]
            peer = (hi * lo + at.l, fj)

            line = dgp_ref.at[fj, at.l, hi]

            def away(rows=rows, line=line, peer=peer, m=m):
                send(rows, back_ref.at[at.m], bs.at[m], br.at[at.m], peer)
                send(line, dgb_ref.at[at.m], tbs.at[m], tbr.at[at.m], peer)

            if hh:
                away()
            else:

                @pl.when(j == 0)
                def _(rows=rows, line=line):
                    pltpu.make_async_copy(rows, back_ref.at[at.m], br.at[at.m]).start()
                    pltpu.make_async_copy(line, dgb_ref.at[at.m], tbr.at[at.m]).start()

                pl.when(j > 0)(away)

    take(0)
    take(1)
    settle(g_ref.at[at.l1], gqr.at[0])
    settle(g_ref.at[at.l3], gqr.at[2])
    for f2 in range(ranks):
        for h2 in range(his):
            for w in range(3):
                block = w_ref.at[
                    w, f2 * head_rows : (f2 + 1) * head_rows, h2 * ff : (h2 + 1) * ff
                ]
                settle(block, wr.at[f2 * his + h2, w])

    def step(t, _):
        @pl.when(t < ranks)
        def _():
            pass_on(t)
            compute(t)
            to_core(t)

        @pl.when(t + 2 < ranks)
        def _():
            take(t + 2)

        @pl.when((t >= 1) & (t <= ranks))
        def _():
            to_side(t - 1)

        @pl.when(t >= 2)
        def _():
            to_home(t - 2)

        return 0

    lax.fori_loop(0, ranks + 2, step, 0)

    gw_ref[...] = acc_ref[...].astype(BF16)
    pltpu.make_async_copy(gw_ref, gw_hbm, last_sem.at[4]).start()

    for m in range(E):
        settle(back_ref.at[m], br.at[m])
        settle(dgb_ref.at[m], tbr.at[m])
    pltpu.make_async_copy(back_ref, back_hbm, last_sem.at[5]).start()
    pltpu.make_async_copy(dgb_ref, dgb_hbm, last_sem.at[6]).start()

    for j in range(1, ranks):
        settle(tile_ref, zs.at[j])
    for j in range(ranks):
        for t in range(4):
            settle(tile_ref, ps.at[j, t])
        for t in range(3):
            settle(tile_ref, cs.at[t, j])

    @pl.when(at.f < ranks - 1)
    def _():
        settle(tail, hs)

    for k in range(1, E):
        settle(grow_ref.at[0:MOST], gs.at[k])
        settle(x_ref.at[0:MOST], xs.at[k])
        settle(gates_ref.at[0], ts.at[k])
        for w in range(3):
            settle(w_ref.at[0, 0:head_rows, 0:ff], ws.at[k, w])
    for i in range(3):
        settle(g_ref.at[0], gas.at[i])
    for f2 in range(ranks):
        for i in range(3):
            settle(xb_ref.at[0, 0], qs.at[f2, i])
            settle(gb_ref.at[0, 0], tqs.at[f2, i])
        for i in range(2):
            settle(r1_ref.at[0, 0], d1s.at[f2, i])
            settle(dr1_ref.at[0, 0], t1s.at[f2, i])
        settle(r2_ref.at[0], d2s.at[f2])
        settle(dr2_ref.at[0], t2s.at[f2])
        settle(op_ref.at[0], last_sem.at[f2])
    for j in range(ranks):
        for hh in range(his):
            if j or hh:
                m = at.member(j, hh)[0]
                settle(back_ref.at[0], bs.at[m])
                settle(dgb_ref.at[0], tbs.at[m])
    settle(gw_ref, last_sem.at[4])
    settle(back_ref, last_sem.at[5])
    settle(dgb_ref, last_sem.at[6])
    for i, (name, _, _) in enumerate(KEPT):
        settle(kept[name], keep_sem.at[i])


SMALL_G1 = EXPERTS_ALL
SMALL_VC = SMALL_G1 + 2
SMALL_C = SMALL_VC + CONSTS
COL_POS, COL_C0, COL_C1, COL_R0, COL_R1, COL_W0, COL_W1 = range(16, 23)


def ahead(groups, ranks, *args):
    tok = args[13]
    w_gate = args[15]
    width = tok.shape[1]
    his = E // ranks
    lo = groups // his
    ff = w_gate.shape[2]
    dma = pltpu.SemaphoreType.DMA
    vm = pltpu.VMEM
    any_spec = pl.BlockSpec(memory_space=pl.ANY)
    block = (width // ranks + 8, 4 * (width // groups))
    rows = (his * MOST, width)
    kept = [(kept_shape(dims, width), dtype) for _, dims, dtype in KEPT]
    results = [
        ((ranks, lo) + rows, BF16),
        ((3, width, ff * his), BF16),
        ((E, MOST, width), BF16),
        ((E, 8, 128), F32),
    ]
    return pl.pallas_call(
        ahead_kernel,
        out_shape=[sds(*k) for k in kept + results],
        in_specs=[pl.BlockSpec(memory_space=pltpu.SMEM)] + whole(14) + [any_spec] * 3,
        out_specs=[any_spec] * (len(kept) + len(results)),
        scratch_shapes=[vm(*k) for k in kept]
        + [
            vm(block, BF16),
            vm((128, 128), F32),
            vm((groups, ranks) + block, BF16),
            vm((ROWS, width), BF16),
            vm((ROWS, width), BF16),
            vm((E, 8, 128), F32),
            vm((3, width, ff * his), BF16),
            vm((lo, ranks) + rows, BF16),
            vm((ranks, lo) + rows, BF16),
            vm((ranks, lo, his, 8, 128), F32),
            vm((ranks, lo) + rows, BF16),
            vm((ranks, lo) + rows, BF16),
            vm((ranks, 2) + rows, BF16),
            vm((ranks,) + rows, BF16),
            vm((ranks, lo, his, 8, 128), F32),
            vm((ranks, 2, his, 8, 128), F32),
            vm((ranks, his, 8, 128), F32),
            vm((3, width, ff * his), F32),
            vm((3, width, ff * his), BF16),
            vm((E, MOST, width), BF16),
            vm((E, 8, 128), F32),
            dma((len(kept),)),
            dma((8,)),
            dma((4,)),
            dma((4, 4)),
            dma((3, 4)),
            dma,
            dma((E,)),
            dma((E, 3)),
            dma((3,)),
            dma((groups, ranks)),
            dma,
            dma((E,)),
            dma((E, 3)),
            dma((3,)),
            dma((E,)),
            dma((E,)),
            dma((4, 3)),
            dma((4, 3)),
            dma((4, 2)),
            dma((4, 2)),
            dma((4,)),
            dma((4,)),
            dma((E,)),
            dma((E,)),
            dma((E,)),
            dma((E,)),
            dma((4, 3)),
            dma((4, 3)),
            dma((4, 2)),
            dma((4, 2)),
            dma((4,)),
            dma((4,)),
            dma((E,)),
            dma((E,)),
        ],
        compiler_params=params(63, collective_id=1, has_side_effects=True),
        name="ahead",
    )(*args)


def end_kernel(
    cot_ref,
    tok_ref,
    prev_ref,
    wmix_ref,
    back_hbm,
    dgb_hbm,
    op_hbm,
    gw_hbm,
    *rest,
):
    n = len(KEPT)
    kept_hbm = by_name(rest[:n])
    (
        out_ref,
        dres_ref,
        gprev_ref,
        down_ref,
        back_ref,
        fin_ref,
        gmix_ref,
        t_ref,
    ) = rest[n : n + 8]
    kept = by_name(rest[n + 8 : 2 * n + 8])
    (
        dx_ref,
        dgb_ref,
        opl_ref,
        r1o_ref,
        r2o_ref,
        outb_ref,
        flat_ref,
        dhalo_ref,
        dm_ref,
        dq_ref,
        dk_ref,
        dv_ref,
        dqr_ref,
        dkr_ref,
        dvr_ref,
        full_ref,
        p_ref,
        r1_ref,
        r2_ref,
        r3_ref,
        r4_ref,
        mx_ref,
        mr_ref,
        mz_ref,
        load_sem,
        more_sem,
        o1s,
        o1r,
        o2s,
        o2r,
        obs,
        obr,
        ts,
        tr,
        hs,
        hr,
        s1,
        e1,
        s2,
        e2,
        s3,
        e3,
        s4,
        e4,
        ms,
        me,
        zs,
        ze,
    ) = rest[2 * n + 8 :]
    wf_ref, s_ref, halo_ref, cols_ref = kept["wf"], kept["s"], kept["halo"], kept["cols"]
    q_ref, k_ref, v_ref, n1_ref = kept["q"], kept["k"], kept["v"], kept["n1"]
    mix_ref, lse_ref = kept["mix"], kept["lse"]
    names = [item[0] for item in KEPT]

    def load(*which):
        for name in which:
            pltpu.make_async_copy(
                kept_hbm[name], kept[name], load_sem.at[names.index(name)]
            ).start()

    def ready(*which):
        for name in which:
            settle(kept[name], load_sem.at[names.index(name)])

    ranks = p_ref.shape[1]
    his = E // ranks
    groups = p_ref.shape[0]
    lo = groups // his
    at = Place(his, lo)
    width = cot_ref.shape[1]
    tile = t_ref.shape[2:]
    core = (at.core_peer, at.f)
    side = (at.side_peer, at.f)
    upper = (lo * (1 - at.hi) + at.l, at.f)
    peers = at.others() + [core, side]
    call(peers)
    pltpu.make_async_copy(back_hbm, dx_ref, more_sem.at[0]).start()
    pltpu.make_async_copy(dgb_hbm, dgb_ref, more_sem.at[1]).start()
    load("cols", "s", "resid", "probs", "mix", "wf", "q", "k", "v", "lse")
    for f2 in range(ranks):
        for i, l2 in enumerate((at.l, at.l2)):
            pltpu.make_async_copy(
                op_hbm.at[f2, l2], opl_ref.at[f2, i], more_sem.at[2 + 2 * f2 + i]
            ).start()
    load("cos", "sin", "n1", "inv1", "halo", "part")
    answer(peers)

    for f2 in range(ranks):
        send(op_hbm.at[f2, at.l1], r1o_ref.at[f2, 0], o1s.at[f2, 0], o1r.at[f2, 0], core)
        send(op_hbm.at[f2, at.l3], r1o_ref.at[f2, 1], o1s.at[f2, 1], o1r.at[f2, 1], core)

    for j in range(ranks):
        for hh in range(his):
            e, peer = at.member(j, hh)
            rows = pl.ds(aligned(e // his * tile[0], 16), tile[0])
            lanes_at = pl.ds(aligned(lax.rem(e, his) * tile[1], 128), tile[1])
            n = j * his + hh
            for w in range(3):
                block = gw_hbm.at[w, rows, lanes_at]
                if n == 0:
                    pltpu.make_async_copy(block, t_ref.at[at.m, w], tr.at[at.m, w]).start()
                else:
                    send(block, t_ref.at[at.m, w], ts.at[n, w], tr.at[at.m, w], peer)

    def add(ref, other):
        ref[...] = (ref[...].astype(F32) + other[...].astype(F32)).astype(BF16)

    ready("cols", "s", "resid", "probs")
    settle(dx_ref, more_sem.at[0])
    settle(dgb_ref, more_sem.at[1])
    flat = s_ref[...].T
    gain1 = flat[SMALL_G1 : SMALL_G1 + 1, :]
    gain2 = flat[SMALL_G1 + 1 : SMALL_G1 + 2, :]
    vc = flat[SMALL_VC : SMALL_VC + CONSTS, :]
    g = cot_ref[...].astype(F32)
    lanes = lane_iota(TOK_DEV)
    cols = cols_ref[...]

    def col(i):
        return pick(cols, lanes == i)

    gate0, gate1, gate_id, inv2 = col(0), col(1), col(2), col(3)
    resid = kept["resid"][...]
    unit2 = resid * inv2
    normed = unit2 * gain2
    narrow = normed.astype(BF16)
    c0, c1, r0, r1, wide0, wide1 = (
        col(COL_POS + 1 + i).astype(jnp.int32) for i in range(6)
    )
    slot = lane_iota(TOK_DEV, ROWS)
    hot0 = jnp.where(slot == c0, 1.0, 0.0).astype(BF16)
    hot1 = jnp.where(slot == c1, 1.0, 0.0).astype(BF16)
    dg0 = jnp.zeros((TOK_DEV, 1), F32)
    dg1 = jnp.zeros((TOK_DEV, 1), F32)
    for e in range(E):
        line = jnp.broadcast_to(dgb_ref[e][0:1, :], (TOK_DEV, 128))
        dg0 = dg0 + pick(line, lanes + e * 128 == wide0)
        dg1 = dg1 + pick(line, lanes + e * 128 == wide1)
    a_n = jnp.sum(g * normed, axis=1, keepdims=True)
    dg0 = jnp.where(r0 == E + 1, a_n, dg0)
    dg1 = jnp.where(r1 == E + 1, a_n, dg1)
    g_scale = gate_id
    dl = jnp.zeros((TOK_DEV, 128), F32)
    vmix = jnp.zeros((TOK_DEV, 128), F32)
    for c in range(CONSTS):
        gate_c, ma, mb = col(4 + 3 * c), col(5 + 3 * c), col(6 + 3 * c)
        a_v = jnp.sum(g * vc[c : c + 1, :], axis=1, keepdims=True)
        branch = ma * a_n + mb * a_v
        dg0 = jnp.where(r0 == E + 2 + c, branch, dg0)
        dg1 = jnp.where(r1 == E + 2 + c, branch, dg1)
        g_scale = g_scale + gate_c * ma
        da = gate_c * a_n
        db = gate_c * a_v
        mean = ma * da + mb * db
        dl = jnp.where(lanes == SMALL_C + 2 * c, ma * (da - mean), dl)
        dl = jnp.where(lanes == SMALL_C + 1 + 2 * c, mb * (db - mean), dl)
        vmix = jnp.where(lanes == SMALL_VC + c, gate_c * mb, vmix)
    probs = kept["probs"][...]
    d_probs = jnp.where(lanes == r0, dg0, 0.0) + jnp.where(lanes == r1, dg1, 0.0)
    d_logits = probs * (d_probs - jnp.sum(probs * d_probs, axis=1, keepdims=True))
    dl = jnp.where(lanes < EXPERTS_ALL, d_logits, dl)
    high = dl.astype(BF16)
    low = (dl - high.astype(F32)).astype(BF16)
    wr = s_ref[...].astype(BF16)
    d_normed = g_scale * g + mm(hot0 + hot1, dx_ref[...].reshape(ROWS, width))
    d_normed = d_normed + mm(high, wr, NT) + mm(low, wr, NT)
    vhigh = vmix.astype(BF16)
    vlow = (vmix - vhigh.astype(F32)).astype(BF16)
    tiny = mm(high, narrow, TN) + mm(low, narrow, TN)
    tiny = tiny + mm(vhigh, cot_ref[...], TN) + mm(vlow, cot_ref[...], TN)
    row_id = lax.broadcasted_iota(jnp.int32, (128, width), 0)
    dg2 = jnp.sum(d_normed * unit2, axis=0, keepdims=True)
    flat_ref[...] = jnp.where(row_id == SMALL_G1 + 1, dg2, tiny)
    n = d_normed * gain2
    dres_ref[...] = g + inv2 * (n - unit2 * jnp.mean(n * unit2, axis=1, keepdims=True))
    wmix = jnp.concatenate(
        [wmix_ref[...].astype(F32), jnp.zeros((EXPERTS_ALL, 128 - EXPERTS_ALL), F32)], axis=1
    ).astype(BF16)
    gprev_ref[...] = mm(wmix, high, NT) + mm(wmix, low, NT)
    prev = prev_ref[...]
    phigh = prev.astype(BF16)
    plow = (prev - phigh.astype(F32)).astype(BF16)
    mx_ref[0] = jnp.zeros(mx_ref.shape[1:], F32)
    mx_ref[0, 0:EXPERTS_ALL, :] = mm(phigh, high) + mm(phigh, low) + mm(plow, high)
    send(mx_ref.at[0], mr_ref.at[0], ms.at[0], me.at[0], core)

    for f2 in range(ranks):
        settle(opl_ref.at[f2, 1], more_sem.at[3 + 2 * f2])
        settle(r1o_ref.at[f2, 1], o1r.at[f2, 1])
        add(opl_ref.at[f2, 1], r1o_ref.at[f2, 1])
        send(opl_ref.at[f2, 1], r2o_ref.at[f2], o2s.at[f2], o2r.at[f2], side)
        settle(opl_ref.at[f2, 0], more_sem.at[2 + 2 * f2])
        settle(r1o_ref.at[f2, 0], o1r.at[f2, 0])
        add(opl_ref.at[f2, 0], r1o_ref.at[f2, 0])

    ready("mix", "wf", "q", "k", "v", "lse")
    scale = HEAD_DIM ** (-0.5)
    d_attn = dres_ref[...].astype(BF16)
    full_ref[3] = mm(mix_ref[...], d_attn, TN).astype(BF16)
    dm_ref[...] = mm(d_attn, wf_ref[3], NT).astype(BF16)
    dk_ref[...] = jnp.zeros_like(dk_ref)
    dv_ref[...] = jnp.zeros_like(dv_ref)

    def pair(p, _):
        span = pl.ds(pl.multiple_of(p * 128, 128), 128)
        for first, count in QBLOCKS:
            keys = key_span(first)
            ok = allowed_mask(cols_ref, first, count, COL_POS)[:, :keys]
            q = q_ref[pl.ds(first, count), span]
            dm = dm_ref[pl.ds(first, count), span]
            k = k_ref[pl.ds(first, keys), span]
            v = v_ref[pl.ds(first, keys), span]
            lane = lane_iota(count)
            key_lane = lane_iota(keys)
            lse = lse_ref[pl.ds(first, count), :]
            dq = dk = dv = None
            for h in range(2):
                mine = (lane < HEAD_DIM) if h == 0 else (lane >= HEAD_DIM)
                key_mine = (key_lane < HEAD_DIM) if h == 0 else (key_lane >= HEAD_DIM)
                qh = jnp.where(mine, q, jnp.zeros_like(q))
                dmh = jnp.where(mine, dm, jnp.zeros_like(dm))
                s = jnp.where(ok, mm(qh, k, NT) * scale, NEG)
                pr = jnp.where(ok, jnp.exp(s - pick(lse, lane == 2 * p + h)), 0.0)
                dp = mm(dmh, v, NT)
                delta = jnp.sum(pr * dp, axis=1, keepdims=True)
                ds = (pr * (dp - delta)).astype(BF16)
                pb = pr.astype(BF16)
                dqh = mm(ds, k)
                dkh = mm(ds, q, TN)
                dvh = mm(pb, dm, TN)
                dq = dqh if h == 0 else jnp.where(mine, dqh, dq)
                dk = dkh if h == 0 else jnp.where(key_mine, dkh, dk)
                dv = dvh if h == 0 else jnp.where(key_mine, dvh, dv)
            dq_ref[pl.ds(first, count), span] = dq * scale
            dk_ref[pl.ds(first, keys), span] += dk * scale
            dv_ref[pl.ds(first, keys), span] += dv

        @pl.when(p == 2)
        def _():
            for j in range(ranks):
                fj = xor4(at.f, j)
                settle(r2o_ref.at[fj], o2r.at[fj])
                add(opl_ref.at[fj, 0], r2o_ref.at[fj])
                for hh in range(his):
                    m, peer = at.member(j, hh)
                    hi = flip(at.hi, hh)
                    rows = opl_ref.at[fj, 0, pl.ds(aligned(hi * MOST, 16), MOST)]
                    if j or hh:
                        send(rows, outb_ref.at[at.m], obs.at[m], obr.at[at.m], peer)
                    else:
                        pltpu.make_async_copy(rows, outb_ref.at[at.m], obr.at[at.m]).start()

        return 0

    lax.fori_loop(0, HEADS // 2, pair, 0)

    ready("cos", "sin", "n1", "inv1", "halo", "part")

    def unturn(i, _):
        span = pl.ds(pl.multiple_of(i * 256, 256), 256)
        cos = kept["cos"][...]
        sin = kept["sin"][...]
        dqr_ref[:, span] = turn(dq_ref[:, span], cos[HALO:], -sin[HALO:]).astype(BF16)
        dkr_ref[:, span] = turn(dk_ref[:, span], cos, -sin).astype(BF16)
        dvr_ref[:, span] = dv_ref[:, span].astype(BF16)
        return 0

    lax.fori_loop(0, width // 256, unturn, 0)
    d_all = mm(dkr_ref[...], wf_ref[1], NT) + mm(dvr_ref[...], wf_ref[2], NT)
    dhalo_ref[...] = (d_all[:HALO] * gain1).astype(BF16)

    @pl.when(at.f > 0)
    def _():
        send(dhalo_ref, back_ref, hs, hr, (at.g, at.f - 1))

    @pl.when(at.f == ranks - 1)
    def _():
        back_ref[...] = jnp.zeros_like(back_ref)

    full_ref[0] = mm(n1_ref[HALO:, :], dqr_ref[...], TN).astype(BF16)
    full_ref[1] = mm(n1_ref[...], dkr_ref[...], TN).astype(BF16)
    full_ref[2] = mm(n1_ref[...], dvr_ref[...], TN).astype(BF16)
    d_own = d_all[HALO:] + mm(dqr_ref[...], wf_ref[0], NT)
    inv1 = kept["inv1"][:, 0:1]
    unit_own = tok_ref[...].astype(F32) * inv1[HALO:]
    unit_halo = halo_ref[...].astype(F32) * inv1[:HALO]
    dg1 = jnp.sum(d_own * unit_own, axis=0, keepdims=True) + jnp.sum(
        d_all[:HALO] * unit_halo, axis=0, keepdims=True
    )
    down_ref[...] = d_own * gain1
    flat_ref[...] = jnp.where(row_id == SMALL_G1, dg1, flat_ref[...])

    part_cols = width // groups
    head_rows = width // ranks

    def pack(f2, _):
        rows = pl.ds(aligned(f2 * head_rows, 16), head_rows)
        for g2 in range(groups):
            pieces = [
                full_ref[w, rows, g2 * part_cols : (g2 + 1) * part_cols] for w in range(4)
            ]
            p_ref[g2, f2, 0:head_rows, :] = jnp.concatenate(pieces, axis=1)
        return 0

    lax.fori_loop(0, ranks, pack, 0)
    column = flat_ref[...].T
    per = width // (groups * ranks)
    for g2 in range(groups):
        for f2 in range(ranks):
            base = (g2 * ranks + f2) * per
            pieces = [column[base + 8 * i : base + 8 * i + 8, :] for i in range(per // 8)]
            p_ref[g2, f2, head_rows : head_rows + 8, :] = jnp.concatenate(
                pieces, axis=1
            ).astype(BF16)

    c = lax.rem(at.g, 2)
    x = lax.rem(at.g // 2, 2)
    y = at.hi

    def block(y2, x2, c2):
        return (y2 * 2 + x2) * 2 + c2

    half = ranks // 2
    quads = [(1 - y, 1 - x), (y, 1 - x), (1 - y, x), (y, x)]
    for i, (y2, x2) in enumerate(quads):
        spot = y2 * 2 + x2
        send(p_ref.at[block(y2, x2, 1 - c)], r1_ref.at[spot], s1.at[i], e1.at[spot], core)
    settle(mr_ref.at[0], me.at[0])
    mx_ref[1] = mx_ref[0] + mr_ref[0]
    send(mx_ref.at[1], mr_ref.at[1], ms.at[1], me.at[1], side)
    for i, (y2, x2) in enumerate(quads):
        spot = y2 * 2 + x2
        settle(r1_ref.at[spot], e1.at[spot])
        add(p_ref.at[block(y2, x2, c)], r1_ref.at[spot])
        if i == 0:
            here = p_ref.at[block(1 - y, 1 - x, c)]
            send(here.at[0:half], r2_ref.at[0, 1 - y], s2.at[0, 0], e2.at[0, 1 - y], side)
            send(here.at[half:], r2_ref.at[1, 1 - x], s2.at[1, 0], e2.at[1, 1 - x], upper)
        if i == 1:
            here = p_ref.at[block(y, 1 - x, c)]
            send(here.at[0:half], r2_ref.at[0, y], s2.at[0, 1], e2.at[0, y], side)
        if i == 2:
            here = p_ref.at[block(1 - y, x, c)]
            send(here.at[half:], r2_ref.at[1, x], s2.at[1, 1], e2.at[1, x], upper)
    settle(mr_ref.at[1], me.at[1])
    mx_ref[2] = mx_ref[1] + mr_ref[1]
    send(mx_ref.at[2], mr_ref.at[2], ms.at[2], me.at[2], upper)
    settle(r2_ref.at[0, 1 - y], e2.at[0, 1 - y])
    add(p_ref.at[block(1 - y, x, c), 0:half], r2_ref.at[0, 1 - y])
    send(
        p_ref.at[block(1 - y, x, c), 0:half], r3_ref.at[0], s3.at[0], e3.at[0], upper
    )
    settle(r2_ref.at[1, 1 - x], e2.at[1, 1 - x])
    add(p_ref.at[block(y, 1 - x, c), half:], r2_ref.at[1, 1 - x])
    send(p_ref.at[block(y, 1 - x, c), half:], r3_ref.at[1], s3.at[1], e3.at[1], side)
    settle(r2_ref.at[0, y], e2.at[0, y])
    add(p_ref.at[at.g, 0:half], r2_ref.at[0, y])
    settle(r2_ref.at[1, x], e2.at[1, x])
    add(p_ref.at[at.g, half:], r2_ref.at[1, x])
    settle(mr_ref.at[2], me.at[2])
    mx_ref[3] = mx_ref[2] + mr_ref[2]
    mz_ref[at.f] = mx_ref[3]
    for i in range(2):
        settle(r3_ref.at[i], e3.at[i])
        add(p_ref.at[at.g, i * half : (i + 1) * half], r3_ref.at[i])
    for j in range(1, ranks):
        f2 = xor4(at.f, j)
        send(p_ref.at[at.g, f2], r4_ref.at[at.f], s4.at[j], e4.at[at.f], (at.g, f2))
        send(mx_ref.at[3], mz_ref.at[at.f], zs.at[j], ze.at[at.f], (at.g, f2))
    for m in range(E):
        settle(outb_ref.at[m], obr.at[m])
    rows = outb_ref[...].reshape(ROWS, width)
    cols = cols_ref[...]
    c0 = pick(cols, lanes == COL_C0).astype(jnp.int32)
    c1 = pick(cols, lanes == COL_C1).astype(jnp.int32)
    y0 = mm(jnp.where(slot == c0, 1.0, 0.0).astype(BF16), rows)
    y1 = mm(jnp.where(slot == c1, 1.0, 0.0).astype(BF16), rows)
    gate0 = pick(cols, lanes == 0)
    gate1 = pick(cols, lanes == 1)
    out_ref[...] = (kept["part"][...] + gate0 * y0 + gate1 * y1).astype(BF16)

    total = p_ref[at.g, at.f].astype(F32)
    for j in range(1, ranks):
        f2 = xor4(at.f, j)
        settle(r4_ref.at[f2], e4.at[f2])
        total = total + r4_ref[f2].astype(F32)
        settle(mz_ref.at[f2], ze.at[f2])
    fin_ref[...] = total
    gmix_ref[...] = (mz_ref[0] + mz_ref[1]) + (mz_ref[2] + mz_ref[3])

    for f2 in range(ranks):
        for i in range(2):
            settle(r1o_ref.at[0, 0], o1s.at[f2, i])
        settle(r2o_ref.at[0], o2s.at[f2])
    for j in range(ranks):
        for hh in range(his):
            if j or hh:
                settle(outb_ref.at[0], obs.at[at.member(j, hh)[0]])
    for m in range(E):
        for w in range(3):
            settle(t_ref.at[m, w], tr.at[m, w])
    for i in range(1, E):
        for w in range(3):
            settle(t_ref.at[0, w], ts.at[i, w])

    @pl.when(at.f > 0)
    def _():
        settle(dhalo_ref, hs)

    @pl.when(at.f < ranks - 1)
    def _():
        settle(back_ref, hr)

    for i in range(4):
        settle(r1_ref.at[0], s1.at[i])
    for i in range(2):
        for n2 in range(2):
            settle(r2_ref.at[0, 0], s2.at[i, n2])
        settle(r3_ref.at[0], s3.at[i])
    for i in range(3):
        settle(mr_ref.at[0], ms.at[i])
    for j in range(1, ranks):
        settle(r4_ref.at[0], s4.at[j])
        settle(mz_ref.at[0], zs.at[j])


def end(groups, ranks, tile, *args):
    cot = args[0]
    width = cot.shape[1]
    dma = pltpu.SemaphoreType.DMA
    vm = pltpu.VMEM
    block = (width // ranks + 8, 4 * (width // groups))
    half = ranks // 2
    rows = (E // ranks * MOST, width)
    kept = [(kept_shape(dims, width), dtype) for _, dims, dtype in KEPT]
    any_spec = pl.BlockSpec(memory_space=pl.ANY)
    return pl.pallas_call(
        end_kernel,
        out_shape=[
            sds((TOK_DEV, width), BF16),
            sds((TOK_DEV, width), F32),
            sds((EXPERTS_ALL, TOK_DEV), F32),
            sds((TOK_DEV, width), F32),
            sds((HALO, width), BF16),
            sds(block, F32),
            sds((16, 128), F32),
            sds((E, 3) + tile, BF16),
        ],
        in_specs=whole(4) + [any_spec] * (4 + len(kept)),
        out_specs=whole(7) + [any_spec],
        scratch_shapes=[vm(*k) for k in kept]
        + [
            vm((E, MOST, width), BF16),
            vm((E, 8, 128), F32),
            vm((ranks, 2) + rows, BF16),
            vm((ranks, 2) + rows, BF16),
            vm((ranks,) + rows, BF16),
            vm((E, MOST, width), BF16),
            vm((128, width), F32),
            vm((HALO, width), BF16),
            vm((TOK_DEV, width), BF16),
            vm((TOK_DEV, width), F32),
            vm((KEYS, width), F32),
            vm((KEYS, width), F32),
            vm((TOK_DEV, width), BF16),
            vm((KEYS, width), BF16),
            vm((KEYS, width), BF16),
            vm((4, width, width), BF16),
            vm((groups, ranks) + block, BF16),
            vm((4, ranks) + block, BF16),
            vm((2, 2, half) + block, BF16),
            vm((2, half) + block, BF16),
            vm((ranks,) + block, BF16),
            vm((4, 16, 128), F32),
            vm((3, 16, 128), F32),
            vm((ranks, 16, 128), F32),
            dma((len(kept),)),
            dma((2 + 2 * ranks,)),
            dma((ranks, 2)),
            dma((ranks, 2)),
            dma((ranks,)),
            dma((ranks,)),
            dma((E,)),
            dma((E,)),
            dma((E, 3)),
            dma((E, 3)),
            dma,
            dma,
            dma((4,)),
            dma((4,)),
            dma((2, 2)),
            dma((2, 2)),
            dma((2,)),
            dma((2,)),
            dma((4,)),
            dma((4,)),
            dma((3,)),
            dma((3,)),
            dma((4,)),
            dma((4,)),
        ],
        compiler_params=params(63, collective_id=3, has_side_effects=True),
        name="end",
    )(*args)


def store_kernel(
    t_ref,
    fin_ref,
    dres_ref,
    down_ref,
    back_ref,
    tok_ref,
    inv1_ref,
    gate_ref,
    up_ref,
    downw_ref,
    gq_ref,
    gk_ref,
    gv_ref,
    go_ref,
    router_ref,
    const_ref,
    vconst_ref,
    gain1_ref,
    gain2_ref,
    gtok_ref,
):
    for e in range(E):
        gate_ref[e] = t_ref[e, 0].astype(F32)
        up_ref[e] = t_ref[e, 1].astype(F32)
        downw_ref[e] = t_ref[e, 2].astype(F32)
    head_rows, part_cols = gq_ref.shape
    for w, ref in enumerate((gq_ref, gk_ref, gv_ref, go_ref)):
        ref[...] = fin_ref[0:head_rows, w * part_cols : (w + 1) * part_cols]
    per = router_ref.shape[1]
    column = jnp.concatenate(
        [
            fin_ref[head_rows : head_rows + 8, 128 * i : 128 * i + 128]
            for i in range(per // 8)
        ]
        + [jnp.zeros((128 - per, 128), F32)],
        axis=0,
    )
    flat = column.T[:, 0:per]
    router_ref[...] = flat[0:EXPERTS_ALL]
    gain1_ref[...] = flat[SMALL_G1 : SMALL_G1 + 1]
    gain2_ref[...] = flat[SMALL_G1 + 1 : SMALL_G1 + 2]
    vconst_ref[...] = flat[SMALL_VC : SMALL_VC + CONSTS]
    const_ref[...] = flat[SMALL_C : SMALL_C + 2 * CONSTS]
    width = tok_ref.shape[1]
    inv1 = inv1_ref[HALO:, 0:1]
    unit = tok_ref[...].astype(F32) * inv1
    m = jnp.concatenate(
        [down_ref[: TOK_DEV - HALO, :], down_ref[TOK_DEV - HALO :, :] + back_ref[...]], axis=0
    )
    d_dealt = inv1 * (m - unit * jnp.mean(m * unit, axis=1, keepdims=True))
    gtok_ref[...] = dres_ref[...] + d_dealt.astype(BF16).astype(F32)


def store(t, fin, dres, down, back, tok, inv1, groups, ranks):
    width = tok.shape[1]
    rows, cols = t.shape[2:]
    per = width // (groups * ranks)
    return pl.pallas_call(
        store_kernel,
        out_shape=[sds((E, rows, cols), F32)] * 3
        + [sds((width // ranks, width // groups), F32)] * 4
        + [
            sds((EXPERTS_ALL, per), F32),
            sds((2 * CONSTS, per), F32),
            sds((CONSTS, per), F32),
            sds((1, per), F32),
            sds((1, per), F32),
            sds(tok.shape, F32),
        ],
        in_specs=whole(7),
        out_specs=whole(13),
        compiler_params=params(48),
        name="store",
    )(t, fin, dres, down, back, tok, inv1)


def fast_device(
    tokens,
    cotangent,
    prev_logits,
    lengths,
    dealing,
    routes,
    gain_one,
    w_query,
    w_key,
    w_value,
    w_out,
    gain_two,
    w_router,
    w_mix,
    w_const,
    v_const,
    w_gate,
    w_up,
    w_down,
):
    groups = lax.axis_size("grp")
    ranks = lax.axis_size("fsdp")
    kept = len(KEPT)
    prev = prev_logits.T
    outs = ahead(
        groups,
        ranks,
        lengths,
        routes.T,
        prev,
        w_mix,
        w_router.T,
        gain_one[None, :],
        gain_two[None, :],
        w_const.T,
        v_const.T,
        w_query,
        w_key,
        w_value,
        w_out,
        tokens,
        cotangent,
        w_gate,
        w_up,
        w_down.transpose(0, 2, 1),
    )
    parts, grads, dx, routed = outs[kept:]
    output, dres, gprev, down, back, fin, gmix, tiles = end(
        groups,
        ranks,
        w_gate.shape[1:],
        cotangent,
        tokens,
        prev,
        w_mix,
        dx,
        routed,
        parts,
        grads,
        *outs[:kept],
    )
    inv1 = by_name(outs[:kept])["inv1"]
    gate, up, downw, gq, gk, gv, go, router, const, vconst, gain1, gain2, grad_tokens = store(
        tiles, fin, dres, down, back, tokens, inv1, groups, ranks
    )
    return (
        output,
        grad_tokens,
        gprev.T,
        gain1[0],
        gq,
        gk,
        gv,
        go,
        gain2[0],
        router.T,
        gmix[:EXPERTS_ALL, :EXPERTS_ALL],
        const.T,
        vconst.T,
        gate,
        up,
        downw.transpose(0, 2, 1),
    )


def suits(mesh):
    return mesh.shape["fsdp"] == 4 and mesh.shape["grp"] == 8


def solution(mesh):
    return jax.shard_map(
        fast_device if suits(mesh) else per_device,
        mesh=mesh,
        in_specs=(
            P(("grp", "fsdp"), None),
            P(("grp", "fsdp"), None),
            P(("grp", "fsdp"), None),
            P("grp", None),
            P("grp", None),
            P(("grp", "fsdp"), None),
            P(("grp", "fsdp")),
            P("fsdp", "grp"),
            P("fsdp", "grp"),
            P("fsdp", "grp"),
            P("fsdp", "grp"),
            P(("grp", "fsdp")),
            P(("grp", "fsdp"), None),
            P(),
            P(("grp", "fsdp"), None),
            P(("grp", "fsdp"), None),
            P(None, "fsdp", "grp"),
            P(None, "fsdp", "grp"),
            P(None, "grp", "fsdp"),
        ),
        out_specs=(
            P(("grp", "fsdp"), None),
            P(("grp", "fsdp"), None),
            P(("grp", "fsdp"), None),
            P(("grp", "fsdp")),
            P("fsdp", "grp"),
            P("fsdp", "grp"),
            P("fsdp", "grp"),
            P("fsdp", "grp"),
            P(("grp", "fsdp")),
            P(("grp", "fsdp"), None),
            P(),
            P(("grp", "fsdp"), None),
            P(("grp", "fsdp"), None),
            P(None, "fsdp", "grp"),
            P(None, "fsdp", "grp"),
            P(None, "grp", "fsdp"),
        ),
        check_vma=False,
    )
```

```python
import math

import jax
import jax.numpy as jnp
from jax import lax
from jax.experimental import pallas as pl
from jax.experimental.pallas import tpu as pltpu
from jax.sharding import PartitionSpec as P

HEADS = 12
HEAD_DIM = 64
E = 8
CONSTS = 2
BLOCK = 128
EXPERTS_ALL = 12
CAP = 384
TOK_DEV = 320
MOST = 80


NORM_EPS = 1e-05
EXACT = lax.Precision.HIGHEST


def rotation_tables(positions, head_dim):
    half_dim = head_dim // 2
    inv_freq = jnp.exp(
        jnp.arange(half_dim, dtype=jnp.float32) * (-2.0 * math.log(10000.0) / head_dim)
    )
    angles = positions.astype(jnp.float32)[:, None] * inv_freq[None, :]
    return (jnp.cos(angles), jnp.sin(angles))


def rotate(values, cos_table, sin_table):
    row_count = values.shape[0]
    half_dim = cos_table.shape[1]
    heads_view = values.reshape(row_count, -1, 2 * half_dim)
    front_half = heads_view[:, :, :half_dim]
    back_half = heads_view[:, :, half_dim:]
    cos_view = cos_table[:, None, :]
    sin_view = sin_table[:, None, :]
    turned = jnp.concatenate(
        [
            front_half * cos_view - back_half * sin_view,
            back_half * cos_view + front_half * sin_view,
        ],
        axis=2,
    )
    return turned.reshape(row_count, -1)


def exact_dot(left_side, right_side):
    return jnp.dot(left_side, right_side, precision=EXACT, preferred_element_type=jnp.float32)


def per_device(
    tokens,
    cotangent,
    prev_logits,
    lengths,
    dealing,
    routes,
    gain_one,
    w_query,
    w_key,
    w_value,
    w_out,
    gain_two,
    w_router,
    w_mix,
    w_const,
    v_const,
    w_gate,
    w_up,
    w_down,
):
    groups = lax.axis_size("grp")
    dealers = lax.axis_size("fsdp")
    device = lax.axis_index("fsdp")
    model_width = tokens.shape[1]
    per_shard = model_width // (groups * dealers)
    pairs = HEADS // 2
    pair_width = 2 * HEAD_DIM
    scale = HEAD_DIM ** (-0.5)
    seq_len = lengths[0]
    deal_order = dealing[0]
    seq_count = seq_len.shape[0]
    seq_ids = jnp.arange(seq_count, dtype=jnp.int32)
    seq_ends = jnp.cumsum(seq_len)
    starts = seq_ends - seq_len
    padded = (seq_len + BLOCK - 1) // BLOCK * BLOCK
    order_hot = (deal_order[:, None] == seq_ids[None, :]).astype(jnp.int32)
    dealt_len = jnp.sum(order_hot * seq_len[None, :], axis=1)
    dealt_pad = jnp.sum(order_hot * padded[None, :], axis=1)
    dealt_start = jnp.sum(order_hot * starts[None, :], axis=1)
    slot_of = jnp.sum(order_hot * seq_ids[:, None], axis=0)
    pair_index = 2 * device
    row_ids = jnp.arange(CAP, dtype=jnp.int32)
    in_second = row_ids >= dealt_pad[pair_index]
    position = row_ids - jnp.where(in_second, dealt_pad[pair_index], 0)
    seq_limit = jnp.where(in_second, dealt_len[pair_index + 1], dealt_len[pair_index])
    live_rows = position < seq_limit
    source = jnp.where(in_second, dealt_start[pair_index + 1], dealt_start[pair_index]) + position
    source = jnp.where(live_rows, source, -1)
    given_rows = device * TOK_DEV + jnp.arange(TOK_DEV, dtype=jnp.int32)
    seq_hot = (
        (given_rows[:, None] >= starts[None, :]) & (given_rows[:, None] < seq_ends[None, :])
    ).astype(jnp.int32)
    offset_in = given_rows - jnp.sum(seq_hot * starts[None, :], axis=1)
    slot_rank = jnp.sum(seq_hot * slot_of[None, :], axis=1)
    is_second = slot_rank % 2
    lead_pad = jnp.take(dealt_pad, slot_rank - is_second)
    target = slot_rank // 2 * CAP + jnp.where(is_second == 1, lead_pad, 0) + offset_in

    def deal(values):
        shard_rows = lax.all_gather(values, "fsdp", axis=0, tiled=True)
        row_span = shard_rows.shape[0]
        inside = (source >= 0) & (source < row_span)
        taken_rows = jnp.take(shard_rows, jnp.clip(source, 0, row_span - 1), axis=0)
        return jnp.where(inside[:, None], taken_rows, jnp.zeros((CAP, model_width), jnp.bfloat16))

    def give_back(values):
        shard_rows = lax.all_gather(values, "fsdp", axis=0, tiled=True)
        row_span = shard_rows.shape[0]
        inside = (target >= 0) & (target < row_span)
        taken_rows = jnp.take(shard_rows, jnp.clip(target, 0, row_span - 1), axis=0)
        return jnp.where(
            inside[:, None], taken_rows, jnp.zeros((TOK_DEV, model_width), jnp.bfloat16)
        )

    def collect():
        gate_in, up_in, down_in = (w_gate, w_up, w_down)
        sectioned = (
            lax.all_gather(gain_one, "fsdp", axis=0, tiled=True),
            lax.all_gather(w_query, "fsdp", axis=0, tiled=True),
            lax.all_gather(w_key, "fsdp", axis=0, tiled=True),
            lax.all_gather(w_value, "fsdp", axis=0, tiled=True),
            lax.all_gather(w_out, "fsdp", axis=0, tiled=True),
            lax.all_gather(gain_two, "fsdp", axis=0, tiled=True),
            lax.all_gather(w_router, "fsdp", axis=0, tiled=True),
            lax.all_gather(w_const, "fsdp", axis=0, tiled=True),
            lax.all_gather(v_const, "fsdp", axis=0, tiled=True),
            lax.all_gather(gate_in, "fsdp", axis=1, tiled=True),
            lax.all_gather(up_in, "fsdp", axis=1, tiled=True),
            lax.all_gather(down_in, "fsdp", axis=2, tiled=True),
        )
        (
            part_g1,
            part_q,
            part_k,
            part_v,
            part_o,
            part_g2,
            part_r,
            part_c,
            part_vc,
            part_gate,
            part_up,
            part_down,
        ) = sectioned
        small = (
            lax.all_gather(part_g1, "grp", axis=0, tiled=True),
            lax.all_gather(part_q, "grp", axis=1, tiled=True),
            lax.all_gather(part_k, "grp", axis=1, tiled=True),
            lax.all_gather(part_v, "grp", axis=1, tiled=True),
            lax.all_gather(part_o, "grp", axis=1, tiled=True),
            lax.all_gather(part_g2, "grp", axis=0, tiled=True),
            lax.all_gather(part_r, "grp", axis=0, tiled=True),
            lax.all_gather(part_c, "grp", axis=0, tiled=True),
            lax.all_gather(part_vc, "grp", axis=0, tiled=True),
        )
        experts = (
            lax.all_gather(part_gate, "grp", axis=2, tiled=True),
            lax.all_gather(part_up, "grp", axis=2, tiled=True),
            lax.all_gather(part_down, "grp", axis=1, tiled=True),
        )
        return tuple(small) + tuple(experts)

    (
        gain1,
        weight_q,
        weight_k,
        weight_v,
        weight_o,
        gain2,
        router,
        wconst,
        vconst,
        wgate,
        wup,
        wdown,
    ) = collect()
    dealt = deal(tokens)
    dealt_f = dealt.astype(jnp.float32)
    inv_one = lax.rsqrt(jnp.mean(dealt_f * dealt_f, axis=1, keepdims=True) + NORM_EPS)
    unit_one = dealt_f * inv_one
    gain1_f = gain1.astype(jnp.float32)
    normed_one = (unit_one * gain1_f).astype(jnp.bfloat16)
    cos_table, sin_table = rotation_tables(position, HEAD_DIM)
    query = rotate(
        jnp.dot(normed_one, weight_q, preferred_element_type=jnp.float32), cos_table, sin_table
    ).astype(jnp.bfloat16)
    keyed = rotate(
        jnp.dot(normed_one, weight_k, preferred_element_type=jnp.float32), cos_table, sin_table
    ).astype(jnp.bfloat16)
    values_proj = jnp.dot(normed_one, weight_v, preferred_element_type=jnp.float32).astype(
        jnp.bfloat16
    )
    allowed = (
        (in_second[:, None] == in_second[None, :])
        & (position[None, :] <= position[:, None])
        & live_rows[None, :]
    )

    def by_pairs(values):
        return values.reshape(CAP, pairs, pair_width).transpose(1, 0, 2)

    def from_pairs(values):
        return values.transpose(1, 0, 2).reshape(CAP, model_width)

    def pair_scores(q_pair, k_pair):
        query_heads = q_pair.reshape(CAP, 2, HEAD_DIM)
        key_heads = k_pair.reshape(CAP, 2, HEAD_DIM)
        scores = (
            jnp.einsum("qhd,khd->hqk", query_heads, key_heads, preferred_element_type=jnp.float32)
            * scale
        )
        return (jnp.where(allowed[None], scores, -1e30), query_heads, key_heads)

    def attend(pair_items):
        q_pair, k_pair, v_pair = pair_items
        scores, query_heads, key_heads = pair_scores(q_pair, k_pair)
        row_top = jnp.max(scores, axis=-1, keepdims=True)
        weights_exp = jnp.exp(scores - row_top)
        row_total = jnp.sum(weights_exp, axis=-1, keepdims=True)
        attn_probs = weights_exp / row_total
        value_heads = v_pair.reshape(CAP, 2, HEAD_DIM)
        mixed_pair = jnp.einsum(
            "hqk,khd->qhd",
            attn_probs.astype(jnp.bfloat16),
            value_heads,
            preferred_element_type=jnp.float32,
        )
        return (mixed_pair.reshape(CAP, pair_width), (row_top + jnp.log(row_total))[:, :, 0])

    mixed_pairs, log_sums = lax.map(
        attend, (by_pairs(query), by_pairs(keyed), by_pairs(values_proj))
    )
    mixed = from_pairs(mixed_pairs).astype(jnp.bfloat16)
    attn_out = jnp.dot(mixed, weight_o, preferred_element_type=jnp.float32).astype(jnp.bfloat16)
    returned = give_back(attn_out)
    resid = tokens.astype(jnp.float32) + returned.astype(jnp.float32)
    inv_two = lax.rsqrt(jnp.mean(resid * resid, axis=1, keepdims=True) + NORM_EPS)
    unit_two = resid * inv_two
    gain2_f = gain2.astype(jnp.float32)
    normed = unit_two * gain2_f
    narrow = normed.astype(jnp.bfloat16)
    mix_f = w_mix.astype(jnp.float32)
    router_f = router.astype(jnp.float32)
    wconst_f = wconst.astype(jnp.float32)
    logits = jnp.dot(narrow, router, preferred_element_type=jnp.float32) + exact_dot(
        prev_logits, mix_f
    )
    logit_top = jnp.max(logits, axis=1, keepdims=True)
    logit_exp = jnp.exp(logits - logit_top)
    route_probs = logit_exp / jnp.sum(logit_exp, axis=1, keepdims=True)
    expert_ids = jnp.arange(EXPERTS_ALL, dtype=jnp.int32)
    chosen = (
        (routes[:, 0:1] == expert_ids[None, :]) | (routes[:, 1:2] == expert_ids[None, :])
    ).astype(jnp.float32)
    gate_weights = route_probs * chosen
    result = resid + gate_weights[:, E + 1 : E + 2] * normed
    const_logits = jnp.dot(narrow, wconst, preferred_element_type=jnp.float32)
    vconst_f = vconst.astype(jnp.float32)
    const_mixes = []
    const_branches = []
    for const_idx in range(CONSTS):
        part_logits = const_logits[:, 2 * const_idx : 2 * const_idx + 2]
        part_exp = jnp.exp(part_logits - jnp.max(part_logits, axis=1, keepdims=True))
        const_mix = part_exp / jnp.sum(part_exp, axis=1, keepdims=True)
        branch = const_mix[:, 0:1] * normed + const_mix[:, 1:2] * vconst_f[:, const_idx][None, :]
        const_mixes.append(const_mix)
        const_branches.append(branch)
        result = result + gate_weights[:, E + 2 + const_idx : E + 3 + const_idx] * branch
    slot_list = []
    filled_list = []
    slot_gate_list = []
    for expert in range(E):
        member = (routes[:, 0] == expert) | (routes[:, 1] == expert)
        place_at = jnp.cumsum(member.astype(jnp.int32)) - 1
        slot_table = (
            jnp.zeros((MOST,), jnp.int32)
            .at[jnp.where(member, place_at, MOST)]
            .set(jnp.arange(TOK_DEV, dtype=jnp.int32), mode="drop")
        )
        filled = jnp.arange(MOST, dtype=jnp.int32) < jnp.sum(member.astype(jnp.int32))
        slot_list.append(slot_table)
        filled_list.append(filled)
        slot_gate_list.append(jnp.where(filled, jnp.take(gate_weights[:, expert], slot_table), 0.0))
    slot_tables = jnp.stack(slot_list, axis=0)
    filled_all = jnp.stack(filled_list, axis=0)
    slot_gates = jnp.stack(slot_gate_list, axis=0)
    expert_kept = []
    out_list = []
    for expert in range(E):
        picked = jnp.take(narrow, slot_tables[expert], axis=0)
        gate_part = jnp.dot(picked, wgate[expert], preferred_element_type=jnp.float32)
        up_part = jnp.dot(picked, wup[expert], preferred_element_type=jnp.float32)
        hidden = (jax.nn.silu(gate_part) * up_part).astype(jnp.bfloat16)
        out_list.append(jnp.dot(hidden, wdown[expert], preferred_element_type=jnp.float32))
        expert_kept.append((picked, gate_part, up_part, hidden))
    expert_outs = jnp.stack(out_list, axis=0)
    for expert in range(E):
        result = result.at[slot_tables[expert]].add(
            slot_gates[expert][:, None] * expert_outs[expert]
        )
    output = result.astype(jnp.bfloat16)
    (
        gain1,
        weight_q,
        weight_k,
        weight_v,
        weight_o,
        gain2,
        router,
        wconst,
        vconst,
        wgate,
        wup,
        wdown,
    ) = collect()
    gain1_f = gain1.astype(jnp.float32)
    gain2_f = gain2.astype(jnp.float32)
    router_f = router.astype(jnp.float32)
    wconst_f = wconst.astype(jnp.float32)
    vconst_f = vconst.astype(jnp.float32)
    grad_out = cotangent.astype(jnp.float32)
    d_gate_cols = [jnp.zeros((TOK_DEV,), jnp.float32) for expert in range(EXPERTS_ALL)]
    d_gate_cols[E + 1] = jnp.sum(grad_out * normed, axis=1)
    d_normed = gate_weights[:, E + 1 : E + 2] * grad_out
    d_const_parts = []
    d_vconst_cols = []
    for const_idx in range(CONSTS):
        const_mix = const_mixes[const_idx]
        gate_col = gate_weights[:, E + 2 + const_idx]
        d_gate_cols[E + 2 + const_idx] = jnp.sum(grad_out * const_branches[const_idx], axis=1)
        d_piece = gate_col[:, None] * grad_out
        d_normed = d_normed + const_mix[:, 0:1] * d_piece
        d_cmix = jnp.stack(
            [
                jnp.sum(d_piece * normed, axis=1),
                jnp.sum(d_piece * vconst_f[:, const_idx][None, :], axis=1),
            ],
            axis=1,
        )
        d_const_parts.append(
            const_mix * (d_cmix - jnp.sum(const_mix * d_cmix, axis=1, keepdims=True))
        )
        d_vconst_cols.append(exact_dot(const_mix[:, 1] * gate_col, grad_out))
    d_const_logits = jnp.concatenate(d_const_parts, axis=1)
    grad_rows_all = jnp.take(grad_out, slot_tables.reshape(-1), axis=0).reshape(
        E, MOST, model_width
    )
    d_slot_gates = jnp.where(filled_all, jnp.sum(grad_rows_all * expert_outs, axis=2), 0.0)
    for expert in range(E):
        d_gate_cols[expert] = (
            jnp.zeros((TOK_DEV,), jnp.float32).at[slot_tables[expert]].add(d_slot_gates[expert])
        )
    d_expert_all = (slot_gates[:, :, None] * grad_rows_all).astype(jnp.bfloat16)
    d_wgate_list = []
    d_wup_list = []
    d_wdown_list = []
    d_picked_list = []
    for expert in range(E):
        picked, gate_part, up_part, hidden = expert_kept[expert]
        d_expert = d_expert_all[expert]
        d_wdown_list.append(jnp.dot(hidden.T, d_expert, preferred_element_type=jnp.float32))
        d_hidden = jnp.dot(d_expert, wdown[expert].T, preferred_element_type=jnp.float32)
        sigmoid_g = jax.nn.sigmoid(gate_part)
        d_up_part = (d_hidden * gate_part * sigmoid_g).astype(jnp.bfloat16)
        d_gate_part = (
            d_hidden * up_part * sigmoid_g * (1.0 + gate_part * (1.0 - sigmoid_g))
        ).astype(jnp.bfloat16)
        d_wgate_list.append(jnp.dot(picked.T, d_gate_part, preferred_element_type=jnp.float32))
        d_wup_list.append(jnp.dot(picked.T, d_up_part, preferred_element_type=jnp.float32))
        d_picked_list.append(
            jnp.dot(d_gate_part, wgate[expert].T, preferred_element_type=jnp.float32)
            + jnp.dot(d_up_part, wup[expert].T, preferred_element_type=jnp.float32)
        )
    d_picked_all = jnp.stack(d_picked_list, axis=0)
    d_wgate_full = jnp.stack(d_wgate_list, axis=0)
    d_wup_full = jnp.stack(d_wup_list, axis=0)
    d_wdown_full = jnp.stack(d_wdown_list, axis=0)
    d_narrow = jnp.zeros((TOK_DEV, model_width), jnp.float32)
    for expert in range(E):
        d_narrow = d_narrow.at[slot_tables[expert]].add(
            jnp.where(filled_all[expert][:, None], d_picked_all[expert], 0.0)
        )
    d_gate_w = jnp.stack(d_gate_cols, axis=1)
    d_probs = d_gate_w * chosen
    d_logits = route_probs * (d_probs - jnp.sum(route_probs * d_probs, axis=1, keepdims=True))
    narrow_f = narrow.astype(jnp.float32)
    d_narrow = d_narrow + exact_dot(d_logits, router_f.T) + exact_dot(d_const_logits, wconst_f.T)
    d_router_full = exact_dot(narrow_f.T, d_logits)
    d_wconst_full = exact_dot(narrow_f.T, d_const_logits)
    d_vconst_full = jnp.stack(d_vconst_cols, axis=1)
    d_mix_full = exact_dot(prev_logits.T, d_logits)
    grad_prev = exact_dot(d_logits, mix_f.T)
    d_normed_total = d_normed + d_narrow
    d_gain2_full = jnp.sum(d_normed_total * unit_two, axis=0)
    d_unit_two = d_normed_total * gain2_f
    d_resid = grad_out + inv_two * (
        d_unit_two - unit_two * jnp.mean(d_unit_two * unit_two, axis=1, keepdims=True)
    )
    d_attn = deal(d_resid.astype(jnp.bfloat16))
    d_wo_full = jnp.dot(mixed.T, d_attn, preferred_element_type=jnp.float32)
    d_mixed = jnp.dot(d_attn, weight_o.T, preferred_element_type=jnp.float32).astype(jnp.bfloat16)

    def attend_back(pair_items):
        q_pair, k_pair, v_pair, dm_pair, lse_pair = pair_items
        scores, query_heads, key_heads = pair_scores(q_pair, k_pair)
        attn_probs = jnp.where(allowed[None], jnp.exp(scores - lse_pair[:, :, None]), 0.0)
        value_heads = v_pair.reshape(CAP, 2, HEAD_DIM)
        dm_heads = dm_pair.reshape(CAP, 2, HEAD_DIM)
        d_p = jnp.einsum("qhd,khd->hqk", dm_heads, value_heads, preferred_element_type=jnp.float32)
        row_delta = jnp.sum(attn_probs * d_p, axis=-1, keepdims=True)
        d_scores = (attn_probs * (d_p - row_delta)).astype(jnp.bfloat16)
        d_q = (
            jnp.einsum("hqk,khd->qhd", d_scores, key_heads, preferred_element_type=jnp.float32)
            * scale
        )
        d_k = (
            jnp.einsum("hqk,qhd->khd", d_scores, query_heads, preferred_element_type=jnp.float32)
            * scale
        )
        d_v = jnp.einsum(
            "hqk,qhd->khd",
            attn_probs.astype(jnp.bfloat16),
            dm_heads,
            preferred_element_type=jnp.float32,
        )
        return (
            d_q.reshape(CAP, pair_width),
            d_k.reshape(CAP, pair_width),
            d_v.reshape(CAP, pair_width),
        )

    dq_pairs, dk_pairs, dv_pairs = lax.map(
        attend_back,
        (by_pairs(query), by_pairs(keyed), by_pairs(values_proj), by_pairs(d_mixed), log_sums),
    )
    d_query = rotate(from_pairs(dq_pairs), cos_table, -sin_table).astype(jnp.bfloat16)
    d_key = rotate(from_pairs(dk_pairs), cos_table, -sin_table).astype(jnp.bfloat16)
    d_value = from_pairs(dv_pairs).astype(jnp.bfloat16)
    d_wq_full = jnp.dot(normed_one.T, d_query, preferred_element_type=jnp.float32)
    d_wk_full = jnp.dot(normed_one.T, d_key, preferred_element_type=jnp.float32)
    d_wv_full = jnp.dot(normed_one.T, d_value, preferred_element_type=jnp.float32)
    d_normed_one = (
        jnp.dot(d_query, weight_q.T, preferred_element_type=jnp.float32)
        + jnp.dot(d_key, weight_k.T, preferred_element_type=jnp.float32)
        + jnp.dot(d_value, weight_v.T, preferred_element_type=jnp.float32)
    )
    d_gain1_full = jnp.sum(d_normed_one * unit_one, axis=0)
    d_unit_one = d_normed_one * gain1_f
    d_dealt = (
        inv_one * (d_unit_one - unit_one * jnp.mean(d_unit_one * unit_one, axis=1, keepdims=True))
    ).astype(jnp.bfloat16)
    grad_tokens = d_resid + give_back(d_dealt).astype(jnp.float32)

    def regroup(grads_in):
        tail_shape = grads_in.shape[1:]
        split_view = grads_in.reshape((groups, dealers, per_shard) + tail_shape)
        return jnp.swapaxes(split_view, 0, 1).reshape((model_width,) + tail_shape)

    mix_tile = jnp.broadcast_to(d_mix_full[None], (dealers, EXPERTS_ALL, EXPERTS_ALL))
    sectioned = (
        lax.psum_scatter(
            regroup(d_gain1_full).astype(jnp.bfloat16), "fsdp", scatter_dimension=0, tiled=True
        ).astype(jnp.float32),
        lax.psum_scatter(
            d_wq_full.astype(jnp.bfloat16), "fsdp", scatter_dimension=0, tiled=True
        ).astype(jnp.float32),
        lax.psum_scatter(
            d_wk_full.astype(jnp.bfloat16), "fsdp", scatter_dimension=0, tiled=True
        ).astype(jnp.float32),
        lax.psum_scatter(
            d_wv_full.astype(jnp.bfloat16), "fsdp", scatter_dimension=0, tiled=True
        ).astype(jnp.float32),
        lax.psum_scatter(
            d_wo_full.astype(jnp.bfloat16), "fsdp", scatter_dimension=0, tiled=True
        ).astype(jnp.float32),
        lax.psum_scatter(
            regroup(d_gain2_full).astype(jnp.bfloat16), "fsdp", scatter_dimension=0, tiled=True
        ).astype(jnp.float32),
        lax.psum_scatter(
            regroup(d_router_full).astype(jnp.bfloat16), "fsdp", scatter_dimension=0, tiled=True
        ).astype(jnp.float32),
        lax.psum_scatter(
            regroup(d_wconst_full).astype(jnp.bfloat16), "fsdp", scatter_dimension=0, tiled=True
        ).astype(jnp.float32),
        lax.psum_scatter(
            regroup(d_vconst_full).astype(jnp.bfloat16), "fsdp", scatter_dimension=0, tiled=True
        ).astype(jnp.float32),
        lax.psum_scatter(
            mix_tile.astype(jnp.bfloat16), "fsdp", scatter_dimension=0, tiled=True
        ).astype(jnp.float32),
        lax.psum_scatter(
            d_wgate_full.astype(jnp.bfloat16), "fsdp", scatter_dimension=1, tiled=True
        ).astype(jnp.float32),
        lax.psum_scatter(
            d_wup_full.astype(jnp.bfloat16), "fsdp", scatter_dimension=1, tiled=True
        ).astype(jnp.float32),
        lax.psum_scatter(
            d_wdown_full.astype(jnp.bfloat16), "fsdp", scatter_dimension=2, tiled=True
        ).astype(jnp.float32),
    )
    s_g1, s_q, s_k, s_v, s_o, s_g2, s_r, s_c, s_vc, s_mix, s_gate, s_up, s_down = sectioned
    summed = (
        lax.psum_scatter(s_g1.astype(jnp.bfloat16), "grp", scatter_dimension=0, tiled=True).astype(
            jnp.float32
        ),
        lax.psum_scatter(s_q.astype(jnp.bfloat16), "grp", scatter_dimension=1, tiled=True).astype(
            jnp.float32
        ),
        lax.psum_scatter(s_k.astype(jnp.bfloat16), "grp", scatter_dimension=1, tiled=True).astype(
            jnp.float32
        ),
        lax.psum_scatter(s_v.astype(jnp.bfloat16), "grp", scatter_dimension=1, tiled=True).astype(
            jnp.float32
        ),
        lax.psum_scatter(s_o.astype(jnp.bfloat16), "grp", scatter_dimension=1, tiled=True).astype(
            jnp.float32
        ),
        lax.psum_scatter(s_g2.astype(jnp.bfloat16), "grp", scatter_dimension=0, tiled=True).astype(
            jnp.float32
        ),
        lax.psum_scatter(s_r.astype(jnp.bfloat16), "grp", scatter_dimension=0, tiled=True).astype(
            jnp.float32
        ),
        lax.psum_scatter(s_c.astype(jnp.bfloat16), "grp", scatter_dimension=0, tiled=True).astype(
            jnp.float32
        ),
        lax.psum_scatter(s_vc.astype(jnp.bfloat16), "grp", scatter_dimension=0, tiled=True).astype(
            jnp.float32
        ),
        lax.psum_scatter(
            jnp.broadcast_to(s_mix, (groups, EXPERTS_ALL, EXPERTS_ALL)).astype(jnp.bfloat16),
            "grp",
            scatter_dimension=0,
            tiled=True,
        ).astype(jnp.float32),
    )
    (
        grad_gain_one,
        grad_query,
        grad_key,
        grad_value,
        grad_out_proj,
        grad_gain_two,
        grad_router,
        grad_const,
        grad_vconst,
        mix_part,
    ) = summed
    grad_mix = mix_part[0]
    grad_gate, grad_up, grad_down = (
        lax.psum_scatter(
            s_gate.astype(jnp.bfloat16), "grp", scatter_dimension=2, tiled=True
        ).astype(jnp.float32),
        lax.psum_scatter(s_up.astype(jnp.bfloat16), "grp", scatter_dimension=2, tiled=True).astype(
            jnp.float32
        ),
        lax.psum_scatter(
            s_down.astype(jnp.bfloat16), "grp", scatter_dimension=1, tiled=True
        ).astype(jnp.float32),
    )
    return (
        output,
        grad_tokens,
        grad_prev,
        grad_gain_one,
        grad_query,
        grad_key,
        grad_value,
        grad_out_proj,
        grad_gain_two,
        grad_router,
        grad_mix,
        grad_const,
        grad_vconst,
        grad_gate,
        grad_up,
        grad_down,
    )


HALO = 256
KEYS = HALO + TOK_DEV
ROWS = E * MOST
NEG = -1e30
F32 = jnp.float32
BF16 = jnp.bfloat16
NT = (((1,), (1,)), ((), ()))
TN = (((0,), (0,)), ((), ()))
NN = (((1,), (0,)), ((), ()))


def mm(a, b, dims=NN):
    return lax.dot_general(a, b, dims, preferred_element_type=F32)


def lane_iota(rows, width=128):
    return lax.broadcasted_iota(jnp.int32, (rows, width), 1)


def pick(values, lane_mask):
    return jnp.sum(jnp.where(lane_mask, values, 0.0), axis=1, keepdims=True)


def params(mb, **kw):
    return pltpu.CompilerParams(vmem_limit_bytes=mb << 20, **kw)


def whole(count):
    return [pl.BlockSpec(memory_space=pltpu.VMEM) for _ in range(count)]


def sds(shape, dtype):
    return jax.ShapeDtypeStruct(shape, dtype)


MESH_ID = pl.DeviceIdType.MESH


def send(src, dst, send_sem, recv_sem, device):
    pltpu.make_async_remote_copy(
        src_ref=src,
        dst_ref=dst,
        send_sem=send_sem,
        recv_sem=recv_sem,
        device_id=device,
        device_id_type=MESH_ID,
    ).start()


def settle(ref, sem):
    pltpu.make_async_copy(ref, ref, sem).wait()


def flip(a, b):
    return a + b - 2 * a * b


def xor4(a, b):
    return flip(a // 2, b // 2) * 2 + flip(lax.rem(a, 2), lax.rem(b, 2))


def aligned(value, to):
    return pl.multiple_of(value, to)


class Place:
    def __init__(self, his, lo):
        self.g = lax.axis_index("grp")
        self.f = lax.axis_index("fsdp")
        self.his, self.lo = his, lo
        self.hi = self.g // lo
        self.l = lax.rem(self.g, lo)
        self.m = self.f * his + self.hi
        core = lax.rem(self.g, 2)
        side = lax.rem(self.g // 2, 2)
        self.core_peer = self.g + 1 - 2 * core
        self.side_peer = self.g + 2 - 4 * side
        self.l1 = lax.rem(self.core_peer, lo)
        self.l2 = lax.rem(self.side_peer, lo)
        self.l3 = lo - 1 - self.l

    def member(self, j, hh):
        f = xor4(self.f, j)
        hi = flip(self.hi, hh)
        return f * self.his + hi, (hi * self.lo + self.l, f)

    def others(self):
        peers = []
        for j in range(4):
            for hh in range(self.his):
                if j or hh:
                    peers.append(self.member(j, hh)[1])
        return peers


def call(peers):
    barrier = pltpu.get_barrier_semaphore()
    for peer in peers:
        pl.semaphore_signal(barrier, inc=1, device_id=peer, device_id_type=MESH_ID)


def answer(peers):
    pl.semaphore_wait(pltpu.get_barrier_semaphore(), len(peers))


def turn(values, cos, sin):
    half = HEAD_DIM // 2
    width = values.shape[1]
    reps = width // 128
    front = lax.rem(lane_iota(values.shape[0], width), HEAD_DIM) < half
    swapped = jnp.where(
        front, pltpu.roll(values, width - half, 1), pltpu.roll(values, half, 1)
    )
    cos_w = jnp.concatenate([cos] * reps, axis=1)
    sin_w = jnp.concatenate([sin] * reps, axis=1)
    return values * cos_w + swapped * sin_w


QBLOCKS = [(0, 128), (128, 128), (256, 64)]


def allowed_mask(pos_ref, first, count, lane):
    ii = lax.broadcasted_iota(jnp.int32, (count, 384), 0) + HALO
    jj = lax.broadcasted_iota(jnp.int32, (count, 384), 1)
    pos = pos_ref[pl.ds(first, count), lane : lane + 1].astype(jnp.int32)
    return (jj <= ii) & (jj >= ii - pos)


def key_span(first):
    return min(384, KEYS - first)


KEPT = (
    ("wf", (4, None, None), BF16),
    ("s", (None, 128), F32),
    ("halo", (HALO, None), BF16),
    ("q", (TOK_DEV, None), BF16),
    ("k", (KEYS, None), BF16),
    ("v", (KEYS, None), BF16),
    ("n1", (KEYS, None), BF16),
    ("inv1", (KEYS, 128), F32),
    ("mix", (TOK_DEV, None), BF16),
    ("lse", (TOK_DEV, 128), F32),
    ("resid", (TOK_DEV, None), F32),
    ("part", (TOK_DEV, None), F32),
    ("probs", (TOK_DEV, 128), F32),
    ("cols", (TOK_DEV, 128), F32),
    ("cos", (KEYS, 128), F32),
    ("sin", (KEYS, 128), F32),
)


def kept_shape(dims, width):
    return tuple(width if d is None else d for d in dims)


def by_name(refs):
    return {name: ref for (name, _, _), ref in zip(KEPT, refs)}


def token_places(len_ref, at):
    row = lax.broadcasted_iota(jnp.int32, (KEYS, 128), 0) + (at.f * TOK_DEV - HALO)
    first = jnp.zeros((KEYS, 128), jnp.int32)
    reached = jnp.int32(0)
    for i in range(len_ref.shape[1]):
        reached = reached + len_ref[0, i]
        first = jnp.where(row >= reached, reached, first)
    return jnp.maximum(row - first, 0)


def ahead_kernel(
    len_ref,
    routes_ref,
    prev_ref,
    wmix_ref,
    router_ref,
    gain1_ref,
    gain2_ref,
    const_ref,
    vconst_ref,
    wq_ref,
    wk_ref,
    wv_ref,
    wo_ref,
    tok_ref,
    cot_ref,
    wg_hbm,
    wu_hbm,
    wd_hbm,
    *rest,
):
    n = len(KEPT)
    kept_hbm = by_name(rest[:n])
    op_hbm, gw_hbm, back_hbm, dgb_hbm = rest[n : n + 4]
    kept = by_name(rest[n + 4 : 2 * n + 4])
    (
        tile_ref,
        small_ref,
        p_ref,
        grow_ref,
        x_ref,
        gates_ref,
        wgu_ref,
        wd_ref,
        g_ref,
        xb_ref,
        gb_ref,
        od_ref,
        op_ref,
        r1_ref,
        r2_ref,
        dgp_ref,
        dr1_ref,
        dr2_ref,
        accgu_ref,
        accd_ref,
        hid_ref,
        dgu_ref,
        gw_ref,
        back_ref,
        dgb_ref,
        keep_sem,
        last_sem,
        zs,
        ps,
        cs,
        hs,
        gs,
        ws,
        gas,
        agr,
        hr,
        gr,
        wr,
        gqr,
        xs,
        ts,
        qs,
        tqs,
        d1s,
        t1s,
        d2s,
        t2s,
        bs,
        tbs,
        xr,
        tr,
        qr,
        tqr,
        d1r,
        t1r,
        d2r,
        t2r,
        br,
        tbr,
    ) = rest[2 * n + 4 :]
    wf_ref, s_ref, halo_ref = kept["wf"], kept["s"], kept["halo"]
    q_ref, k_ref, v_ref, n1_ref = kept["q"], kept["k"], kept["v"], kept["n1"]
    mix_ref, lse_ref = kept["mix"], kept["lse"]
    lo, ranks = g_ref.shape[:2]
    his = E // ranks
    at = Place(his, lo)
    width = tok_ref.shape[1]
    head_rows, part_cols = wq_ref.shape
    ff = wg_hbm.shape[2]
    diag = lo * (1 - at.hi) + at.l2
    upper = lo * (1 - at.hi) + at.l
    near = [(at.core_peer, at.f), (at.side_peer, at.f), (upper, at.f), (diag, at.f)]
    core, side = near[0], near[1]
    peers = at.others() + [near[0], near[1], near[3]]
    call(peers)

    def keep(*names):
        for name in names:
            i = [k[0] for k in KEPT].index(name)
            pltpu.make_async_copy(kept[name], kept_hbm[name], keep_sem.at[i]).start()

    tile_ref[0:head_rows, :] = jnp.concatenate(
        [wq_ref[...], wk_ref[...], wv_ref[...], wo_ref[...]], axis=1
    )
    small_ref[...] = jnp.zeros_like(small_ref)
    per = router_ref.shape[1]
    small_ref[0:EXPERTS_ALL, 0:per] = router_ref[...].astype(F32)
    small_ref[SMALL_G1 : SMALL_G1 + 1, 0:per] = gain1_ref[...].astype(F32)
    small_ref[SMALL_G1 + 1 : SMALL_G1 + 2, 0:per] = gain2_ref[...].astype(F32)
    small_ref[SMALL_VC : SMALL_VC + CONSTS, 0:per] = vconst_ref[...].astype(F32)
    small_ref[SMALL_C : SMALL_C + 2 * CONSTS, 0:per] = const_ref[...].astype(F32)
    turned = small_ref[...].T
    tile_ref[head_rows : head_rows + 8, :] = jnp.concatenate(
        [turned[8 * i : 8 * i + 8, :] for i in range(per // 8)], axis=1
    ).astype(BF16)
    answer(peers)

    p_ref[at.g, at.f] = tile_ref[...]
    for j in range(1, ranks):
        f2 = xor4(at.f, j)
        send(tile_ref, p_ref.at[at.g, at.f], zs.at[j], agr.at[at.g, at.f], (at.g, f2))

    def spread(j, f2, src):
        for t, peer in enumerate(near):
            send(src, p_ref.at[at.g, f2], ps.at[j, t], agr.at[at.g, f2], peer)

    spread(0, at.f, tile_ref)
    halo_rows = halo_ref.shape[0]
    tail = tok_ref.at[pl.ds(tok_ref.shape[0] - halo_rows, halo_rows)]

    @pl.when(at.f < ranks - 1)
    def _():
        send(tail, halo_ref, hs, hr, (at.g, at.f + 1))

    @pl.when(at.f == 0)
    def _():
        halo_ref[...] = jnp.zeros_like(halo_ref)

    lanes = lane_iota(TOK_DEV)
    routes = jnp.concatenate(
        [
            jnp.broadcast_to(routes_ref[0:1, :], (8, TOK_DEV)),
            jnp.broadcast_to(routes_ref[1:2, :], (8, TOK_DEV)),
        ],
        axis=0,
    ).T
    r0 = routes[:, 0:1]
    r1 = routes[:, 8:9]
    hot0 = lanes == r0
    hot1 = lanes == r1
    named = jnp.where(hot0 | hot1, 1.0, 0.0).astype(BF16)
    earlier = (
        lax.broadcasted_iota(jnp.int32, (TOK_DEV, TOK_DEV), 1)
        < lax.broadcasted_iota(jnp.int32, (TOK_DEV, TOK_DEV), 0)
    )
    rank = mm(jnp.where(earlier, 1.0, 0.0).astype(BF16), named)
    rank0 = pick(rank, hot0).astype(jnp.int32)
    rank1 = pick(rank, hot1).astype(jnp.int32)
    c0 = jnp.where(r0 < E, r0 * MOST + rank0, -1)
    c1 = jnp.where(r1 < E, r1 * MOST + rank1, -1)
    slot = lane_iota(TOK_DEV, ROWS)
    spots0 = jnp.where(slot == c0, 1.0, 0.0).astype(BF16)
    spots1 = jnp.where(slot == c1, 1.0, 0.0).astype(BF16)
    grow_ref[...] = mm(spots0 + spots1, cot_ref[...], TN).astype(BF16)

    for j in range(1, ranks):
        f2 = xor4(at.f, j)
        settle(p_ref.at[at.g, f2], agr.at[at.g, f2])
        spread(j, f2, p_ref.at[at.g, f2])

    own_rows = pl.ds(aligned(at.f * head_rows, 16), head_rows)
    own_cols = pl.ds(aligned(at.hi * ff, 128), ff)
    own_spot = pl.ds(aligned(at.hi * MOST, 16), MOST)

    for j in range(ranks):
        for hh in range(his):
            e, peer = at.member(j, hh)
            rows = grow_ref.at[pl.ds(aligned(e * MOST, 16), MOST)]
            spot = g_ref.at[at.l, at.f, own_spot]
            if j == 0 and hh == 0:
                pltpu.make_async_copy(rows, spot, gr.at[at.m]).start()
            else:
                send(rows, spot, gs.at[j * his + hh], gr.at[at.m], peer)

    def dispatch():
        for j in range(ranks):
            for hh in range(his):
                e, peer = at.member(j, hh)
                sources = (wg_hbm.at[e], wu_hbm.at[e], wd_hbm.at[e])
                for w in range(3):
                    first = aligned(w * his * ff + at.hi * ff, 128)
                    spot = (
                        wd_ref.at[own_rows, own_cols]
                        if w == 2
                        else wgu_ref.at[own_rows, pl.ds(first, ff)]
                    )
                    if j == 0 and hh == 0:
                        pltpu.make_async_copy(sources[w], spot, wr.at[at.m, w]).start()
                    else:
                        send(sources[w], spot, ws.at[j * his + hh, w], wr.at[at.m, w], peer)

    pos = token_places(len_ref, at).astype(F32)
    half_dim = HEAD_DIM // 2
    lane_k = lane_iota(KEYS)
    freq = jnp.exp(
        lax.rem(lane_k, half_dim).astype(F32) * (-2.0 * math.log(10000.0) / HEAD_DIM)
    )
    kept["cos"][...] = jnp.cos(pos * freq)
    sine = jnp.sin(pos * freq)
    kept["sin"][...] = jnp.where(lax.rem(lane_k, HEAD_DIM) < half_dim, -sine, sine)
    pos_own = pos[HALO:]
    pos_ref = kept["cols"]
    pos_ref[...] = pos_own

    for j in range(ranks):
        f2 = xor4(at.f, j)
        for t in range(1, 4):
            g2 = near[t][0]
            settle(p_ref.at[g2, f2], agr.at[g2, f2])
            send(p_ref.at[g2, f2], p_ref.at[g2, f2], cs.at[t - 1, j], agr.at[g2, f2], near[0])
    sibling_upper = lo * (1 - at.hi) + at.l1
    for j in range(ranks):
        f2 = xor4(at.f, j)
        for g2 in (
            at.core_peer,
            at.hi * lo + at.l3,
            sibling_upper,
            lo * (1 - at.hi) + at.l3,
        ):
            settle(p_ref.at[g2, f2], agr.at[g2, f2])

    dispatch()

    groups = p_ref.shape[0]
    for g2 in range(groups):
        for f2 in range(ranks):
            piece = p_ref[g2, f2, head_rows : head_rows + 8, :].astype(F32)
            for i in range(per // 8):
                base = (g2 * ranks + f2) * per + 8 * i
                s_ref[base : base + 8, :] = piece[:, 128 * i : 128 * i + 128]

    def lay(f2, _):
        rows = pl.ds(aligned(f2 * head_rows, 16), head_rows)
        for w in range(4):
            for half in range(2):
                pieces = [
                    p_ref[
                        half * (groups // 2) + i,
                        f2,
                        0:head_rows,
                        w * part_cols : (w + 1) * part_cols,
                    ]
                    for i in range(groups // 2)
                ]
                wf_ref[w, rows, half * (width // 2) : (half + 1) * (width // 2)] = (
                    jnp.concatenate(pieces, axis=1)
                )
        return 0

    lax.fori_loop(0, ranks, lay, 0)

    @pl.when(at.f > 0)
    def _():
        settle(halo_ref, hr)

    scale = HEAD_DIM ** (-0.5)
    flat = s_ref[...].T
    g1 = flat[SMALL_G1 : SMALL_G1 + 1, :]
    g2 = flat[SMALL_G1 + 1 : SMALL_G1 + 2, :]
    vc = flat[SMALL_VC : SMALL_VC + CONSTS, :]
    keep("wf", "s", "halo")
    rows = jnp.concatenate([halo_ref[...], tok_ref[...]], axis=0).astype(F32)
    inv1 = lax.rsqrt(jnp.mean(rows * rows, axis=1, keepdims=True) + NORM_EPS)
    kept["inv1"][...] = jnp.broadcast_to(inv1, (KEYS, 128))
    n1_ref[...] = (rows * inv1 * g1).astype(BF16)

    def project(i, _):
        span = pl.ds(pl.multiple_of(i * 256, 256), 256)
        cos = kept["cos"][...]
        sin = kept["sin"][...]
        q = mm(n1_ref[HALO:, :], wf_ref[0, :, span])
        q_ref[:, span] = turn(q, cos[HALO:], sin[HALO:]).astype(BF16)
        k = mm(n1_ref[...], wf_ref[1, :, span])
        k_ref[:, span] = turn(k, cos, sin).astype(BF16)
        v_ref[:, span] = mm(n1_ref[...], wf_ref[2, :, span]).astype(BF16)
        return 0

    lax.fori_loop(0, width // 256, project, 0)
    keep("q", "k", "v", "n1", "inv1", "cos", "sin")
    lse_ref[...] = jnp.zeros((TOK_DEV, 128), F32)

    for f2 in range(ranks):
        for h2 in range(his):
            settle(
                g_ref.at[at.l, f2, h2 * MOST : (h2 + 1) * MOST], gr.at[f2 * his + h2]
            )
    send(g_ref.at[at.l], g_ref.at[at.l], gas.at[0], gqr.at[0], near[0])
    send(g_ref.at[at.l], g_ref.at[at.l], gas.at[1], gqr.at[1], near[1])

    def pair(p, _):
        span = pl.ds(pl.multiple_of(p * 128, 128), 128)
        for first, count in QBLOCKS:
            keys = key_span(first)
            ok = allowed_mask(pos_ref, first, count, 0)[:, :keys]
            q = q_ref[pl.ds(first, count), span]
            k = k_ref[pl.ds(first, keys), span]
            v = v_ref[pl.ds(first, keys), span]
            lane = lane_iota(count)
            out = None
            lse = lse_ref[pl.ds(first, count), :]
            for h in range(2):
                mine = (lane < HEAD_DIM) if h == 0 else (lane >= HEAD_DIM)
                qh = jnp.where(mine, q, jnp.zeros_like(q))
                sc = jnp.where(ok, mm(qh, k, NT) * scale, NEG)
                top = jnp.max(sc, axis=1, keepdims=True)
                ex = jnp.exp(sc - top)
                total = jnp.sum(ex, axis=1, keepdims=True)
                o = mm((ex / total).astype(BF16), v)
                out = o if h == 0 else jnp.where(mine, o, out)
                lse = jnp.where(lane == 2 * p + h, top + jnp.log(total), lse)
            mix_ref[pl.ds(first, count), span] = out.astype(BF16)
            lse_ref[pl.ds(first, count), :] = lse
        return 0

    lax.fori_loop(0, HEADS // 2, pair, 0)
    settle(g_ref.at[at.l2], gqr.at[1])
    send(g_ref.at[at.l2], g_ref.at[at.l2], gas.at[2], gqr.at[2], near[0])

    attn_out = mm(mix_ref[...], wf_ref[3]).astype(BF16)
    resid = tok_ref[...].astype(F32) + attn_out.astype(F32)
    kept["resid"][...] = resid
    inv2 = lax.rsqrt(jnp.mean(resid * resid, axis=1, keepdims=True) + NORM_EPS)
    normed = resid * inv2 * g2
    narrow = normed.astype(BF16)
    raw = mm(narrow, s_ref[...].astype(BF16))
    prev = prev_ref[...]
    wmix = jnp.concatenate(
        [wmix_ref[...].astype(F32), jnp.zeros((EXPERTS_ALL, 128 - EXPERTS_ALL), F32)], axis=1
    ).astype(BF16)
    phigh = prev.astype(BF16)
    prest = prev - phigh.astype(F32)
    pmid = prest.astype(BF16)
    plow = (prest - pmid.astype(F32)).astype(BF16)
    mixed_prev = mm(phigh, wmix, TN) + (mm(pmid, wmix, TN) + mm(plow, wmix, TN))
    logits = jnp.where(lanes < EXPERTS_ALL, raw + mixed_prev, NEG)
    top = jnp.max(logits, axis=1, keepdims=True)
    ex = jnp.exp(logits - top)
    probs = ex / jnp.sum(ex, axis=1, keepdims=True)
    kept["probs"][...] = probs
    gate0 = pick(probs, hot0)
    gate1 = pick(probs, hot1)

    def gate_of(expert):
        return jnp.where(r0 == expert, gate0, 0.0) + jnp.where(r1 == expert, gate1, 0.0)

    gate_id = gate_of(E + 1)
    part = resid + gate_id * normed
    cols = jnp.where(lanes == 0, gate0, 0.0)
    cols = jnp.where(lanes == 1, gate1, cols)
    cols = jnp.where(lanes == 2, gate_id, cols)
    cols = jnp.where(lanes == 3, inv2, cols)
    for c in range(CONSTS):
        la = pick(raw, lanes == SMALL_C + 2 * c)
        lb = pick(raw, lanes == SMALL_C + 1 + 2 * c)
        big = jnp.maximum(la, lb)
        ea = jnp.exp(la - big)
        eb = jnp.exp(lb - big)
        ma = ea / (ea + eb)
        mb = eb / (ea + eb)
        gate_c = gate_of(E + 2 + c)
        part = part + gate_c * (ma * normed + mb * vc[c : c + 1, :])
        cols = jnp.where(lanes == 4 + 3 * c, gate_c, cols)
        cols = jnp.where(lanes == 5 + 3 * c, ma, cols)
        cols = jnp.where(lanes == 6 + 3 * c, mb, cols)
    kept["part"][...] = part
    wide0 = jnp.where(r0 < E, r0 * 128 + rank0, -1)
    wide1 = jnp.where(r1 < E, r1 * 128 + rank1, -1)
    more = (pos_own[:, 0:1], c0, c1, r0, r1, wide0, wide1)
    for i, value in enumerate(more):
        cols = jnp.where(lanes == COL_POS + i, value.astype(F32), cols)
    kept["cols"][...] = cols
    keep("mix", "lse", "resid", "part", "probs", "cols")
    x_ref[...] = mm(spots0 + spots1, narrow, TN).astype(BF16)
    for e in range(E):
        lane = lanes + e * 128
        row = jnp.sum(
            jnp.where(lane == wide0, gate0, 0.0) + jnp.where(lane == wide1, gate1, 0.0),
            axis=0,
            keepdims=True,
        )
        gates_ref[e] = jnp.broadcast_to(row, (8, 128))


    def give(j):
        for hh in range(his):
            e, peer = at.member(j, hh)
            k = j * his + hh
            rows = x_ref.at[pl.ds(aligned(e * MOST, 16), MOST)]
            spot = xb_ref.at[at.f, at.l, own_spot]
            line = gb_ref.at[at.f, at.l, at.hi]
            if k == 0:
                pltpu.make_async_copy(rows, spot, xr.at[at.m]).start()
                pltpu.make_async_copy(gates_ref.at[e], line, tr.at[at.m]).start()
            else:
                send(rows, spot, xs.at[k], xr.at[at.m], peer)
                send(gates_ref.at[e], line, ts.at[k], tr.at[at.m], peer)

    give(0)
    give(1)
    accgu_ref[...] = jnp.zeros_like(accgu_ref)
    accd_ref[...] = jnp.zeros_like(accd_ref)

    def take(j):
        fj = xor4(at.f, j)
        for hh in range(his):
            hi = flip(at.hi, hh)
            m = fj * his + hi
            settle(xb_ref.at[fj, at.l, pl.ds(aligned(hi * MOST, 16), MOST)], xr.at[m])
            settle(gb_ref.at[fj, at.l, hi], tr.at[m])
        for i, peer in enumerate((core, side)):
            send(xb_ref.at[fj, at.l], xb_ref.at[fj, at.l], qs.at[fj, i], qr.at[fj, i], peer)
            send(gb_ref.at[fj, at.l], gb_ref.at[fj, at.l], tqs.at[fj, i], tqr.at[fj, i], peer)

    def pass_on(j):
        fj = xor4(at.f, j)
        settle(xb_ref.at[fj, at.l2], qr.at[fj, 1])
        settle(gb_ref.at[fj, at.l2], tqr.at[fj, 1])
        send(xb_ref.at[fj, at.l2], xb_ref.at[fj, at.l2], qs.at[fj, 2], qr.at[fj, 2], core)
        send(gb_ref.at[fj, at.l2], gb_ref.at[fj, at.l2], tqs.at[fj, 2], tqr.at[fj, 2], core)

    def compute(j):
        fj = xor4(at.f, j)
        settle(xb_ref.at[fj, at.l1], qr.at[fj, 0])
        settle(gb_ref.at[fj, at.l1], tqr.at[fj, 0])
        settle(xb_ref.at[fj, at.l3], qr.at[fj, 2])
        settle(gb_ref.at[fj, at.l3], tqr.at[fj, 2])
        slot_of_chunk = lax.rem(j, 2)

        @pl.when(j >= 2)
        def _():
            settle(op_ref.at[slot_of_chunk], last_sem.at[slot_of_chunk])

        diagonal = lax.broadcasted_iota(jnp.int32, (MOST, 128), 0) == lane_iota(MOST)
        pair_rows = 2 * his * MOST

        def rows_of(i, _):
            l2 = pl.ds(2 * i, 2)
            x = xb_ref[fj, l2].reshape(pair_rows, width)
            g = g_ref[l2, fj].reshape(pair_rows, width)
            gate = jnp.concatenate(
                [
                    pick(
                        jnp.broadcast_to(gb_ref[fj, 2 * i + i2, h][0:1, :], (MOST, 128)), diagonal
                    )
                    for i2 in range(2)
                    for h in range(his)
                ],
                axis=0,
            )
            these = pl.ds(aligned(i * pair_rows, 16), pair_rows)
            grow_ref[these, :] = (g.astype(F32) * gate).astype(BF16)
            wgu = wgu_ref[...]
            wd = wd_ref[...]
            ab = mm(x, wgu)
            inner = ab.shape[1] // 2
            a = ab[:, :inner]
            b = ab[:, inner:]
            sig = 1.0 / (1.0 + jnp.exp(-a))
            act = a * sig
            hidden = (act * b).astype(BF16)
            hid_ref[these, :] = hidden
            shape = (2, his * MOST, width)
            op_ref[slot_of_chunk, l2] = mm(hidden, wd, NT).astype(BF16).reshape(shape)
            dh_raw = mm(g, wd)
            d_route = jnp.sum(hidden.astype(F32) * dh_raw, axis=1, keepdims=True)
            for i2 in range(2):
                for h in range(his):
                    first = (i2 * his + h) * MOST
                    line = jnp.sum(
                        jnp.where(diagonal, d_route[first : first + MOST], 0.0),
                        axis=0,
                        keepdims=True,
                    )
                    dgp_ref[fj, 2 * i + i2, h] = jnp.broadcast_to(line, (8, 128))
            dh = dh_raw * gate
            d_up = (dh * act).astype(BF16)
            d_gate = (dh * b * (sig + act * (1.0 - sig))).astype(BF16)
            dgu = jnp.concatenate([d_gate, d_up], axis=1)
            dgu_ref[these, :] = dgu
            od_ref[fj, l2] = mm(dgu, wgu, NT).astype(BF16).reshape(shape)
            return 0

        lax.fori_loop(0, lo // 2, rows_of, 0)
        x_all = xb_ref[fj].reshape(lo * his * MOST, width)
        accgu_ref[...] += mm(x_all, dgu_ref[...], TN)
        accd_ref[...] += mm(grow_ref[...], hid_ref[...], TN)
        pltpu.make_async_copy(
            op_ref.at[slot_of_chunk], op_hbm.at[fj], last_sem.at[slot_of_chunk]
        ).start()

    def to_core(j):
        fj = xor4(at.f, j)
        send(od_ref.at[fj, at.l1], r1_ref.at[fj, 0], d1s.at[fj, 0], d1r.at[fj, 0], core)
        send(od_ref.at[fj, at.l3], r1_ref.at[fj, 1], d1s.at[fj, 1], d1r.at[fj, 1], core)
        send(dgp_ref.at[fj, at.l1], dr1_ref.at[fj, 0], t1s.at[fj, 0], t1r.at[fj, 0], core)
        send(dgp_ref.at[fj, at.l3], dr1_ref.at[fj, 1], t1s.at[fj, 1], t1r.at[fj, 1], core)

    def add(ref, other):
        ref[...] = (ref[...].astype(F32) + other[...].astype(F32)).astype(BF16)

    def to_side(j):
        fj = xor4(at.f, j)
        settle(r1_ref.at[fj, 1], d1r.at[fj, 1])
        add(od_ref.at[fj, at.l2], r1_ref.at[fj, 1])
        send(od_ref.at[fj, at.l2], r2_ref.at[fj], d2s.at[fj], d2r.at[fj], side)
        settle(dr1_ref.at[fj, 1], t1r.at[fj, 1])
        dgp_ref[fj, at.l2] += dr1_ref[fj, 1]
        send(dgp_ref.at[fj, at.l2], dr2_ref.at[fj], t2s.at[fj], t2r.at[fj], side)
        settle(r1_ref.at[fj, 0], d1r.at[fj, 0])
        add(od_ref.at[fj, at.l], r1_ref.at[fj, 0])
        settle(dr1_ref.at[fj, 0], t1r.at[fj, 0])
        dgp_ref[fj, at.l] += dr1_ref[fj, 0]

    def to_home(j):
        fj = xor4(at.f, j)
        settle(r2_ref.at[fj], d2r.at[fj])
        add(od_ref.at[fj, at.l], r2_ref.at[fj])
        settle(dr2_ref.at[fj], t2r.at[fj])
        dgp_ref[fj, at.l] += dr2_ref[fj]
        for hh in range(his):
            hi = flip(at.hi, hh)
            m = fj * his + hi
            rows = od_ref.at[fj, at.l, pl.ds(aligned(hi * MOST, 16), MOST)]
            peer = (hi * lo + at.l, fj)

            line = dgp_ref.at[fj, at.l, hi]

            def away(rows=rows, line=line, peer=peer, m=m):
                send(rows, back_ref.at[at.m], bs.at[m], br.at[at.m], peer)
                send(line, dgb_ref.at[at.m], tbs.at[m], tbr.at[at.m], peer)

            if hh:
                away()
            else:

                @pl.when(j == 0)
                def _(rows=rows, line=line):
                    pltpu.make_async_copy(rows, back_ref.at[at.m], br.at[at.m]).start()
                    pltpu.make_async_copy(line, dgb_ref.at[at.m], tbr.at[at.m]).start()

                pl.when(j > 0)(away)

    take(0)
    pass_on(0)
    settle(g_ref.at[at.l1], gqr.at[0])
    settle(g_ref.at[at.l3], gqr.at[2])
    for k in range(1, E):
        settle(grow_ref.at[0:MOST], gs.at[k])
    for m in range(E):
        for w in range(3):
            settle(wd_ref.at[0:head_rows, 0:ff], wr.at[m, w])
    give(2)

    def step(t, _):
        @pl.when(t + 1 < ranks)
        def _():
            take(t + 1)

        @pl.when(t == 1)
        def _():
            give(3)

        compute(t)
        to_core(t)

        @pl.when(t + 1 < ranks)
        def _():
            pass_on(t + 1)

        to_side(t)

        @pl.when(t >= 1)
        def _():
            to_home(t - 1)

        return 0

    lax.fori_loop(0, ranks, step, 0)
    to_home(ranks - 1)

    inner = wd_ref.shape[1]
    gw_ref[0] = accgu_ref[:, :inner].astype(BF16)
    gw_ref[1] = accgu_ref[:, inner:].astype(BF16)
    gw_ref[2] = accd_ref[...].astype(BF16)
    pltpu.make_async_copy(gw_ref, gw_hbm, last_sem.at[4]).start()

    for m in range(E):
        settle(back_ref.at[m], br.at[m])
        settle(dgb_ref.at[m], tbr.at[m])
    pltpu.make_async_copy(back_ref, back_hbm, last_sem.at[5]).start()
    pltpu.make_async_copy(dgb_ref, dgb_hbm, last_sem.at[6]).start()

    for j in range(1, ranks):
        settle(tile_ref, zs.at[j])
    for j in range(ranks):
        for t in range(4):
            settle(tile_ref, ps.at[j, t])
        for t in range(3):
            settle(tile_ref, cs.at[t, j])

    @pl.when(at.f < ranks - 1)
    def _():
        settle(tail, hs)

    for k in range(1, E):
        settle(x_ref.at[0:MOST], xs.at[k])
        settle(gates_ref.at[0], ts.at[k])
        for w in range(3):
            settle(wd_ref.at[0:head_rows, 0:ff], ws.at[k, w])
    for i in range(3):
        settle(g_ref.at[0], gas.at[i])
    for f2 in range(ranks):
        for i in range(3):
            settle(xb_ref.at[0, 0], qs.at[f2, i])
            settle(gb_ref.at[0, 0], tqs.at[f2, i])
        for i in range(2):
            settle(r1_ref.at[0, 0], d1s.at[f2, i])
            settle(dr1_ref.at[0, 0], t1s.at[f2, i])
        settle(r2_ref.at[0], d2s.at[f2])
        settle(dr2_ref.at[0], t2s.at[f2])
    for j in range(ranks):
        for hh in range(his):
            if j or hh:
                m = at.member(j, hh)[0]
                settle(back_ref.at[0], bs.at[m])
                settle(dgb_ref.at[0], tbs.at[m])
    settle(op_ref.at[0], last_sem.at[0])
    settle(op_ref.at[1], last_sem.at[1])
    settle(gw_ref, last_sem.at[4])
    settle(back_ref, last_sem.at[5])
    settle(dgb_ref, last_sem.at[6])
    for i, (name, _, _) in enumerate(KEPT):
        settle(kept[name], keep_sem.at[i])


SMALL_G1 = EXPERTS_ALL
SMALL_VC = SMALL_G1 + 2
SMALL_C = SMALL_VC + CONSTS
COL_POS, COL_C0, COL_C1, COL_R0, COL_R1, COL_W0, COL_W1 = range(16, 23)


def ahead(groups, ranks, *args):
    tok = args[13]
    w_gate = args[15]
    width = tok.shape[1]
    his = E // ranks
    lo = groups // his
    ff = w_gate.shape[2]
    dma = pltpu.SemaphoreType.DMA
    vm = pltpu.VMEM
    any_spec = pl.BlockSpec(memory_space=pl.ANY)
    block = (width // ranks + 8, 4 * (width // groups))
    rows = (his * MOST, width)
    kept = [(kept_shape(dims, width), dtype) for _, dims, dtype in KEPT]
    results = [
        ((ranks, lo) + rows, BF16),
        ((3, width, ff * his), BF16),
        ((E, MOST, width), BF16),
        ((E, 8, 128), F32),
    ]
    return pl.pallas_call(
        ahead_kernel,
        out_shape=[sds(*k) for k in kept + results],
        in_specs=[pl.BlockSpec(memory_space=pltpu.SMEM)] + whole(14) + [any_spec] * 3,
        out_specs=[any_spec] * (len(kept) + len(results)),
        scratch_shapes=[vm(*k) for k in kept]
        + [
            vm(block, BF16),
            vm((128, 128), F32),
            vm((groups, ranks) + block, BF16),
            vm((ROWS, width), BF16),
            vm((ROWS, width), BF16),
            vm((E, 8, 128), F32),
            vm((width, 2 * ff * his), BF16),
            vm((width, ff * his), BF16),
            vm((lo, ranks) + rows, BF16),
            vm((ranks, lo) + rows, BF16),
            vm((ranks, lo, his, 8, 128), F32),
            vm((ranks, lo) + rows, BF16),
            vm((2, lo) + rows, BF16),
            vm((ranks, 2) + rows, BF16),
            vm((ranks,) + rows, BF16),
            vm((ranks, lo, his, 8, 128), F32),
            vm((ranks, 2, his, 8, 128), F32),
            vm((ranks, his, 8, 128), F32),
            vm((width, 2 * ff * his), F32),
            vm((width, ff * his), F32),
            vm((lo * rows[0], ff * his), BF16),
            vm((lo * rows[0], 2 * ff * his), BF16),
            vm((3, width, ff * his), BF16),
            vm((E, MOST, width), BF16),
            vm((E, 8, 128), F32),
            dma((len(kept),)),
            dma((8,)),
            dma((4,)),
            dma((4, 4)),
            dma((3, 4)),
            dma,
            dma((E,)),
            dma((E, 3)),
            dma((3,)),
            dma((groups, ranks)),
            dma,
            dma((E,)),
            dma((E, 3)),
            dma((3,)),
            dma((E,)),
            dma((E,)),
            dma((4, 3)),
            dma((4, 3)),
            dma((4, 2)),
            dma((4, 2)),
            dma((4,)),
            dma((4,)),
            dma((E,)),
            dma((E,)),
            dma((E,)),
            dma((E,)),
            dma((4, 3)),
            dma((4, 3)),
            dma((4, 2)),
            dma((4, 2)),
            dma((4,)),
            dma((4,)),
            dma((E,)),
            dma((E,)),
        ],
        compiler_params=params(63, collective_id=1, has_side_effects=True),
        name="ahead",
    )(*args)


def end_kernel(
    cot_ref,
    tok_ref,
    prev_ref,
    wmix_ref,
    back_hbm,
    dgb_hbm,
    op_hbm,
    gw_hbm,
    *rest,
):
    n = len(KEPT)
    kept_hbm = by_name(rest[:n])
    (
        out_ref,
        dres_ref,
        gprev_ref,
        down_ref,
        back_ref,
        fin_ref,
        gmix_ref,
        t_ref,
    ) = rest[n : n + 8]
    kept = by_name(rest[n + 8 : 2 * n + 8])
    (
        dx_ref,
        dgb_ref,
        opl_ref,
        r1o_ref,
        r2o_ref,
        outb_ref,
        flat_ref,
        dhalo_ref,
        dm_ref,
        dq_ref,
        dk_ref,
        dv_ref,
        dqr_ref,
        dkr_ref,
        dvr_ref,
        full_ref,
        p_ref,
        r1_ref,
        r2_ref,
        r3_ref,
        r4_ref,
        mx_ref,
        mr_ref,
        mz_ref,
        load_sem,
        more_sem,
        o1s,
        o1r,
        o2s,
        o2r,
        obs,
        obr,
        ts,
        tr,
        hs,
        hr,
        s1,
        e1,
        s2,
        e2,
        s3,
        e3,
        s4,
        e4,
        ms,
        me,
        zs,
        ze,
    ) = rest[2 * n + 8 :]
    wf_ref, s_ref, halo_ref, cols_ref = kept["wf"], kept["s"], kept["halo"], kept["cols"]
    q_ref, k_ref, v_ref, n1_ref = kept["q"], kept["k"], kept["v"], kept["n1"]
    mix_ref, lse_ref = kept["mix"], kept["lse"]
    names = [item[0] for item in KEPT]

    def load(*which):
        for name in which:
            pltpu.make_async_copy(
                kept_hbm[name], kept[name], load_sem.at[names.index(name)]
            ).start()

    def ready(*which):
        for name in which:
            settle(kept[name], load_sem.at[names.index(name)])

    ranks = p_ref.shape[1]
    his = E // ranks
    groups = p_ref.shape[0]
    lo = groups // his
    at = Place(his, lo)
    width = cot_ref.shape[1]
    tile = t_ref.shape[2:]
    core = (at.core_peer, at.f)
    side = (at.side_peer, at.f)
    upper = (lo * (1 - at.hi) + at.l, at.f)
    peers = at.others() + [core, side]
    call(peers)
    pltpu.make_async_copy(back_hbm, dx_ref, more_sem.at[0]).start()
    pltpu.make_async_copy(dgb_hbm, dgb_ref, more_sem.at[1]).start()
    load("cols", "s", "resid", "probs", "mix", "wf", "q", "k", "v", "lse")
    for f2 in range(ranks):
        for i, l2 in enumerate((at.l, at.l2)):
            pltpu.make_async_copy(
                op_hbm.at[f2, l2], opl_ref.at[f2, i], more_sem.at[2 + 2 * f2 + i]
            ).start()
    load("cos", "sin", "n1", "inv1", "halo", "part")
    answer(peers)

    for f2 in range(ranks):
        send(op_hbm.at[f2, at.l1], r1o_ref.at[f2, 0], o1s.at[f2, 0], o1r.at[f2, 0], core)
        send(op_hbm.at[f2, at.l3], r1o_ref.at[f2, 1], o1s.at[f2, 1], o1r.at[f2, 1], core)

    for j in range(ranks):
        for hh in range(his):
            e, peer = at.member(j, hh)
            rows = pl.ds(aligned(e // his * tile[0], 16), tile[0])
            lanes_at = pl.ds(aligned(lax.rem(e, his) * tile[1], 128), tile[1])
            n = j * his + hh
            for w in range(3):
                block = gw_hbm.at[w, rows, lanes_at]
                if n == 0:
                    pltpu.make_async_copy(block, t_ref.at[at.m, w], tr.at[at.m, w]).start()
                else:
                    send(block, t_ref.at[at.m, w], ts.at[n, w], tr.at[at.m, w], peer)

    def add(ref, other):
        ref[...] = (ref[...].astype(F32) + other[...].astype(F32)).astype(BF16)

    ready("cols", "s", "resid", "probs")
    settle(dx_ref, more_sem.at[0])
    settle(dgb_ref, more_sem.at[1])
    flat = s_ref[...].T
    gain1 = flat[SMALL_G1 : SMALL_G1 + 1, :]
    gain2 = flat[SMALL_G1 + 1 : SMALL_G1 + 2, :]
    vc = flat[SMALL_VC : SMALL_VC + CONSTS, :]
    g = cot_ref[...].astype(F32)
    lanes = lane_iota(TOK_DEV)
    cols = cols_ref[...]

    def col(i):
        return pick(cols, lanes == i)

    gate0, gate1, gate_id, inv2 = col(0), col(1), col(2), col(3)
    resid = kept["resid"][...]
    unit2 = resid * inv2
    normed = unit2 * gain2
    narrow = normed.astype(BF16)
    c0, c1, r0, r1, wide0, wide1 = (
        col(COL_POS + 1 + i).astype(jnp.int32) for i in range(6)
    )
    slot = lane_iota(TOK_DEV, ROWS)
    hot0 = jnp.where(slot == c0, 1.0, 0.0).astype(BF16)
    hot1 = jnp.where(slot == c1, 1.0, 0.0).astype(BF16)
    dg0 = jnp.zeros((TOK_DEV, 1), F32)
    dg1 = jnp.zeros((TOK_DEV, 1), F32)
    for e in range(E):
        line = jnp.broadcast_to(dgb_ref[e][0:1, :], (TOK_DEV, 128))
        dg0 = dg0 + pick(line, lanes + e * 128 == wide0)
        dg1 = dg1 + pick(line, lanes + e * 128 == wide1)
    a_n = jnp.sum(g * normed, axis=1, keepdims=True)
    dg0 = jnp.where(r0 == E + 1, a_n, dg0)
    dg1 = jnp.where(r1 == E + 1, a_n, dg1)
    g_scale = gate_id
    dl = jnp.zeros((TOK_DEV, 128), F32)
    vmix = jnp.zeros((TOK_DEV, 128), F32)
    for c in range(CONSTS):
        gate_c, ma, mb = col(4 + 3 * c), col(5 + 3 * c), col(6 + 3 * c)
        a_v = jnp.sum(g * vc[c : c + 1, :], axis=1, keepdims=True)
        branch = ma * a_n + mb * a_v
        dg0 = jnp.where(r0 == E + 2 + c, branch, dg0)
        dg1 = jnp.where(r1 == E + 2 + c, branch, dg1)
        g_scale = g_scale + gate_c * ma
        da = gate_c * a_n
        db = gate_c * a_v
        mean = ma * da + mb * db
        dl = jnp.where(lanes == SMALL_C + 2 * c, ma * (da - mean), dl)
        dl = jnp.where(lanes == SMALL_C + 1 + 2 * c, mb * (db - mean), dl)
        vmix = jnp.where(lanes == SMALL_VC + c, gate_c * mb, vmix)
    probs = kept["probs"][...]
    d_probs = jnp.where(lanes == r0, dg0, 0.0) + jnp.where(lanes == r1, dg1, 0.0)
    d_logits = probs * (d_probs - jnp.sum(probs * d_probs, axis=1, keepdims=True))
    dl = jnp.where(lanes < EXPERTS_ALL, d_logits, dl)
    high = dl.astype(BF16)
    low = (dl - high.astype(F32)).astype(BF16)
    wr = s_ref[...].astype(BF16)
    d_normed = g_scale * g + mm(hot0 + hot1, dx_ref[...].reshape(ROWS, width))
    d_normed = d_normed + mm(high, wr, NT) + mm(low, wr, NT)
    vhigh = vmix.astype(BF16)
    vlow = (vmix - vhigh.astype(F32)).astype(BF16)
    tiny = mm(high, narrow, TN) + mm(low, narrow, TN)
    tiny = tiny + mm(vhigh, cot_ref[...], TN) + mm(vlow, cot_ref[...], TN)
    row_id = lax.broadcasted_iota(jnp.int32, (128, width), 0)
    dg2 = jnp.sum(d_normed * unit2, axis=0, keepdims=True)
    flat_ref[...] = jnp.where(row_id == SMALL_G1 + 1, dg2, tiny)
    n = d_normed * gain2
    dres_ref[...] = g + inv2 * (n - unit2 * jnp.mean(n * unit2, axis=1, keepdims=True))
    wmix = jnp.concatenate(
        [wmix_ref[...].astype(F32), jnp.zeros((EXPERTS_ALL, 128 - EXPERTS_ALL), F32)], axis=1
    ).astype(BF16)
    gprev_ref[...] = mm(wmix, high, NT) + mm(wmix, low, NT)
    prev = prev_ref[...]
    phigh = prev.astype(BF16)
    plow = (prev - phigh.astype(F32)).astype(BF16)
    mx_ref[0] = jnp.zeros(mx_ref.shape[1:], F32)
    mx_ref[0, 0:EXPERTS_ALL, :] = mm(phigh, high) + mm(phigh, low) + mm(plow, high)
    send(mx_ref.at[0], mr_ref.at[0], ms.at[0], me.at[0], core)

    for f2 in range(ranks):
        settle(opl_ref.at[f2, 1], more_sem.at[3 + 2 * f2])
        settle(r1o_ref.at[f2, 1], o1r.at[f2, 1])
        add(opl_ref.at[f2, 1], r1o_ref.at[f2, 1])
        send(opl_ref.at[f2, 1], r2o_ref.at[f2], o2s.at[f2], o2r.at[f2], side)
        settle(opl_ref.at[f2, 0], more_sem.at[2 + 2 * f2])
        settle(r1o_ref.at[f2, 0], o1r.at[f2, 0])
        add(opl_ref.at[f2, 0], r1o_ref.at[f2, 0])

    ready("mix", "wf", "q", "k", "v", "lse")
    scale = HEAD_DIM ** (-0.5)
    d_attn = dres_ref[...].astype(BF16)
    full_ref[3] = mm(mix_ref[...], d_attn, TN).astype(BF16)
    dm_ref[...] = mm(d_attn, wf_ref[3], NT).astype(BF16)
    dk_ref[...] = jnp.zeros_like(dk_ref)
    dv_ref[...] = jnp.zeros_like(dv_ref)

    def pair(p, _):
        span = pl.ds(pl.multiple_of(p * 128, 128), 128)
        for first, count in QBLOCKS:
            keys = key_span(first)
            ok = allowed_mask(cols_ref, first, count, COL_POS)[:, :keys]
            q = q_ref[pl.ds(first, count), span]
            dm = dm_ref[pl.ds(first, count), span]
            k = k_ref[pl.ds(first, keys), span]
            v = v_ref[pl.ds(first, keys), span]
            lane = lane_iota(count)
            key_lane = lane_iota(keys)
            lse = lse_ref[pl.ds(first, count), :]
            dq = dk = dv = None
            for h in range(2):
                mine = (lane < HEAD_DIM) if h == 0 else (lane >= HEAD_DIM)
                key_mine = (key_lane < HEAD_DIM) if h == 0 else (key_lane >= HEAD_DIM)
                qh = jnp.where(mine, q, jnp.zeros_like(q))
                dmh = jnp.where(mine, dm, jnp.zeros_like(dm))
                s = jnp.where(ok, mm(qh, k, NT) * scale, NEG)
                pr = jnp.where(ok, jnp.exp(s - pick(lse, lane == 2 * p + h)), 0.0)
                dp = mm(dmh, v, NT)
                delta = jnp.sum(pr * dp, axis=1, keepdims=True)
                ds = (pr * (dp - delta)).astype(BF16)
                pb = pr.astype(BF16)
                dqh = mm(ds, k)
                dkh = mm(ds, q, TN)
                dvh = mm(pb, dm, TN)
                dq = dqh if h == 0 else jnp.where(mine, dqh, dq)
                dk = dkh if h == 0 else jnp.where(key_mine, dkh, dk)
                dv = dvh if h == 0 else jnp.where(key_mine, dvh, dv)
            dq_ref[pl.ds(first, count), span] = dq * scale
            dk_ref[pl.ds(first, keys), span] += dk * scale
            dv_ref[pl.ds(first, keys), span] += dv

        @pl.when(p == 2)
        def _():
            for j in range(ranks):
                fj = xor4(at.f, j)
                settle(r2o_ref.at[fj], o2r.at[fj])
                add(opl_ref.at[fj, 0], r2o_ref.at[fj])
                for hh in range(his):
                    m, peer = at.member(j, hh)
                    hi = flip(at.hi, hh)
                    rows = opl_ref.at[fj, 0, pl.ds(aligned(hi * MOST, 16), MOST)]
                    if j or hh:
                        send(rows, outb_ref.at[at.m], obs.at[m], obr.at[at.m], peer)
                    else:
                        pltpu.make_async_copy(rows, outb_ref.at[at.m], obr.at[at.m]).start()

        return 0

    lax.fori_loop(0, HEADS // 2, pair, 0)

    ready("cos", "sin", "n1", "inv1", "halo", "part")

    def unturn(i, _):
        span = pl.ds(pl.multiple_of(i * 256, 256), 256)
        cos = kept["cos"][...]
        sin = kept["sin"][...]
        dqr_ref[:, span] = turn(dq_ref[:, span], cos[HALO:], -sin[HALO:]).astype(BF16)
        dkr_ref[:, span] = turn(dk_ref[:, span], cos, -sin).astype(BF16)
        dvr_ref[:, span] = dv_ref[:, span].astype(BF16)
        return 0

    lax.fori_loop(0, width // 256, unturn, 0)
    d_all = mm(dkr_ref[...], wf_ref[1], NT) + mm(dvr_ref[...], wf_ref[2], NT)
    dhalo_ref[...] = (d_all[:HALO] * gain1).astype(BF16)

    @pl.when(at.f > 0)
    def _():
        send(dhalo_ref, back_ref, hs, hr, (at.g, at.f - 1))

    @pl.when(at.f == ranks - 1)
    def _():
        back_ref[...] = jnp.zeros_like(back_ref)

    full_ref[0] = mm(n1_ref[HALO:, :], dqr_ref[...], TN).astype(BF16)
    full_ref[1] = mm(n1_ref[...], dkr_ref[...], TN).astype(BF16)
    full_ref[2] = mm(n1_ref[...], dvr_ref[...], TN).astype(BF16)
    d_own = d_all[HALO:] + mm(dqr_ref[...], wf_ref[0], NT)
    inv1 = kept["inv1"][:, 0:1]
    unit_own = tok_ref[...].astype(F32) * inv1[HALO:]
    unit_halo = halo_ref[...].astype(F32) * inv1[:HALO]
    dg1 = jnp.sum(d_own * unit_own, axis=0, keepdims=True) + jnp.sum(
        d_all[:HALO] * unit_halo, axis=0, keepdims=True
    )
    down_ref[...] = d_own * gain1
    flat_ref[...] = jnp.where(row_id == SMALL_G1, dg1, flat_ref[...])

    part_cols = width // groups
    head_rows = width // ranks

    def pack(f2, _):
        rows = pl.ds(aligned(f2 * head_rows, 16), head_rows)
        for g2 in range(groups):
            pieces = [
                full_ref[w, rows, g2 * part_cols : (g2 + 1) * part_cols] for w in range(4)
            ]
            p_ref[g2, f2, 0:head_rows, :] = jnp.concatenate(pieces, axis=1)
        return 0

    lax.fori_loop(0, ranks, pack, 0)
    column = flat_ref[...].T
    per = width // (groups * ranks)
    for g2 in range(groups):
        for f2 in range(ranks):
            base = (g2 * ranks + f2) * per
            pieces = [column[base + 8 * i : base + 8 * i + 8, :] for i in range(per // 8)]
            p_ref[g2, f2, head_rows : head_rows + 8, :] = jnp.concatenate(
                pieces, axis=1
            ).astype(BF16)

    c = lax.rem(at.g, 2)
    x = lax.rem(at.g // 2, 2)
    y = at.hi

    def block(y2, x2, c2):
        return (y2 * 2 + x2) * 2 + c2

    half = ranks // 2
    quads = [(1 - y, 1 - x), (y, 1 - x), (1 - y, x), (y, x)]
    for i, (y2, x2) in enumerate(quads):
        spot = y2 * 2 + x2
        send(p_ref.at[block(y2, x2, 1 - c)], r1_ref.at[spot], s1.at[i], e1.at[spot], core)
    settle(mr_ref.at[0], me.at[0])
    mx_ref[1] = mx_ref[0] + mr_ref[0]
    send(mx_ref.at[1], mr_ref.at[1], ms.at[1], me.at[1], side)
    for i, (y2, x2) in enumerate(quads):
        spot = y2 * 2 + x2
        settle(r1_ref.at[spot], e1.at[spot])
        add(p_ref.at[block(y2, x2, c)], r1_ref.at[spot])
        if i == 0:
            here = p_ref.at[block(1 - y, 1 - x, c)]
            send(here.at[0:half], r2_ref.at[0, 1 - y], s2.at[0, 0], e2.at[0, 1 - y], side)
            send(here.at[half:], r2_ref.at[1, 1 - x], s2.at[1, 0], e2.at[1, 1 - x], upper)
        if i == 1:
            here = p_ref.at[block(y, 1 - x, c)]
            send(here.at[0:half], r2_ref.at[0, y], s2.at[0, 1], e2.at[0, y], side)
        if i == 2:
            here = p_ref.at[block(1 - y, x, c)]
            send(here.at[half:], r2_ref.at[1, x], s2.at[1, 1], e2.at[1, x], upper)
    settle(mr_ref.at[1], me.at[1])
    mx_ref[2] = mx_ref[1] + mr_ref[1]
    send(mx_ref.at[2], mr_ref.at[2], ms.at[2], me.at[2], upper)
    settle(r2_ref.at[0, 1 - y], e2.at[0, 1 - y])
    add(p_ref.at[block(1 - y, x, c), 0:half], r2_ref.at[0, 1 - y])
    send(
        p_ref.at[block(1 - y, x, c), 0:half], r3_ref.at[0], s3.at[0], e3.at[0], upper
    )
    settle(r2_ref.at[1, 1 - x], e2.at[1, 1 - x])
    add(p_ref.at[block(y, 1 - x, c), half:], r2_ref.at[1, 1 - x])
    send(p_ref.at[block(y, 1 - x, c), half:], r3_ref.at[1], s3.at[1], e3.at[1], side)
    settle(r2_ref.at[0, y], e2.at[0, y])
    add(p_ref.at[at.g, 0:half], r2_ref.at[0, y])
    settle(r2_ref.at[1, x], e2.at[1, x])
    add(p_ref.at[at.g, half:], r2_ref.at[1, x])
    settle(mr_ref.at[2], me.at[2])
    mx_ref[3] = mx_ref[2] + mr_ref[2]
    mz_ref[at.f] = mx_ref[3]
    for i in range(2):
        settle(r3_ref.at[i], e3.at[i])
        add(p_ref.at[at.g, i * half : (i + 1) * half], r3_ref.at[i])
    for j in range(1, ranks):
        f2 = xor4(at.f, j)
        send(p_ref.at[at.g, f2], r4_ref.at[at.f], s4.at[j], e4.at[at.f], (at.g, f2))
        send(mx_ref.at[3], mz_ref.at[at.f], zs.at[j], ze.at[at.f], (at.g, f2))
    for m in range(E):
        settle(outb_ref.at[m], obr.at[m])
    rows = outb_ref[...].reshape(ROWS, width)
    cols = cols_ref[...]
    c0 = pick(cols, lanes == COL_C0).astype(jnp.int32)
    c1 = pick(cols, lanes == COL_C1).astype(jnp.int32)
    y0 = mm(jnp.where(slot == c0, 1.0, 0.0).astype(BF16), rows)
    y1 = mm(jnp.where(slot == c1, 1.0, 0.0).astype(BF16), rows)
    gate0 = pick(cols, lanes == 0)
    gate1 = pick(cols, lanes == 1)
    out_ref[...] = (kept["part"][...] + gate0 * y0 + gate1 * y1).astype(BF16)

    total = p_ref[at.g, at.f].astype(F32)
    for j in range(1, ranks):
        f2 = xor4(at.f, j)
        settle(r4_ref.at[f2], e4.at[f2])
        total = total + r4_ref[f2].astype(F32)
        settle(mz_ref.at[f2], ze.at[f2])
    fin_ref[...] = total
    gmix_ref[...] = (mz_ref[0] + mz_ref[1]) + (mz_ref[2] + mz_ref[3])

    for f2 in range(ranks):
        for i in range(2):
            settle(r1o_ref.at[0, 0], o1s.at[f2, i])
        settle(r2o_ref.at[0], o2s.at[f2])
    for j in range(ranks):
        for hh in range(his):
            if j or hh:
                settle(outb_ref.at[0], obs.at[at.member(j, hh)[0]])
    for m in range(E):
        for w in range(3):
            settle(t_ref.at[m, w], tr.at[m, w])
    for i in range(1, E):
        for w in range(3):
            settle(t_ref.at[0, w], ts.at[i, w])

    @pl.when(at.f > 0)
    def _():
        settle(dhalo_ref, hs)

    @pl.when(at.f < ranks - 1)
    def _():
        settle(back_ref, hr)

    for i in range(4):
        settle(r1_ref.at[0], s1.at[i])
    for i in range(2):
        for n2 in range(2):
            settle(r2_ref.at[0, 0], s2.at[i, n2])
        settle(r3_ref.at[0], s3.at[i])
    for i in range(3):
        settle(mr_ref.at[0], ms.at[i])
    for j in range(1, ranks):
        settle(r4_ref.at[0], s4.at[j])
        settle(mz_ref.at[0], zs.at[j])


def end(groups, ranks, tile, *args):
    cot = args[0]
    width = cot.shape[1]
    dma = pltpu.SemaphoreType.DMA
    vm = pltpu.VMEM
    block = (width // ranks + 8, 4 * (width // groups))
    half = ranks // 2
    rows = (E // ranks * MOST, width)
    kept = [(kept_shape(dims, width), dtype) for _, dims, dtype in KEPT]
    any_spec = pl.BlockSpec(memory_space=pl.ANY)
    return pl.pallas_call(
        end_kernel,
        out_shape=[
            sds((TOK_DEV, width), BF16),
            sds((TOK_DEV, width), F32),
            sds((EXPERTS_ALL, TOK_DEV), F32),
            sds((TOK_DEV, width), F32),
            sds((HALO, width), BF16),
            sds(block, F32),
            sds((16, 128), F32),
            sds((E, 3) + tile, BF16),
        ],
        in_specs=whole(4) + [any_spec] * (4 + len(kept)),
        out_specs=whole(7) + [any_spec],
        scratch_shapes=[vm(*k) for k in kept]
        + [
            vm((E, MOST, width), BF16),
            vm((E, 8, 128), F32),
            vm((ranks, 2) + rows, BF16),
            vm((ranks, 2) + rows, BF16),
            vm((ranks,) + rows, BF16),
            vm((E, MOST, width), BF16),
            vm((128, width), F32),
            vm((HALO, width), BF16),
            vm((TOK_DEV, width), BF16),
            vm((TOK_DEV, width), F32),
            vm((KEYS, width), F32),
            vm((KEYS, width), F32),
            vm((TOK_DEV, width), BF16),
            vm((KEYS, width), BF16),
            vm((KEYS, width), BF16),
            vm((4, width, width), BF16),
            vm((groups, ranks) + block, BF16),
            vm((4, ranks) + block, BF16),
            vm((2, 2, half) + block, BF16),
            vm((2, half) + block, BF16),
            vm((ranks,) + block, BF16),
            vm((4, 16, 128), F32),
            vm((3, 16, 128), F32),
            vm((ranks, 16, 128), F32),
            dma((len(kept),)),
            dma((2 + 2 * ranks,)),
            dma((ranks, 2)),
            dma((ranks, 2)),
            dma((ranks,)),
            dma((ranks,)),
            dma((E,)),
            dma((E,)),
            dma((E, 3)),
            dma((E, 3)),
            dma,
            dma,
            dma((4,)),
            dma((4,)),
            dma((2, 2)),
            dma((2, 2)),
            dma((2,)),
            dma((2,)),
            dma((4,)),
            dma((4,)),
            dma((3,)),
            dma((3,)),
            dma((4,)),
            dma((4,)),
        ],
        compiler_params=params(63, collective_id=3, has_side_effects=True),
        name="end",
    )(*args)


def store_kernel(
    t_ref,
    fin_ref,
    dres_ref,
    down_ref,
    back_ref,
    tok_ref,
    inv1_ref,
    gate_ref,
    up_ref,
    downw_ref,
    gq_ref,
    gk_ref,
    gv_ref,
    go_ref,
    router_ref,
    const_ref,
    vconst_ref,
    gain1_ref,
    gain2_ref,
    gtok_ref,
):
    for e in range(E):
        gate_ref[e] = t_ref[e, 0].astype(F32)
        up_ref[e] = t_ref[e, 1].astype(F32)
        downw_ref[e] = t_ref[e, 2].astype(F32)
    head_rows, part_cols = gq_ref.shape
    for w, ref in enumerate((gq_ref, gk_ref, gv_ref, go_ref)):
        ref[...] = fin_ref[0:head_rows, w * part_cols : (w + 1) * part_cols]
    per = router_ref.shape[1]
    column = jnp.concatenate(
        [
            fin_ref[head_rows : head_rows + 8, 128 * i : 128 * i + 128]
            for i in range(per // 8)
        ]
        + [jnp.zeros((128 - per, 128), F32)],
        axis=0,
    )
    flat = column.T[:, 0:per]
    router_ref[...] = flat[0:EXPERTS_ALL]
    gain1_ref[...] = flat[SMALL_G1 : SMALL_G1 + 1]
    gain2_ref[...] = flat[SMALL_G1 + 1 : SMALL_G1 + 2]
    vconst_ref[...] = flat[SMALL_VC : SMALL_VC + CONSTS]
    const_ref[...] = flat[SMALL_C : SMALL_C + 2 * CONSTS]
    width = tok_ref.shape[1]
    inv1 = inv1_ref[HALO:, 0:1]
    unit = tok_ref[...].astype(F32) * inv1
    m = jnp.concatenate(
        [down_ref[: TOK_DEV - HALO, :], down_ref[TOK_DEV - HALO :, :] + back_ref[...]], axis=0
    )
    d_dealt = inv1 * (m - unit * jnp.mean(m * unit, axis=1, keepdims=True))
    gtok_ref[...] = dres_ref[...] + d_dealt.astype(BF16).astype(F32)


def store(t, fin, dres, down, back, tok, inv1, groups, ranks):
    width = tok.shape[1]
    rows, cols = t.shape[2:]
    per = width // (groups * ranks)
    return pl.pallas_call(
        store_kernel,
        out_shape=[sds((E, rows, cols), F32)] * 3
        + [sds((width // ranks, width // groups), F32)] * 4
        + [
            sds((EXPERTS_ALL, per), F32),
            sds((2 * CONSTS, per), F32),
            sds((CONSTS, per), F32),
            sds((1, per), F32),
            sds((1, per), F32),
            sds(tok.shape, F32),
        ],
        in_specs=whole(7),
        out_specs=whole(13),
        compiler_params=params(48),
        name="store",
    )(t, fin, dres, down, back, tok, inv1)


def fast_device(
    tokens,
    cotangent,
    prev_logits,
    lengths,
    dealing,
    routes,
    gain_one,
    w_query,
    w_key,
    w_value,
    w_out,
    gain_two,
    w_router,
    w_mix,
    w_const,
    v_const,
    w_gate,
    w_up,
    w_down,
):
    groups = lax.axis_size("grp")
    ranks = lax.axis_size("fsdp")
    kept = len(KEPT)
    prev = prev_logits.T
    outs = ahead(
        groups,
        ranks,
        lengths,
        routes.T,
        prev,
        w_mix,
        w_router.T,
        gain_one[None, :],
        gain_two[None, :],
        w_const.T,
        v_const.T,
        w_query,
        w_key,
        w_value,
        w_out,
        tokens,
        cotangent,
        w_gate,
        w_up,
        w_down.transpose(0, 2, 1),
    )
    parts, grads, dx, routed = outs[kept:]
    output, dres, gprev, down, back, fin, gmix, tiles = end(
        groups,
        ranks,
        w_gate.shape[1:],
        cotangent,
        tokens,
        prev,
        w_mix,
        dx,
        routed,
        parts,
        grads,
        *outs[:kept],
    )
    inv1 = by_name(outs[:kept])["inv1"]
    gate, up, downw, gq, gk, gv, go, router, const, vconst, gain1, gain2, grad_tokens = store(
        tiles, fin, dres, down, back, tokens, inv1, groups, ranks
    )
    return (
        output,
        grad_tokens,
        gprev.T,
        gain1[0],
        gq,
        gk,
        gv,
        go,
        gain2[0],
        router.T,
        gmix[:EXPERTS_ALL, :EXPERTS_ALL],
        const.T,
        vconst.T,
        gate,
        up,
        downw.transpose(0, 2, 1),
    )


def suits(mesh):
    return mesh.shape["fsdp"] == 4 and mesh.shape["grp"] == 8


def solution(mesh):
    return jax.shard_map(
        fast_device if suits(mesh) else per_device,
        mesh=mesh,
        in_specs=(
            P(("grp", "fsdp"), None),
            P(("grp", "fsdp"), None),
            P(("grp", "fsdp"), None),
            P("grp", None),
            P("grp", None),
            P(("grp", "fsdp"), None),
            P(("grp", "fsdp")),
            P("fsdp", "grp"),
            P("fsdp", "grp"),
            P("fsdp", "grp"),
            P("fsdp", "grp"),
            P(("grp", "fsdp")),
            P(("grp", "fsdp"), None),
            P(),
            P(("grp", "fsdp"), None),
            P(("grp", "fsdp"), None),
            P(None, "fsdp", "grp"),
            P(None, "fsdp", "grp"),
            P(None, "grp", "fsdp"),
        ),
        out_specs=(
            P(("grp", "fsdp"), None),
            P(("grp", "fsdp"), None),
            P(("grp", "fsdp"), None),
            P(("grp", "fsdp")),
            P("fsdp", "grp"),
            P("fsdp", "grp"),
            P("fsdp", "grp"),
            P("fsdp", "grp"),
            P(("grp", "fsdp")),
            P(("grp", "fsdp"), None),
            P(),
            P(("grp", "fsdp"), None),
            P(("grp", "fsdp"), None),
            P(None, "fsdp", "grp"),
            P(None, "fsdp", "grp"),
            P(None, "grp", "fsdp"),
        ),
        check_vma=False,
    )
```

```python
import math

import jax
import jax.numpy as jnp
from jax import lax
from jax.experimental import pallas as pl
from jax.experimental.pallas import tpu as pltpu
from jax.sharding import PartitionSpec as P

HEADS = 12
HEAD_DIM = 64
E = 8
CONSTS = 2
BLOCK = 128
EXPERTS_ALL = 12
CAP = 384
TOK_DEV = 320
MOST = 80


NORM_EPS = 1e-05
EXACT = lax.Precision.HIGHEST


def rotation_tables(positions, head_dim):
    half_dim = head_dim // 2
    inv_freq = jnp.exp(
        jnp.arange(half_dim, dtype=jnp.float32) * (-2.0 * math.log(10000.0) / head_dim)
    )
    angles = positions.astype(jnp.float32)[:, None] * inv_freq[None, :]
    return (jnp.cos(angles), jnp.sin(angles))


def rotate(values, cos_table, sin_table):
    row_count = values.shape[0]
    half_dim = cos_table.shape[1]
    heads_view = values.reshape(row_count, -1, 2 * half_dim)
    front_half = heads_view[:, :, :half_dim]
    back_half = heads_view[:, :, half_dim:]
    cos_view = cos_table[:, None, :]
    sin_view = sin_table[:, None, :]
    turned = jnp.concatenate(
        [
            front_half * cos_view - back_half * sin_view,
            back_half * cos_view + front_half * sin_view,
        ],
        axis=2,
    )
    return turned.reshape(row_count, -1)


def exact_dot(left_side, right_side):
    return jnp.dot(left_side, right_side, precision=EXACT, preferred_element_type=jnp.float32)


def per_device(
    tokens,
    cotangent,
    prev_logits,
    lengths,
    dealing,
    routes,
    gain_one,
    w_query,
    w_key,
    w_value,
    w_out,
    gain_two,
    w_router,
    w_mix,
    w_const,
    v_const,
    w_gate,
    w_up,
    w_down,
):
    groups = lax.axis_size("grp")
    dealers = lax.axis_size("fsdp")
    device = lax.axis_index("fsdp")
    model_width = tokens.shape[1]
    per_shard = model_width // (groups * dealers)
    pairs = HEADS // 2
    pair_width = 2 * HEAD_DIM
    scale = HEAD_DIM ** (-0.5)
    seq_len = lengths[0]
    deal_order = dealing[0]
    seq_count = seq_len.shape[0]
    seq_ids = jnp.arange(seq_count, dtype=jnp.int32)
    seq_ends = jnp.cumsum(seq_len)
    starts = seq_ends - seq_len
    padded = (seq_len + BLOCK - 1) // BLOCK * BLOCK
    order_hot = (deal_order[:, None] == seq_ids[None, :]).astype(jnp.int32)
    dealt_len = jnp.sum(order_hot * seq_len[None, :], axis=1)
    dealt_pad = jnp.sum(order_hot * padded[None, :], axis=1)
    dealt_start = jnp.sum(order_hot * starts[None, :], axis=1)
    slot_of = jnp.sum(order_hot * seq_ids[:, None], axis=0)
    pair_index = 2 * device
    row_ids = jnp.arange(CAP, dtype=jnp.int32)
    in_second = row_ids >= dealt_pad[pair_index]
    position = row_ids - jnp.where(in_second, dealt_pad[pair_index], 0)
    seq_limit = jnp.where(in_second, dealt_len[pair_index + 1], dealt_len[pair_index])
    live_rows = position < seq_limit
    source = jnp.where(in_second, dealt_start[pair_index + 1], dealt_start[pair_index]) + position
    source = jnp.where(live_rows, source, -1)
    given_rows = device * TOK_DEV + jnp.arange(TOK_DEV, dtype=jnp.int32)
    seq_hot = (
        (given_rows[:, None] >= starts[None, :]) & (given_rows[:, None] < seq_ends[None, :])
    ).astype(jnp.int32)
    offset_in = given_rows - jnp.sum(seq_hot * starts[None, :], axis=1)
    slot_rank = jnp.sum(seq_hot * slot_of[None, :], axis=1)
    is_second = slot_rank % 2
    lead_pad = jnp.take(dealt_pad, slot_rank - is_second)
    target = slot_rank // 2 * CAP + jnp.where(is_second == 1, lead_pad, 0) + offset_in

    def deal(values):
        shard_rows = lax.all_gather(values, "fsdp", axis=0, tiled=True)
        row_span = shard_rows.shape[0]
        inside = (source >= 0) & (source < row_span)
        taken_rows = jnp.take(shard_rows, jnp.clip(source, 0, row_span - 1), axis=0)
        return jnp.where(inside[:, None], taken_rows, jnp.zeros((CAP, model_width), jnp.bfloat16))

    def give_back(values):
        shard_rows = lax.all_gather(values, "fsdp", axis=0, tiled=True)
        row_span = shard_rows.shape[0]
        inside = (target >= 0) & (target < row_span)
        taken_rows = jnp.take(shard_rows, jnp.clip(target, 0, row_span - 1), axis=0)
        return jnp.where(
            inside[:, None], taken_rows, jnp.zeros((TOK_DEV, model_width), jnp.bfloat16)
        )

    def collect():
        gate_in, up_in, down_in = (w_gate, w_up, w_down)
        sectioned = (
            lax.all_gather(gain_one, "fsdp", axis=0, tiled=True),
            lax.all_gather(w_query, "fsdp", axis=0, tiled=True),
            lax.all_gather(w_key, "fsdp", axis=0, tiled=True),
            lax.all_gather(w_value, "fsdp", axis=0, tiled=True),
            lax.all_gather(w_out, "fsdp", axis=0, tiled=True),
            lax.all_gather(gain_two, "fsdp", axis=0, tiled=True),
            lax.all_gather(w_router, "fsdp", axis=0, tiled=True),
            lax.all_gather(w_const, "fsdp", axis=0, tiled=True),
            lax.all_gather(v_const, "fsdp", axis=0, tiled=True),
            lax.all_gather(gate_in, "fsdp", axis=1, tiled=True),
            lax.all_gather(up_in, "fsdp", axis=1, tiled=True),
            lax.all_gather(down_in, "fsdp", axis=2, tiled=True),
        )
        (
            part_g1,
            part_q,
            part_k,
            part_v,
            part_o,
            part_g2,
            part_r,
            part_c,
            part_vc,
            part_gate,
            part_up,
            part_down,
        ) = sectioned
        small = (
            lax.all_gather(part_g1, "grp", axis=0, tiled=True),
            lax.all_gather(part_q, "grp", axis=1, tiled=True),
            lax.all_gather(part_k, "grp", axis=1, tiled=True),
            lax.all_gather(part_v, "grp", axis=1, tiled=True),
            lax.all_gather(part_o, "grp", axis=1, tiled=True),
            lax.all_gather(part_g2, "grp", axis=0, tiled=True),
            lax.all_gather(part_r, "grp", axis=0, tiled=True),
            lax.all_gather(part_c, "grp", axis=0, tiled=True),
            lax.all_gather(part_vc, "grp", axis=0, tiled=True),
        )
        experts = (
            lax.all_gather(part_gate, "grp", axis=2, tiled=True),
            lax.all_gather(part_up, "grp", axis=2, tiled=True),
            lax.all_gather(part_down, "grp", axis=1, tiled=True),
        )
        return tuple(small) + tuple(experts)

    (
        gain1,
        weight_q,
        weight_k,
        weight_v,
        weight_o,
        gain2,
        router,
        wconst,
        vconst,
        wgate,
        wup,
        wdown,
    ) = collect()
    dealt = deal(tokens)
    dealt_f = dealt.astype(jnp.float32)
    inv_one = lax.rsqrt(jnp.mean(dealt_f * dealt_f, axis=1, keepdims=True) + NORM_EPS)
    unit_one = dealt_f * inv_one
    gain1_f = gain1.astype(jnp.float32)
    normed_one = (unit_one * gain1_f).astype(jnp.bfloat16)
    cos_table, sin_table = rotation_tables(position, HEAD_DIM)
    query = rotate(
        jnp.dot(normed_one, weight_q, preferred_element_type=jnp.float32), cos_table, sin_table
    ).astype(jnp.bfloat16)
    keyed = rotate(
        jnp.dot(normed_one, weight_k, preferred_element_type=jnp.float32), cos_table, sin_table
    ).astype(jnp.bfloat16)
    values_proj = jnp.dot(normed_one, weight_v, preferred_element_type=jnp.float32).astype(
        jnp.bfloat16
    )
    allowed = (
        (in_second[:, None] == in_second[None, :])
        & (position[None, :] <= position[:, None])
        & live_rows[None, :]
    )

    def by_pairs(values):
        return values.reshape(CAP, pairs, pair_width).transpose(1, 0, 2)

    def from_pairs(values):
        return values.transpose(1, 0, 2).reshape(CAP, model_width)

    def pair_scores(q_pair, k_pair):
        query_heads = q_pair.reshape(CAP, 2, HEAD_DIM)
        key_heads = k_pair.reshape(CAP, 2, HEAD_DIM)
        scores = (
            jnp.einsum("qhd,khd->hqk", query_heads, key_heads, preferred_element_type=jnp.float32)
            * scale
        )
        return (jnp.where(allowed[None], scores, -1e30), query_heads, key_heads)

    def attend(pair_items):
        q_pair, k_pair, v_pair = pair_items
        scores, query_heads, key_heads = pair_scores(q_pair, k_pair)
        row_top = jnp.max(scores, axis=-1, keepdims=True)
        weights_exp = jnp.exp(scores - row_top)
        row_total = jnp.sum(weights_exp, axis=-1, keepdims=True)
        attn_probs = weights_exp / row_total
        value_heads = v_pair.reshape(CAP, 2, HEAD_DIM)
        mixed_pair = jnp.einsum(
            "hqk,khd->qhd",
            attn_probs.astype(jnp.bfloat16),
            value_heads,
            preferred_element_type=jnp.float32,
        )
        return (mixed_pair.reshape(CAP, pair_width), (row_top + jnp.log(row_total))[:, :, 0])

    mixed_pairs, log_sums = lax.map(
        attend, (by_pairs(query), by_pairs(keyed), by_pairs(values_proj))
    )
    mixed = from_pairs(mixed_pairs).astype(jnp.bfloat16)
    attn_out = jnp.dot(mixed, weight_o, preferred_element_type=jnp.float32).astype(jnp.bfloat16)
    returned = give_back(attn_out)
    resid = tokens.astype(jnp.float32) + returned.astype(jnp.float32)
    inv_two = lax.rsqrt(jnp.mean(resid * resid, axis=1, keepdims=True) + NORM_EPS)
    unit_two = resid * inv_two
    gain2_f = gain2.astype(jnp.float32)
    normed = unit_two * gain2_f
    narrow = normed.astype(jnp.bfloat16)
    mix_f = w_mix.astype(jnp.float32)
    router_f = router.astype(jnp.float32)
    wconst_f = wconst.astype(jnp.float32)
    logits = jnp.dot(narrow, router, preferred_element_type=jnp.float32) + exact_dot(
        prev_logits, mix_f
    )
    logit_top = jnp.max(logits, axis=1, keepdims=True)
    logit_exp = jnp.exp(logits - logit_top)
    route_probs = logit_exp / jnp.sum(logit_exp, axis=1, keepdims=True)
    expert_ids = jnp.arange(EXPERTS_ALL, dtype=jnp.int32)
    chosen = (
        (routes[:, 0:1] == expert_ids[None, :]) | (routes[:, 1:2] == expert_ids[None, :])
    ).astype(jnp.float32)
    gate_weights = route_probs * chosen
    result = resid + gate_weights[:, E + 1 : E + 2] * normed
    const_logits = jnp.dot(narrow, wconst, preferred_element_type=jnp.float32)
    vconst_f = vconst.astype(jnp.float32)
    const_mixes = []
    const_branches = []
    for const_idx in range(CONSTS):
        part_logits = const_logits[:, 2 * const_idx : 2 * const_idx + 2]
        part_exp = jnp.exp(part_logits - jnp.max(part_logits, axis=1, keepdims=True))
        const_mix = part_exp / jnp.sum(part_exp, axis=1, keepdims=True)
        branch = const_mix[:, 0:1] * normed + const_mix[:, 1:2] * vconst_f[:, const_idx][None, :]
        const_mixes.append(const_mix)
        const_branches.append(branch)
        result = result + gate_weights[:, E + 2 + const_idx : E + 3 + const_idx] * branch
    slot_list = []
    filled_list = []
    slot_gate_list = []
    for expert in range(E):
        member = (routes[:, 0] == expert) | (routes[:, 1] == expert)
        place_at = jnp.cumsum(member.astype(jnp.int32)) - 1
        slot_table = (
            jnp.zeros((MOST,), jnp.int32)
            .at[jnp.where(member, place_at, MOST)]
            .set(jnp.arange(TOK_DEV, dtype=jnp.int32), mode="drop")
        )
        filled = jnp.arange(MOST, dtype=jnp.int32) < jnp.sum(member.astype(jnp.int32))
        slot_list.append(slot_table)
        filled_list.append(filled)
        slot_gate_list.append(jnp.where(filled, jnp.take(gate_weights[:, expert], slot_table), 0.0))
    slot_tables = jnp.stack(slot_list, axis=0)
    filled_all = jnp.stack(filled_list, axis=0)
    slot_gates = jnp.stack(slot_gate_list, axis=0)
    expert_kept = []
    out_list = []
    for expert in range(E):
        picked = jnp.take(narrow, slot_tables[expert], axis=0)
        gate_part = jnp.dot(picked, wgate[expert], preferred_element_type=jnp.float32)
        up_part = jnp.dot(picked, wup[expert], preferred_element_type=jnp.float32)
        hidden = (jax.nn.silu(gate_part) * up_part).astype(jnp.bfloat16)
        out_list.append(jnp.dot(hidden, wdown[expert], preferred_element_type=jnp.float32))
        expert_kept.append((picked, gate_part, up_part, hidden))
    expert_outs = jnp.stack(out_list, axis=0)
    for expert in range(E):
        result = result.at[slot_tables[expert]].add(
            slot_gates[expert][:, None] * expert_outs[expert]
        )
    output = result.astype(jnp.bfloat16)
    (
        gain1,
        weight_q,
        weight_k,
        weight_v,
        weight_o,
        gain2,
        router,
        wconst,
        vconst,
        wgate,
        wup,
        wdown,
    ) = collect()
    gain1_f = gain1.astype(jnp.float32)
    gain2_f = gain2.astype(jnp.float32)
    router_f = router.astype(jnp.float32)
    wconst_f = wconst.astype(jnp.float32)
    vconst_f = vconst.astype(jnp.float32)
    grad_out = cotangent.astype(jnp.float32)
    d_gate_cols = [jnp.zeros((TOK_DEV,), jnp.float32) for expert in range(EXPERTS_ALL)]
    d_gate_cols[E + 1] = jnp.sum(grad_out * normed, axis=1)
    d_normed = gate_weights[:, E + 1 : E + 2] * grad_out
    d_const_parts = []
    d_vconst_cols = []
    for const_idx in range(CONSTS):
        const_mix = const_mixes[const_idx]
        gate_col = gate_weights[:, E + 2 + const_idx]
        d_gate_cols[E + 2 + const_idx] = jnp.sum(grad_out * const_branches[const_idx], axis=1)
        d_piece = gate_col[:, None] * grad_out
        d_normed = d_normed + const_mix[:, 0:1] * d_piece
        d_cmix = jnp.stack(
            [
                jnp.sum(d_piece * normed, axis=1),
                jnp.sum(d_piece * vconst_f[:, const_idx][None, :], axis=1),
            ],
            axis=1,
        )
        d_const_parts.append(
            const_mix * (d_cmix - jnp.sum(const_mix * d_cmix, axis=1, keepdims=True))
        )
        d_vconst_cols.append(exact_dot(const_mix[:, 1] * gate_col, grad_out))
    d_const_logits = jnp.concatenate(d_const_parts, axis=1)
    grad_rows_all = jnp.take(grad_out, slot_tables.reshape(-1), axis=0).reshape(
        E, MOST, model_width
    )
    d_slot_gates = jnp.where(filled_all, jnp.sum(grad_rows_all * expert_outs, axis=2), 0.0)
    for expert in range(E):
        d_gate_cols[expert] = (
            jnp.zeros((TOK_DEV,), jnp.float32).at[slot_tables[expert]].add(d_slot_gates[expert])
        )
    d_expert_all = (slot_gates[:, :, None] * grad_rows_all).astype(jnp.bfloat16)
    d_wgate_list = []
    d_wup_list = []
    d_wdown_list = []
    d_picked_list = []
    for expert in range(E):
        picked, gate_part, up_part, hidden = expert_kept[expert]
        d_expert = d_expert_all[expert]
        d_wdown_list.append(jnp.dot(hidden.T, d_expert, preferred_element_type=jnp.float32))
        d_hidden = jnp.dot(d_expert, wdown[expert].T, preferred_element_type=jnp.float32)
        sigmoid_g = jax.nn.sigmoid(gate_part)
        d_up_part = (d_hidden * gate_part * sigmoid_g).astype(jnp.bfloat16)
        d_gate_part = (
            d_hidden * up_part * sigmoid_g * (1.0 + gate_part * (1.0 - sigmoid_g))
        ).astype(jnp.bfloat16)
        d_wgate_list.append(jnp.dot(picked.T, d_gate_part, preferred_element_type=jnp.float32))
        d_wup_list.append(jnp.dot(picked.T, d_up_part, preferred_element_type=jnp.float32))
        d_picked_list.append(
            jnp.dot(d_gate_part, wgate[expert].T, preferred_element_type=jnp.float32)
            + jnp.dot(d_up_part, wup[expert].T, preferred_element_type=jnp.float32)
        )
    d_picked_all = jnp.stack(d_picked_list, axis=0)
    d_wgate_full = jnp.stack(d_wgate_list, axis=0)
    d_wup_full = jnp.stack(d_wup_list, axis=0)
    d_wdown_full = jnp.stack(d_wdown_list, axis=0)
    d_narrow = jnp.zeros((TOK_DEV, model_width), jnp.float32)
    for expert in range(E):
        d_narrow = d_narrow.at[slot_tables[expert]].add(
            jnp.where(filled_all[expert][:, None], d_picked_all[expert], 0.0)
        )
    d_gate_w = jnp.stack(d_gate_cols, axis=1)
    d_probs = d_gate_w * chosen
    d_logits = route_probs * (d_probs - jnp.sum(route_probs * d_probs, axis=1, keepdims=True))
    narrow_f = narrow.astype(jnp.float32)
    d_narrow = d_narrow + exact_dot(d_logits, router_f.T) + exact_dot(d_const_logits, wconst_f.T)
    d_router_full = exact_dot(narrow_f.T, d_logits)
    d_wconst_full = exact_dot(narrow_f.T, d_const_logits)
    d_vconst_full = jnp.stack(d_vconst_cols, axis=1)
    d_mix_full = exact_dot(prev_logits.T, d_logits)
    grad_prev = exact_dot(d_logits, mix_f.T)
    d_normed_total = d_normed + d_narrow
    d_gain2_full = jnp.sum(d_normed_total * unit_two, axis=0)
    d_unit_two = d_normed_total * gain2_f
    d_resid = grad_out + inv_two * (
        d_unit_two - unit_two * jnp.mean(d_unit_two * unit_two, axis=1, keepdims=True)
    )
    d_attn = deal(d_resid.astype(jnp.bfloat16))
    d_wo_full = jnp.dot(mixed.T, d_attn, preferred_element_type=jnp.float32)
    d_mixed = jnp.dot(d_attn, weight_o.T, preferred_element_type=jnp.float32).astype(jnp.bfloat16)

    def attend_back(pair_items):
        q_pair, k_pair, v_pair, dm_pair, lse_pair = pair_items
        scores, query_heads, key_heads = pair_scores(q_pair, k_pair)
        attn_probs = jnp.where(allowed[None], jnp.exp(scores - lse_pair[:, :, None]), 0.0)
        value_heads = v_pair.reshape(CAP, 2, HEAD_DIM)
        dm_heads = dm_pair.reshape(CAP, 2, HEAD_DIM)
        d_p = jnp.einsum("qhd,khd->hqk", dm_heads, value_heads, preferred_element_type=jnp.float32)
        row_delta = jnp.sum(attn_probs * d_p, axis=-1, keepdims=True)
        d_scores = (attn_probs * (d_p - row_delta)).astype(jnp.bfloat16)
        d_q = (
            jnp.einsum("hqk,khd->qhd", d_scores, key_heads, preferred_element_type=jnp.float32)
            * scale
        )
        d_k = (
            jnp.einsum("hqk,qhd->khd", d_scores, query_heads, preferred_element_type=jnp.float32)
            * scale
        )
        d_v = jnp.einsum(
            "hqk,qhd->khd",
            attn_probs.astype(jnp.bfloat16),
            dm_heads,
            preferred_element_type=jnp.float32,
        )
        return (
            d_q.reshape(CAP, pair_width),
            d_k.reshape(CAP, pair_width),
            d_v.reshape(CAP, pair_width),
        )

    dq_pairs, dk_pairs, dv_pairs = lax.map(
        attend_back,
        (by_pairs(query), by_pairs(keyed), by_pairs(values_proj), by_pairs(d_mixed), log_sums),
    )
    d_query = rotate(from_pairs(dq_pairs), cos_table, -sin_table).astype(jnp.bfloat16)
    d_key = rotate(from_pairs(dk_pairs), cos_table, -sin_table).astype(jnp.bfloat16)
    d_value = from_pairs(dv_pairs).astype(jnp.bfloat16)
    d_wq_full = jnp.dot(normed_one.T, d_query, preferred_element_type=jnp.float32)
    d_wk_full = jnp.dot(normed_one.T, d_key, preferred_element_type=jnp.float32)
    d_wv_full = jnp.dot(normed_one.T, d_value, preferred_element_type=jnp.float32)
    d_normed_one = (
        jnp.dot(d_query, weight_q.T, preferred_element_type=jnp.float32)
        + jnp.dot(d_key, weight_k.T, preferred_element_type=jnp.float32)
        + jnp.dot(d_value, weight_v.T, preferred_element_type=jnp.float32)
    )
    d_gain1_full = jnp.sum(d_normed_one * unit_one, axis=0)
    d_unit_one = d_normed_one * gain1_f
    d_dealt = (
        inv_one * (d_unit_one - unit_one * jnp.mean(d_unit_one * unit_one, axis=1, keepdims=True))
    ).astype(jnp.bfloat16)
    grad_tokens = d_resid + give_back(d_dealt).astype(jnp.float32)

    def regroup(grads_in):
        tail_shape = grads_in.shape[1:]
        split_view = grads_in.reshape((groups, dealers, per_shard) + tail_shape)
        return jnp.swapaxes(split_view, 0, 1).reshape((model_width,) + tail_shape)

    mix_tile = jnp.broadcast_to(d_mix_full[None], (dealers, EXPERTS_ALL, EXPERTS_ALL))
    sectioned = (
        lax.psum_scatter(
            regroup(d_gain1_full).astype(jnp.bfloat16), "fsdp", scatter_dimension=0, tiled=True
        ).astype(jnp.float32),
        lax.psum_scatter(
            d_wq_full.astype(jnp.bfloat16), "fsdp", scatter_dimension=0, tiled=True
        ).astype(jnp.float32),
        lax.psum_scatter(
            d_wk_full.astype(jnp.bfloat16), "fsdp", scatter_dimension=0, tiled=True
        ).astype(jnp.float32),
        lax.psum_scatter(
            d_wv_full.astype(jnp.bfloat16), "fsdp", scatter_dimension=0, tiled=True
        ).astype(jnp.float32),
        lax.psum_scatter(
            d_wo_full.astype(jnp.bfloat16), "fsdp", scatter_dimension=0, tiled=True
        ).astype(jnp.float32),
        lax.psum_scatter(
            regroup(d_gain2_full).astype(jnp.bfloat16), "fsdp", scatter_dimension=0, tiled=True
        ).astype(jnp.float32),
        lax.psum_scatter(
            regroup(d_router_full).astype(jnp.bfloat16), "fsdp", scatter_dimension=0, tiled=True
        ).astype(jnp.float32),
        lax.psum_scatter(
            regroup(d_wconst_full).astype(jnp.bfloat16), "fsdp", scatter_dimension=0, tiled=True
        ).astype(jnp.float32),
        lax.psum_scatter(
            regroup(d_vconst_full).astype(jnp.bfloat16), "fsdp", scatter_dimension=0, tiled=True
        ).astype(jnp.float32),
        lax.psum_scatter(
            mix_tile.astype(jnp.bfloat16), "fsdp", scatter_dimension=0, tiled=True
        ).astype(jnp.float32),
        lax.psum_scatter(
            d_wgate_full.astype(jnp.bfloat16), "fsdp", scatter_dimension=1, tiled=True
        ).astype(jnp.float32),
        lax.psum_scatter(
            d_wup_full.astype(jnp.bfloat16), "fsdp", scatter_dimension=1, tiled=True
        ).astype(jnp.float32),
        lax.psum_scatter(
            d_wdown_full.astype(jnp.bfloat16), "fsdp", scatter_dimension=2, tiled=True
        ).astype(jnp.float32),
    )
    s_g1, s_q, s_k, s_v, s_o, s_g2, s_r, s_c, s_vc, s_mix, s_gate, s_up, s_down = sectioned
    summed = (
        lax.psum_scatter(s_g1.astype(jnp.bfloat16), "grp", scatter_dimension=0, tiled=True).astype(
            jnp.float32
        ),
        lax.psum_scatter(s_q.astype(jnp.bfloat16), "grp", scatter_dimension=1, tiled=True).astype(
            jnp.float32
        ),
        lax.psum_scatter(s_k.astype(jnp.bfloat16), "grp", scatter_dimension=1, tiled=True).astype(
            jnp.float32
        ),
        lax.psum_scatter(s_v.astype(jnp.bfloat16), "grp", scatter_dimension=1, tiled=True).astype(
            jnp.float32
        ),
        lax.psum_scatter(s_o.astype(jnp.bfloat16), "grp", scatter_dimension=1, tiled=True).astype(
            jnp.float32
        ),
        lax.psum_scatter(s_g2.astype(jnp.bfloat16), "grp", scatter_dimension=0, tiled=True).astype(
            jnp.float32
        ),
        lax.psum_scatter(s_r.astype(jnp.bfloat16), "grp", scatter_dimension=0, tiled=True).astype(
            jnp.float32
        ),
        lax.psum_scatter(s_c.astype(jnp.bfloat16), "grp", scatter_dimension=0, tiled=True).astype(
            jnp.float32
        ),
        lax.psum_scatter(s_vc.astype(jnp.bfloat16), "grp", scatter_dimension=0, tiled=True).astype(
            jnp.float32
        ),
        lax.psum_scatter(
            jnp.broadcast_to(s_mix, (groups, EXPERTS_ALL, EXPERTS_ALL)).astype(jnp.bfloat16),
            "grp",
            scatter_dimension=0,
            tiled=True,
        ).astype(jnp.float32),
    )
    (
        grad_gain_one,
        grad_query,
        grad_key,
        grad_value,
        grad_out_proj,
        grad_gain_two,
        grad_router,
        grad_const,
        grad_vconst,
        mix_part,
    ) = summed
    grad_mix = mix_part[0]
    grad_gate, grad_up, grad_down = (
        lax.psum_scatter(
            s_gate.astype(jnp.bfloat16), "grp", scatter_dimension=2, tiled=True
        ).astype(jnp.float32),
        lax.psum_scatter(s_up.astype(jnp.bfloat16), "grp", scatter_dimension=2, tiled=True).astype(
            jnp.float32
        ),
        lax.psum_scatter(
            s_down.astype(jnp.bfloat16), "grp", scatter_dimension=1, tiled=True
        ).astype(jnp.float32),
    )
    return (
        output,
        grad_tokens,
        grad_prev,
        grad_gain_one,
        grad_query,
        grad_key,
        grad_value,
        grad_out_proj,
        grad_gain_two,
        grad_router,
        grad_mix,
        grad_const,
        grad_vconst,
        grad_gate,
        grad_up,
        grad_down,
    )


HALO = 256
KEYS = HALO + TOK_DEV
ROWS = E * MOST
NEG = -1e30
F32 = jnp.float32
BF16 = jnp.bfloat16
NT = (((1,), (1,)), ((), ()))
TN = (((0,), (0,)), ((), ()))
NN = (((1,), (0,)), ((), ()))


def mm(a, b, dims=NN):
    return lax.dot_general(a, b, dims, preferred_element_type=F32)


def lane_iota(rows, width=128):
    return lax.broadcasted_iota(jnp.int32, (rows, width), 1)


def pick(values, lane_mask):
    return jnp.sum(jnp.where(lane_mask, values, 0.0), axis=1, keepdims=True)


def params(mb, **kw):
    return pltpu.CompilerParams(vmem_limit_bytes=mb << 20, **kw)


def whole(count):
    return [pl.BlockSpec(memory_space=pltpu.VMEM) for _ in range(count)]


def sds(shape, dtype):
    return jax.ShapeDtypeStruct(shape, dtype)


MESH_ID = pl.DeviceIdType.MESH


def send(src, dst, send_sem, recv_sem, device):
    pltpu.make_async_remote_copy(
        src_ref=src,
        dst_ref=dst,
        send_sem=send_sem,
        recv_sem=recv_sem,
        device_id=device,
        device_id_type=MESH_ID,
    ).start()


def settle(ref, sem):
    pltpu.make_async_copy(ref, ref, sem).wait()


def flip(a, b):
    return a + b - 2 * a * b


def xor4(a, b):
    return flip(a // 2, b // 2) * 2 + flip(lax.rem(a, 2), lax.rem(b, 2))


def aligned(value, to):
    return pl.multiple_of(value, to)


class Place:
    def __init__(self, his, lo):
        self.g = lax.axis_index("grp")
        self.f = lax.axis_index("fsdp")
        self.his, self.lo = his, lo
        self.hi = self.g // lo
        self.l = lax.rem(self.g, lo)
        self.m = self.f * his + self.hi
        core = lax.rem(self.g, 2)
        side = lax.rem(self.g // 2, 2)
        self.core_peer = self.g + 1 - 2 * core
        self.side_peer = self.g + 2 - 4 * side
        self.l1 = lax.rem(self.core_peer, lo)
        self.l2 = lax.rem(self.side_peer, lo)
        self.l3 = lo - 1 - self.l

    def member(self, j, hh):
        f = xor4(self.f, j)
        hi = flip(self.hi, hh)
        return f * self.his + hi, (hi * self.lo + self.l, f)

    def others(self):
        peers = []
        for j in range(4):
            for hh in range(self.his):
                if j or hh:
                    peers.append(self.member(j, hh)[1])
        return peers


def call(peers):
    barrier = pltpu.get_barrier_semaphore()
    for peer in peers:
        pl.semaphore_signal(barrier, inc=1, device_id=peer, device_id_type=MESH_ID)


def answer(peers):
    pl.semaphore_wait(pltpu.get_barrier_semaphore(), len(peers))


def turn(values, cos, sin):
    half = HEAD_DIM // 2
    width = values.shape[1]
    reps = width // 128
    front = lax.rem(lane_iota(values.shape[0], width), HEAD_DIM) < half
    swapped = jnp.where(
        front, pltpu.roll(values, width - half, 1), pltpu.roll(values, half, 1)
    )
    cos_w = jnp.concatenate([cos] * reps, axis=1)
    sin_w = jnp.concatenate([sin] * reps, axis=1)
    return values * cos_w + swapped * sin_w


QBLOCKS = [(0, 128), (128, 128), (256, 64)]


def allowed_mask(pos_ref, first, count, lane):
    ii = lax.broadcasted_iota(jnp.int32, (count, 384), 0) + HALO
    jj = lax.broadcasted_iota(jnp.int32, (count, 384), 1)
    pos = pos_ref[pl.ds(first, count), lane : lane + 1].astype(jnp.int32)
    return (jj <= ii) & (jj >= ii - pos)


def key_span(first):
    return min(384, KEYS - first)


KEPT = (
    ("wf", (4, None, None), BF16),
    ("s", (None, 128), F32),
    ("halo", (HALO, None), BF16),
    ("q", (TOK_DEV, None), BF16),
    ("k", (KEYS, None), BF16),
    ("v", (KEYS, None), BF16),
    ("n1", (KEYS, None), BF16),
    ("inv1", (KEYS, 128), F32),
    ("mix", (TOK_DEV, None), BF16),
    ("lse", (TOK_DEV, 128), F32),
    ("resid", (TOK_DEV, None), F32),
    ("part", (TOK_DEV, None), F32),
    ("probs", (TOK_DEV, 128), F32),
    ("cols", (TOK_DEV, 128), F32),
    ("cos", (KEYS, 128), F32),
    ("sin", (KEYS, 128), F32),
)


def kept_shape(dims, width):
    return tuple(width if d is None else d for d in dims)


def by_name(refs):
    return {name: ref for (name, _, _), ref in zip(KEPT, refs)}


def token_places(len_ref, at):
    row = lax.broadcasted_iota(jnp.int32, (KEYS, 128), 0) + (at.f * TOK_DEV - HALO)
    first = jnp.zeros((KEYS, 128), jnp.int32)
    reached = jnp.int32(0)
    for i in range(len_ref.shape[1]):
        reached = reached + len_ref[0, i]
        first = jnp.where(row >= reached, reached, first)
    return jnp.maximum(row - first, 0)


def ahead_kernel(
    len_ref,
    routes_ref,
    prev_ref,
    wmix_ref,
    router_ref,
    gain1_ref,
    gain2_ref,
    const_ref,
    vconst_ref,
    wq_ref,
    wk_ref,
    wv_ref,
    wo_ref,
    tok_ref,
    cot_ref,
    wg_hbm,
    wu_hbm,
    wd_hbm,
    *rest,
):
    n = len(KEPT)
    kept_hbm = by_name(rest[:n])
    op_hbm, gw_hbm, back_hbm, dgb_hbm = rest[n : n + 4]
    kept = by_name(rest[n + 4 : 2 * n + 4])
    (
        tile_ref,
        small_ref,
        p_ref,
        grow_ref,
        x_ref,
        gates_ref,
        wgu_ref,
        wd_ref,
        g_ref,
        xb_ref,
        gb_ref,
        od_ref,
        op_ref,
        r1_ref,
        r2_ref,
        dgp_ref,
        dr1_ref,
        dr2_ref,
        accgu_ref,
        accd_ref,
        hid_ref,
        dgu_ref,
        gw_ref,
        back_ref,
        dgb_ref,
        keep_sem,
        last_sem,
        zs,
        ps,
        cs,
        hs,
        gs,
        ws,
        gas,
        agr,
        hr,
        gr,
        wr,
        gqr,
        xs,
        ts,
        qs,
        tqs,
        d1s,
        t1s,
        d2s,
        t2s,
        bs,
        tbs,
        xr,
        tr,
        qr,
        tqr,
        d1r,
        t1r,
        d2r,
        t2r,
        br,
        tbr,
    ) = rest[2 * n + 4 :]
    wf_ref, s_ref, halo_ref = kept["wf"], kept["s"], kept["halo"]
    q_ref, k_ref, v_ref, n1_ref = kept["q"], kept["k"], kept["v"], kept["n1"]
    mix_ref, lse_ref = kept["mix"], kept["lse"]
    lo, ranks = g_ref.shape[:2]
    his = E // ranks
    at = Place(his, lo)
    width = tok_ref.shape[1]
    head_rows, part_cols = wq_ref.shape
    ff = wg_hbm.shape[2]
    diag = lo * (1 - at.hi) + at.l2
    upper = lo * (1 - at.hi) + at.l
    near = [(at.core_peer, at.f), (at.side_peer, at.f), (upper, at.f), (diag, at.f)]
    core, side = near[0], near[1]
    peers = at.others() + [near[0], near[1], near[3]]
    call(peers)

    def keep(*names):
        for name in names:
            i = [k[0] for k in KEPT].index(name)
            pltpu.make_async_copy(kept[name], kept_hbm[name], keep_sem.at[i]).start()

    tile_ref[0:head_rows, :] = jnp.concatenate(
        [wq_ref[...], wk_ref[...], wv_ref[...], wo_ref[...]], axis=1
    )
    small_ref[...] = jnp.zeros_like(small_ref)
    per = router_ref.shape[1]
    small_ref[0:EXPERTS_ALL, 0:per] = router_ref[...].astype(F32)
    small_ref[SMALL_G1 : SMALL_G1 + 1, 0:per] = gain1_ref[...].astype(F32)
    small_ref[SMALL_G1 + 1 : SMALL_G1 + 2, 0:per] = gain2_ref[...].astype(F32)
    small_ref[SMALL_VC : SMALL_VC + CONSTS, 0:per] = vconst_ref[...].astype(F32)
    small_ref[SMALL_C : SMALL_C + 2 * CONSTS, 0:per] = const_ref[...].astype(F32)
    turned = small_ref[...].T
    tile_ref[head_rows : head_rows + 8, :] = jnp.concatenate(
        [turned[8 * i : 8 * i + 8, :] for i in range(per // 8)], axis=1
    ).astype(BF16)
    answer(peers)

    p_ref[at.g, at.f] = tile_ref[...]
    for j in range(1, ranks):
        f2 = xor4(at.f, j)
        send(tile_ref, p_ref.at[at.g, at.f], zs.at[j], agr.at[at.g, at.f], (at.g, f2))

    def spread(j, f2, src):
        for t, peer in enumerate(near):
            send(src, p_ref.at[at.g, f2], ps.at[j, t], agr.at[at.g, f2], peer)

    spread(0, at.f, tile_ref)
    halo_rows = halo_ref.shape[0]
    tail = tok_ref.at[pl.ds(tok_ref.shape[0] - halo_rows, halo_rows)]

    @pl.when(at.f < ranks - 1)
    def _():
        send(tail, halo_ref, hs, hr, (at.g, at.f + 1))

    @pl.when(at.f == 0)
    def _():
        halo_ref[...] = jnp.zeros_like(halo_ref)

    lanes = lane_iota(TOK_DEV)
    routes = jnp.concatenate(
        [
            jnp.broadcast_to(routes_ref[0:1, :], (8, TOK_DEV)),
            jnp.broadcast_to(routes_ref[1:2, :], (8, TOK_DEV)),
        ],
        axis=0,
    ).T
    r0 = routes[:, 0:1]
    r1 = routes[:, 8:9]
    hot0 = lanes == r0
    hot1 = lanes == r1
    named = jnp.where(hot0 | hot1, 1.0, 0.0).astype(BF16)
    earlier = (
        lax.broadcasted_iota(jnp.int32, (TOK_DEV, TOK_DEV), 1)
        < lax.broadcasted_iota(jnp.int32, (TOK_DEV, TOK_DEV), 0)
    )
    rank = mm(jnp.where(earlier, 1.0, 0.0).astype(BF16), named)
    rank0 = pick(rank, hot0).astype(jnp.int32)
    rank1 = pick(rank, hot1).astype(jnp.int32)
    c0 = jnp.where(r0 < E, r0 * MOST + rank0, -1)
    c1 = jnp.where(r1 < E, r1 * MOST + rank1, -1)
    slot = lane_iota(TOK_DEV, ROWS)
    spots0 = jnp.where(slot == c0, 1.0, 0.0).astype(BF16)
    spots1 = jnp.where(slot == c1, 1.0, 0.0).astype(BF16)
    grow_ref[...] = mm(spots0 + spots1, cot_ref[...], TN).astype(BF16)

    for j in range(1, ranks):
        f2 = xor4(at.f, j)
        settle(p_ref.at[at.g, f2], agr.at[at.g, f2])
        spread(j, f2, p_ref.at[at.g, f2])

    own_rows = pl.ds(aligned(at.f * head_rows, 16), head_rows)
    own_cols = pl.ds(aligned(at.hi * ff, 128), ff)
    own_spot = pl.ds(aligned(at.hi * MOST, 16), MOST)

    for j in range(ranks):
        for hh in range(his):
            e, peer = at.member(j, hh)
            rows = grow_ref.at[pl.ds(aligned(e * MOST, 16), MOST)]
            spot = g_ref.at[at.l, at.f, own_spot]
            if j == 0 and hh == 0:
                pltpu.make_async_copy(rows, spot, gr.at[at.m]).start()
            else:
                send(rows, spot, gs.at[j * his + hh], gr.at[at.m], peer)

    def dispatch():
        for j in range(ranks):
            for hh in range(his):
                e, peer = at.member(j, hh)
                sources = (wg_hbm.at[e], wu_hbm.at[e], wd_hbm.at[e])
                for w in range(3):
                    first = aligned(w * his * ff + at.hi * ff, 128)
                    spot = (
                        wd_ref.at[own_rows, own_cols]
                        if w == 2
                        else wgu_ref.at[own_rows, pl.ds(first, ff)]
                    )
                    if j == 0 and hh == 0:
                        pltpu.make_async_copy(sources[w], spot, wr.at[at.m, w]).start()
                    else:
                        send(sources[w], spot, ws.at[j * his + hh, w], wr.at[at.m, w], peer)

    pos = token_places(len_ref, at).astype(F32)
    half_dim = HEAD_DIM // 2
    lane_k = lane_iota(KEYS)
    freq = jnp.exp(
        lax.rem(lane_k, half_dim).astype(F32) * (-2.0 * math.log(10000.0) / HEAD_DIM)
    )
    kept["cos"][...] = jnp.cos(pos * freq)
    sine = jnp.sin(pos * freq)
    kept["sin"][...] = jnp.where(lax.rem(lane_k, HEAD_DIM) < half_dim, -sine, sine)
    pos_own = pos[HALO:]
    pos_ref = kept["cols"]
    pos_ref[...] = pos_own

    for j in range(ranks):
        f2 = xor4(at.f, j)
        for t in range(1, 4):
            g2 = near[t][0]
            settle(p_ref.at[g2, f2], agr.at[g2, f2])
            send(p_ref.at[g2, f2], p_ref.at[g2, f2], cs.at[t - 1, j], agr.at[g2, f2], near[0])
    sibling_upper = lo * (1 - at.hi) + at.l1
    for j in range(ranks):
        f2 = xor4(at.f, j)
        for g2 in (
            at.core_peer,
            at.hi * lo + at.l3,
            sibling_upper,
            lo * (1 - at.hi) + at.l3,
        ):
            settle(p_ref.at[g2, f2], agr.at[g2, f2])

    dispatch()

    groups = p_ref.shape[0]
    for g2 in range(groups):
        for f2 in range(ranks):
            piece = p_ref[g2, f2, head_rows : head_rows + 8, :].astype(F32)
            for i in range(per // 8):
                base = (g2 * ranks + f2) * per + 8 * i
                s_ref[base : base + 8, :] = piece[:, 128 * i : 128 * i + 128]

    def lay(f2, _):
        rows = pl.ds(aligned(f2 * head_rows, 16), head_rows)
        for w in range(4):
            for half in range(2):
                pieces = [
                    p_ref[
                        half * (groups // 2) + i,
                        f2,
                        0:head_rows,
                        w * part_cols : (w + 1) * part_cols,
                    ]
                    for i in range(groups // 2)
                ]
                wf_ref[w, rows, half * (width // 2) : (half + 1) * (width // 2)] = (
                    jnp.concatenate(pieces, axis=1)
                )
        return 0

    lax.fori_loop(0, ranks, lay, 0)

    @pl.when(at.f > 0)
    def _():
        settle(halo_ref, hr)

    scale = HEAD_DIM ** (-0.5)
    flat = s_ref[...].T
    g1 = flat[SMALL_G1 : SMALL_G1 + 1, :]
    g2 = flat[SMALL_G1 + 1 : SMALL_G1 + 2, :]
    vc = flat[SMALL_VC : SMALL_VC + CONSTS, :]
    keep("wf", "s", "halo")
    rows = jnp.concatenate([halo_ref[...], tok_ref[...]], axis=0).astype(F32)
    inv1 = lax.rsqrt(jnp.mean(rows * rows, axis=1, keepdims=True) + NORM_EPS)
    kept["inv1"][...] = jnp.broadcast_to(inv1, (KEYS, 128))
    n1_ref[...] = (rows * inv1 * g1).astype(BF16)

    def project(i, _):
        span = pl.ds(pl.multiple_of(i * 256, 256), 256)
        cos = kept["cos"][...]
        sin = kept["sin"][...]
        q = mm(n1_ref[HALO:, :], wf_ref[0, :, span])
        q_ref[:, span] = turn(q, cos[HALO:], sin[HALO:]).astype(BF16)
        k = mm(n1_ref[...], wf_ref[1, :, span])
        k_ref[:, span] = turn(k, cos, sin).astype(BF16)
        v_ref[:, span] = mm(n1_ref[...], wf_ref[2, :, span]).astype(BF16)
        return 0

    lax.fori_loop(0, width // 256, project, 0)
    keep("q", "k", "v", "n1", "inv1", "cos", "sin")
    lse_ref[...] = jnp.zeros((TOK_DEV, 128), F32)

    for f2 in range(ranks):
        for h2 in range(his):
            settle(
                g_ref.at[at.l, f2, h2 * MOST : (h2 + 1) * MOST], gr.at[f2 * his + h2]
            )
    send(g_ref.at[at.l], g_ref.at[at.l], gas.at[0], gqr.at[0], near[0])
    send(g_ref.at[at.l], g_ref.at[at.l], gas.at[1], gqr.at[1], near[1])

    def pair(p, _):
        span = pl.ds(pl.multiple_of(p * 128, 128), 128)
        for first, count in QBLOCKS:
            keys = key_span(first)
            ok = allowed_mask(pos_ref, first, count, 0)[:, :keys]
            q = q_ref[pl.ds(first, count), span]
            k = k_ref[pl.ds(first, keys), span]
            v = v_ref[pl.ds(first, keys), span]
            lane = lane_iota(count)
            out = None
            lse = lse_ref[pl.ds(first, count), :]
            for h in range(2):
                mine = (lane < HEAD_DIM) if h == 0 else (lane >= HEAD_DIM)
                qh = jnp.where(mine, q, jnp.zeros_like(q))
                sc = jnp.where(ok, mm(qh, k, NT) * scale, NEG)
                top = jnp.max(sc, axis=1, keepdims=True)
                ex = jnp.exp(sc - top)
                total = jnp.sum(ex, axis=1, keepdims=True)
                o = mm((ex / total).astype(BF16), v)
                out = o if h == 0 else jnp.where(mine, o, out)
                lse = jnp.where(lane == 2 * p + h, top + jnp.log(total), lse)
            mix_ref[pl.ds(first, count), span] = out.astype(BF16)
            lse_ref[pl.ds(first, count), :] = lse
        return 0

    lax.fori_loop(0, HEADS // 2, pair, 0)
    settle(g_ref.at[at.l2], gqr.at[1])
    send(g_ref.at[at.l2], g_ref.at[at.l2], gas.at[2], gqr.at[2], near[0])

    attn_out = mm(mix_ref[...], wf_ref[3]).astype(BF16)
    resid = tok_ref[...].astype(F32) + attn_out.astype(F32)
    kept["resid"][...] = resid
    inv2 = lax.rsqrt(jnp.mean(resid * resid, axis=1, keepdims=True) + NORM_EPS)
    normed = resid * inv2 * g2
    narrow = normed.astype(BF16)
    raw = mm(narrow, s_ref[...].astype(BF16))
    prev = prev_ref[...]
    wmix = jnp.concatenate(
        [wmix_ref[...].astype(F32), jnp.zeros((EXPERTS_ALL, 128 - EXPERTS_ALL), F32)], axis=1
    ).astype(BF16)
    phigh = prev.astype(BF16)
    prest = prev - phigh.astype(F32)
    pmid = prest.astype(BF16)
    plow = (prest - pmid.astype(F32)).astype(BF16)
    mixed_prev = mm(phigh, wmix, TN) + (mm(pmid, wmix, TN) + mm(plow, wmix, TN))
    logits = jnp.where(lanes < EXPERTS_ALL, raw + mixed_prev, NEG)
    top = jnp.max(logits, axis=1, keepdims=True)
    ex = jnp.exp(logits - top)
    probs = ex / jnp.sum(ex, axis=1, keepdims=True)
    kept["probs"][...] = probs
    gate0 = pick(probs, hot0)
    gate1 = pick(probs, hot1)

    def gate_of(expert):
        return jnp.where(r0 == expert, gate0, 0.0) + jnp.where(r1 == expert, gate1, 0.0)

    gate_id = gate_of(E + 1)
    part = resid + gate_id * normed
    cols = jnp.where(lanes == 0, gate0, 0.0)
    cols = jnp.where(lanes == 1, gate1, cols)
    cols = jnp.where(lanes == 2, gate_id, cols)
    cols = jnp.where(lanes == 3, inv2, cols)
    for c in range(CONSTS):
        la = pick(raw, lanes == SMALL_C + 2 * c)
        lb = pick(raw, lanes == SMALL_C + 1 + 2 * c)
        big = jnp.maximum(la, lb)
        ea = jnp.exp(la - big)
        eb = jnp.exp(lb - big)
        ma = ea / (ea + eb)
        mb = eb / (ea + eb)
        gate_c = gate_of(E + 2 + c)
        part = part + gate_c * (ma * normed + mb * vc[c : c + 1, :])
        cols = jnp.where(lanes == 4 + 3 * c, gate_c, cols)
        cols = jnp.where(lanes == 5 + 3 * c, ma, cols)
        cols = jnp.where(lanes == 6 + 3 * c, mb, cols)
    kept["part"][...] = part
    wide0 = jnp.where(r0 < E, r0 * 128 + rank0, -1)
    wide1 = jnp.where(r1 < E, r1 * 128 + rank1, -1)
    more = (pos_own[:, 0:1], c0, c1, r0, r1, wide0, wide1)
    for i, value in enumerate(more):
        cols = jnp.where(lanes == COL_POS + i, value.astype(F32), cols)
    kept["cols"][...] = cols
    keep("mix", "lse", "resid", "part", "probs", "cols")
    x_ref[...] = mm(spots0 + spots1, narrow, TN).astype(BF16)
    for e in range(E):
        lane = lanes + e * 128
        row = jnp.sum(
            jnp.where(lane == wide0, gate0, 0.0) + jnp.where(lane == wide1, gate1, 0.0),
            axis=0,
            keepdims=True,
        )
        gates_ref[e] = jnp.broadcast_to(row, (8, 128))


    def give(j):
        for hh in range(his):
            e, peer = at.member(j, hh)
            k = j * his + hh
            rows = x_ref.at[pl.ds(aligned(e * MOST, 16), MOST)]
            spot = xb_ref.at[at.f, at.l, own_spot]
            line = gb_ref.at[at.f, at.l, at.hi]
            if k == 0:
                pltpu.make_async_copy(rows, spot, xr.at[at.m]).start()
                pltpu.make_async_copy(gates_ref.at[e], line, tr.at[at.m]).start()
            else:
                send(rows, spot, xs.at[k], xr.at[at.m], peer)
                send(gates_ref.at[e], line, ts.at[k], tr.at[at.m], peer)

    give(0)
    give(1)
    accgu_ref[...] = jnp.zeros_like(accgu_ref)
    accd_ref[...] = jnp.zeros_like(accd_ref)

    def take(j):
        fj = xor4(at.f, j)
        for hh in range(his):
            hi = flip(at.hi, hh)
            m = fj * his + hi
            settle(xb_ref.at[fj, at.l, pl.ds(aligned(hi * MOST, 16), MOST)], xr.at[m])
            settle(gb_ref.at[fj, at.l, hi], tr.at[m])
        for i, peer in enumerate((core, side)):
            send(xb_ref.at[fj, at.l], xb_ref.at[fj, at.l], qs.at[fj, i], qr.at[fj, i], peer)
            send(gb_ref.at[fj, at.l], gb_ref.at[fj, at.l], tqs.at[fj, i], tqr.at[fj, i], peer)

    def pass_on(j):
        fj = xor4(at.f, j)
        settle(xb_ref.at[fj, at.l2], qr.at[fj, 1])
        settle(gb_ref.at[fj, at.l2], tqr.at[fj, 1])
        send(xb_ref.at[fj, at.l2], xb_ref.at[fj, at.l2], qs.at[fj, 2], qr.at[fj, 2], core)
        send(gb_ref.at[fj, at.l2], gb_ref.at[fj, at.l2], tqs.at[fj, 2], tqr.at[fj, 2], core)

    def compute(j):
        fj = xor4(at.f, j)
        settle(xb_ref.at[fj, at.l1], qr.at[fj, 0])
        settle(gb_ref.at[fj, at.l1], tqr.at[fj, 0])
        settle(xb_ref.at[fj, at.l3], qr.at[fj, 2])
        settle(gb_ref.at[fj, at.l3], tqr.at[fj, 2])
        slot_of_chunk = lax.rem(j, 2)

        @pl.when(j >= 2)
        def _():
            settle(op_ref.at[slot_of_chunk], last_sem.at[slot_of_chunk])

        diagonal = lax.broadcasted_iota(jnp.int32, (MOST, 128), 0) == lane_iota(MOST)
        pair_rows = 2 * his * MOST

        def rows_of(i, _):
            pl.when((i == 1) & (j >= 1))(lambda: to_side(j - 1))
            l2 = pl.ds(2 * i, 2)
            x = xb_ref[fj, l2].reshape(pair_rows, width)
            g = g_ref[l2, fj].reshape(pair_rows, width)
            gate = jnp.concatenate(
                [
                    pick(
                        jnp.broadcast_to(gb_ref[fj, 2 * i + i2, h][0:1, :], (MOST, 128)), diagonal
                    )
                    for i2 in range(2)
                    for h in range(his)
                ],
                axis=0,
            )
            these = pl.ds(aligned(i * pair_rows, 16), pair_rows)
            grow_ref[these, :] = (g.astype(F32) * gate).astype(BF16)
            wgu = wgu_ref[...]
            wd = wd_ref[...]
            ab = mm(x, wgu)
            inner = ab.shape[1] // 2
            a = ab[:, :inner]
            b = ab[:, inner:]
            sig = 1.0 / (1.0 + jnp.exp(-a))
            act = a * sig
            hidden = (act * b).astype(BF16)
            hid_ref[these, :] = hidden
            shape = (2, his * MOST, width)
            op_ref[slot_of_chunk, l2] = mm(hidden, wd, NT).astype(BF16).reshape(shape)
            dh_raw = mm(g, wd)
            d_route = jnp.sum(hidden.astype(F32) * dh_raw, axis=1, keepdims=True)
            for i2 in range(2):
                for h in range(his):
                    first = (i2 * his + h) * MOST
                    line = jnp.sum(
                        jnp.where(diagonal, d_route[first : first + MOST], 0.0),
                        axis=0,
                        keepdims=True,
                    )
                    dgp_ref[fj, 2 * i + i2, h] = jnp.broadcast_to(line, (8, 128))
            dh = dh_raw * gate
            d_up = (dh * act).astype(BF16)
            d_gate = (dh * b * (sig + act * (1.0 - sig))).astype(BF16)
            dgu = jnp.concatenate([d_gate, d_up], axis=1)
            dgu_ref[these, :] = dgu
            od_ref[fj, l2] = mm(dgu, wgu, NT).astype(BF16).reshape(shape)
            return 0

        lax.fori_loop(0, lo // 2, rows_of, 0)
        x_all = xb_ref[fj].reshape(lo * his * MOST, width)
        accgu_ref[...] += mm(x_all, dgu_ref[...], TN)
        accd_ref[...] += mm(grow_ref[...], hid_ref[...], TN)
        pltpu.make_async_copy(
            op_ref.at[slot_of_chunk], op_hbm.at[fj], last_sem.at[slot_of_chunk]
        ).start()

    def to_core(j):
        fj = xor4(at.f, j)
        send(od_ref.at[fj, at.l1], r1_ref.at[fj, 0], d1s.at[fj, 0], d1r.at[fj, 0], core)
        send(od_ref.at[fj, at.l3], r1_ref.at[fj, 1], d1s.at[fj, 1], d1r.at[fj, 1], core)
        send(dgp_ref.at[fj, at.l1], dr1_ref.at[fj, 0], t1s.at[fj, 0], t1r.at[fj, 0], core)
        send(dgp_ref.at[fj, at.l3], dr1_ref.at[fj, 1], t1s.at[fj, 1], t1r.at[fj, 1], core)

    def add(ref, other):
        ref[...] = (ref[...].astype(F32) + other[...].astype(F32)).astype(BF16)

    def to_side(j):
        fj = xor4(at.f, j)
        settle(r1_ref.at[fj, 1], d1r.at[fj, 1])
        add(od_ref.at[fj, at.l2], r1_ref.at[fj, 1])
        send(od_ref.at[fj, at.l2], r2_ref.at[fj], d2s.at[fj], d2r.at[fj], side)
        settle(dr1_ref.at[fj, 1], t1r.at[fj, 1])
        dgp_ref[fj, at.l2] += dr1_ref[fj, 1]
        send(dgp_ref.at[fj, at.l2], dr2_ref.at[fj], t2s.at[fj], t2r.at[fj], side)
        settle(r1_ref.at[fj, 0], d1r.at[fj, 0])
        add(od_ref.at[fj, at.l], r1_ref.at[fj, 0])
        settle(dr1_ref.at[fj, 0], t1r.at[fj, 0])
        dgp_ref[fj, at.l] += dr1_ref[fj, 0]

    def to_home(j):
        fj = xor4(at.f, j)
        settle(r2_ref.at[fj], d2r.at[fj])
        add(od_ref.at[fj, at.l], r2_ref.at[fj])
        settle(dr2_ref.at[fj], t2r.at[fj])
        dgp_ref[fj, at.l] += dr2_ref[fj]
        for hh in range(his):
            hi = flip(at.hi, hh)
            m = fj * his + hi
            rows = od_ref.at[fj, at.l, pl.ds(aligned(hi * MOST, 16), MOST)]
            peer = (hi * lo + at.l, fj)

            line = dgp_ref.at[fj, at.l, hi]

            def away(rows=rows, line=line, peer=peer, m=m):
                send(rows, back_ref.at[at.m], bs.at[m], br.at[at.m], peer)
                send(line, dgb_ref.at[at.m], tbs.at[m], tbr.at[at.m], peer)

            if hh:
                away()
            else:

                @pl.when(j == 0)
                def _(rows=rows, line=line):
                    pltpu.make_async_copy(rows, back_ref.at[at.m], br.at[at.m]).start()
                    pltpu.make_async_copy(line, dgb_ref.at[at.m], tbr.at[at.m]).start()

                pl.when(j > 0)(away)

    take(0)
    pass_on(0)
    settle(g_ref.at[at.l1], gqr.at[0])
    settle(g_ref.at[at.l3], gqr.at[2])
    for k in range(1, E):
        settle(grow_ref.at[0:MOST], gs.at[k])
    for m in range(E):
        for w in range(3):
            settle(wd_ref.at[0:head_rows, 0:ff], wr.at[m, w])
    give(2)

    def step(t, _):
        @pl.when(t + 1 < ranks)
        def _():
            take(t + 1)

        @pl.when(t == 1)
        def _():
            give(3)

        compute(t)
        to_core(t)

        @pl.when(t + 1 < ranks)
        def _():
            pass_on(t + 1)

        @pl.when(t >= 1)
        def _():
            to_home(t - 1)

        return 0

    lax.fori_loop(0, ranks, step, 0)
    to_side(ranks - 1)
    to_home(ranks - 1)

    inner = wd_ref.shape[1]
    gw_ref[0] = accgu_ref[:, :inner].astype(BF16)
    gw_ref[1] = accgu_ref[:, inner:].astype(BF16)
    gw_ref[2] = accd_ref[...].astype(BF16)
    pltpu.make_async_copy(gw_ref, gw_hbm, last_sem.at[4]).start()

    for m in range(E):
        settle(back_ref.at[m], br.at[m])
        settle(dgb_ref.at[m], tbr.at[m])
    pltpu.make_async_copy(back_ref, back_hbm, last_sem.at[5]).start()
    pltpu.make_async_copy(dgb_ref, dgb_hbm, last_sem.at[6]).start()

    for j in range(1, ranks):
        settle(tile_ref, zs.at[j])
    for j in range(ranks):
        for t in range(4):
            settle(tile_ref, ps.at[j, t])
        for t in range(3):
            settle(tile_ref, cs.at[t, j])

    @pl.when(at.f < ranks - 1)
    def _():
        settle(tail, hs)

    for k in range(1, E):
        settle(x_ref.at[0:MOST], xs.at[k])
        settle(gates_ref.at[0], ts.at[k])
        for w in range(3):
            settle(wd_ref.at[0:head_rows, 0:ff], ws.at[k, w])
    for i in range(3):
        settle(g_ref.at[0], gas.at[i])
    for f2 in range(ranks):
        for i in range(3):
            settle(xb_ref.at[0, 0], qs.at[f2, i])
            settle(gb_ref.at[0, 0], tqs.at[f2, i])
        for i in range(2):
            settle(r1_ref.at[0, 0], d1s.at[f2, i])
            settle(dr1_ref.at[0, 0], t1s.at[f2, i])
        settle(r2_ref.at[0], d2s.at[f2])
        settle(dr2_ref.at[0], t2s.at[f2])
    for j in range(ranks):
        for hh in range(his):
            if j or hh:
                m = at.member(j, hh)[0]
                settle(back_ref.at[0], bs.at[m])
                settle(dgb_ref.at[0], tbs.at[m])
    settle(op_ref.at[0], last_sem.at[0])
    settle(op_ref.at[1], last_sem.at[1])
    settle(gw_ref, last_sem.at[4])
    settle(back_ref, last_sem.at[5])
    settle(dgb_ref, last_sem.at[6])
    for i, (name, _, _) in enumerate(KEPT):
        settle(kept[name], keep_sem.at[i])


SMALL_G1 = EXPERTS_ALL
SMALL_VC = SMALL_G1 + 2
SMALL_C = SMALL_VC + CONSTS
COL_POS, COL_C0, COL_C1, COL_R0, COL_R1, COL_W0, COL_W1 = range(16, 23)


def ahead(groups, ranks, *args):
    tok = args[13]
    w_gate = args[15]
    width = tok.shape[1]
    his = E // ranks
    lo = groups // his
    ff = w_gate.shape[2]
    dma = pltpu.SemaphoreType.DMA
    vm = pltpu.VMEM
    any_spec = pl.BlockSpec(memory_space=pl.ANY)
    block = (width // ranks + 8, 4 * (width // groups))
    rows = (his * MOST, width)
    kept = [(kept_shape(dims, width), dtype) for _, dims, dtype in KEPT]
    results = [
        ((ranks, lo) + rows, BF16),
        ((3, width, ff * his), BF16),
        ((E, MOST, width), BF16),
        ((E, 8, 128), F32),
    ]
    return pl.pallas_call(
        ahead_kernel,
        out_shape=[sds(*k) for k in kept + results],
        in_specs=[pl.BlockSpec(memory_space=pltpu.SMEM)] + whole(14) + [any_spec] * 3,
        out_specs=[any_spec] * (len(kept) + len(results)),
        scratch_shapes=[vm(*k) for k in kept]
        + [
            vm(block, BF16),
            vm((128, 128), F32),
            vm((groups, ranks) + block, BF16),
            vm((ROWS, width), BF16),
            vm((ROWS, width), BF16),
            vm((E, 8, 128), F32),
            vm((width, 2 * ff * his), BF16),
            vm((width, ff * his), BF16),
            vm((lo, ranks) + rows, BF16),
            vm((ranks, lo) + rows, BF16),
            vm((ranks, lo, his, 8, 128), F32),
            vm((ranks, lo) + rows, BF16),
            vm((2, lo) + rows, BF16),
            vm((ranks, 2) + rows, BF16),
            vm((ranks,) + rows, BF16),
            vm((ranks, lo, his, 8, 128), F32),
            vm((ranks, 2, his, 8, 128), F32),
            vm((ranks, his, 8, 128), F32),
            vm((width, 2 * ff * his), F32),
            vm((width, ff * his), F32),
            vm((lo * rows[0], ff * his), BF16),
            vm((lo * rows[0], 2 * ff * his), BF16),
            vm((3, width, ff * his), BF16),
            vm((E, MOST, width), BF16),
            vm((E, 8, 128), F32),
            dma((len(kept),)),
            dma((8,)),
            dma((4,)),
            dma((4, 4)),
            dma((3, 4)),
            dma,
            dma((E,)),
            dma((E, 3)),
            dma((3,)),
            dma((groups, ranks)),
            dma,
            dma((E,)),
            dma((E, 3)),
            dma((3,)),
            dma((E,)),
            dma((E,)),
            dma((4, 3)),
            dma((4, 3)),
            dma((4, 2)),
            dma((4, 2)),
            dma((4,)),
            dma((4,)),
            dma((E,)),
            dma((E,)),
            dma((E,)),
            dma((E,)),
            dma((4, 3)),
            dma((4, 3)),
            dma((4, 2)),
            dma((4, 2)),
            dma((4,)),
            dma((4,)),
            dma((E,)),
            dma((E,)),
        ],
        compiler_params=params(63, collective_id=1, has_side_effects=True),
        name="ahead",
    )(*args)


def end_kernel(
    cot_ref,
    tok_ref,
    prev_ref,
    wmix_ref,
    back_hbm,
    dgb_hbm,
    op_hbm,
    gw_hbm,
    *rest,
):
    n = len(KEPT)
    kept_hbm = by_name(rest[:n])
    (
        out_ref,
        dres_ref,
        gprev_ref,
        down_ref,
        back_ref,
        fin_ref,
        gmix_ref,
        t_ref,
    ) = rest[n : n + 8]
    kept = by_name(rest[n + 8 : 2 * n + 8])
    (
        dx_ref,
        dgb_ref,
        opl_ref,
        r1o_ref,
        r2o_ref,
        outb_ref,
        flat_ref,
        dhalo_ref,
        dm_ref,
        dq_ref,
        dk_ref,
        dv_ref,
        dqr_ref,
        dkr_ref,
        dvr_ref,
        full_ref,
        p_ref,
        r1_ref,
        r2_ref,
        r3_ref,
        r4_ref,
        mx_ref,
        mr_ref,
        mz_ref,
        load_sem,
        more_sem,
        o1s,
        o1r,
        o2s,
        o2r,
        obs,
        obr,
        ts,
        tr,
        hs,
        hr,
        s1,
        e1,
        s2,
        e2,
        s3,
        e3,
        s4,
        e4,
        ms,
        me,
        zs,
        ze,
    ) = rest[2 * n + 8 :]
    wf_ref, s_ref, halo_ref, cols_ref = kept["wf"], kept["s"], kept["halo"], kept["cols"]
    q_ref, k_ref, v_ref, n1_ref = kept["q"], kept["k"], kept["v"], kept["n1"]
    mix_ref, lse_ref = kept["mix"], kept["lse"]
    names = [item[0] for item in KEPT]

    def load(*which):
        for name in which:
            pltpu.make_async_copy(
                kept_hbm[name], kept[name], load_sem.at[names.index(name)]
            ).start()

    def ready(*which):
        for name in which:
            settle(kept[name], load_sem.at[names.index(name)])

    ranks = p_ref.shape[1]
    his = E // ranks
    groups = p_ref.shape[0]
    lo = groups // his
    at = Place(his, lo)
    width = cot_ref.shape[1]
    tile = t_ref.shape[2:]
    core = (at.core_peer, at.f)
    side = (at.side_peer, at.f)
    upper = (lo * (1 - at.hi) + at.l, at.f)
    peers = at.others() + [core, side]
    call(peers)
    pltpu.make_async_copy(back_hbm, dx_ref, more_sem.at[0]).start()
    pltpu.make_async_copy(dgb_hbm, dgb_ref, more_sem.at[1]).start()
    load("cols", "s", "resid", "probs", "mix", "wf", "q", "k", "v", "lse")
    for f2 in range(ranks):
        for i, l2 in enumerate((at.l, at.l2)):
            pltpu.make_async_copy(
                op_hbm.at[f2, l2], opl_ref.at[f2, i], more_sem.at[2 + 2 * f2 + i]
            ).start()
    load("cos", "sin", "n1", "inv1", "halo", "part")
    answer(peers)

    for f2 in range(ranks):
        send(op_hbm.at[f2, at.l1], r1o_ref.at[f2, 0], o1s.at[f2, 0], o1r.at[f2, 0], core)
        send(op_hbm.at[f2, at.l3], r1o_ref.at[f2, 1], o1s.at[f2, 1], o1r.at[f2, 1], core)

    for j in range(ranks):
        for hh in range(his):
            e, peer = at.member(j, hh)
            rows = pl.ds(aligned(e // his * tile[0], 16), tile[0])
            lanes_at = pl.ds(aligned(lax.rem(e, his) * tile[1], 128), tile[1])
            n = j * his + hh
            for w in range(3):
                block = gw_hbm.at[w, rows, lanes_at]
                if n == 0:
                    pltpu.make_async_copy(block, t_ref.at[at.m, w], tr.at[at.m, w]).start()
                else:
                    send(block, t_ref.at[at.m, w], ts.at[n, w], tr.at[at.m, w], peer)

    def add(ref, other):
        ref[...] = (ref[...].astype(F32) + other[...].astype(F32)).astype(BF16)

    ready("cols", "s", "resid", "probs")
    settle(dx_ref, more_sem.at[0])
    settle(dgb_ref, more_sem.at[1])
    flat = s_ref[...].T
    gain1 = flat[SMALL_G1 : SMALL_G1 + 1, :]
    gain2 = flat[SMALL_G1 + 1 : SMALL_G1 + 2, :]
    vc = flat[SMALL_VC : SMALL_VC + CONSTS, :]
    g = cot_ref[...].astype(F32)
    lanes = lane_iota(TOK_DEV)
    cols = cols_ref[...]

    def col(i):
        return pick(cols, lanes == i)

    gate0, gate1, gate_id, inv2 = col(0), col(1), col(2), col(3)
    resid = kept["resid"][...]
    unit2 = resid * inv2
    normed = unit2 * gain2
    narrow = normed.astype(BF16)
    c0, c1, r0, r1, wide0, wide1 = (
        col(COL_POS + 1 + i).astype(jnp.int32) for i in range(6)
    )
    slot = lane_iota(TOK_DEV, ROWS)
    hot0 = jnp.where(slot == c0, 1.0, 0.0).astype(BF16)
    hot1 = jnp.where(slot == c1, 1.0, 0.0).astype(BF16)
    dg0 = jnp.zeros((TOK_DEV, 1), F32)
    dg1 = jnp.zeros((TOK_DEV, 1), F32)
    for e in range(E):
        line = jnp.broadcast_to(dgb_ref[e][0:1, :], (TOK_DEV, 128))
        dg0 = dg0 + pick(line, lanes + e * 128 == wide0)
        dg1 = dg1 + pick(line, lanes + e * 128 == wide1)
    a_n = jnp.sum(g * normed, axis=1, keepdims=True)
    dg0 = jnp.where(r0 == E + 1, a_n, dg0)
    dg1 = jnp.where(r1 == E + 1, a_n, dg1)
    g_scale = gate_id
    dl = jnp.zeros((TOK_DEV, 128), F32)
    vmix = jnp.zeros((TOK_DEV, 128), F32)
    for c in range(CONSTS):
        gate_c, ma, mb = col(4 + 3 * c), col(5 + 3 * c), col(6 + 3 * c)
        a_v = jnp.sum(g * vc[c : c + 1, :], axis=1, keepdims=True)
        branch = ma * a_n + mb * a_v
        dg0 = jnp.where(r0 == E + 2 + c, branch, dg0)
        dg1 = jnp.where(r1 == E + 2 + c, branch, dg1)
        g_scale = g_scale + gate_c * ma
        da = gate_c * a_n
        db = gate_c * a_v
        mean = ma * da + mb * db
        dl = jnp.where(lanes == SMALL_C + 2 * c, ma * (da - mean), dl)
        dl = jnp.where(lanes == SMALL_C + 1 + 2 * c, mb * (db - mean), dl)
        vmix = jnp.where(lanes == SMALL_VC + c, gate_c * mb, vmix)
    probs = kept["probs"][...]
    d_probs = jnp.where(lanes == r0, dg0, 0.0) + jnp.where(lanes == r1, dg1, 0.0)
    d_logits = probs * (d_probs - jnp.sum(probs * d_probs, axis=1, keepdims=True))
    dl = jnp.where(lanes < EXPERTS_ALL, d_logits, dl)
    high = dl.astype(BF16)
    low = (dl - high.astype(F32)).astype(BF16)
    wr = s_ref[...].astype(BF16)
    d_normed = g_scale * g + mm(hot0 + hot1, dx_ref[...].reshape(ROWS, width))
    d_normed = d_normed + mm(high, wr, NT) + mm(low, wr, NT)
    vhigh = vmix.astype(BF16)
    vlow = (vmix - vhigh.astype(F32)).astype(BF16)
    tiny = mm(high, narrow, TN) + mm(low, narrow, TN)
    tiny = tiny + mm(vhigh, cot_ref[...], TN) + mm(vlow, cot_ref[...], TN)
    row_id = lax.broadcasted_iota(jnp.int32, (128, width), 0)
    dg2 = jnp.sum(d_normed * unit2, axis=0, keepdims=True)
    flat_ref[...] = jnp.where(row_id == SMALL_G1 + 1, dg2, tiny)
    n = d_normed * gain2
    dres_ref[...] = g + inv2 * (n - unit2 * jnp.mean(n * unit2, axis=1, keepdims=True))
    wmix = jnp.concatenate(
        [wmix_ref[...].astype(F32), jnp.zeros((EXPERTS_ALL, 128 - EXPERTS_ALL), F32)], axis=1
    ).astype(BF16)
    gprev_ref[...] = mm(wmix, high, NT) + mm(wmix, low, NT)
    prev = prev_ref[...]
    phigh = prev.astype(BF16)
    plow = (prev - phigh.astype(F32)).astype(BF16)
    mx_ref[0] = jnp.zeros(mx_ref.shape[1:], F32)
    mx_ref[0, 0:EXPERTS_ALL, :] = mm(phigh, high) + mm(phigh, low) + mm(plow, high)
    send(mx_ref.at[0], mr_ref.at[0], ms.at[0], me.at[0], core)

    for f2 in range(ranks):
        settle(opl_ref.at[f2, 1], more_sem.at[3 + 2 * f2])
        settle(r1o_ref.at[f2, 1], o1r.at[f2, 1])
        add(opl_ref.at[f2, 1], r1o_ref.at[f2, 1])
        send(opl_ref.at[f2, 1], r2o_ref.at[f2], o2s.at[f2], o2r.at[f2], side)
        settle(opl_ref.at[f2, 0], more_sem.at[2 + 2 * f2])
        settle(r1o_ref.at[f2, 0], o1r.at[f2, 0])
        add(opl_ref.at[f2, 0], r1o_ref.at[f2, 0])

    ready("mix", "wf", "q", "k", "v", "lse")
    scale = HEAD_DIM ** (-0.5)
    d_attn = dres_ref[...].astype(BF16)
    full_ref[3] = mm(mix_ref[...], d_attn, TN).astype(BF16)
    dm_ref[...] = mm(d_attn, wf_ref[3], NT).astype(BF16)
    dk_ref[...] = jnp.zeros_like(dk_ref)
    dv_ref[...] = jnp.zeros_like(dv_ref)

    def pair(p, _):
        span = pl.ds(pl.multiple_of(p * 128, 128), 128)
        for first, count in QBLOCKS:
            keys = key_span(first)
            ok = allowed_mask(cols_ref, first, count, COL_POS)[:, :keys]
            q = q_ref[pl.ds(first, count), span]
            dm = dm_ref[pl.ds(first, count), span]
            k = k_ref[pl.ds(first, keys), span]
            v = v_ref[pl.ds(first, keys), span]
            lane = lane_iota(count)
            key_lane = lane_iota(keys)
            lse = lse_ref[pl.ds(first, count), :]
            dq = dk = dv = None
            for h in range(2):
                mine = (lane < HEAD_DIM) if h == 0 else (lane >= HEAD_DIM)
                key_mine = (key_lane < HEAD_DIM) if h == 0 else (key_lane >= HEAD_DIM)
                qh = jnp.where(mine, q, jnp.zeros_like(q))
                dmh = jnp.where(mine, dm, jnp.zeros_like(dm))
                s = jnp.where(ok, mm(qh, k, NT) * scale, NEG)
                pr = jnp.where(ok, jnp.exp(s - pick(lse, lane == 2 * p + h)), 0.0)
                dp = mm(dmh, v, NT)
                delta = jnp.sum(pr * dp, axis=1, keepdims=True)
                ds = (pr * (dp - delta)).astype(BF16)
                pb = pr.astype(BF16)
                dqh = mm(ds, k)
                dkh = mm(ds, q, TN)
                dvh = mm(pb, dm, TN)
                dq = dqh if h == 0 else jnp.where(mine, dqh, dq)
                dk = dkh if h == 0 else jnp.where(key_mine, dkh, dk)
                dv = dvh if h == 0 else jnp.where(key_mine, dvh, dv)
            dq_ref[pl.ds(first, count), span] = dq * scale
            dk_ref[pl.ds(first, keys), span] += dk * scale
            dv_ref[pl.ds(first, keys), span] += dv

        return 0

    lax.fori_loop(0, HEADS // 2, pair, 0)

    ready("cos", "sin", "n1", "inv1", "halo", "part")

    for j in range(ranks):
        fj = xor4(at.f, j)
        settle(r2o_ref.at[fj], o2r.at[fj])
        add(opl_ref.at[fj, 0], r2o_ref.at[fj])
        for hh in range(his):
            m, peer = at.member(j, hh)
            rows = opl_ref.at[fj, 0, pl.ds(aligned(flip(at.hi, hh) * MOST, 16), MOST)]
            if j or hh:
                send(rows, outb_ref.at[at.m], obs.at[m], obr.at[at.m], peer)
            else:
                pltpu.make_async_copy(rows, outb_ref.at[at.m], obr.at[at.m]).start()

    def unturn(i, _):
        span = pl.ds(pl.multiple_of(i * 256, 256), 256)
        cos = kept["cos"][...]
        sin = kept["sin"][...]
        dqr_ref[:, span] = turn(dq_ref[:, span], cos[HALO:], -sin[HALO:]).astype(BF16)
        dkr_ref[:, span] = turn(dk_ref[:, span], cos, -sin).astype(BF16)
        dvr_ref[:, span] = dv_ref[:, span].astype(BF16)
        return 0

    lax.fori_loop(0, width // 256, unturn, 0)
    d_all = mm(dkr_ref[...], wf_ref[1], NT) + mm(dvr_ref[...], wf_ref[2], NT)
    dhalo_ref[...] = (d_all[:HALO] * gain1).astype(BF16)

    @pl.when(at.f > 0)
    def _():
        send(dhalo_ref, back_ref, hs, hr, (at.g, at.f - 1))

    @pl.when(at.f == ranks - 1)
    def _():
        back_ref[...] = jnp.zeros_like(back_ref)

    full_ref[0] = mm(n1_ref[HALO:, :], dqr_ref[...], TN).astype(BF16)
    full_ref[1] = mm(n1_ref[...], dkr_ref[...], TN).astype(BF16)
    full_ref[2] = mm(n1_ref[...], dvr_ref[...], TN).astype(BF16)
    d_own = d_all[HALO:] + mm(dqr_ref[...], wf_ref[0], NT)
    inv1 = kept["inv1"][:, 0:1]
    unit_own = tok_ref[...].astype(F32) * inv1[HALO:]
    unit_halo = halo_ref[...].astype(F32) * inv1[:HALO]
    dg1 = jnp.sum(d_own * unit_own, axis=0, keepdims=True) + jnp.sum(
        d_all[:HALO] * unit_halo, axis=0, keepdims=True
    )
    down_ref[...] = d_own * gain1
    flat_ref[...] = jnp.where(row_id == SMALL_G1, dg1, flat_ref[...])

    part_cols = width // groups
    head_rows = width // ranks

    def pack(f2, _):
        rows = pl.ds(aligned(f2 * head_rows, 16), head_rows)
        for g2 in range(groups):
            pieces = [
                full_ref[w, rows, g2 * part_cols : (g2 + 1) * part_cols] for w in range(4)
            ]
            p_ref[g2, f2, 0:head_rows, :] = jnp.concatenate(pieces, axis=1)
        return 0

    lax.fori_loop(0, ranks, pack, 0)
    column = flat_ref[...].T
    per = width // (groups * ranks)
    for g2 in range(groups):
        for f2 in range(ranks):
            base = (g2 * ranks + f2) * per
            pieces = [column[base + 8 * i : base + 8 * i + 8, :] for i in range(per // 8)]
            p_ref[g2, f2, head_rows : head_rows + 8, :] = jnp.concatenate(
                pieces, axis=1
            ).astype(BF16)

    c = lax.rem(at.g, 2)
    x = lax.rem(at.g // 2, 2)
    y = at.hi

    def block(y2, x2, c2):
        return (y2 * 2 + x2) * 2 + c2

    half = ranks // 2
    quads = [(1 - y, 1 - x), (y, 1 - x), (1 - y, x), (y, x)]
    for i, (y2, x2) in enumerate(quads):
        spot = y2 * 2 + x2
        send(p_ref.at[block(y2, x2, 1 - c)], r1_ref.at[spot], s1.at[i], e1.at[spot], core)
    settle(mr_ref.at[0], me.at[0])
    mx_ref[1] = mx_ref[0] + mr_ref[0]
    send(mx_ref.at[1], mr_ref.at[1], ms.at[1], me.at[1], side)
    for i, (y2, x2) in enumerate(quads):
        spot = y2 * 2 + x2
        settle(r1_ref.at[spot], e1.at[spot])
        add(p_ref.at[block(y2, x2, c)], r1_ref.at[spot])
        if i == 0:
            here = p_ref.at[block(1 - y, 1 - x, c)]
            send(here.at[0:half], r2_ref.at[0, 1 - y], s2.at[0, 0], e2.at[0, 1 - y], side)
            send(here.at[half:], r2_ref.at[1, 1 - x], s2.at[1, 0], e2.at[1, 1 - x], upper)
        if i == 1:
            here = p_ref.at[block(y, 1 - x, c)]
            send(here.at[0:half], r2_ref.at[0, y], s2.at[0, 1], e2.at[0, y], side)
        if i == 2:
            here = p_ref.at[block(1 - y, x, c)]
            send(here.at[half:], r2_ref.at[1, x], s2.at[1, 1], e2.at[1, x], upper)
    settle(mr_ref.at[1], me.at[1])
    mx_ref[2] = mx_ref[1] + mr_ref[1]
    send(mx_ref.at[2], mr_ref.at[2], ms.at[2], me.at[2], upper)
    settle(r2_ref.at[0, 1 - y], e2.at[0, 1 - y])
    add(p_ref.at[block(1 - y, x, c), 0:half], r2_ref.at[0, 1 - y])
    send(
        p_ref.at[block(1 - y, x, c), 0:half], r3_ref.at[0], s3.at[0], e3.at[0], upper
    )
    settle(r2_ref.at[1, 1 - x], e2.at[1, 1 - x])
    add(p_ref.at[block(y, 1 - x, c), half:], r2_ref.at[1, 1 - x])
    send(p_ref.at[block(y, 1 - x, c), half:], r3_ref.at[1], s3.at[1], e3.at[1], side)
    settle(r2_ref.at[0, y], e2.at[0, y])
    add(p_ref.at[at.g, 0:half], r2_ref.at[0, y])
    settle(r2_ref.at[1, x], e2.at[1, x])
    add(p_ref.at[at.g, half:], r2_ref.at[1, x])
    settle(mr_ref.at[2], me.at[2])
    mx_ref[3] = mx_ref[2] + mr_ref[2]
    mz_ref[at.f] = mx_ref[3]
    for i in range(2):
        settle(r3_ref.at[i], e3.at[i])
        add(p_ref.at[at.g, i * half : (i + 1) * half], r3_ref.at[i])
    for j in range(1, ranks):
        f2 = xor4(at.f, j)
        send(p_ref.at[at.g, f2], r4_ref.at[at.f], s4.at[j], e4.at[at.f], (at.g, f2))
        send(mx_ref.at[3], mz_ref.at[at.f], zs.at[j], ze.at[at.f], (at.g, f2))
    for m in range(E):
        settle(outb_ref.at[m], obr.at[m])
    rows = outb_ref[...].reshape(ROWS, width)
    cols = cols_ref[...]
    c0 = pick(cols, lanes == COL_C0).astype(jnp.int32)
    c1 = pick(cols, lanes == COL_C1).astype(jnp.int32)
    y0 = mm(jnp.where(slot == c0, 1.0, 0.0).astype(BF16), rows)
    y1 = mm(jnp.where(slot == c1, 1.0, 0.0).astype(BF16), rows)
    gate0 = pick(cols, lanes == 0)
    gate1 = pick(cols, lanes == 1)
    out_ref[...] = (kept["part"][...] + gate0 * y0 + gate1 * y1).astype(BF16)

    total = p_ref[at.g, at.f].astype(F32)
    for j in range(1, ranks):
        f2 = xor4(at.f, j)
        settle(r4_ref.at[f2], e4.at[f2])
        total = total + r4_ref[f2].astype(F32)
        settle(mz_ref.at[f2], ze.at[f2])
    fin_ref[...] = total
    gmix_ref[...] = (mz_ref[0] + mz_ref[1]) + (mz_ref[2] + mz_ref[3])

    for f2 in range(ranks):
        for i in range(2):
            settle(r1o_ref.at[0, 0], o1s.at[f2, i])
        settle(r2o_ref.at[0], o2s.at[f2])
    for j in range(ranks):
        for hh in range(his):
            if j or hh:
                settle(outb_ref.at[0], obs.at[at.member(j, hh)[0]])
    for m in range(E):
        for w in range(3):
            settle(t_ref.at[m, w], tr.at[m, w])
    for i in range(1, E):
        for w in range(3):
            settle(t_ref.at[0, w], ts.at[i, w])

    @pl.when(at.f > 0)
    def _():
        settle(dhalo_ref, hs)

    @pl.when(at.f < ranks - 1)
    def _():
        settle(back_ref, hr)

    for i in range(4):
        settle(r1_ref.at[0], s1.at[i])
    for i in range(2):
        for n2 in range(2):
            settle(r2_ref.at[0, 0], s2.at[i, n2])
        settle(r3_ref.at[0], s3.at[i])
    for i in range(3):
        settle(mr_ref.at[0], ms.at[i])
    for j in range(1, ranks):
        settle(r4_ref.at[0], s4.at[j])
        settle(mz_ref.at[0], zs.at[j])


def end(groups, ranks, tile, *args):
    cot = args[0]
    width = cot.shape[1]
    dma = pltpu.SemaphoreType.DMA
    vm = pltpu.VMEM
    block = (width // ranks + 8, 4 * (width // groups))
    half = ranks // 2
    rows = (E // ranks * MOST, width)
    kept = [(kept_shape(dims, width), dtype) for _, dims, dtype in KEPT]
    any_spec = pl.BlockSpec(memory_space=pl.ANY)
    return pl.pallas_call(
        end_kernel,
        out_shape=[
            sds((TOK_DEV, width), BF16),
            sds((TOK_DEV, width), F32),
            sds((EXPERTS_ALL, TOK_DEV), F32),
            sds((TOK_DEV, width), F32),
            sds((HALO, width), BF16),
            sds(block, F32),
            sds((16, 128), F32),
            sds((E, 3) + tile, BF16),
        ],
        in_specs=whole(4) + [any_spec] * (4 + len(kept)),
        out_specs=whole(7) + [any_spec],
        scratch_shapes=[vm(*k) for k in kept]
        + [
            vm((E, MOST, width), BF16),
            vm((E, 8, 128), F32),
            vm((ranks, 2) + rows, BF16),
            vm((ranks, 2) + rows, BF16),
            vm((ranks,) + rows, BF16),
            vm((E, MOST, width), BF16),
            vm((128, width), F32),
            vm((HALO, width), BF16),
            vm((TOK_DEV, width), BF16),
            vm((TOK_DEV, width), F32),
            vm((KEYS, width), F32),
            vm((KEYS, width), F32),
            vm((TOK_DEV, width), BF16),
            vm((KEYS, width), BF16),
            vm((KEYS, width), BF16),
            vm((4, width, width), BF16),
            vm((groups, ranks) + block, BF16),
            vm((4, ranks) + block, BF16),
            vm((2, 2, half) + block, BF16),
            vm((2, half) + block, BF16),
            vm((ranks,) + block, BF16),
            vm((4, 16, 128), F32),
            vm((3, 16, 128), F32),
            vm((ranks, 16, 128), F32),
            dma((len(kept),)),
            dma((2 + 2 * ranks,)),
            dma((ranks, 2)),
            dma((ranks, 2)),
            dma((ranks,)),
            dma((ranks,)),
            dma((E,)),
            dma((E,)),
            dma((E, 3)),
            dma((E, 3)),
            dma,
            dma,
            dma((4,)),
            dma((4,)),
            dma((2, 2)),
            dma((2, 2)),
            dma((2,)),
            dma((2,)),
            dma((4,)),
            dma((4,)),
            dma((3,)),
            dma((3,)),
            dma((4,)),
            dma((4,)),
        ],
        compiler_params=params(63, collective_id=3, has_side_effects=True),
        name="end",
    )(*args)


def store_kernel(
    t_hbm,
    fin_hbm,
    dres_hbm,
    down_hbm,
    back_hbm,
    tok_hbm,
    inv1_hbm,
    out_from,
    gprev_from,
    gmix_from,
    gate_hbm,
    up_hbm,
    downw_hbm,
    gq_ref,
    gk_ref,
    gv_ref,
    go_ref,
    router_ref,
    const_ref,
    vconst_ref,
    gain1_ref,
    gain2_ref,
    gtok_hbm,
    out_to,
    gprev_to,
    gmix_ref,
    t_ref,
    wide_ref,
    fin_ref,
    dres_ref,
    down_ref,
    back_ref,
    tok_ref,
    inv1_ref,
    gtok_ref,
    mixin_ref,
    out_ref,
    gprev_ref,
    t_sem,
    wide_sem,
    in_sem,
    gtok_sem,
    pass_sem,
):
    pairs = [
        (dres_hbm, dres_ref),
        (down_hbm, down_ref),
        (back_hbm, back_ref),
        (tok_hbm, tok_ref),
        (inv1_hbm, inv1_ref),
        (fin_hbm, fin_ref),
        (gmix_from, mixin_ref),
        (out_from, out_ref),
        (gprev_from, gprev_ref),
    ]
    for i, (src, dst) in enumerate(pairs):
        pltpu.make_async_copy(src, dst, in_sem.at[i]).start()
    for e in range(E):
        pltpu.make_async_copy(t_hbm.at[e], t_ref.at[e], t_sem.at[e]).start()
    for i in range(5):
        settle(pairs[i][1], in_sem.at[i])
    width = tok_ref.shape[1]
    inv1 = inv1_ref[HALO:, 0:1]
    unit = tok_ref[...].astype(F32) * inv1
    m = jnp.concatenate(
        [down_ref[: TOK_DEV - HALO, :], down_ref[TOK_DEV - HALO :, :] + back_ref[...]], axis=0
    )
    d_dealt = inv1 * (m - unit * jnp.mean(m * unit, axis=1, keepdims=True))
    gtok_ref[...] = dres_ref[...] + d_dealt.astype(BF16).astype(F32)
    pltpu.make_async_copy(gtok_ref, gtok_hbm, gtok_sem).start()
    settle(out_ref, in_sem.at[7])
    pltpu.make_async_copy(out_ref, out_to, pass_sem.at[0]).start()
    settle(gprev_ref, in_sem.at[8])
    pltpu.make_async_copy(gprev_ref, gprev_to, pass_sem.at[1]).start()
    for e in range(E):
        settle(t_ref.at[e], t_sem.at[e])
        wide_ref[e] = t_ref[e].astype(F32)
        for w, out in enumerate((gate_hbm, up_hbm, downw_hbm)):
            pltpu.make_async_copy(wide_ref.at[e, w], out.at[e], wide_sem.at[e, w]).start()
    settle(fin_ref, in_sem.at[5])
    head_rows, part_cols = gq_ref.shape
    for w, ref in enumerate((gq_ref, gk_ref, gv_ref, go_ref)):
        ref[...] = fin_ref[0:head_rows, w * part_cols : (w + 1) * part_cols]
    per = router_ref.shape[1]
    column = jnp.concatenate(
        [
            fin_ref[head_rows : head_rows + 8, 128 * i : 128 * i + 128]
            for i in range(per // 8)
        ]
        + [jnp.zeros((128 - per, 128), F32)],
        axis=0,
    )
    flat = column.T[:, 0:per]
    router_ref[...] = flat[0:EXPERTS_ALL]
    gain1_ref[...] = flat[SMALL_G1 : SMALL_G1 + 1]
    gain2_ref[...] = flat[SMALL_G1 + 1 : SMALL_G1 + 2]
    vconst_ref[...] = flat[SMALL_VC : SMALL_VC + CONSTS]
    const_ref[...] = flat[SMALL_C : SMALL_C + 2 * CONSTS]
    settle(mixin_ref, in_sem.at[6])
    gmix_ref[...] = mixin_ref[0:EXPERTS_ALL, 0:EXPERTS_ALL]
    settle(out_ref, pass_sem.at[0])
    settle(gprev_ref, pass_sem.at[1])
    settle(gtok_ref, gtok_sem)
    for e in range(E):
        for w in range(3):
            settle(wide_ref.at[e, w], wide_sem.at[e, w])


def store(t, fin, dres, down, back, tok, inv1, out, gprev, gmix, groups, ranks):
    width = tok.shape[1]
    rows, cols = t.shape[2:]
    per = width // (groups * ranks)
    any_spec = pl.BlockSpec(memory_space=pl.ANY)
    dma = pltpu.SemaphoreType.DMA
    vm = pltpu.VMEM
    return pl.pallas_call(
        store_kernel,
        out_shape=[sds((E, rows, cols), F32)] * 3
        + [sds((width // ranks, width // groups), F32)] * 4
        + [
            sds((EXPERTS_ALL, per), F32),
            sds((2 * CONSTS, per), F32),
            sds((CONSTS, per), F32),
            sds((1, per), F32),
            sds((1, per), F32),
            sds(tok.shape, F32),
            sds(out.shape, BF16),
            sds(gprev.shape, F32),
            sds((EXPERTS_ALL, EXPERTS_ALL), F32),
        ],
        in_specs=[any_spec] * 10,
        out_specs=[any_spec] * 3 + whole(9) + [any_spec] * 3 + whole(1),
        scratch_shapes=[
            vm(t.shape, BF16),
            vm(t.shape, F32),
            vm(fin.shape, F32),
            vm(dres.shape, F32),
            vm(down.shape, F32),
            vm(back.shape, BF16),
            vm(tok.shape, BF16),
            vm(inv1.shape, F32),
            vm(tok.shape, F32),
            vm(gmix.shape, F32),
            vm(out.shape, BF16),
            vm(gprev.shape, F32),
            dma((E,)),
            dma((E, 3)),
            dma((9,)),
            dma,
            dma((2,)),
        ],
        compiler_params=params(63),
        name="store",
    )(t, fin, dres, down, back, tok, inv1, out, gprev, gmix)


def fast_device(
    tokens,
    cotangent,
    prev_logits,
    lengths,
    dealing,
    routes,
    gain_one,
    w_query,
    w_key,
    w_value,
    w_out,
    gain_two,
    w_router,
    w_mix,
    w_const,
    v_const,
    w_gate,
    w_up,
    w_down,
):
    groups = lax.axis_size("grp")
    ranks = lax.axis_size("fsdp")
    kept = len(KEPT)
    prev = prev_logits.T
    outs = ahead(
        groups,
        ranks,
        lengths,
        routes.T,
        prev,
        w_mix,
        w_router.T,
        gain_one[None, :],
        gain_two[None, :],
        w_const.T,
        v_const.T,
        w_query,
        w_key,
        w_value,
        w_out,
        tokens,
        cotangent,
        w_gate,
        w_up,
        w_down.transpose(0, 2, 1),
    )
    parts, grads, dx, routed = outs[kept:]
    output, dres, gprev, down, back, fin, gmix, tiles = end(
        groups,
        ranks,
        w_gate.shape[1:],
        cotangent,
        tokens,
        prev,
        w_mix,
        dx,
        routed,
        parts,
        grads,
        *outs[:kept],
    )
    inv1 = by_name(outs[:kept])["inv1"]
    (
        gate,
        up,
        downw,
        gq,
        gk,
        gv,
        go,
        router,
        const,
        vconst,
        gain1,
        gain2,
        grad_tokens,
        output,
        gprev,
        gmix,
    ) = store(
        tiles, fin, dres, down, back, tokens, inv1, output, gprev, gmix, groups, ranks
    )
    return (
        output,
        grad_tokens,
        gprev.T,
        gain1[0],
        gq,
        gk,
        gv,
        go,
        gain2[0],
        router.T,
        gmix,
        const.T,
        vconst.T,
        gate,
        up,
        downw.transpose(0, 2, 1),
    )


def suits(mesh):
    return mesh.shape["fsdp"] == 4 and mesh.shape["grp"] == 8


def solution(mesh):
    return jax.shard_map(
        fast_device if suits(mesh) else per_device,
        mesh=mesh,
        in_specs=(
            P(("grp", "fsdp"), None),
            P(("grp", "fsdp"), None),
            P(("grp", "fsdp"), None),
            P("grp", None),
            P("grp", None),
            P(("grp", "fsdp"), None),
            P(("grp", "fsdp")),
            P("fsdp", "grp"),
            P("fsdp", "grp"),
            P("fsdp", "grp"),
            P("fsdp", "grp"),
            P(("grp", "fsdp")),
            P(("grp", "fsdp"), None),
            P(),
            P(("grp", "fsdp"), None),
            P(("grp", "fsdp"), None),
            P(None, "fsdp", "grp"),
            P(None, "fsdp", "grp"),
            P(None, "grp", "fsdp"),
        ),
        out_specs=(
            P(("grp", "fsdp"), None),
            P(("grp", "fsdp"), None),
            P(("grp", "fsdp"), None),
            P(("grp", "fsdp")),
            P("fsdp", "grp"),
            P("fsdp", "grp"),
            P("fsdp", "grp"),
            P("fsdp", "grp"),
            P(("grp", "fsdp")),
            P(("grp", "fsdp"), None),
            P(),
            P(("grp", "fsdp"), None),
            P(("grp", "fsdp"), None),
            P(None, "fsdp", "grp"),
            P(None, "fsdp", "grp"),
            P(None, "grp", "fsdp"),
        ),
        check_vma=False,
    )
```

```python
import math

import jax
import jax.numpy as jnp
from jax import lax
from jax.experimental import pallas as pl
from jax.experimental.pallas import tpu as pltpu
from jax.sharding import PartitionSpec as P

HEADS = 12
HEAD_DIM = 64
E = 8
CONSTS = 2
BLOCK = 128
EXPERTS_ALL = 12
CAP = 384
TOK_DEV = 320
MOST = 80


NORM_EPS = 1e-05
EXACT = lax.Precision.HIGHEST


def rotation_tables(positions, head_dim):
    half_dim = head_dim // 2
    inv_freq = jnp.exp(
        jnp.arange(half_dim, dtype=jnp.float32) * (-2.0 * math.log(10000.0) / head_dim)
    )
    angles = positions.astype(jnp.float32)[:, None] * inv_freq[None, :]
    return (jnp.cos(angles), jnp.sin(angles))


def rotate(values, cos_table, sin_table):
    row_count = values.shape[0]
    half_dim = cos_table.shape[1]
    heads_view = values.reshape(row_count, -1, 2 * half_dim)
    front_half = heads_view[:, :, :half_dim]
    back_half = heads_view[:, :, half_dim:]
    cos_view = cos_table[:, None, :]
    sin_view = sin_table[:, None, :]
    turned = jnp.concatenate(
        [
            front_half * cos_view - back_half * sin_view,
            back_half * cos_view + front_half * sin_view,
        ],
        axis=2,
    )
    return turned.reshape(row_count, -1)


def exact_dot(left_side, right_side):
    return jnp.dot(left_side, right_side, precision=EXACT, preferred_element_type=jnp.float32)


def per_device(
    tokens,
    cotangent,
    prev_logits,
    lengths,
    dealing,
    routes,
    gain_one,
    w_query,
    w_key,
    w_value,
    w_out,
    gain_two,
    w_router,
    w_mix,
    w_const,
    v_const,
    w_gate,
    w_up,
    w_down,
):
    groups = lax.axis_size("grp")
    dealers = lax.axis_size("fsdp")
    device = lax.axis_index("fsdp")
    model_width = tokens.shape[1]
    per_shard = model_width // (groups * dealers)
    pairs = HEADS // 2
    pair_width = 2 * HEAD_DIM
    scale = HEAD_DIM ** (-0.5)
    seq_len = lengths[0]
    deal_order = dealing[0]
    seq_count = seq_len.shape[0]
    seq_ids = jnp.arange(seq_count, dtype=jnp.int32)
    seq_ends = jnp.cumsum(seq_len)
    starts = seq_ends - seq_len
    padded = (seq_len + BLOCK - 1) // BLOCK * BLOCK
    order_hot = (deal_order[:, None] == seq_ids[None, :]).astype(jnp.int32)
    dealt_len = jnp.sum(order_hot * seq_len[None, :], axis=1)
    dealt_pad = jnp.sum(order_hot * padded[None, :], axis=1)
    dealt_start = jnp.sum(order_hot * starts[None, :], axis=1)
    slot_of = jnp.sum(order_hot * seq_ids[:, None], axis=0)
    pair_index = 2 * device
    row_ids = jnp.arange(CAP, dtype=jnp.int32)
    in_second = row_ids >= dealt_pad[pair_index]
    position = row_ids - jnp.where(in_second, dealt_pad[pair_index], 0)
    seq_limit = jnp.where(in_second, dealt_len[pair_index + 1], dealt_len[pair_index])
    live_rows = position < seq_limit
    source = jnp.where(in_second, dealt_start[pair_index + 1], dealt_start[pair_index]) + position
    source = jnp.where(live_rows, source, -1)
    given_rows = device * TOK_DEV + jnp.arange(TOK_DEV, dtype=jnp.int32)
    seq_hot = (
        (given_rows[:, None] >= starts[None, :]) & (given_rows[:, None] < seq_ends[None, :])
    ).astype(jnp.int32)
    offset_in = given_rows - jnp.sum(seq_hot * starts[None, :], axis=1)
    slot_rank = jnp.sum(seq_hot * slot_of[None, :], axis=1)
    is_second = slot_rank % 2
    lead_pad = jnp.take(dealt_pad, slot_rank - is_second)
    target = slot_rank // 2 * CAP + jnp.where(is_second == 1, lead_pad, 0) + offset_in

    def deal(values):
        shard_rows = lax.all_gather(values, "fsdp", axis=0, tiled=True)
        row_span = shard_rows.shape[0]
        inside = (source >= 0) & (source < row_span)
        taken_rows = jnp.take(shard_rows, jnp.clip(source, 0, row_span - 1), axis=0)
        return jnp.where(inside[:, None], taken_rows, jnp.zeros((CAP, model_width), jnp.bfloat16))

    def give_back(values):
        shard_rows = lax.all_gather(values, "fsdp", axis=0, tiled=True)
        row_span = shard_rows.shape[0]
        inside = (target >= 0) & (target < row_span)
        taken_rows = jnp.take(shard_rows, jnp.clip(target, 0, row_span - 1), axis=0)
        return jnp.where(
            inside[:, None], taken_rows, jnp.zeros((TOK_DEV, model_width), jnp.bfloat16)
        )

    def collect():
        gate_in, up_in, down_in = (w_gate, w_up, w_down)
        sectioned = (
            lax.all_gather(gain_one, "fsdp", axis=0, tiled=True),
            lax.all_gather(w_query, "fsdp", axis=0, tiled=True),
            lax.all_gather(w_key, "fsdp", axis=0, tiled=True),
            lax.all_gather(w_value, "fsdp", axis=0, tiled=True),
            lax.all_gather(w_out, "fsdp", axis=0, tiled=True),
            lax.all_gather(gain_two, "fsdp", axis=0, tiled=True),
            lax.all_gather(w_router, "fsdp", axis=0, tiled=True),
            lax.all_gather(w_const, "fsdp", axis=0, tiled=True),
            lax.all_gather(v_const, "fsdp", axis=0, tiled=True),
            lax.all_gather(gate_in, "fsdp", axis=1, tiled=True),
            lax.all_gather(up_in, "fsdp", axis=1, tiled=True),
            lax.all_gather(down_in, "fsdp", axis=2, tiled=True),
        )
        (
            part_g1,
            part_q,
            part_k,
            part_v,
            part_o,
            part_g2,
            part_r,
            part_c,
            part_vc,
            part_gate,
            part_up,
            part_down,
        ) = sectioned
        small = (
            lax.all_gather(part_g1, "grp", axis=0, tiled=True),
            lax.all_gather(part_q, "grp", axis=1, tiled=True),
            lax.all_gather(part_k, "grp", axis=1, tiled=True),
            lax.all_gather(part_v, "grp", axis=1, tiled=True),
            lax.all_gather(part_o, "grp", axis=1, tiled=True),
            lax.all_gather(part_g2, "grp", axis=0, tiled=True),
            lax.all_gather(part_r, "grp", axis=0, tiled=True),
            lax.all_gather(part_c, "grp", axis=0, tiled=True),
            lax.all_gather(part_vc, "grp", axis=0, tiled=True),
        )
        experts = (
            lax.all_gather(part_gate, "grp", axis=2, tiled=True),
            lax.all_gather(part_up, "grp", axis=2, tiled=True),
            lax.all_gather(part_down, "grp", axis=1, tiled=True),
        )
        return tuple(small) + tuple(experts)

    (
        gain1,
        weight_q,
        weight_k,
        weight_v,
        weight_o,
        gain2,
        router,
        wconst,
        vconst,
        wgate,
        wup,
        wdown,
    ) = collect()
    dealt = deal(tokens)
    dealt_f = dealt.astype(jnp.float32)
    inv_one = lax.rsqrt(jnp.mean(dealt_f * dealt_f, axis=1, keepdims=True) + NORM_EPS)
    unit_one = dealt_f * inv_one
    gain1_f = gain1.astype(jnp.float32)
    normed_one = (unit_one * gain1_f).astype(jnp.bfloat16)
    cos_table, sin_table = rotation_tables(position, HEAD_DIM)
    query = rotate(
        jnp.dot(normed_one, weight_q, preferred_element_type=jnp.float32), cos_table, sin_table
    ).astype(jnp.bfloat16)
    keyed = rotate(
        jnp.dot(normed_one, weight_k, preferred_element_type=jnp.float32), cos_table, sin_table
    ).astype(jnp.bfloat16)
    values_proj = jnp.dot(normed_one, weight_v, preferred_element_type=jnp.float32).astype(
        jnp.bfloat16
    )
    allowed = (
        (in_second[:, None] == in_second[None, :])
        & (position[None, :] <= position[:, None])
        & live_rows[None, :]
    )

    def by_pairs(values):
        return values.reshape(CAP, pairs, pair_width).transpose(1, 0, 2)

    def from_pairs(values):
        return values.transpose(1, 0, 2).reshape(CAP, model_width)

    def pair_scores(q_pair, k_pair):
        query_heads = q_pair.reshape(CAP, 2, HEAD_DIM)
        key_heads = k_pair.reshape(CAP, 2, HEAD_DIM)
        scores = (
            jnp.einsum("qhd,khd->hqk", query_heads, key_heads, preferred_element_type=jnp.float32)
            * scale
        )
        return (jnp.where(allowed[None], scores, -1e30), query_heads, key_heads)

    def attend(pair_items):
        q_pair, k_pair, v_pair = pair_items
        scores, query_heads, key_heads = pair_scores(q_pair, k_pair)
        row_top = jnp.max(scores, axis=-1, keepdims=True)
        weights_exp = jnp.exp(scores - row_top)
        row_total = jnp.sum(weights_exp, axis=-1, keepdims=True)
        attn_probs = weights_exp / row_total
        value_heads = v_pair.reshape(CAP, 2, HEAD_DIM)
        mixed_pair = jnp.einsum(
            "hqk,khd->qhd",
            attn_probs.astype(jnp.bfloat16),
            value_heads,
            preferred_element_type=jnp.float32,
        )
        return (mixed_pair.reshape(CAP, pair_width), (row_top + jnp.log(row_total))[:, :, 0])

    mixed_pairs, log_sums = lax.map(
        attend, (by_pairs(query), by_pairs(keyed), by_pairs(values_proj))
    )
    mixed = from_pairs(mixed_pairs).astype(jnp.bfloat16)
    attn_out = jnp.dot(mixed, weight_o, preferred_element_type=jnp.float32).astype(jnp.bfloat16)
    returned = give_back(attn_out)
    resid = tokens.astype(jnp.float32) + returned.astype(jnp.float32)
    inv_two = lax.rsqrt(jnp.mean(resid * resid, axis=1, keepdims=True) + NORM_EPS)
    unit_two = resid * inv_two
    gain2_f = gain2.astype(jnp.float32)
    normed = unit_two * gain2_f
    narrow = normed.astype(jnp.bfloat16)
    mix_f = w_mix.astype(jnp.float32)
    router_f = router.astype(jnp.float32)
    wconst_f = wconst.astype(jnp.float32)
    logits = jnp.dot(narrow, router, preferred_element_type=jnp.float32) + exact_dot(
        prev_logits, mix_f
    )
    logit_top = jnp.max(logits, axis=1, keepdims=True)
    logit_exp = jnp.exp(logits - logit_top)
    route_probs = logit_exp / jnp.sum(logit_exp, axis=1, keepdims=True)
    expert_ids = jnp.arange(EXPERTS_ALL, dtype=jnp.int32)
    chosen = (
        (routes[:, 0:1] == expert_ids[None, :]) | (routes[:, 1:2] == expert_ids[None, :])
    ).astype(jnp.float32)
    gate_weights = route_probs * chosen
    result = resid + gate_weights[:, E + 1 : E + 2] * normed
    const_logits = jnp.dot(narrow, wconst, preferred_element_type=jnp.float32)
    vconst_f = vconst.astype(jnp.float32)
    const_mixes = []
    const_branches = []
    for const_idx in range(CONSTS):
        part_logits = const_logits[:, 2 * const_idx : 2 * const_idx + 2]
        part_exp = jnp.exp(part_logits - jnp.max(part_logits, axis=1, keepdims=True))
        const_mix = part_exp / jnp.sum(part_exp, axis=1, keepdims=True)
        branch = const_mix[:, 0:1] * normed + const_mix[:, 1:2] * vconst_f[:, const_idx][None, :]
        const_mixes.append(const_mix)
        const_branches.append(branch)
        result = result + gate_weights[:, E + 2 + const_idx : E + 3 + const_idx] * branch
    slot_list = []
    filled_list = []
    slot_gate_list = []
    for expert in range(E):
        member = (routes[:, 0] == expert) | (routes[:, 1] == expert)
        place_at = jnp.cumsum(member.astype(jnp.int32)) - 1
        slot_table = (
            jnp.zeros((MOST,), jnp.int32)
            .at[jnp.where(member, place_at, MOST)]
            .set(jnp.arange(TOK_DEV, dtype=jnp.int32), mode="drop")
        )
        filled = jnp.arange(MOST, dtype=jnp.int32) < jnp.sum(member.astype(jnp.int32))
        slot_list.append(slot_table)
        filled_list.append(filled)
        slot_gate_list.append(jnp.where(filled, jnp.take(gate_weights[:, expert], slot_table), 0.0))
    slot_tables = jnp.stack(slot_list, axis=0)
    filled_all = jnp.stack(filled_list, axis=0)
    slot_gates = jnp.stack(slot_gate_list, axis=0)
    expert_kept = []
    out_list = []
    for expert in range(E):
        picked = jnp.take(narrow, slot_tables[expert], axis=0)
        gate_part = jnp.dot(picked, wgate[expert], preferred_element_type=jnp.float32)
        up_part = jnp.dot(picked, wup[expert], preferred_element_type=jnp.float32)
        hidden = (jax.nn.silu(gate_part) * up_part).astype(jnp.bfloat16)
        out_list.append(jnp.dot(hidden, wdown[expert], preferred_element_type=jnp.float32))
        expert_kept.append((picked, gate_part, up_part, hidden))
    expert_outs = jnp.stack(out_list, axis=0)
    for expert in range(E):
        result = result.at[slot_tables[expert]].add(
            slot_gates[expert][:, None] * expert_outs[expert]
        )
    output = result.astype(jnp.bfloat16)
    (
        gain1,
        weight_q,
        weight_k,
        weight_v,
        weight_o,
        gain2,
        router,
        wconst,
        vconst,
        wgate,
        wup,
        wdown,
    ) = collect()
    gain1_f = gain1.astype(jnp.float32)
    gain2_f = gain2.astype(jnp.float32)
    router_f = router.astype(jnp.float32)
    wconst_f = wconst.astype(jnp.float32)
    vconst_f = vconst.astype(jnp.float32)
    grad_out = cotangent.astype(jnp.float32)
    d_gate_cols = [jnp.zeros((TOK_DEV,), jnp.float32) for expert in range(EXPERTS_ALL)]
    d_gate_cols[E + 1] = jnp.sum(grad_out * normed, axis=1)
    d_normed = gate_weights[:, E + 1 : E + 2] * grad_out
    d_const_parts = []
    d_vconst_cols = []
    for const_idx in range(CONSTS):
        const_mix = const_mixes[const_idx]
        gate_col = gate_weights[:, E + 2 + const_idx]
        d_gate_cols[E + 2 + const_idx] = jnp.sum(grad_out * const_branches[const_idx], axis=1)
        d_piece = gate_col[:, None] * grad_out
        d_normed = d_normed + const_mix[:, 0:1] * d_piece
        d_cmix = jnp.stack(
            [
                jnp.sum(d_piece * normed, axis=1),
                jnp.sum(d_piece * vconst_f[:, const_idx][None, :], axis=1),
            ],
            axis=1,
        )
        d_const_parts.append(
            const_mix * (d_cmix - jnp.sum(const_mix * d_cmix, axis=1, keepdims=True))
        )
        d_vconst_cols.append(exact_dot(const_mix[:, 1] * gate_col, grad_out))
    d_const_logits = jnp.concatenate(d_const_parts, axis=1)
    grad_rows_all = jnp.take(grad_out, slot_tables.reshape(-1), axis=0).reshape(
        E, MOST, model_width
    )
    d_slot_gates = jnp.where(filled_all, jnp.sum(grad_rows_all * expert_outs, axis=2), 0.0)
    for expert in range(E):
        d_gate_cols[expert] = (
            jnp.zeros((TOK_DEV,), jnp.float32).at[slot_tables[expert]].add(d_slot_gates[expert])
        )
    d_expert_all = (slot_gates[:, :, None] * grad_rows_all).astype(jnp.bfloat16)
    d_wgate_list = []
    d_wup_list = []
    d_wdown_list = []
    d_picked_list = []
    for expert in range(E):
        picked, gate_part, up_part, hidden = expert_kept[expert]
        d_expert = d_expert_all[expert]
        d_wdown_list.append(jnp.dot(hidden.T, d_expert, preferred_element_type=jnp.float32))
        d_hidden = jnp.dot(d_expert, wdown[expert].T, preferred_element_type=jnp.float32)
        sigmoid_g = jax.nn.sigmoid(gate_part)
        d_up_part = (d_hidden * gate_part * sigmoid_g).astype(jnp.bfloat16)
        d_gate_part = (
            d_hidden * up_part * sigmoid_g * (1.0 + gate_part * (1.0 - sigmoid_g))
        ).astype(jnp.bfloat16)
        d_wgate_list.append(jnp.dot(picked.T, d_gate_part, preferred_element_type=jnp.float32))
        d_wup_list.append(jnp.dot(picked.T, d_up_part, preferred_element_type=jnp.float32))
        d_picked_list.append(
            jnp.dot(d_gate_part, wgate[expert].T, preferred_element_type=jnp.float32)
            + jnp.dot(d_up_part, wup[expert].T, preferred_element_type=jnp.float32)
        )
    d_picked_all = jnp.stack(d_picked_list, axis=0)
    d_wgate_full = jnp.stack(d_wgate_list, axis=0)
    d_wup_full = jnp.stack(d_wup_list, axis=0)
    d_wdown_full = jnp.stack(d_wdown_list, axis=0)
    d_narrow = jnp.zeros((TOK_DEV, model_width), jnp.float32)
    for expert in range(E):
        d_narrow = d_narrow.at[slot_tables[expert]].add(
            jnp.where(filled_all[expert][:, None], d_picked_all[expert], 0.0)
        )
    d_gate_w = jnp.stack(d_gate_cols, axis=1)
    d_probs = d_gate_w * chosen
    d_logits = route_probs * (d_probs - jnp.sum(route_probs * d_probs, axis=1, keepdims=True))
    narrow_f = narrow.astype(jnp.float32)
    d_narrow = d_narrow + exact_dot(d_logits, router_f.T) + exact_dot(d_const_logits, wconst_f.T)
    d_router_full = exact_dot(narrow_f.T, d_logits)
    d_wconst_full = exact_dot(narrow_f.T, d_const_logits)
    d_vconst_full = jnp.stack(d_vconst_cols, axis=1)
    d_mix_full = exact_dot(prev_logits.T, d_logits)
    grad_prev = exact_dot(d_logits, mix_f.T)
    d_normed_total = d_normed + d_narrow
    d_gain2_full = jnp.sum(d_normed_total * unit_two, axis=0)
    d_unit_two = d_normed_total * gain2_f
    d_resid = grad_out + inv_two * (
        d_unit_two - unit_two * jnp.mean(d_unit_two * unit_two, axis=1, keepdims=True)
    )
    d_attn = deal(d_resid.astype(jnp.bfloat16))
    d_wo_full = jnp.dot(mixed.T, d_attn, preferred_element_type=jnp.float32)
    d_mixed = jnp.dot(d_attn, weight_o.T, preferred_element_type=jnp.float32).astype(jnp.bfloat16)

    def attend_back(pair_items):
        q_pair, k_pair, v_pair, dm_pair, lse_pair = pair_items
        scores, query_heads, key_heads = pair_scores(q_pair, k_pair)
        attn_probs = jnp.where(allowed[None], jnp.exp(scores - lse_pair[:, :, None]), 0.0)
        value_heads = v_pair.reshape(CAP, 2, HEAD_DIM)
        dm_heads = dm_pair.reshape(CAP, 2, HEAD_DIM)
        d_p = jnp.einsum("qhd,khd->hqk", dm_heads, value_heads, preferred_element_type=jnp.float32)
        row_delta = jnp.sum(attn_probs * d_p, axis=-1, keepdims=True)
        d_scores = (attn_probs * (d_p - row_delta)).astype(jnp.bfloat16)
        d_q = (
            jnp.einsum("hqk,khd->qhd", d_scores, key_heads, preferred_element_type=jnp.float32)
            * scale
        )
        d_k = (
            jnp.einsum("hqk,qhd->khd", d_scores, query_heads, preferred_element_type=jnp.float32)
            * scale
        )
        d_v = jnp.einsum(
            "hqk,qhd->khd",
            attn_probs.astype(jnp.bfloat16),
            dm_heads,
            preferred_element_type=jnp.float32,
        )
        return (
            d_q.reshape(CAP, pair_width),
            d_k.reshape(CAP, pair_width),
            d_v.reshape(CAP, pair_width),
        )

    dq_pairs, dk_pairs, dv_pairs = lax.map(
        attend_back,
        (by_pairs(query), by_pairs(keyed), by_pairs(values_proj), by_pairs(d_mixed), log_sums),
    )
    d_query = rotate(from_pairs(dq_pairs), cos_table, -sin_table).astype(jnp.bfloat16)
    d_key = rotate(from_pairs(dk_pairs), cos_table, -sin_table).astype(jnp.bfloat16)
    d_value = from_pairs(dv_pairs).astype(jnp.bfloat16)
    d_wq_full = jnp.dot(normed_one.T, d_query, preferred_element_type=jnp.float32)
    d_wk_full = jnp.dot(normed_one.T, d_key, preferred_element_type=jnp.float32)
    d_wv_full = jnp.dot(normed_one.T, d_value, preferred_element_type=jnp.float32)
    d_normed_one = (
        jnp.dot(d_query, weight_q.T, preferred_element_type=jnp.float32)
        + jnp.dot(d_key, weight_k.T, preferred_element_type=jnp.float32)
        + jnp.dot(d_value, weight_v.T, preferred_element_type=jnp.float32)
    )
    d_gain1_full = jnp.sum(d_normed_one * unit_one, axis=0)
    d_unit_one = d_normed_one * gain1_f
    d_dealt = (
        inv_one * (d_unit_one - unit_one * jnp.mean(d_unit_one * unit_one, axis=1, keepdims=True))
    ).astype(jnp.bfloat16)
    grad_tokens = d_resid + give_back(d_dealt).astype(jnp.float32)

    def regroup(grads_in):
        tail_shape = grads_in.shape[1:]
        split_view = grads_in.reshape((groups, dealers, per_shard) + tail_shape)
        return jnp.swapaxes(split_view, 0, 1).reshape((model_width,) + tail_shape)

    mix_tile = jnp.broadcast_to(d_mix_full[None], (dealers, EXPERTS_ALL, EXPERTS_ALL))
    sectioned = (
        lax.psum_scatter(
            regroup(d_gain1_full).astype(jnp.bfloat16), "fsdp", scatter_dimension=0, tiled=True
        ).astype(jnp.float32),
        lax.psum_scatter(
            d_wq_full.astype(jnp.bfloat16), "fsdp", scatter_dimension=0, tiled=True
        ).astype(jnp.float32),
        lax.psum_scatter(
            d_wk_full.astype(jnp.bfloat16), "fsdp", scatter_dimension=0, tiled=True
        ).astype(jnp.float32),
        lax.psum_scatter(
            d_wv_full.astype(jnp.bfloat16), "fsdp", scatter_dimension=0, tiled=True
        ).astype(jnp.float32),
        lax.psum_scatter(
            d_wo_full.astype(jnp.bfloat16), "fsdp", scatter_dimension=0, tiled=True
        ).astype(jnp.float32),
        lax.psum_scatter(
            regroup(d_gain2_full).astype(jnp.bfloat16), "fsdp", scatter_dimension=0, tiled=True
        ).astype(jnp.float32),
        lax.psum_scatter(
            regroup(d_router_full).astype(jnp.bfloat16), "fsdp", scatter_dimension=0, tiled=True
        ).astype(jnp.float32),
        lax.psum_scatter(
            regroup(d_wconst_full).astype(jnp.bfloat16), "fsdp", scatter_dimension=0, tiled=True
        ).astype(jnp.float32),
        lax.psum_scatter(
            regroup(d_vconst_full).astype(jnp.bfloat16), "fsdp", scatter_dimension=0, tiled=True
        ).astype(jnp.float32),
        lax.psum_scatter(
            mix_tile.astype(jnp.bfloat16), "fsdp", scatter_dimension=0, tiled=True
        ).astype(jnp.float32),
        lax.psum_scatter(
            d_wgate_full.astype(jnp.bfloat16), "fsdp", scatter_dimension=1, tiled=True
        ).astype(jnp.float32),
        lax.psum_scatter(
            d_wup_full.astype(jnp.bfloat16), "fsdp", scatter_dimension=1, tiled=True
        ).astype(jnp.float32),
        lax.psum_scatter(
            d_wdown_full.astype(jnp.bfloat16), "fsdp", scatter_dimension=2, tiled=True
        ).astype(jnp.float32),
    )
    s_g1, s_q, s_k, s_v, s_o, s_g2, s_r, s_c, s_vc, s_mix, s_gate, s_up, s_down = sectioned
    summed = (
        lax.psum_scatter(s_g1.astype(jnp.bfloat16), "grp", scatter_dimension=0, tiled=True).astype(
            jnp.float32
        ),
        lax.psum_scatter(s_q.astype(jnp.bfloat16), "grp", scatter_dimension=1, tiled=True).astype(
            jnp.float32
        ),
        lax.psum_scatter(s_k.astype(jnp.bfloat16), "grp", scatter_dimension=1, tiled=True).astype(
            jnp.float32
        ),
        lax.psum_scatter(s_v.astype(jnp.bfloat16), "grp", scatter_dimension=1, tiled=True).astype(
            jnp.float32
        ),
        lax.psum_scatter(s_o.astype(jnp.bfloat16), "grp", scatter_dimension=1, tiled=True).astype(
            jnp.float32
        ),
        lax.psum_scatter(s_g2.astype(jnp.bfloat16), "grp", scatter_dimension=0, tiled=True).astype(
            jnp.float32
        ),
        lax.psum_scatter(s_r.astype(jnp.bfloat16), "grp", scatter_dimension=0, tiled=True).astype(
            jnp.float32
        ),
        lax.psum_scatter(s_c.astype(jnp.bfloat16), "grp", scatter_dimension=0, tiled=True).astype(
            jnp.float32
        ),
        lax.psum_scatter(s_vc.astype(jnp.bfloat16), "grp", scatter_dimension=0, tiled=True).astype(
            jnp.float32
        ),
        lax.psum_scatter(
            jnp.broadcast_to(s_mix, (groups, EXPERTS_ALL, EXPERTS_ALL)).astype(jnp.bfloat16),
            "grp",
            scatter_dimension=0,
            tiled=True,
        ).astype(jnp.float32),
    )
    (
        grad_gain_one,
        grad_query,
        grad_key,
        grad_value,
        grad_out_proj,
        grad_gain_two,
        grad_router,
        grad_const,
        grad_vconst,
        mix_part,
    ) = summed
    grad_mix = mix_part[0]
    grad_gate, grad_up, grad_down = (
        lax.psum_scatter(
            s_gate.astype(jnp.bfloat16), "grp", scatter_dimension=2, tiled=True
        ).astype(jnp.float32),
        lax.psum_scatter(s_up.astype(jnp.bfloat16), "grp", scatter_dimension=2, tiled=True).astype(
            jnp.float32
        ),
        lax.psum_scatter(
            s_down.astype(jnp.bfloat16), "grp", scatter_dimension=1, tiled=True
        ).astype(jnp.float32),
    )
    return (
        output,
        grad_tokens,
        grad_prev,
        grad_gain_one,
        grad_query,
        grad_key,
        grad_value,
        grad_out_proj,
        grad_gain_two,
        grad_router,
        grad_mix,
        grad_const,
        grad_vconst,
        grad_gate,
        grad_up,
        grad_down,
    )


HALO = 256
KEYS = HALO + TOK_DEV
ROWS = E * MOST
NEG = -1e30
F32 = jnp.float32
BF16 = jnp.bfloat16
NT = (((1,), (1,)), ((), ()))
TN = (((0,), (0,)), ((), ()))
NN = (((1,), (0,)), ((), ()))


def mm(a, b, dims=NN):
    return lax.dot_general(a, b, dims, preferred_element_type=F32)


def lane_iota(rows, width=128):
    return lax.broadcasted_iota(jnp.int32, (rows, width), 1)


def pick(values, lane_mask):
    return jnp.sum(jnp.where(lane_mask, values, 0.0), axis=1, keepdims=True)


def params(mb, **kw):
    return pltpu.CompilerParams(vmem_limit_bytes=mb << 20, **kw)


def whole(count):
    return [pl.BlockSpec(memory_space=pltpu.VMEM) for _ in range(count)]


def sds(shape, dtype):
    return jax.ShapeDtypeStruct(shape, dtype)


MESH_ID = pl.DeviceIdType.MESH


def send(src, dst, send_sem, recv_sem, device):
    pltpu.make_async_remote_copy(
        src_ref=src,
        dst_ref=dst,
        send_sem=send_sem,
        recv_sem=recv_sem,
        device_id=device,
        device_id_type=MESH_ID,
    ).start()


def settle(ref, sem):
    pltpu.make_async_copy(ref, ref, sem).wait()


def flip(a, b):
    return a + b - 2 * a * b


def xor4(a, b):
    return flip(a // 2, b // 2) * 2 + flip(lax.rem(a, 2), lax.rem(b, 2))


def aligned(value, to):
    return pl.multiple_of(value, to)


class Place:
    def __init__(self, his, lo):
        self.g = lax.axis_index("grp")
        self.f = lax.axis_index("fsdp")
        self.his, self.lo = his, lo
        self.hi = self.g // lo
        self.l = lax.rem(self.g, lo)
        self.m = self.f * his + self.hi
        core = lax.rem(self.g, 2)
        side = lax.rem(self.g // 2, 2)
        self.core_peer = self.g + 1 - 2 * core
        self.side_peer = self.g + 2 - 4 * side
        self.l1 = lax.rem(self.core_peer, lo)
        self.l2 = lax.rem(self.side_peer, lo)
        self.l3 = lo - 1 - self.l

    def member(self, j, hh):
        f = xor4(self.f, j)
        hi = flip(self.hi, hh)
        return f * self.his + hi, (hi * self.lo + self.l, f)

    def others(self):
        peers = []
        for j in range(4):
            for hh in range(self.his):
                if j or hh:
                    peers.append(self.member(j, hh)[1])
        return peers


def call(peers):
    barrier = pltpu.get_barrier_semaphore()
    for peer in peers:
        pl.semaphore_signal(barrier, inc=1, device_id=peer, device_id_type=MESH_ID)


def answer(peers):
    pl.semaphore_wait(pltpu.get_barrier_semaphore(), len(peers))


def turn(values, cos, sin):
    half = HEAD_DIM // 2
    width = values.shape[1]
    reps = width // 128
    front = lax.rem(lane_iota(values.shape[0], width), HEAD_DIM) < half
    swapped = jnp.where(
        front, pltpu.roll(values, width - half, 1), pltpu.roll(values, half, 1)
    )
    cos_w = jnp.concatenate([cos] * reps, axis=1)
    sin_w = jnp.concatenate([sin] * reps, axis=1)
    return values * cos_w + swapped * sin_w


QBLOCKS = [(0, 128), (128, 128), (256, 64)]


def allowed_mask(pos_ref, first, count, lane):
    ii = lax.broadcasted_iota(jnp.int32, (count, 384), 0) + HALO
    jj = lax.broadcasted_iota(jnp.int32, (count, 384), 1)
    pos = pos_ref[pl.ds(first, count), lane : lane + 1].astype(jnp.int32)
    return (jj <= ii) & (jj >= ii - pos)


def key_span(first):
    return min(384, KEYS - first)


KEPT = (
    ("wf", (4, None, None), BF16),
    ("s", (None, 128), F32),
    ("halo", (HALO, None), BF16),
    ("q", (TOK_DEV, None), BF16),
    ("k", (KEYS, None), BF16),
    ("v", (KEYS, None), BF16),
    ("n1", (KEYS, None), BF16),
    ("inv1", (KEYS, 128), F32),
    ("mix", (TOK_DEV, None), BF16),
    ("lse", (TOK_DEV, 128), F32),
    ("resid", (TOK_DEV, None), F32),
    ("part", (TOK_DEV, None), F32),
    ("probs", (TOK_DEV, 128), F32),
    ("cols", (TOK_DEV, 128), F32),
    ("cos", (KEYS, 128), F32),
    ("sin", (KEYS, 128), F32),
)


def kept_shape(dims, width):
    return tuple(width if d is None else d for d in dims)


def by_name(refs):
    return {name: ref for (name, _, _), ref in zip(KEPT, refs)}


def token_places(len_ref, at):
    row = lax.broadcasted_iota(jnp.int32, (KEYS, 128), 0) + (at.f * TOK_DEV - HALO)
    first = jnp.zeros((KEYS, 128), jnp.int32)
    reached = jnp.int32(0)
    for i in range(len_ref.shape[1]):
        reached = reached + len_ref[0, i]
        first = jnp.where(row >= reached, reached, first)
    return jnp.maximum(row - first, 0)


def ahead_kernel(
    len_ref,
    routes_ref,
    prev_ref,
    wmix_ref,
    router_ref,
    gain1_ref,
    gain2_ref,
    const_ref,
    vconst_ref,
    wq_ref,
    wk_ref,
    wv_ref,
    wo_ref,
    tok_ref,
    cot_ref,
    wg_hbm,
    wu_hbm,
    wd_hbm,
    *rest,
):
    n = len(KEPT)
    kept_hbm = by_name(rest[:n])
    op_hbm, gw_hbm, back_hbm, dgb_hbm = rest[n : n + 4]
    kept = by_name(rest[n + 4 : 2 * n + 4])
    (
        tile_ref,
        small_ref,
        p_ref,
        grow_ref,
        x_ref,
        gates_ref,
        wgu_ref,
        wd_ref,
        g_ref,
        xb_ref,
        gb_ref,
        od_ref,
        op_ref,
        r1_ref,
        r2_ref,
        dgp_ref,
        dr1_ref,
        dr2_ref,
        accgu_ref,
        accd_ref,
        hid_ref,
        dgu_ref,
        gw_ref,
        back_ref,
        dgb_ref,
        keep_sem,
        last_sem,
        zs,
        ps,
        cs,
        hs,
        gs,
        ws,
        gas,
        agr,
        hr,
        gr,
        wr,
        gqr,
        xs,
        ts,
        qs,
        tqs,
        d1s,
        t1s,
        d2s,
        t2s,
        bs,
        tbs,
        xr,
        tr,
        qr,
        tqr,
        d1r,
        t1r,
        d2r,
        t2r,
        br,
        tbr,
    ) = rest[2 * n + 4 :]
    wf_ref, s_ref, halo_ref = kept["wf"], kept["s"], kept["halo"]
    q_ref, k_ref, v_ref, n1_ref = kept["q"], kept["k"], kept["v"], kept["n1"]
    mix_ref, lse_ref = kept["mix"], kept["lse"]
    lo, ranks = g_ref.shape[:2]
    his = E // ranks
    at = Place(his, lo)
    width = tok_ref.shape[1]
    head_rows, part_cols = wq_ref.shape
    ff = wg_hbm.shape[2]
    diag = lo * (1 - at.hi) + at.l2
    upper = lo * (1 - at.hi) + at.l
    near = [(at.core_peer, at.f), (at.side_peer, at.f), (upper, at.f), (diag, at.f)]
    core, side = near[0], near[1]
    peers = at.others() + [near[0], near[1], near[3]]
    call(peers)

    def keep(*names):
        for name in names:
            i = [k[0] for k in KEPT].index(name)
            pltpu.make_async_copy(kept[name], kept_hbm[name], keep_sem.at[i]).start()

    tile_ref[0:head_rows, :] = jnp.concatenate(
        [wq_ref[...], wk_ref[...], wv_ref[...], wo_ref[...]], axis=1
    )
    small_ref[...] = jnp.zeros_like(small_ref)
    per = router_ref.shape[1]
    small_ref[0:EXPERTS_ALL, 0:per] = router_ref[...].astype(F32)
    small_ref[SMALL_G1 : SMALL_G1 + 1, 0:per] = gain1_ref[...].astype(F32)
    small_ref[SMALL_G1 + 1 : SMALL_G1 + 2, 0:per] = gain2_ref[...].astype(F32)
    small_ref[SMALL_VC : SMALL_VC + CONSTS, 0:per] = vconst_ref[...].astype(F32)
    small_ref[SMALL_C : SMALL_C + 2 * CONSTS, 0:per] = const_ref[...].astype(F32)
    turned = small_ref[...].T
    tile_ref[head_rows : head_rows + 8, :] = jnp.concatenate(
        [turned[8 * i : 8 * i + 8, :] for i in range(per // 8)], axis=1
    ).astype(BF16)
    answer(peers)

    p_ref[at.g, at.f] = tile_ref[...]
    for j in range(1, ranks):
        f2 = xor4(at.f, j)
        send(tile_ref, p_ref.at[at.g, at.f], zs.at[j], agr.at[at.g, at.f], (at.g, f2))

    def spread(j, f2, src):
        for t, peer in enumerate(near):
            send(src, p_ref.at[at.g, f2], ps.at[j, t], agr.at[at.g, f2], peer)

    spread(0, at.f, tile_ref)
    halo_rows = halo_ref.shape[0]
    tail = tok_ref.at[pl.ds(tok_ref.shape[0] - halo_rows, halo_rows)]

    @pl.when(at.f < ranks - 1)
    def _():
        send(tail, halo_ref, hs, hr, (at.g, at.f + 1))

    @pl.when(at.f == 0)
    def _():
        halo_ref[...] = jnp.zeros_like(halo_ref)

    lanes = lane_iota(TOK_DEV)
    routes = jnp.concatenate(
        [
            jnp.broadcast_to(routes_ref[0:1, :], (8, TOK_DEV)),
            jnp.broadcast_to(routes_ref[1:2, :], (8, TOK_DEV)),
        ],
        axis=0,
    ).T
    r0 = routes[:, 0:1]
    r1 = routes[:, 8:9]
    hot0 = lanes == r0
    hot1 = lanes == r1
    named = jnp.where(hot0 | hot1, 1.0, 0.0).astype(BF16)
    earlier = (
        lax.broadcasted_iota(jnp.int32, (TOK_DEV, TOK_DEV), 1)
        < lax.broadcasted_iota(jnp.int32, (TOK_DEV, TOK_DEV), 0)
    )
    rank = mm(jnp.where(earlier, 1.0, 0.0).astype(BF16), named)
    rank0 = pick(rank, hot0).astype(jnp.int32)
    rank1 = pick(rank, hot1).astype(jnp.int32)
    c0 = jnp.where(r0 < E, r0 * MOST + rank0, -1)
    c1 = jnp.where(r1 < E, r1 * MOST + rank1, -1)
    slot = lane_iota(TOK_DEV, ROWS)
    spots0 = jnp.where(slot == c0, 1.0, 0.0).astype(BF16)
    spots1 = jnp.where(slot == c1, 1.0, 0.0).astype(BF16)
    grow_ref[...] = mm(spots0 + spots1, cot_ref[...], TN).astype(BF16)

    for j in range(1, ranks):
        f2 = xor4(at.f, j)
        settle(p_ref.at[at.g, f2], agr.at[at.g, f2])
        spread(j, f2, p_ref.at[at.g, f2])

    own_rows = pl.ds(aligned(at.f * head_rows, 16), head_rows)
    own_cols = pl.ds(aligned(at.hi * ff, 128), ff)
    own_spot = pl.ds(aligned(at.hi * MOST, 16), MOST)

    for j in range(ranks):
        for hh in range(his):
            e, peer = at.member(j, hh)
            rows = grow_ref.at[pl.ds(aligned(e * MOST, 16), MOST)]
            spot = g_ref.at[at.l, at.f, own_spot]
            if j == 0 and hh == 0:
                pltpu.make_async_copy(rows, spot, gr.at[at.m]).start()
            else:
                send(rows, spot, gs.at[j * his + hh], gr.at[at.m], peer)

    def dispatch():
        for j in range(ranks):
            for hh in range(his):
                e, peer = at.member(j, hh)
                sources = (wg_hbm.at[e], wu_hbm.at[e], wd_hbm.at[e])
                for w in range(3):
                    first = aligned(w * his * ff + at.hi * ff, 128)
                    spot = (
                        wd_ref.at[own_rows, own_cols]
                        if w == 2
                        else wgu_ref.at[own_rows, pl.ds(first, ff)]
                    )
                    if j == 0 and hh == 0:
                        pltpu.make_async_copy(sources[w], spot, wr.at[at.m, w]).start()
                    else:
                        send(sources[w], spot, ws.at[j * his + hh, w], wr.at[at.m, w], peer)

    pos = token_places(len_ref, at).astype(F32)
    half_dim = HEAD_DIM // 2
    lane_k = lane_iota(KEYS)
    freq = jnp.exp(
        lax.rem(lane_k, half_dim).astype(F32) * (-2.0 * math.log(10000.0) / HEAD_DIM)
    )
    kept["cos"][...] = jnp.cos(pos * freq)
    sine = jnp.sin(pos * freq)
    kept["sin"][...] = jnp.where(lax.rem(lane_k, HEAD_DIM) < half_dim, -sine, sine)
    pos_own = pos[HALO:]
    pos_ref = kept["cols"]
    pos_ref[...] = pos_own

    for j in range(ranks):
        f2 = xor4(at.f, j)
        for t in range(1, 4):
            g2 = near[t][0]
            settle(p_ref.at[g2, f2], agr.at[g2, f2])
            send(p_ref.at[g2, f2], p_ref.at[g2, f2], cs.at[t - 1, j], agr.at[g2, f2], near[0])
    sibling_upper = lo * (1 - at.hi) + at.l1
    for j in range(ranks):
        f2 = xor4(at.f, j)
        for g2 in (
            at.core_peer,
            at.hi * lo + at.l3,
            sibling_upper,
            lo * (1 - at.hi) + at.l3,
        ):
            settle(p_ref.at[g2, f2], agr.at[g2, f2])

    dispatch()

    groups = p_ref.shape[0]
    for g2 in range(groups):
        for f2 in range(ranks):
            piece = p_ref[g2, f2, head_rows : head_rows + 8, :].astype(F32)
            for i in range(per // 8):
                base = (g2 * ranks + f2) * per + 8 * i
                s_ref[base : base + 8, :] = piece[:, 128 * i : 128 * i + 128]

    def lay(f2, _):
        rows = pl.ds(aligned(f2 * head_rows, 16), head_rows)
        for w in range(4):
            for half in range(2):
                pieces = [
                    p_ref[
                        half * (groups // 2) + i,
                        f2,
                        0:head_rows,
                        w * part_cols : (w + 1) * part_cols,
                    ]
                    for i in range(groups // 2)
                ]
                wf_ref[w, rows, half * (width // 2) : (half + 1) * (width // 2)] = (
                    jnp.concatenate(pieces, axis=1)
                )
        return 0

    lax.fori_loop(0, ranks, lay, 0)

    @pl.when(at.f > 0)
    def _():
        settle(halo_ref, hr)

    scale = HEAD_DIM ** (-0.5)
    flat = s_ref[...].T
    g1 = flat[SMALL_G1 : SMALL_G1 + 1, :]
    g2 = flat[SMALL_G1 + 1 : SMALL_G1 + 2, :]
    vc = flat[SMALL_VC : SMALL_VC + CONSTS, :]
    keep("wf", "s", "halo")
    rows = jnp.concatenate([halo_ref[...], tok_ref[...]], axis=0).astype(F32)
    inv1 = lax.rsqrt(jnp.mean(rows * rows, axis=1, keepdims=True) + NORM_EPS)
    kept["inv1"][...] = jnp.broadcast_to(inv1, (KEYS, 128))
    n1_ref[...] = (rows * inv1 * g1).astype(BF16)

    def project(i, _):
        span = pl.ds(pl.multiple_of(i * 256, 256), 256)
        cos = kept["cos"][...]
        sin = kept["sin"][...]
        q = mm(n1_ref[HALO:, :], wf_ref[0, :, span])
        q_ref[:, span] = turn(q, cos[HALO:], sin[HALO:]).astype(BF16)
        k = mm(n1_ref[...], wf_ref[1, :, span])
        k_ref[:, span] = turn(k, cos, sin).astype(BF16)
        v_ref[:, span] = mm(n1_ref[...], wf_ref[2, :, span]).astype(BF16)
        return 0

    lax.fori_loop(0, width // 256, project, 0)
    keep("q", "k", "v", "n1", "inv1", "cos", "sin")
    lse_ref[...] = jnp.zeros((TOK_DEV, 128), F32)

    for f2 in range(ranks):
        for h2 in range(his):
            settle(
                g_ref.at[at.l, f2, h2 * MOST : (h2 + 1) * MOST], gr.at[f2 * his + h2]
            )
    send(g_ref.at[at.l], g_ref.at[at.l], gas.at[0], gqr.at[0], near[0])
    send(g_ref.at[at.l], g_ref.at[at.l], gas.at[1], gqr.at[1], near[1])

    def pair(p, _):
        span = pl.ds(pl.multiple_of(p * 128, 128), 128)
        for first, count in QBLOCKS:
            keys = key_span(first)
            ok = allowed_mask(pos_ref, first, count, 0)[:, :keys]
            q = q_ref[pl.ds(first, count), span]
            k = k_ref[pl.ds(first, keys), span]
            v = v_ref[pl.ds(first, keys), span]
            lane = lane_iota(count)
            out = None
            lse = lse_ref[pl.ds(first, count), :]
            for h in range(2):
                mine = (lane < HEAD_DIM) if h == 0 else (lane >= HEAD_DIM)
                qh = jnp.where(mine, q, jnp.zeros_like(q))
                sc = jnp.where(ok, mm(qh, k, NT) * scale, NEG)
                top = jnp.max(sc, axis=1, keepdims=True)
                ex = jnp.exp(sc - top)
                total = jnp.sum(ex, axis=1, keepdims=True)
                o = mm((ex / total).astype(BF16), v)
                out = o if h == 0 else jnp.where(mine, o, out)
                lse = jnp.where(lane == 2 * p + h, top + jnp.log(total), lse)
            mix_ref[pl.ds(first, count), span] = out.astype(BF16)
            lse_ref[pl.ds(first, count), :] = lse
        return 0

    lax.fori_loop(0, HEADS // 2, pair, 0)
    settle(g_ref.at[at.l2], gqr.at[1])
    send(g_ref.at[at.l2], g_ref.at[at.l2], gas.at[2], gqr.at[2], near[0])

    attn_out = mm(mix_ref[...], wf_ref[3]).astype(BF16)
    resid = tok_ref[...].astype(F32) + attn_out.astype(F32)
    kept["resid"][...] = resid
    inv2 = lax.rsqrt(jnp.mean(resid * resid, axis=1, keepdims=True) + NORM_EPS)
    normed = resid * inv2 * g2
    narrow = normed.astype(BF16)
    raw = mm(narrow, s_ref[...].astype(BF16))
    prev = prev_ref[...]
    wmix = jnp.concatenate(
        [wmix_ref[...].astype(F32), jnp.zeros((EXPERTS_ALL, 128 - EXPERTS_ALL), F32)], axis=1
    ).astype(BF16)
    phigh = prev.astype(BF16)
    prest = prev - phigh.astype(F32)
    pmid = prest.astype(BF16)
    plow = (prest - pmid.astype(F32)).astype(BF16)
    mixed_prev = mm(phigh, wmix, TN) + (mm(pmid, wmix, TN) + mm(plow, wmix, TN))
    logits = jnp.where(lanes < EXPERTS_ALL, raw + mixed_prev, NEG)
    top = jnp.max(logits, axis=1, keepdims=True)
    ex = jnp.exp(logits - top)
    probs = ex / jnp.sum(ex, axis=1, keepdims=True)
    kept["probs"][...] = probs
    gate0 = pick(probs, hot0)
    gate1 = pick(probs, hot1)

    def gate_of(expert):
        return jnp.where(r0 == expert, gate0, 0.0) + jnp.where(r1 == expert, gate1, 0.0)

    gate_id = gate_of(E + 1)
    part = resid + gate_id * normed
    cols = jnp.where(lanes == 0, gate0, 0.0)
    cols = jnp.where(lanes == 1, gate1, cols)
    cols = jnp.where(lanes == 2, gate_id, cols)
    cols = jnp.where(lanes == 3, inv2, cols)
    for c in range(CONSTS):
        la = pick(raw, lanes == SMALL_C + 2 * c)
        lb = pick(raw, lanes == SMALL_C + 1 + 2 * c)
        big = jnp.maximum(la, lb)
        ea = jnp.exp(la - big)
        eb = jnp.exp(lb - big)
        ma = ea / (ea + eb)
        mb = eb / (ea + eb)
        gate_c = gate_of(E + 2 + c)
        part = part + gate_c * (ma * normed + mb * vc[c : c + 1, :])
        cols = jnp.where(lanes == 4 + 3 * c, gate_c, cols)
        cols = jnp.where(lanes == 5 + 3 * c, ma, cols)
        cols = jnp.where(lanes == 6 + 3 * c, mb, cols)
    kept["part"][...] = part
    wide0 = jnp.where(r0 < E, r0 * 128 + rank0, -1)
    wide1 = jnp.where(r1 < E, r1 * 128 + rank1, -1)
    more = (pos_own[:, 0:1], c0, c1, r0, r1, wide0, wide1)
    for i, value in enumerate(more):
        cols = jnp.where(lanes == COL_POS + i, value.astype(F32), cols)
    kept["cols"][...] = cols
    keep("mix", "lse", "resid", "part", "probs", "cols")
    x_ref[...] = mm(spots0 + spots1, narrow, TN).astype(BF16)
    for e in range(E):
        lane = lanes + e * 128
        row = jnp.sum(
            jnp.where(lane == wide0, gate0, 0.0) + jnp.where(lane == wide1, gate1, 0.0),
            axis=0,
            keepdims=True,
        )
        gates_ref[e] = jnp.broadcast_to(row, (8, 128))


    def give(j):
        for hh in range(his):
            e, peer = at.member(j, hh)
            k = j * his + hh
            rows = x_ref.at[pl.ds(aligned(e * MOST, 16), MOST)]
            spot = xb_ref.at[at.f, at.l, own_spot]
            line = gb_ref.at[at.f, at.l, at.hi]
            if k == 0:
                pltpu.make_async_copy(rows, spot, xr.at[at.m]).start()
                pltpu.make_async_copy(gates_ref.at[e], line, tr.at[at.m]).start()
            else:
                send(rows, spot, xs.at[k], xr.at[at.m], peer)
                send(gates_ref.at[e], line, ts.at[k], tr.at[at.m], peer)

    give(0)
    give(1)
    accgu_ref[...] = jnp.zeros_like(accgu_ref)
    accd_ref[...] = jnp.zeros_like(accd_ref)

    def take(j):
        fj = xor4(at.f, j)
        for hh in range(his):
            hi = flip(at.hi, hh)
            m = fj * his + hi
            settle(xb_ref.at[fj, at.l, pl.ds(aligned(hi * MOST, 16), MOST)], xr.at[m])
            settle(gb_ref.at[fj, at.l, hi], tr.at[m])
        for i, peer in enumerate((core, side)):
            send(xb_ref.at[fj, at.l], xb_ref.at[fj, at.l], qs.at[fj, i], qr.at[fj, i], peer)
            send(gb_ref.at[fj, at.l], gb_ref.at[fj, at.l], tqs.at[fj, i], tqr.at[fj, i], peer)

    def pass_on(j):
        fj = xor4(at.f, j)
        settle(xb_ref.at[fj, at.l2], qr.at[fj, 1])
        settle(gb_ref.at[fj, at.l2], tqr.at[fj, 1])
        send(xb_ref.at[fj, at.l2], xb_ref.at[fj, at.l2], qs.at[fj, 2], qr.at[fj, 2], core)
        send(gb_ref.at[fj, at.l2], gb_ref.at[fj, at.l2], tqs.at[fj, 2], tqr.at[fj, 2], core)

    diagonal = lax.broadcasted_iota(jnp.int32, (MOST, 128), 0) == lane_iota(MOST)

    def arithmetic(x, g, gate, these):
        grow_ref[these, :] = (g.astype(F32) * gate).astype(BF16)
        wgu = wgu_ref[...]
        ab = mm(x, wgu)
        inner = ab.shape[1] // 2
        a = ab[:, :inner]
        b = ab[:, inner:]
        sig = 1.0 / (1.0 + jnp.exp(-a))
        act = a * sig
        hidden = (act * b).astype(BF16)
        hid_ref[these, :] = hidden
        dh_raw = mm(g, wd_ref[...])
        d_route = jnp.sum(hidden.astype(F32) * dh_raw, axis=1, keepdims=True)
        lines = []
        for n in range(x.shape[0] // MOST):
            line = jnp.where(diagonal, d_route[n * MOST : (n + 1) * MOST], 0.0)
            lines.append(jnp.broadcast_to(jnp.sum(line, axis=0, keepdims=True), (8, 128)))
        dh = dh_raw * gate
        d_up = (dh * act).astype(BF16)
        d_gate = (dh * b * (sig + act * (1.0 - sig))).astype(BF16)
        dgu = jnp.concatenate([d_gate, d_up], axis=1)
        dgu_ref[these, :] = dgu
        return mm(dgu, wgu, NT).astype(BF16), lines

    def column(line):
        return pick(jnp.broadcast_to(line, (MOST, 128)), diagonal)

    def compute(j):
        fj = xor4(at.f, j)
        settle(xb_ref.at[fj, at.l1], qr.at[fj, 0])
        settle(gb_ref.at[fj, at.l1], tqr.at[fj, 0])
        settle(xb_ref.at[fj, at.l3], qr.at[fj, 2])
        settle(gb_ref.at[fj, at.l3], tqr.at[fj, 2])
        pair_rows = 2 * his * MOST

        def rows_of(i, _):
            l2 = pl.ds(2 * i, 2)
            x = xb_ref[fj, l2].reshape(pair_rows, width)
            g = g_ref[l2, fj].reshape(pair_rows, width)
            gate = jnp.concatenate(
                [
                    column(gb_ref[fj, 2 * i + i2, h][0:1, :])
                    for i2 in range(2)
                    for h in range(his)
                ],
                axis=0,
            )
            these = pl.ds(aligned(i * pair_rows, 16), pair_rows)
            dx, lines = arithmetic(x, g, gate, these)
            for n, line in enumerate(lines):
                dgp_ref[fj, 2 * i + n // his, n % his] = line
            od_ref[fj, l2] = dx.reshape((2, his * MOST, width))
            return 0

        lax.fori_loop(0, lo // 2, rows_of, 0)

    def outputs_of(j):
        fj = xor4(at.f, j)
        slot = lax.rem(j, 2)
        pl.when(j >= 2)(lambda: settle(op_ref.at[slot], last_sem.at[slot]))
        op_ref[slot] = mm(hid_ref[...], wd_ref[...], NT).astype(BF16).reshape(
            (lo, his * MOST, width)
        )
        pltpu.make_async_copy(op_ref.at[slot], op_hbm.at[fj], last_sem.at[slot]).start()

    def weights_of(j):
        x_all = xb_ref[xor4(at.f, j)].reshape(lo * his * MOST, width)
        accgu_ref[...] += mm(x_all, dgu_ref[...], TN)
        accd_ref[...] += mm(grow_ref[...], hid_ref[...], TN)

    def to_core(j):
        fj = xor4(at.f, j)
        send(od_ref.at[fj, at.l1], r1_ref.at[fj, 0], d1s.at[fj, 0], d1r.at[fj, 0], core)
        send(od_ref.at[fj, at.l3], r1_ref.at[fj, 1], d1s.at[fj, 1], d1r.at[fj, 1], core)
        send(dgp_ref.at[fj, at.l1], dr1_ref.at[fj, 0], t1s.at[fj, 0], t1r.at[fj, 0], core)
        send(dgp_ref.at[fj, at.l3], dr1_ref.at[fj, 1], t1s.at[fj, 1], t1r.at[fj, 1], core)

    def add(ref, other):
        ref[...] = (ref[...].astype(F32) + other[...].astype(F32)).astype(BF16)

    def to_side(j):
        fj = xor4(at.f, j)
        settle(r1_ref.at[fj, 1], d1r.at[fj, 1])
        add(od_ref.at[fj, at.l2], r1_ref.at[fj, 1])
        send(od_ref.at[fj, at.l2], r2_ref.at[fj], d2s.at[fj], d2r.at[fj], side)
        settle(dr1_ref.at[fj, 1], t1r.at[fj, 1])
        dgp_ref[fj, at.l2] += dr1_ref[fj, 1]
        send(dgp_ref.at[fj, at.l2], dr2_ref.at[fj], t2s.at[fj], t2r.at[fj], side)
        settle(r1_ref.at[fj, 0], d1r.at[fj, 0])
        add(od_ref.at[fj, at.l], r1_ref.at[fj, 0])
        settle(dr1_ref.at[fj, 0], t1r.at[fj, 0])
        dgp_ref[fj, at.l] += dr1_ref[fj, 0]

    def to_home(j):
        fj = xor4(at.f, j)
        settle(r2_ref.at[fj], d2r.at[fj])
        add(od_ref.at[fj, at.l], r2_ref.at[fj])
        settle(dr2_ref.at[fj], t2r.at[fj])
        dgp_ref[fj, at.l] += dr2_ref[fj]
        for hh in range(his):
            hi = flip(at.hi, hh)
            m = fj * his + hi
            rows = od_ref.at[fj, at.l, pl.ds(aligned(hi * MOST, 16), MOST)]
            peer = (hi * lo + at.l, fj)

            line = dgp_ref.at[fj, at.l, hi]

            def away(rows=rows, line=line, peer=peer, m=m):
                send(rows, back_ref.at[at.m], bs.at[m], br.at[at.m], peer)
                send(line, dgb_ref.at[at.m], tbs.at[m], tbr.at[at.m], peer)

            if hh:
                away()
            else:

                @pl.when(j == 0)
                def _(rows=rows, line=line):
                    pltpu.make_async_copy(rows, back_ref.at[at.m], br.at[at.m]).start()
                    pltpu.make_async_copy(line, dgb_ref.at[at.m], tbr.at[at.m]).start()

                pl.when(j > 0)(away)

    last = ranks - 1
    fl = xor4(at.f, last)

    def half(hh):
        hi = flip(at.hi, hh)
        return hi, pl.ds(aligned(hi * MOST, 16), MOST), (fl if hh == 0 else ranks)

    def half_give(hh):
        k = last * his + hh
        e, peer = at.member(last, hh)
        rows = x_ref.at[pl.ds(aligned(e * MOST, 16), MOST)]
        send(rows, xb_ref.at[at.f, at.l, own_spot], xs.at[k], xr.at[at.m], peer)
        send(gates_ref.at[e], gb_ref.at[at.f, at.l, at.hi], ts.at[k], tr.at[at.m], peer)

    def half_take(hh):
        hi, spot, n = half(hh)
        m = fl * his + hi
        rows, line = xb_ref.at[fl, at.l, spot], gb_ref.at[fl, at.l, hi]
        settle(rows, xr.at[m])
        settle(line, tr.at[m])
        for i, peer in enumerate((core, side)):
            send(rows, rows, qs.at[n, i], qr.at[n, i], peer)
            send(line, line, tqs.at[n, i], tqr.at[n, i], peer)

    def half_pass(hh):
        hi, spot, n = half(hh)
        rows, line = xb_ref.at[fl, at.l2, spot], gb_ref.at[fl, at.l2, hi]
        settle(rows, qr.at[n, 1])
        settle(line, tqr.at[n, 1])
        send(rows, rows, qs.at[n, 2], qr.at[n, 2], core)
        send(line, line, tqs.at[n, 2], tqr.at[n, 2], core)

    half_rows = lo * MOST

    def half_compute(hh):
        hi, spot, n = half(hh)
        for quarter, i in ((at.l1, 0), (at.l3, 2)):
            settle(xb_ref.at[fl, quarter, spot], qr.at[n, i])
            settle(gb_ref.at[fl, quarter, hi], tqr.at[n, i])
        x = xb_ref[fl, :, spot].reshape(half_rows, width)
        g = g_ref[:, fl, spot].reshape(half_rows, width)
        gate = jnp.concatenate([column(gb_ref[fl, i, hi][0:1, :]) for i in range(lo)], axis=0)
        dx, lines = arithmetic(x, g, gate, pl.ds(hh * half_rows, half_rows))
        for i, line in enumerate(lines):
            dgp_ref[fl, i, hi] = line
        od_ref[fl, :, spot] = dx.reshape((lo, MOST, width))
        for i, quarter in enumerate((at.l1, at.l3)):
            send(
                od_ref.at[fl, quarter, spot],
                r1_ref.at[fl, i, spot],
                d1s.at[n, i],
                d1r.at[n, i],
                core,
            )
            send(
                dgp_ref.at[fl, quarter, hi],
                dr1_ref.at[fl, i, hi],
                t1s.at[n, i],
                t1r.at[n, i],
                core,
            )

    def half_side(hh):
        hi, spot, n = half(hh)
        settle(r1_ref.at[fl, 1, spot], d1r.at[n, 1])
        add(od_ref.at[fl, at.l2, spot], r1_ref.at[fl, 1, spot])
        send(od_ref.at[fl, at.l2, spot], r2_ref.at[fl, spot], d2s.at[n], d2r.at[n], side)
        settle(dr1_ref.at[fl, 1, hi], t1r.at[n, 1])
        dgp_ref[fl, at.l2, hi] += dr1_ref[fl, 1, hi]
        send(dgp_ref.at[fl, at.l2, hi], dr2_ref.at[fl, hi], t2s.at[n], t2r.at[n], side)
        settle(r1_ref.at[fl, 0, spot], d1r.at[n, 0])
        add(od_ref.at[fl, at.l, spot], r1_ref.at[fl, 0, spot])
        settle(dr1_ref.at[fl, 0, hi], t1r.at[n, 0])
        dgp_ref[fl, at.l, hi] += dr1_ref[fl, 0, hi]

    def half_home(hh):
        hi, spot, n = half(hh)
        m, peer = at.member(last, hh)
        settle(r2_ref.at[fl, spot], d2r.at[n])
        add(od_ref.at[fl, at.l, spot], r2_ref.at[fl, spot])
        settle(dr2_ref.at[fl, hi], t2r.at[n])
        dgp_ref[fl, at.l, hi] += dr2_ref[fl, hi]
        send(od_ref.at[fl, at.l, spot], back_ref.at[at.m], bs.at[m], br.at[at.m], peer)
        send(dgp_ref.at[fl, at.l, hi], dgb_ref.at[at.m], tbs.at[m], tbr.at[at.m], peer)

    take(0)
    pass_on(0)
    settle(g_ref.at[at.l1], gqr.at[0])
    settle(g_ref.at[at.l3], gqr.at[2])
    for k in range(1, E):
        settle(grow_ref.at[0:MOST], gs.at[k])
    for m in range(E):
        for w in range(3):
            settle(wd_ref.at[0:head_rows, 0:ff], wr.at[m, w])
    give(2)

    def step(t, _):
        @pl.when(t + 1 < last)
        def _():
            take(t + 1)

        @pl.when(t == 1)
        def _():
            half_give(0)

        @pl.when(t == last - 1)
        def _():
            half_take(0)
            half_give(1)

        compute(t)
        to_core(t)

        @pl.when(t + 1 < last)
        def _():
            pass_on(t + 1)

        pl.when(t == last - 1)(lambda: half_pass(0))
        outputs_of(t)
        to_side(t)

        @pl.when(t >= 1)
        def _():
            to_home(t - 1)

        weights_of(t)
        return 0

    lax.fori_loop(0, last, step, 0)
    half_take(1)
    half_compute(0)
    half_pass(1)
    to_home(last - 1)
    half_side(0)
    half_compute(1)
    half_home(0)
    slot = last % 2
    settle(op_ref.at[slot], last_sem.at[slot])
    half_side(1)
    for hh in range(his):
        op_ref[slot, :, half(hh)[1]] = (
            mm(hid_ref[hh * half_rows : (hh + 1) * half_rows, :], wd_ref[...], NT)
            .astype(BF16)
            .reshape((lo, MOST, width))
        )
    pltpu.make_async_copy(op_ref.at[slot], op_hbm.at[fl], last_sem.at[slot]).start()
    half_home(1)
    x_both = jnp.concatenate(
        [xb_ref[fl, :, half(hh)[1]].reshape(half_rows, width) for hh in range(his)], axis=0
    )
    accgu_ref[...] += mm(x_both, dgu_ref[...], TN)
    accd_ref[...] += mm(grow_ref[...], hid_ref[...], TN)

    inner = wd_ref.shape[1]
    gw_ref[0] = accgu_ref[:, :inner].astype(BF16)
    gw_ref[1] = accgu_ref[:, inner:].astype(BF16)
    gw_ref[2] = accd_ref[...].astype(BF16)
    pltpu.make_async_copy(gw_ref, gw_hbm, last_sem.at[4]).start()

    for m in range(E):
        settle(back_ref.at[m], br.at[m])
        settle(dgb_ref.at[m], tbr.at[m])
    pltpu.make_async_copy(back_ref, back_hbm, last_sem.at[5]).start()
    pltpu.make_async_copy(dgb_ref, dgb_hbm, last_sem.at[6]).start()

    for j in range(1, ranks):
        settle(tile_ref, zs.at[j])
    for j in range(ranks):
        for t in range(4):
            settle(tile_ref, ps.at[j, t])
        for t in range(3):
            settle(tile_ref, cs.at[t, j])

    @pl.when(at.f < ranks - 1)
    def _():
        settle(tail, hs)

    for k in range(1, E):
        settle(x_ref.at[0:MOST], xs.at[k])
        settle(gates_ref.at[0], ts.at[k])
        for w in range(3):
            settle(wd_ref.at[0:head_rows, 0:ff], ws.at[k, w])
    for i in range(3):
        settle(g_ref.at[0], gas.at[i])
    for j in range(ranks + 1):
        n = xor4(at.f, j) if j < ranks else ranks
        spot = pl.ds(0, MOST if j >= last else his * MOST)
        lines = pl.ds(0, 1 if j >= last else his)
        for i in range(3):
            settle(xb_ref.at[0, 0, spot], qs.at[n, i])
            settle(gb_ref.at[0, 0, lines], tqs.at[n, i])
        for i in range(2):
            settle(r1_ref.at[0, 0, spot], d1s.at[n, i])
            settle(dr1_ref.at[0, 0, lines], t1s.at[n, i])
        settle(r2_ref.at[0, spot], d2s.at[n])
        settle(dr2_ref.at[0, lines], t2s.at[n])
    for j in range(ranks):
        for hh in range(his):
            if j or hh:
                m = at.member(j, hh)[0]
                settle(back_ref.at[0], bs.at[m])
                settle(dgb_ref.at[0], tbs.at[m])
    settle(op_ref.at[0], last_sem.at[0])
    settle(op_ref.at[1], last_sem.at[1])
    settle(gw_ref, last_sem.at[4])
    settle(back_ref, last_sem.at[5])
    settle(dgb_ref, last_sem.at[6])
    for i, (name, _, _) in enumerate(KEPT):
        settle(kept[name], keep_sem.at[i])


SMALL_G1 = EXPERTS_ALL
SMALL_VC = SMALL_G1 + 2
SMALL_C = SMALL_VC + CONSTS
COL_POS, COL_C0, COL_C1, COL_R0, COL_R1, COL_W0, COL_W1 = range(16, 23)


def ahead(groups, ranks, *args):
    tok = args[13]
    w_gate = args[15]
    width = tok.shape[1]
    his = E // ranks
    lo = groups // his
    ff = w_gate.shape[2]
    dma = pltpu.SemaphoreType.DMA
    vm = pltpu.VMEM
    any_spec = pl.BlockSpec(memory_space=pl.ANY)
    block = (width // ranks + 8, 4 * (width // groups))
    rows = (his * MOST, width)
    kept = [(kept_shape(dims, width), dtype) for _, dims, dtype in KEPT]
    results = [
        ((ranks, lo) + rows, BF16),
        ((3, width, ff * his), BF16),
        ((E, MOST, width), BF16),
        ((E, 8, 128), F32),
    ]
    return pl.pallas_call(
        ahead_kernel,
        out_shape=[sds(*k) for k in kept + results],
        in_specs=[pl.BlockSpec(memory_space=pltpu.SMEM)] + whole(14) + [any_spec] * 3,
        out_specs=[any_spec] * (len(kept) + len(results)),
        scratch_shapes=[vm(*k) for k in kept]
        + [
            vm(block, BF16),
            vm((128, 128), F32),
            vm((groups, ranks) + block, BF16),
            vm((ROWS, width), BF16),
            vm((ROWS, width), BF16),
            vm((E, 8, 128), F32),
            vm((width, 2 * ff * his), BF16),
            vm((width, ff * his), BF16),
            vm((lo, ranks) + rows, BF16),
            vm((ranks, lo) + rows, BF16),
            vm((ranks, lo, his, 8, 128), F32),
            vm((ranks, lo) + rows, BF16),
            vm((2, lo) + rows, BF16),
            vm((ranks, 2) + rows, BF16),
            vm((ranks,) + rows, BF16),
            vm((ranks, lo, his, 8, 128), F32),
            vm((ranks, 2, his, 8, 128), F32),
            vm((ranks, his, 8, 128), F32),
            vm((width, 2 * ff * his), F32),
            vm((width, ff * his), F32),
            vm((lo * rows[0], ff * his), BF16),
            vm((lo * rows[0], 2 * ff * his), BF16),
            vm((3, width, ff * his), BF16),
            vm((E, MOST, width), BF16),
            vm((E, 8, 128), F32),
            dma((len(kept),)),
            dma((8,)),
            dma((4,)),
            dma((4, 4)),
            dma((3, 4)),
            dma,
            dma((E,)),
            dma((E, 3)),
            dma((3,)),
            dma((groups, ranks)),
            dma,
            dma((E,)),
            dma((E, 3)),
            dma((3,)),
            dma((E,)),
            dma((E,)),
            dma((ranks + 1, 3)),
            dma((ranks + 1, 3)),
            dma((ranks + 1, 2)),
            dma((ranks + 1, 2)),
            dma((ranks + 1,)),
            dma((ranks + 1,)),
            dma((E,)),
            dma((E,)),
            dma((E,)),
            dma((E,)),
            dma((ranks + 1, 3)),
            dma((ranks + 1, 3)),
            dma((ranks + 1, 2)),
            dma((ranks + 1, 2)),
            dma((ranks + 1,)),
            dma((ranks + 1,)),
            dma((E,)),
            dma((E,)),
        ],
        compiler_params=params(63, collective_id=1, has_side_effects=True),
        name="ahead",
    )(*args)


def end_kernel(
    cot_ref,
    tok_ref,
    prev_ref,
    wmix_ref,
    back_hbm,
    dgb_hbm,
    op_hbm,
    gw_hbm,
    *rest,
):
    n = len(KEPT)
    kept_hbm = by_name(rest[:n])
    (
        out_ref,
        dres_ref,
        gprev_ref,
        down_ref,
        back_ref,
        fin_ref,
        gmix_ref,
        t_ref,
    ) = rest[n : n + 8]
    kept = by_name(rest[n + 8 : 2 * n + 8])
    (
        dx_ref,
        dgb_ref,
        opl_ref,
        r1o_ref,
        r2o_ref,
        outb_ref,
        flat_ref,
        dhalo_ref,
        dm_ref,
        dq_ref,
        dk_ref,
        dv_ref,
        dqr_ref,
        dkr_ref,
        dvr_ref,
        full_ref,
        p_ref,
        r1_ref,
        r2_ref,
        r3_ref,
        r4_ref,
        mx_ref,
        mr_ref,
        mz_ref,
        load_sem,
        more_sem,
        o1s,
        o1r,
        o2s,
        o2r,
        obs,
        obr,
        ts,
        tr,
        hs,
        hr,
        s1,
        e1,
        s2,
        e2,
        s3,
        e3,
        s4,
        e4,
        ms,
        me,
        zs,
        ze,
    ) = rest[2 * n + 8 :]
    wf_ref, s_ref, halo_ref, cols_ref = kept["wf"], kept["s"], kept["halo"], kept["cols"]
    q_ref, k_ref, v_ref, n1_ref = kept["q"], kept["k"], kept["v"], kept["n1"]
    mix_ref, lse_ref = kept["mix"], kept["lse"]
    names = [item[0] for item in KEPT]

    def load(*which):
        for name in which:
            pltpu.make_async_copy(
                kept_hbm[name], kept[name], load_sem.at[names.index(name)]
            ).start()

    def ready(*which):
        for name in which:
            settle(kept[name], load_sem.at[names.index(name)])

    ranks = p_ref.shape[1]
    his = E // ranks
    groups = p_ref.shape[0]
    lo = groups // his
    at = Place(his, lo)
    width = cot_ref.shape[1]
    tile = t_ref.shape[2:]
    core = (at.core_peer, at.f)
    side = (at.side_peer, at.f)
    upper = (lo * (1 - at.hi) + at.l, at.f)
    peers = at.others() + [core, side]
    call(peers)
    pltpu.make_async_copy(back_hbm, dx_ref, more_sem.at[0]).start()
    pltpu.make_async_copy(dgb_hbm, dgb_ref, more_sem.at[1]).start()
    load("cols", "s", "resid", "probs", "mix", "wf", "q", "k", "v", "lse")
    for f2 in range(ranks):
        for i, l2 in enumerate((at.l, at.l2)):
            pltpu.make_async_copy(
                op_hbm.at[f2, l2], opl_ref.at[f2, i], more_sem.at[2 + 2 * f2 + i]
            ).start()
    load("cos", "sin", "n1", "inv1", "halo", "part")
    answer(peers)

    for f2 in range(ranks):
        send(op_hbm.at[f2, at.l1], r1o_ref.at[f2, 0], o1s.at[f2, 0], o1r.at[f2, 0], core)
        send(op_hbm.at[f2, at.l3], r1o_ref.at[f2, 1], o1s.at[f2, 1], o1r.at[f2, 1], core)

    for j in range(ranks):
        for hh in range(his):
            e, peer = at.member(j, hh)
            rows = pl.ds(aligned(e // his * tile[0], 16), tile[0])
            lanes_at = pl.ds(aligned(lax.rem(e, his) * tile[1], 128), tile[1])
            n = j * his + hh
            for w in range(3):
                block = gw_hbm.at[w, rows, lanes_at]
                if n == 0:
                    pltpu.make_async_copy(block, t_ref.at[at.m, w], tr.at[at.m, w]).start()
                else:
                    send(block, t_ref.at[at.m, w], ts.at[n, w], tr.at[at.m, w], peer)

    def add(ref, other):
        ref[...] = (ref[...].astype(F32) + other[...].astype(F32)).astype(BF16)

    ready("cols", "s", "resid", "probs")
    settle(dx_ref, more_sem.at[0])
    settle(dgb_ref, more_sem.at[1])
    flat = s_ref[...].T
    gain1 = flat[SMALL_G1 : SMALL_G1 + 1, :]
    gain2 = flat[SMALL_G1 + 1 : SMALL_G1 + 2, :]
    vc = flat[SMALL_VC : SMALL_VC + CONSTS, :]
    g = cot_ref[...].astype(F32)
    lanes = lane_iota(TOK_DEV)
    cols = cols_ref[...]

    def col(i):
        return pick(cols, lanes == i)

    gate0, gate1, gate_id, inv2 = col(0), col(1), col(2), col(3)
    resid = kept["resid"][...]
    unit2 = resid * inv2
    normed = unit2 * gain2
    narrow = normed.astype(BF16)
    c0, c1, r0, r1, wide0, wide1 = (
        col(COL_POS + 1 + i).astype(jnp.int32) for i in range(6)
    )
    slot = lane_iota(TOK_DEV, ROWS)
    hot0 = jnp.where(slot == c0, 1.0, 0.0).astype(BF16)
    hot1 = jnp.where(slot == c1, 1.0, 0.0).astype(BF16)
    dg0 = jnp.zeros((TOK_DEV, 1), F32)
    dg1 = jnp.zeros((TOK_DEV, 1), F32)
    for e in range(E):
        line = jnp.broadcast_to(dgb_ref[e][0:1, :], (TOK_DEV, 128))
        dg0 = dg0 + pick(line, lanes + e * 128 == wide0)
        dg1 = dg1 + pick(line, lanes + e * 128 == wide1)
    a_n = jnp.sum(g * normed, axis=1, keepdims=True)
    dg0 = jnp.where(r0 == E + 1, a_n, dg0)
    dg1 = jnp.where(r1 == E + 1, a_n, dg1)
    g_scale = gate_id
    dl = jnp.zeros((TOK_DEV, 128), F32)
    vmix = jnp.zeros((TOK_DEV, 128), F32)
    for c in range(CONSTS):
        gate_c, ma, mb = col(4 + 3 * c), col(5 + 3 * c), col(6 + 3 * c)
        a_v = jnp.sum(g * vc[c : c + 1, :], axis=1, keepdims=True)
        branch = ma * a_n + mb * a_v
        dg0 = jnp.where(r0 == E + 2 + c, branch, dg0)
        dg1 = jnp.where(r1 == E + 2 + c, branch, dg1)
        g_scale = g_scale + gate_c * ma
        da = gate_c * a_n
        db = gate_c * a_v
        mean = ma * da + mb * db
        dl = jnp.where(lanes == SMALL_C + 2 * c, ma * (da - mean), dl)
        dl = jnp.where(lanes == SMALL_C + 1 + 2 * c, mb * (db - mean), dl)
        vmix = jnp.where(lanes == SMALL_VC + c, gate_c * mb, vmix)
    probs = kept["probs"][...]
    d_probs = jnp.where(lanes == r0, dg0, 0.0) + jnp.where(lanes == r1, dg1, 0.0)
    d_logits = probs * (d_probs - jnp.sum(probs * d_probs, axis=1, keepdims=True))
    dl = jnp.where(lanes < EXPERTS_ALL, d_logits, dl)
    high = dl.astype(BF16)
    low = (dl - high.astype(F32)).astype(BF16)
    wr = s_ref[...].astype(BF16)
    d_normed = g_scale * g + mm(hot0 + hot1, dx_ref[...].reshape(ROWS, width))
    d_normed = d_normed + mm(high, wr, NT) + mm(low, wr, NT)
    vhigh = vmix.astype(BF16)
    vlow = (vmix - vhigh.astype(F32)).astype(BF16)
    tiny = mm(high, narrow, TN) + mm(low, narrow, TN)
    tiny = tiny + mm(vhigh, cot_ref[...], TN) + mm(vlow, cot_ref[...], TN)
    row_id = lax.broadcasted_iota(jnp.int32, (128, width), 0)
    dg2 = jnp.sum(d_normed * unit2, axis=0, keepdims=True)
    flat_ref[...] = jnp.where(row_id == SMALL_G1 + 1, dg2, tiny)
    n = d_normed * gain2
    dres_ref[...] = g + inv2 * (n - unit2 * jnp.mean(n * unit2, axis=1, keepdims=True))
    wmix = jnp.concatenate(
        [wmix_ref[...].astype(F32), jnp.zeros((EXPERTS_ALL, 128 - EXPERTS_ALL), F32)], axis=1
    ).astype(BF16)
    gprev_ref[...] = mm(wmix, high, NT) + mm(wmix, low, NT)
    prev = prev_ref[...]
    phigh = prev.astype(BF16)
    plow = (prev - phigh.astype(F32)).astype(BF16)
    mx_ref[0] = jnp.zeros(mx_ref.shape[1:], F32)
    mx_ref[0, 0:EXPERTS_ALL, :] = mm(phigh, high) + mm(phigh, low) + mm(plow, high)
    send(mx_ref.at[0], mr_ref.at[0], ms.at[0], me.at[0], core)

    for f2 in range(ranks):
        settle(opl_ref.at[f2, 1], more_sem.at[3 + 2 * f2])
        settle(r1o_ref.at[f2, 1], o1r.at[f2, 1])
        add(opl_ref.at[f2, 1], r1o_ref.at[f2, 1])
        send(opl_ref.at[f2, 1], r2o_ref.at[f2], o2s.at[f2], o2r.at[f2], side)
        settle(opl_ref.at[f2, 0], more_sem.at[2 + 2 * f2])
        settle(r1o_ref.at[f2, 0], o1r.at[f2, 0])
        add(opl_ref.at[f2, 0], r1o_ref.at[f2, 0])

    ready("mix", "wf", "q", "k", "v", "lse")
    scale = HEAD_DIM ** (-0.5)
    d_attn = dres_ref[...].astype(BF16)
    full_ref[3] = mm(mix_ref[...], d_attn, TN).astype(BF16)
    dm_ref[...] = mm(d_attn, wf_ref[3], NT).astype(BF16)
    dk_ref[...] = jnp.zeros_like(dk_ref)
    dv_ref[...] = jnp.zeros_like(dv_ref)

    def pair(p, _):
        span = pl.ds(pl.multiple_of(p * 128, 128), 128)
        for first, count in QBLOCKS:
            keys = key_span(first)
            ok = allowed_mask(cols_ref, first, count, COL_POS)[:, :keys]
            q = q_ref[pl.ds(first, count), span]
            dm = dm_ref[pl.ds(first, count), span]
            k = k_ref[pl.ds(first, keys), span]
            v = v_ref[pl.ds(first, keys), span]
            lane = lane_iota(count)
            key_lane = lane_iota(keys)
            lse = lse_ref[pl.ds(first, count), :]
            dq = dk = dv = None
            for h in range(2):
                mine = (lane < HEAD_DIM) if h == 0 else (lane >= HEAD_DIM)
                key_mine = (key_lane < HEAD_DIM) if h == 0 else (key_lane >= HEAD_DIM)
                qh = jnp.where(mine, q, jnp.zeros_like(q))
                dmh = jnp.where(mine, dm, jnp.zeros_like(dm))
                s = jnp.where(ok, mm(qh, k, NT) * scale, NEG)
                pr = jnp.where(ok, jnp.exp(s - pick(lse, lane == 2 * p + h)), 0.0)
                dp = mm(dmh, v, NT)
                delta = jnp.sum(pr * dp, axis=1, keepdims=True)
                ds = (pr * (dp - delta)).astype(BF16)
                pb = pr.astype(BF16)
                dqh = mm(ds, k)
                dkh = mm(ds, q, TN)
                dvh = mm(pb, dm, TN)
                dq = dqh if h == 0 else jnp.where(mine, dqh, dq)
                dk = dkh if h == 0 else jnp.where(key_mine, dkh, dk)
                dv = dvh if h == 0 else jnp.where(key_mine, dvh, dv)
            dq_ref[pl.ds(first, count), span] = dq * scale
            dk_ref[pl.ds(first, keys), span] += dk * scale
            dv_ref[pl.ds(first, keys), span] += dv

        return 0

    lax.fori_loop(0, HEADS // 2, pair, 0)

    ready("cos", "sin", "n1", "inv1", "halo", "part")

    for j in range(ranks):
        fj = xor4(at.f, j)
        settle(r2o_ref.at[fj], o2r.at[fj])
        add(opl_ref.at[fj, 0], r2o_ref.at[fj])
        for hh in range(his):
            m, peer = at.member(j, hh)
            rows = opl_ref.at[fj, 0, pl.ds(aligned(flip(at.hi, hh) * MOST, 16), MOST)]
            if j or hh:
                send(rows, outb_ref.at[at.m], obs.at[m], obr.at[at.m], peer)
            else:
                pltpu.make_async_copy(rows, outb_ref.at[at.m], obr.at[at.m]).start()

    def unturn(i, _):
        span = pl.ds(pl.multiple_of(i * 256, 256), 256)
        cos = kept["cos"][...]
        sin = kept["sin"][...]
        dqr_ref[:, span] = turn(dq_ref[:, span], cos[HALO:], -sin[HALO:]).astype(BF16)
        dkr_ref[:, span] = turn(dk_ref[:, span], cos, -sin).astype(BF16)
        dvr_ref[:, span] = dv_ref[:, span].astype(BF16)
        return 0

    lax.fori_loop(0, width // 256, unturn, 0)
    d_all = mm(dkr_ref[...], wf_ref[1], NT) + mm(dvr_ref[...], wf_ref[2], NT)
    dhalo_ref[...] = (d_all[:HALO] * gain1).astype(BF16)

    @pl.when(at.f > 0)
    def _():
        send(dhalo_ref, back_ref, hs, hr, (at.g, at.f - 1))

    @pl.when(at.f == ranks - 1)
    def _():
        back_ref[...] = jnp.zeros_like(back_ref)

    full_ref[0] = mm(n1_ref[HALO:, :], dqr_ref[...], TN).astype(BF16)
    full_ref[1] = mm(n1_ref[...], dkr_ref[...], TN).astype(BF16)
    full_ref[2] = mm(n1_ref[...], dvr_ref[...], TN).astype(BF16)
    d_own = d_all[HALO:] + mm(dqr_ref[...], wf_ref[0], NT)
    inv1 = kept["inv1"][:, 0:1]
    unit_own = tok_ref[...].astype(F32) * inv1[HALO:]
    unit_halo = halo_ref[...].astype(F32) * inv1[:HALO]
    dg1 = jnp.sum(d_own * unit_own, axis=0, keepdims=True) + jnp.sum(
        d_all[:HALO] * unit_halo, axis=0, keepdims=True
    )
    down_ref[...] = d_own * gain1
    flat_ref[...] = jnp.where(row_id == SMALL_G1, dg1, flat_ref[...])

    part_cols = width // groups
    head_rows = width // ranks

    def pack(f2, _):
        rows = pl.ds(aligned(f2 * head_rows, 16), head_rows)
        for g2 in range(groups):
            pieces = [
                full_ref[w, rows, g2 * part_cols : (g2 + 1) * part_cols] for w in range(4)
            ]
            p_ref[g2, f2, 0:head_rows, :] = jnp.concatenate(pieces, axis=1)
        return 0

    lax.fori_loop(0, ranks, pack, 0)
    column = flat_ref[...].T
    per = width // (groups * ranks)
    for g2 in range(groups):
        for f2 in range(ranks):
            base = (g2 * ranks + f2) * per
            pieces = [column[base + 8 * i : base + 8 * i + 8, :] for i in range(per // 8)]
            p_ref[g2, f2, head_rows : head_rows + 8, :] = jnp.concatenate(
                pieces, axis=1
            ).astype(BF16)

    c = lax.rem(at.g, 2)
    x = lax.rem(at.g // 2, 2)
    y = at.hi

    def block(y2, x2, c2):
        return (y2 * 2 + x2) * 2 + c2

    half = ranks // 2
    quads = [(1 - y, 1 - x), (y, 1 - x), (1 - y, x), (y, x)]
    for i, (y2, x2) in enumerate(quads):
        spot = y2 * 2 + x2
        send(p_ref.at[block(y2, x2, 1 - c)], r1_ref.at[spot], s1.at[i], e1.at[spot], core)
    settle(mr_ref.at[0], me.at[0])
    mx_ref[1] = mx_ref[0] + mr_ref[0]
    send(mx_ref.at[1], mr_ref.at[1], ms.at[1], me.at[1], side)
    for i, (y2, x2) in enumerate(quads):
        spot = y2 * 2 + x2
        settle(r1_ref.at[spot], e1.at[spot])
        add(p_ref.at[block(y2, x2, c)], r1_ref.at[spot])
        if i == 0:
            here = p_ref.at[block(1 - y, 1 - x, c)]
            send(here.at[0:half], r2_ref.at[0, 1 - y], s2.at[0, 0], e2.at[0, 1 - y], side)
            send(here.at[half:], r2_ref.at[1, 1 - x], s2.at[1, 0], e2.at[1, 1 - x], upper)
        if i == 1:
            here = p_ref.at[block(y, 1 - x, c)]
            send(here.at[0:half], r2_ref.at[0, y], s2.at[0, 1], e2.at[0, y], side)
        if i == 2:
            here = p_ref.at[block(1 - y, x, c)]
            send(here.at[half:], r2_ref.at[1, x], s2.at[1, 1], e2.at[1, x], upper)
    settle(mr_ref.at[1], me.at[1])
    mx_ref[2] = mx_ref[1] + mr_ref[1]
    send(mx_ref.at[2], mr_ref.at[2], ms.at[2], me.at[2], upper)
    settle(r2_ref.at[0, 1 - y], e2.at[0, 1 - y])
    add(p_ref.at[block(1 - y, x, c), 0:half], r2_ref.at[0, 1 - y])
    send(
        p_ref.at[block(1 - y, x, c), 0:half], r3_ref.at[0], s3.at[0], e3.at[0], upper
    )
    settle(r2_ref.at[1, 1 - x], e2.at[1, 1 - x])
    add(p_ref.at[block(y, 1 - x, c), half:], r2_ref.at[1, 1 - x])
    send(p_ref.at[block(y, 1 - x, c), half:], r3_ref.at[1], s3.at[1], e3.at[1], side)
    settle(r2_ref.at[0, y], e2.at[0, y])
    add(p_ref.at[at.g, 0:half], r2_ref.at[0, y])
    settle(r2_ref.at[1, x], e2.at[1, x])
    add(p_ref.at[at.g, half:], r2_ref.at[1, x])
    settle(mr_ref.at[2], me.at[2])
    mx_ref[3] = mx_ref[2] + mr_ref[2]
    mz_ref[at.f] = mx_ref[3]
    for i in range(2):
        settle(r3_ref.at[i], e3.at[i])
        add(p_ref.at[at.g, i * half : (i + 1) * half], r3_ref.at[i])
    for j in range(1, ranks):
        f2 = xor4(at.f, j)
        send(p_ref.at[at.g, f2], r4_ref.at[at.f], s4.at[j], e4.at[at.f], (at.g, f2))
        send(mx_ref.at[3], mz_ref.at[at.f], zs.at[j], ze.at[at.f], (at.g, f2))
    for m in range(E):
        settle(outb_ref.at[m], obr.at[m])
    rows = outb_ref[...].reshape(ROWS, width)
    cols = cols_ref[...]
    c0 = pick(cols, lanes == COL_C0).astype(jnp.int32)
    c1 = pick(cols, lanes == COL_C1).astype(jnp.int32)
    y0 = mm(jnp.where(slot == c0, 1.0, 0.0).astype(BF16), rows)
    y1 = mm(jnp.where(slot == c1, 1.0, 0.0).astype(BF16), rows)
    gate0 = pick(cols, lanes == 0)
    gate1 = pick(cols, lanes == 1)
    out_ref[...] = (kept["part"][...] + gate0 * y0 + gate1 * y1).astype(BF16)

    total = p_ref[at.g, at.f].astype(F32)
    for j in range(1, ranks):
        f2 = xor4(at.f, j)
        settle(r4_ref.at[f2], e4.at[f2])
        total = total + r4_ref[f2].astype(F32)
        settle(mz_ref.at[f2], ze.at[f2])
    fin_ref[...] = total
    gmix_ref[...] = (mz_ref[0] + mz_ref[1]) + (mz_ref[2] + mz_ref[3])

    for f2 in range(ranks):
        for i in range(2):
            settle(r1o_ref.at[0, 0], o1s.at[f2, i])
        settle(r2o_ref.at[0], o2s.at[f2])
    for j in range(ranks):
        for hh in range(his):
            if j or hh:
                settle(outb_ref.at[0], obs.at[at.member(j, hh)[0]])
    for m in range(E):
        for w in range(3):
            settle(t_ref.at[m, w], tr.at[m, w])
    for i in range(1, E):
        for w in range(3):
            settle(t_ref.at[0, w], ts.at[i, w])

    @pl.when(at.f > 0)
    def _():
        settle(dhalo_ref, hs)

    @pl.when(at.f < ranks - 1)
    def _():
        settle(back_ref, hr)

    for i in range(4):
        settle(r1_ref.at[0], s1.at[i])
    for i in range(2):
        for n2 in range(2):
            settle(r2_ref.at[0, 0], s2.at[i, n2])
        settle(r3_ref.at[0], s3.at[i])
    for i in range(3):
        settle(mr_ref.at[0], ms.at[i])
    for j in range(1, ranks):
        settle(r4_ref.at[0], s4.at[j])
        settle(mz_ref.at[0], zs.at[j])


def end(groups, ranks, tile, *args):
    cot = args[0]
    width = cot.shape[1]
    dma = pltpu.SemaphoreType.DMA
    vm = pltpu.VMEM
    block = (width // ranks + 8, 4 * (width // groups))
    half = ranks // 2
    rows = (E // ranks * MOST, width)
    kept = [(kept_shape(dims, width), dtype) for _, dims, dtype in KEPT]
    any_spec = pl.BlockSpec(memory_space=pl.ANY)
    return pl.pallas_call(
        end_kernel,
        out_shape=[
            sds((TOK_DEV, width), BF16),
            sds((TOK_DEV, width), F32),
            sds((EXPERTS_ALL, TOK_DEV), F32),
            sds((TOK_DEV, width), F32),
            sds((HALO, width), BF16),
            sds(block, F32),
            sds((16, 128), F32),
            sds((E, 3) + tile, BF16),
        ],
        in_specs=whole(4) + [any_spec] * (4 + len(kept)),
        out_specs=whole(7) + [any_spec],
        scratch_shapes=[vm(*k) for k in kept]
        + [
            vm((E, MOST, width), BF16),
            vm((E, 8, 128), F32),
            vm((ranks, 2) + rows, BF16),
            vm((ranks, 2) + rows, BF16),
            vm((ranks,) + rows, BF16),
            vm((E, MOST, width), BF16),
            vm((128, width), F32),
            vm((HALO, width), BF16),
            vm((TOK_DEV, width), BF16),
            vm((TOK_DEV, width), F32),
            vm((KEYS, width), F32),
            vm((KEYS, width), F32),
            vm((TOK_DEV, width), BF16),
            vm((KEYS, width), BF16),
            vm((KEYS, width), BF16),
            vm((4, width, width), BF16),
            vm((groups, ranks) + block, BF16),
            vm((4, ranks) + block, BF16),
            vm((2, 2, half) + block, BF16),
            vm((2, half) + block, BF16),
            vm((ranks,) + block, BF16),
            vm((4, 16, 128), F32),
            vm((3, 16, 128), F32),
            vm((ranks, 16, 128), F32),
            dma((len(kept),)),
            dma((2 + 2 * ranks,)),
            dma((ranks, 2)),
            dma((ranks, 2)),
            dma((ranks,)),
            dma((ranks,)),
            dma((E,)),
            dma((E,)),
            dma((E, 3)),
            dma((E, 3)),
            dma,
            dma,
            dma((4,)),
            dma((4,)),
            dma((2, 2)),
            dma((2, 2)),
            dma((2,)),
            dma((2,)),
            dma((4,)),
            dma((4,)),
            dma((3,)),
            dma((3,)),
            dma((4,)),
            dma((4,)),
        ],
        compiler_params=params(63, collective_id=3, has_side_effects=True),
        name="end",
    )(*args)


def store_kernel(
    t_hbm,
    fin_hbm,
    dres_hbm,
    down_hbm,
    back_hbm,
    tok_hbm,
    inv1_hbm,
    out_from,
    gprev_from,
    gmix_from,
    gate_hbm,
    up_hbm,
    downw_hbm,
    gq_ref,
    gk_ref,
    gv_ref,
    go_ref,
    router_ref,
    const_ref,
    vconst_ref,
    gain1_ref,
    gain2_ref,
    gtok_hbm,
    out_to,
    gprev_to,
    gmix_ref,
    t_ref,
    wide_ref,
    fin_ref,
    dres_ref,
    down_ref,
    back_ref,
    tok_ref,
    inv1_ref,
    gtok_ref,
    mixin_ref,
    out_ref,
    gprev_ref,
    t_sem,
    wide_sem,
    in_sem,
    gtok_sem,
    pass_sem,
):
    pairs = [
        (dres_hbm, dres_ref),
        (down_hbm, down_ref),
        (back_hbm, back_ref),
        (tok_hbm, tok_ref),
        (inv1_hbm, inv1_ref),
        (fin_hbm, fin_ref),
        (gmix_from, mixin_ref),
        (out_from, out_ref),
        (gprev_from, gprev_ref),
    ]
    for i, (src, dst) in enumerate(pairs):
        pltpu.make_async_copy(src, dst, in_sem.at[i]).start()
    for e in range(E):
        pltpu.make_async_copy(t_hbm.at[e], t_ref.at[e], t_sem.at[e]).start()
    for i in range(5):
        settle(pairs[i][1], in_sem.at[i])
    width = tok_ref.shape[1]
    inv1 = inv1_ref[HALO:, 0:1]
    unit = tok_ref[...].astype(F32) * inv1
    m = jnp.concatenate(
        [down_ref[: TOK_DEV - HALO, :], down_ref[TOK_DEV - HALO :, :] + back_ref[...]], axis=0
    )
    d_dealt = inv1 * (m - unit * jnp.mean(m * unit, axis=1, keepdims=True))
    gtok_ref[...] = dres_ref[...] + d_dealt.astype(BF16).astype(F32)
    pltpu.make_async_copy(gtok_ref, gtok_hbm, gtok_sem).start()
    settle(out_ref, in_sem.at[7])
    pltpu.make_async_copy(out_ref, out_to, pass_sem.at[0]).start()
    settle(gprev_ref, in_sem.at[8])
    pltpu.make_async_copy(gprev_ref, gprev_to, pass_sem.at[1]).start()
    for e in range(E):
        settle(t_ref.at[e], t_sem.at[e])
        wide_ref[e] = t_ref[e].astype(F32)
        for w, out in enumerate((gate_hbm, up_hbm, downw_hbm)):
            pltpu.make_async_copy(wide_ref.at[e, w], out.at[e], wide_sem.at[e, w]).start()
    settle(fin_ref, in_sem.at[5])
    head_rows, part_cols = gq_ref.shape
    for w, ref in enumerate((gq_ref, gk_ref, gv_ref, go_ref)):
        ref[...] = fin_ref[0:head_rows, w * part_cols : (w + 1) * part_cols]
    per = router_ref.shape[1]
    column = jnp.concatenate(
        [
            fin_ref[head_rows : head_rows + 8, 128 * i : 128 * i + 128]
            for i in range(per // 8)
        ]
        + [jnp.zeros((128 - per, 128), F32)],
        axis=0,
    )
    flat = column.T[:, 0:per]
    router_ref[...] = flat[0:EXPERTS_ALL]
    gain1_ref[...] = flat[SMALL_G1 : SMALL_G1 + 1]
    gain2_ref[...] = flat[SMALL_G1 + 1 : SMALL_G1 + 2]
    vconst_ref[...] = flat[SMALL_VC : SMALL_VC + CONSTS]
    const_ref[...] = flat[SMALL_C : SMALL_C + 2 * CONSTS]
    settle(mixin_ref, in_sem.at[6])
    gmix_ref[...] = mixin_ref[0:EXPERTS_ALL, 0:EXPERTS_ALL]
    settle(out_ref, pass_sem.at[0])
    settle(gprev_ref, pass_sem.at[1])
    settle(gtok_ref, gtok_sem)
    for e in range(E):
        for w in range(3):
            settle(wide_ref.at[e, w], wide_sem.at[e, w])


def store(t, fin, dres, down, back, tok, inv1, out, gprev, gmix, groups, ranks):
    width = tok.shape[1]
    rows, cols = t.shape[2:]
    per = width // (groups * ranks)
    any_spec = pl.BlockSpec(memory_space=pl.ANY)
    dma = pltpu.SemaphoreType.DMA
    vm = pltpu.VMEM
    return pl.pallas_call(
        store_kernel,
        out_shape=[sds((E, rows, cols), F32)] * 3
        + [sds((width // ranks, width // groups), F32)] * 4
        + [
            sds((EXPERTS_ALL, per), F32),
            sds((2 * CONSTS, per), F32),
            sds((CONSTS, per), F32),
            sds((1, per), F32),
            sds((1, per), F32),
            sds(tok.shape, F32),
            sds(out.shape, BF16),
            sds(gprev.shape, F32),
            sds((EXPERTS_ALL, EXPERTS_ALL), F32),
        ],
        in_specs=[any_spec] * 10,
        out_specs=[any_spec] * 3 + whole(9) + [any_spec] * 3 + whole(1),
        scratch_shapes=[
            vm(t.shape, BF16),
            vm(t.shape, F32),
            vm(fin.shape, F32),
            vm(dres.shape, F32),
            vm(down.shape, F32),
            vm(back.shape, BF16),
            vm(tok.shape, BF16),
            vm(inv1.shape, F32),
            vm(tok.shape, F32),
            vm(gmix.shape, F32),
            vm(out.shape, BF16),
            vm(gprev.shape, F32),
            dma((E,)),
            dma((E, 3)),
            dma((9,)),
            dma,
            dma((2,)),
        ],
        compiler_params=params(63),
        name="store",
    )(t, fin, dres, down, back, tok, inv1, out, gprev, gmix)


def fast_device(
    tokens,
    cotangent,
    prev_logits,
    lengths,
    dealing,
    routes,
    gain_one,
    w_query,
    w_key,
    w_value,
    w_out,
    gain_two,
    w_router,
    w_mix,
    w_const,
    v_const,
    w_gate,
    w_up,
    w_down,
):
    groups = lax.axis_size("grp")
    ranks = lax.axis_size("fsdp")
    kept = len(KEPT)
    prev = prev_logits.T
    outs = ahead(
        groups,
        ranks,
        lengths,
        routes.T,
        prev,
        w_mix,
        w_router.T,
        gain_one[None, :],
        gain_two[None, :],
        w_const.T,
        v_const.T,
        w_query,
        w_key,
        w_value,
        w_out,
        tokens,
        cotangent,
        w_gate,
        w_up,
        w_down.transpose(0, 2, 1),
    )
    parts, grads, dx, routed = outs[kept:]
    output, dres, gprev, down, back, fin, gmix, tiles = end(
        groups,
        ranks,
        w_gate.shape[1:],
        cotangent,
        tokens,
        prev,
        w_mix,
        dx,
        routed,
        parts,
        grads,
        *outs[:kept],
    )
    inv1 = by_name(outs[:kept])["inv1"]
    (
        gate,
        up,
        downw,
        gq,
        gk,
        gv,
        go,
        router,
        const,
        vconst,
        gain1,
        gain2,
        grad_tokens,
        output,
        gprev,
        gmix,
    ) = store(
        tiles, fin, dres, down, back, tokens, inv1, output, gprev, gmix, groups, ranks
    )
    return (
        output,
        grad_tokens,
        gprev.T,
        gain1[0],
        gq,
        gk,
        gv,
        go,
        gain2[0],
        router.T,
        gmix,
        const.T,
        vconst.T,
        gate,
        up,
        downw.transpose(0, 2, 1),
    )


def suits(mesh):
    return mesh.shape["fsdp"] == 4 and mesh.shape["grp"] == 8


def solution(mesh):
    return jax.shard_map(
        fast_device if suits(mesh) else per_device,
        mesh=mesh,
        in_specs=(
            P(("grp", "fsdp"), None),
            P(("grp", "fsdp"), None),
            P(("grp", "fsdp"), None),
            P("grp", None),
            P("grp", None),
            P(("grp", "fsdp"), None),
            P(("grp", "fsdp")),
            P("fsdp", "grp"),
            P("fsdp", "grp"),
            P("fsdp", "grp"),
            P("fsdp", "grp"),
            P(("grp", "fsdp")),
            P(("grp", "fsdp"), None),
            P(),
            P(("grp", "fsdp"), None),
            P(("grp", "fsdp"), None),
            P(None, "fsdp", "grp"),
            P(None, "fsdp", "grp"),
            P(None, "grp", "fsdp"),
        ),
        out_specs=(
            P(("grp", "fsdp"), None),
            P(("grp", "fsdp"), None),
            P(("grp", "fsdp"), None),
            P(("grp", "fsdp")),
            P("fsdp", "grp"),
            P("fsdp", "grp"),
            P("fsdp", "grp"),
            P("fsdp", "grp"),
            P(("grp", "fsdp")),
            P(("grp", "fsdp"), None),
            P(),
            P(("grp", "fsdp"), None),
            P(("grp", "fsdp"), None),
            P(None, "fsdp", "grp"),
            P(None, "fsdp", "grp"),
            P(None, "grp", "fsdp"),
        ),
        check_vma=False,
    )
```
